256 devices in a mesh: tm: 32 (over z, x_hi, core), dish: 8 (over y, x_lo).
Axes of the slice: x: 4 (x_hi: 2, x_lo: 2; x = x_hi * 2 + x_lo), y: 4, z: 8, core: 2. Of those that a mesh axis runs over, the one named last changes fastest.
Arguments:
- voltages: bfloat16 [2, 64, 131072], P(None, 'dish', 'tm'), may hold values from -6 to 6
- beam_weights: bfloat16 [2, 64], P(None, 'dish'), may hold values from -0.75 to 0.75
- phase_bins: int32 [131072], P('tm'), may hold values from 0 to 1023, as said below
Outputs:
- spectrum: float32 [2048, 2, 1024], P('dish', None, 'tm')
The draws below stay inside these ranges and needn't reach their ends.
Inputs may be any that keep to these rules, and one draw needn't show every extreme that they name: `phase_bins`: from each time sample to the next the bin stays or advances by one, wrapping from 1023 to 0; every bin occurs.
All inputs are finite; a program needn't handle non-finite values.
Results may differ from the reference program's by a relative error of at most 0.0039.
Values may be sent and summed in bfloat16 or wider, within the bound.
No kernel may reach another device: no remote copies, remote signals or barrier semaphores. Data moves between devices by JAX's collectives and lax.ppermute only.
A program may use at most 64 MiB of HBM per device.

```python
import math
import jax
import jax.numpy as jnp
from jax import lax

DISHES = 64
PH = 1024
LAGS = 2048
SAMPLES = 131072


def draw_phase_bins(key, part):
    tick_total = 1048576
    first_key, second_key = jax.random.split(jax.random.fold_in(key, 17))
    increments = jax.random.randint(first_key, (SAMPLES,), tick_total // (4 * PH), tick_total // PH)
    offset = jax.random.randint(second_key, (), 0, tick_total)
    phase_ticks = (offset + jnp.cumsum(increments)) % tick_total
    return (phase_ticks * PH // tick_total).astype(jnp.int32)


def steps_of(stream_key, extent, cuts, low, top_value):
    def one(position, shards_of):
        steps = jax.random.uniform(jax.random.fold_in(jax.random.fold_in(stream_key, 6), position), (shards_of,), jnp.float32, low / len(cuts), top_value / len(cuts))
        return jnp.repeat(jnp.exp(steps), extent[position] // shards_of).reshape((-1,) + (1,) * (len(extent) - position - 1))

    gain = one(*cuts[0])
    for cut in cuts[1:]:
        gain = gain * one(*cut)
    return gain


def bell_draw(key, shape, deviation, most, cuts=(), kind=jnp.bfloat16):
    drawn = jax.random.normal(key, shape, jnp.float32) * deviation
    if len(cuts) > 0:
        drawn = steps_of(key, shape, cuts, -0.22, 0.18) * drawn
    return jnp.clip(drawn, min=-most, max=most).astype(kind)


def setup_inputs(seed: int = 0) -> dict:
    arg_keys = jax.random.split(jax.random.key(seed), 4)
    voltages = bell_draw(arg_keys[0], (2, DISHES, SAMPLES), 1.0, 6.0, ((1, 8), (2, 32)))
    beam_weights = bell_draw(arg_keys[1], (2, DISHES), DISHES ** -0.5, 0.75, ((1, 8),))
    phase_bins = draw_phase_bins(jax.random.fold_in(arg_keys[3], 71), 0)
    return {"voltages": voltages, "beam_weights": beam_weights, "phase_bins": phase_bins}


def reference(voltages, beam_weights, phase_bins):
    real_beam = jnp.dot(beam_weights[0], voltages[0], preferred_element_type=jnp.float32) - jnp.dot(beam_weights[1], voltages[1], preferred_element_type=jnp.float32)
    imag_beam = jnp.dot(beam_weights[1], voltages[0], preferred_element_type=jnp.float32) + jnp.dot(beam_weights[0], voltages[1], preferred_element_type=jnp.float32)
    beam_pair = jnp.stack([real_beam, imag_beam]).astype(jnp.bfloat16)
    padded = jnp.pad(beam_pair.astype(jnp.float32), ((0, 0), (0, LAGS)))
    block_rows = min(512, SAMPLES)
    block_total = SAMPLES // block_rows
    lag_grid = jnp.arange(block_rows, dtype=jnp.int32)[:, None] + jnp.arange(LAGS, dtype=jnp.int32)[None, :]

    def fold_step(carry, block_index):
        row_start = (block_index * block_rows).astype(jnp.int32)
        segment = lax.dynamic_slice_in_dim(padded, row_start, block_rows + LAGS, 1)
        hankel = segment[:, lag_grid]
        current = segment[:, :block_rows]
        real_term = current[0][:, None] * hankel[0] + current[1][:, None] * hankel[1]
        imag_term = current[0][:, None] * hankel[1] - current[1][:, None] * hankel[0]
        bin_block = lax.dynamic_slice_in_dim(phase_bins, row_start, block_rows)
        real_sum = jax.ops.segment_sum(real_term, bin_block, PH)
        imag_sum = jax.ops.segment_sum(imag_term, bin_block, PH)
        return ((carry[0] + real_sum, carry[1] + imag_sum), None)
    zero_fold = jnp.zeros((PH, LAGS), jnp.float32)
    folds, unused = lax.scan(fold_step, (zero_fold, zero_fold), jnp.arange(block_total, dtype=jnp.int32))
    scale_factor = 1.0 / math.sqrt(LAGS * SAMPLES / PH)
    transformed = jnp.fft.fft(folds[0] + 1j * folds[1], axis=1) * scale_factor
    real_out = jnp.real(transformed).astype(jnp.float32)
    imag_out = jnp.imag(transformed).astype(jnp.float32)
    return jnp.stack([real_out.T, imag_out.T], 1)
```

```python
import functools
import math

import jax
import jax.numpy as jnp
import numpy as np
from jax import lax
from jax.experimental import pallas as pl
from jax.experimental.pallas import tpu as pltpu
from jax.sharding import PartitionSpec as P

PH = 1024
LAGS = 2048
SAMPLES = 131072
DISH_WAYS = 8
TM_WAYS = 32
CHIPS = 16
LOCAL = SAMPLES // TM_WAYS
GRAIN = 128
GRAINS = SAMPLES // GRAIN
PER_BLOCK = LOCAL // GRAIN
SPAN = LAGS // GRAIN
BINS = PH // TM_WAYS
FREQS = LAGS // DISH_WAYS
SLOTS = 128
GROUP = 8
SCALE = 1.0 / math.sqrt(LAGS * SAMPLES / PH)

F32 = jnp.float32
BF16 = jnp.bfloat16


def dot(a, b, dims=(((1,), (0,)), ((), ()))):
    return lax.dot_general(a, b, dims, preferred_element_type=F32)


def hi_lo(value):
    hi = value.astype(BF16)
    return hi, (value - hi.astype(F32)).astype(BF16)


def tables():
    grain = np.arange(GRAIN)
    freq = np.arange(FREQS)
    angle = 2 * np.pi * np.outer(grain, freq) / LAGS
    base = np.concatenate([np.cos(angle), np.sin(angle)], 1).astype(np.float32)
    eighth = 2 * np.pi * np.outer(grain, np.arange(DISH_WAYS)) / DISH_WAYS
    turn = np.zeros((GRAIN, 128), np.float32)
    turn[:, :8] = np.cos(eighth)
    turn[:, 8:16] = np.sin(eighth)
    fine = 2 * np.pi * np.outer(grain, np.arange(2 * GRAIN)) / (2 * GRAIN)
    cos2, sin2 = np.cos(fine), np.sin(fine)
    fold2 = np.block([[cos2, sin2], [sin2, -cos2]]).astype(np.float32)
    step2 = np.block([[cos2, -sin2], [sin2, cos2]]).astype(np.float32)
    keep = (grain >= 1)[None, :] / (2.0 * GRAIN)
    back = np.block([[cos2.T * keep, -sin2.T * keep], [sin2.T * keep, cos2.T * keep]])
    sixteenth = 2 * np.pi * np.outer(np.arange(SPAN), freq) / SPAN
    phase = np.concatenate([np.cos(sixteenth), np.sin(sixteenth)], 1).astype(np.float32)
    index = np.zeros((GRAINS, 128), np.float32)
    index[:, 0] = np.arange(GRAINS) // SPAN
    index[:, 1] = np.arange(GRAINS) % SPAN
    return (
        jnp.asarray(base),
        jnp.asarray(turn),
        jnp.asarray(fold2).astype(BF16),
        jnp.asarray(step2).astype(BF16),
        jnp.asarray(back.astype(np.float32)).astype(BF16),
        jnp.asarray(phase),
        jnp.asarray(index).astype(BF16),
    )


def beam_kernel(volts_ref, weights_ref, out_ref):
    weights = weights_ref[...]
    first = dot(weights, volts_ref[0])
    second = dot(weights, volts_ref[1])
    real = first[0:1] - second[1:2]
    imag = first[1:2] + second[0:1]
    for row in range(PER_BLOCK):
        part = slice(row * GRAIN, (row + 1) * GRAIN)
        out_ref[0, row : row + 1, :] = real[:, part]
        out_ref[0, PER_BLOCK + row : PER_BLOCK + row + 1, :] = imag[:, part]
    rows = out_ref[0]
    for way in range(1, DISH_WAYS):
        out_ref[way] = rows


def pack_kernel(parts_ref, bins_ref, out_ref):
    total = parts_ref[0]
    for way in range(1, DISH_WAYS):
        total = total + parts_ref[way]
    bins = bins_ref[...]
    high = bins >> 5
    coded = ((bins & 31) + 32).astype(F32)
    for bit in range(5):
        coded = coded * jnp.where((high >> bit) & 1 == 1, float(2 ** (2**bit)), 1.0)
    coded = coded * (2.0**-16)
    rows = jnp.concatenate([total.astype(BF16), coded.astype(BF16)], 0)
    for chip in range(CHIPS):
        out_ref[chip] = rows


def two_to(exponent):
    value = jnp.float32(2.0**-16)
    for bit in range(5):
        value = value * jnp.where((exponent >> bit) & 1 == 1, jnp.float32(2 ** (2**bit)), jnp.float32(1.0))
    return value


def spectrum_kernel(
    ids,
    own_ref, other_ref, base_ref, turn_ref, fold2_ref, step2_ref, back_ref, phase_ref, index_ref,
    out_ref,
    beam_s, code_s, fold_s, step_s, last_s, phase_s, zhi_s, zlo_s,
    gbeam_s, gcode_s, gdft_s, gstep_s, acc_s,
):
    owner, dish, core = ids()
    for chip in range(CHIPS):
        for ref, which in ((own_ref, core), (other_ref, 1 - core)):
            start = pl.multiple_of((2 * chip + which) * PER_BLOCK, PER_BLOCK)
            rows = pl.ds(start, PER_BLOCK)
            beam_s[rows, 0:GRAIN] = ref[chip, 0:PER_BLOCK, :]
            beam_s[rows, GRAIN:] = ref[chip, PER_BLOCK : 2 * PER_BLOCK, :]
            code_s[rows, :] = ref[chip, 2 * PER_BLOCK :, :]
    beam_s[GRAINS:, :] = jnp.zeros((SPAN, 2 * GRAIN), BF16)
    lane = lax.broadcasted_iota(jnp.int32, (GRAIN, 128), 1)
    turn = turn_ref[...]
    cos8 = jnp.sum(jnp.where(lane == dish, turn, 0.0), axis=1, keepdims=True)
    sin8 = jnp.sum(jnp.where(lane == dish + 8, turn, 0.0), axis=1, keepdims=True)
    cos0, sin0 = base_ref[:, :FREQS], base_ref[:, FREQS:]
    cosine = (cos0 * cos8 - sin0 * sin8).astype(BF16)
    sine = (sin0 * cos8 + cos0 * sin8).astype(BF16)
    fold_s[:GRAIN, :FREQS] = cosine
    fold_s[:GRAIN, FREQS : 2 * FREQS] = sine
    fold_s[GRAIN:, :FREQS] = sine
    fold_s[GRAIN:, FREQS : 2 * FREQS] = -cosine
    fold_s[:, 2 * FREQS :] = fold2_ref[...]
    step_s[:GRAIN, :FREQS] = cosine
    step_s[:GRAIN, FREQS:] = -sine
    step_s[GRAIN:, :FREQS] = sine
    step_s[GRAIN:, FREQS:] = cosine
    last_s[:GRAIN, :FREQS] = cosine
    last_s[:GRAIN, FREQS:] = sine
    last_s[GRAIN:, :FREQS] = -sine
    last_s[GRAIN:, FREQS:] = cosine
    cos16, sin16 = phase_ref[:, :FREQS], phase_ref[:, FREQS:]
    phase_s[...] = jnp.zeros(phase_s.shape, BF16)
    for at, part in ((0, cos16), (FREQS, sin16)):
        hi, lo = hi_lo(part)
        phase_s[0:SPAN, at : at + FREQS] = hi
        phase_s[SPAN : 2 * SPAN, at : at + FREQS] = lo
    turns = 128 // SPAN
    cos_rows = jnp.concatenate([cos16] * turns, 0)
    sin_rows = jnp.concatenate([sin16] * turns, 0)
    for tile in range(GRAINS // 128):
        rows = slice(tile * 128, tile * 128 + 128)
        both = dot(beam_s[rows, :], step_s[...])
        real, imag = both[:, :FREQS], both[:, FREQS:]
        zhi_s[rows, :FREQS], zlo_s[rows, :FREQS] = hi_lo(real * cos_rows + imag * sin_rows)
        zhi_s[rows, FREQS:], zlo_s[rows, FREQS:] = hi_lo(imag * cos_rows - real * sin_rows)
    unit = two_to(owner)
    code = code_s[...].astype(F32)
    inside = jnp.where((code >= unit * 32.0) & (code < unit * 64.0), 1.0, 0.0).astype(BF16)
    hits = dot(jnp.ones((8, GRAIN), BF16), inside, (((1,), (1,)), ((), ())))
    mask = jnp.where(hits > 0.0, 1.0, 0.0)
    upper = (
        lax.broadcasted_iota(jnp.int32, (128, 128), 0) <= lax.broadcasted_iota(jnp.int32, (128, 128), 1)
    )
    upper = jnp.where(upper, 1.0, 0.0).astype(BF16)
    before = jnp.zeros((8, 1), F32)
    ranks = []
    for tile in range(GRAINS // 128):
        part = mask[:, tile * 128 : tile * 128 + 128]
        rank = dot(part.astype(BF16), upper) + before
        before = rank[:, 127:128]
        ranks.append(jnp.where(part > 0.0, rank, 0.0))
    ranked = jnp.concatenate(ranks, 1)[0:1, :]
    count = jnp.max(before).astype(jnp.int32)
    acc_s[...] = jnp.zeros(acc_s.shape, F32)
    bin_key = (
        lax.broadcasted_iota(jnp.int32, (BINS, GRAIN), 0).astype(F32) + 32.0
    ) * unit
    slot_iota = lax.broadcasted_iota(jnp.int32, (SLOTS, GRAINS), 0).astype(F32)
    grain_iota = lax.broadcasted_iota(jnp.int32, (SLOTS, GRAINS), 1).astype(F32)
    lane_iota = lax.broadcasted_iota(jnp.int32, (SLOTS, 128), 1).astype(F32)

    def batch_step(batch, carry):
        first = (batch * SLOTS + 1).astype(F32)
        pick = jnp.where(ranked == slot_iota + first, 1.0, 0.0).astype(BF16)
        here = dot(pick, beam_s[0:GRAINS, :])
        ahead = dot(pick, beam_s[SPAN : GRAINS + SPAN, :])
        gbeam_s[...] = here
        gcode_s[...] = dot(pick, code_s[...])
        place = dot(pick, index_ref[...])
        coarse, offset = place[:, 0:1], place[:, 1:2]
        grain = coarse * float(SPAN) + offset
        window = jnp.where((grain_iota >= grain) & (grain_iota < grain + float(SPAN)), 1.0, 0.0)
        window = window.astype(BF16)
        dft = dot(window, zhi_s[...]) + dot(window, zlo_s[...])
        turner = jnp.where((lane_iota == offset) | (lane_iota == offset + float(SPAN)), 1.0, 0.0)
        turned = dot(turner.astype(BF16), phase_s[...])
        real, imag = dft[:, :FREQS], dft[:, FREQS:]
        cos_g, sin_g = turned[:, :FREQS], turned[:, FREQS:]
        gdft_s[:, :FREQS] = real * cos_g - imag * sin_g
        gdft_s[:, FREQS:] = imag * cos_g + real * sin_g
        gstep_s[...] = dot(ahead.astype(BF16), step2_ref[...]) - dot(here.astype(BF16), step2_ref[...])

        def group_step(group, inner):
            rows = pl.ds(pl.multiple_of(group * GROUP, GROUP), GROUP)
            beam8, code8 = gbeam_s[rows, :], gcode_s[rows, :]
            dft8, step8 = gdft_s[rows, :], gstep_s[rows, :]
            left = []
            for k in range(GROUP):
                chosen = code8[k : k + 1, :] == bin_key
                real = jnp.where(chosen, beam8[k : k + 1, :GRAIN], 0.0)
                imag = jnp.where(chosen, beam8[k : k + 1, GRAIN:], 0.0)
                left.append(jnp.concatenate([real, imag], 1))
            left = jnp.concatenate(left, 0).astype(BF16)
            for at, factor in ((0, dft8), (2 * FREQS, step8)):
                folded = dot(left, fold_s[:, at : at + 2 * FREQS])
                real_sum, imag_sum = acc_s[:, at : at + FREQS], acc_s[:, at + FREQS : at + 2 * FREQS]
                for k in range(GROUP):
                    part = slice(k * BINS, k * BINS + BINS)
                    real, imag = folded[part, :FREQS], folded[part, FREQS:]
                    cos_f, sin_f = factor[k : k + 1, :FREQS], factor[k : k + 1, FREQS:]
                    real_sum = real_sum + (real * cos_f - imag * sin_f)
                    imag_sum = imag_sum + (real * sin_f + imag * cos_f)
                acc_s[:, at : at + FREQS] = real_sum
                acc_s[:, at + FREQS : at + 2 * FREQS] = imag_sum
            return inner

        left_over = jnp.minimum(count - batch * SLOTS, SLOTS)
        return lax.fori_loop(0, (left_over + GROUP - 1) // GROUP, group_step, carry)

    lax.fori_loop(0, (count + SLOTS - 1) // SLOTS, batch_step, 0)
    hi, lo = hi_lo(acc_s[:, 2 * FREQS :])
    short = dot(hi, back_ref[...]) + dot(lo, back_ref[...])
    hi, lo = hi_lo(short)
    short = dot(hi, last_s[...]) + dot(lo, last_s[...])
    out_ref[0] = (acc_s[:, :FREQS] + short[:, :FREQS]) * SCALE
    out_ref[1] = (acc_s[:, FREQS : 2 * FREQS] + short[:, FREQS:]) * SCALE


def vmem(count):
    return [pl.BlockSpec(memory_space=pltpu.VMEM)] * count


def spectrum(own, other, ids):
    return pl.pallas_call(
        functools.partial(spectrum_kernel, ids),
        out_shape=jax.ShapeDtypeStruct((2, BINS, FREQS), F32),
        in_specs=vmem(9),
        out_specs=vmem(1)[0],
        scratch_shapes=[
            pltpu.VMEM((GRAINS + SPAN, 2 * GRAIN), BF16),
            pltpu.VMEM((GRAINS, GRAIN), BF16),
            pltpu.VMEM((2 * GRAIN, 4 * FREQS), BF16),
            pltpu.VMEM((2 * GRAIN, 2 * FREQS), BF16),
            pltpu.VMEM((2 * GRAIN, 2 * FREQS), BF16),
            pltpu.VMEM((128, 2 * FREQS), BF16),
            pltpu.VMEM((GRAINS, 2 * FREQS), BF16),
            pltpu.VMEM((GRAINS, 2 * FREQS), BF16),
            pltpu.VMEM((SLOTS, 2 * GRAIN), F32),
            pltpu.VMEM((SLOTS, GRAIN), F32),
            pltpu.VMEM((SLOTS, 2 * FREQS), F32),
            pltpu.VMEM((SLOTS, 2 * FREQS), F32),
            pltpu.VMEM((BINS, 4 * FREQS), F32),
        ],
        name="spectrum",
    )(own, other, *tables())


def per_device(voltages, beam_weights, phase_bins):
    partial_beam = pl.pallas_call(
        beam_kernel,
        out_shape=jax.ShapeDtypeStruct((DISH_WAYS, 2 * PER_BLOCK, GRAIN), F32),
        in_specs=vmem(2),
        out_specs=vmem(1)[0],
        name="beam",
    )(voltages, beam_weights)
    parts = lax.all_to_all(partial_beam, "dish", 0, 0, tiled=True)
    packed = pl.pallas_call(
        pack_kernel,
        out_shape=jax.ShapeDtypeStruct((CHIPS, 3 * PER_BLOCK, GRAIN), BF16),
        in_specs=vmem(2),
        out_specs=vmem(1)[0],
        name="pack",
    )(parts, phase_bins.reshape(PER_BLOCK, GRAIN))
    own = lax.all_to_all(packed, ("z", "xh"), 0, 0, tiled=True)
    other = lax.ppermute(own, "core", [(0, 1), (1, 0)])

    def ids():
        core = lax.axis_index("core")
        owner = (lax.axis_index("z") * 2 + lax.axis_index("xh")) * 2 + core
        return owner, lax.axis_index("dish"), core

    return jnp.transpose(spectrum(own, other, ids), (2, 0, 1))


def solution(mesh):
    split = jax.sharding.Mesh(mesh.devices.reshape(8, 2, 2, 8), ("z", "xh", "core", "dish"))
    time = ("z", "xh", "core")
    return jax.shard_map(
        per_device,
        mesh=split,
        in_specs=(P(None, "dish", time), P(None, "dish"), P(time)),
        out_specs=P("dish", None, time),
        check_vma=False,
    )
```

```python
import functools
import math

import jax
import jax.numpy as jnp
import numpy as np
from jax import lax
from jax.experimental import pallas as pl
from jax.experimental.pallas import tpu as pltpu
from jax.sharding import PartitionSpec as P

PH = 1024
LAGS = 2048
SAMPLES = 131072
DISH_WAYS = 8
TM_WAYS = 32
CHIPS = 16
LOCAL = SAMPLES // TM_WAYS
GRAIN = 128
GRAINS = SAMPLES // GRAIN
PER_BLOCK = LOCAL // GRAIN
SPAN = LAGS // GRAIN
BINS = PH // TM_WAYS
FREQS = LAGS // DISH_WAYS
SLOTS = 128
GROUP = 8
SCALE = 1.0 / math.sqrt(LAGS * SAMPLES / PH)

F32 = jnp.float32
BF16 = jnp.bfloat16


def dot(a, b, dims=(((1,), (0,)), ((), ()))):
    return lax.dot_general(a, b, dims, preferred_element_type=F32)


def hi_lo(value):
    hi = value.astype(BF16)
    return hi, (value - hi.astype(F32)).astype(BF16)


def tables():
    grain = np.arange(GRAIN)
    freq = np.arange(FREQS)
    angle = 2 * np.pi * np.outer(grain, freq) / LAGS
    base = np.concatenate([np.cos(angle), np.sin(angle)], 1).astype(np.float32)
    eighth = 2 * np.pi * np.outer(grain, np.arange(DISH_WAYS)) / DISH_WAYS
    turn = np.zeros((GRAIN, 128), np.float32)
    turn[:, :8] = np.cos(eighth)
    turn[:, 8:16] = np.sin(eighth)
    fine = 2 * np.pi * np.outer(grain, np.arange(2 * GRAIN)) / (2 * GRAIN)
    cos2, sin2 = np.cos(fine), np.sin(fine)
    fold2 = np.block([[cos2, sin2], [sin2, -cos2]]).astype(np.float32)
    step2 = np.block([[cos2, -sin2], [sin2, cos2]]).astype(np.float32)
    keep = (grain >= 1)[None, :] / (2.0 * GRAIN)
    back = np.block([[cos2.T * keep, -sin2.T * keep], [sin2.T * keep, cos2.T * keep]])
    sixteenth = 2 * np.pi * np.outer(np.arange(SPAN), freq) / SPAN
    phase = np.concatenate([np.cos(sixteenth), np.sin(sixteenth)], 1).astype(np.float32)
    index = np.zeros((GRAINS, 128), np.float32)
    index[:, 0] = np.arange(GRAINS) // SPAN
    index[:, 1] = np.arange(GRAINS) % SPAN
    return (
        jnp.asarray(base),
        jnp.asarray(turn),
        jnp.asarray(fold2).astype(BF16),
        jnp.asarray(step2).astype(BF16),
        jnp.asarray(back.astype(np.float32)).astype(BF16),
        jnp.asarray(phase),
        jnp.asarray(index).astype(BF16),
    )


def beam_kernel(volts_ref, weights_ref, out_ref):
    weights = weights_ref[...]
    first = dot(weights, volts_ref[0])
    second = dot(weights, volts_ref[1])
    real = first[0:1] - second[1:2]
    imag = first[1:2] + second[0:1]
    for row in range(PER_BLOCK):
        part = slice(row * GRAIN, (row + 1) * GRAIN)
        out_ref[0, row : row + 1, :] = real[:, part]
        out_ref[0, PER_BLOCK + row : PER_BLOCK + row + 1, :] = imag[:, part]
    rows = out_ref[0]
    for way in range(1, DISH_WAYS):
        out_ref[way] = rows


def pack_kernel(parts_ref, bins_ref, out_ref):
    total = parts_ref[0]
    for way in range(1, DISH_WAYS):
        total = total + parts_ref[way]
    bins = bins_ref[...]
    high = bins >> 5
    coded = ((bins & 31) + 32).astype(F32)
    for bit in range(5):
        coded = coded * jnp.where((high >> bit) & 1 == 1, float(2 ** (2**bit)), 1.0)
    coded = coded * (2.0**-16)
    rows = jnp.concatenate([total.astype(BF16), coded.astype(BF16)], 0)
    for chip in range(CHIPS):
        out_ref[chip] = rows


def two_to(exponent):
    value = jnp.float32(2.0**-16)
    for bit in range(5):
        value = value * jnp.where((exponent >> bit) & 1 == 1, jnp.float32(2 ** (2**bit)), jnp.float32(1.0))
    return value


def spectrum_kernel(
    ids,
    own_ref, other_ref, base_ref, turn_ref, fold2_ref, step2_ref, back_ref, phase_ref, index_ref,
    out_ref,
    beam_s, code_s, fold_s, step_s, last_s, phase_s, zhi_s, zlo_s,
    gbeam_s, gcode_s, gdft_s, gstep_s, acc_s,
):
    owner, dish, core = ids()
    for chip in range(CHIPS):
        for ref, which in ((own_ref, core), (other_ref, 1 - core)):
            start = pl.multiple_of((2 * chip + which) * PER_BLOCK, PER_BLOCK)
            rows = pl.ds(start, PER_BLOCK)
            beam_s[rows, 0:GRAIN] = ref[chip, 0:PER_BLOCK, :]
            beam_s[rows, GRAIN:] = ref[chip, PER_BLOCK : 2 * PER_BLOCK, :]
            code_s[rows, :] = ref[chip, 2 * PER_BLOCK :, :]
    beam_s[GRAINS:, :] = jnp.zeros((SPAN, 2 * GRAIN), BF16)
    lane = lax.broadcasted_iota(jnp.int32, (GRAIN, 128), 1)
    turn = turn_ref[...]
    cos8 = jnp.sum(jnp.where(lane == dish, turn, 0.0), axis=1, keepdims=True)
    sin8 = jnp.sum(jnp.where(lane == dish + 8, turn, 0.0), axis=1, keepdims=True)
    cos0, sin0 = base_ref[:, :FREQS], base_ref[:, FREQS:]
    cosine = (cos0 * cos8 - sin0 * sin8).astype(BF16)
    sine = (sin0 * cos8 + cos0 * sin8).astype(BF16)
    fold_s[:GRAIN, :FREQS] = cosine
    fold_s[:GRAIN, FREQS : 2 * FREQS] = sine
    fold_s[GRAIN:, :FREQS] = sine
    fold_s[GRAIN:, FREQS : 2 * FREQS] = -cosine
    fold_s[:, 2 * FREQS :] = fold2_ref[...]
    step_s[:GRAIN, :FREQS] = cosine
    step_s[:GRAIN, FREQS:] = -sine
    step_s[GRAIN:, :FREQS] = sine
    step_s[GRAIN:, FREQS:] = cosine
    last_s[:GRAIN, :FREQS] = cosine
    last_s[:GRAIN, FREQS:] = sine
    last_s[GRAIN:, :FREQS] = -sine
    last_s[GRAIN:, FREQS:] = cosine
    cos16, sin16 = phase_ref[:, :FREQS], phase_ref[:, FREQS:]
    phase_s[...] = jnp.zeros(phase_s.shape, BF16)
    for at, part in ((0, cos16), (FREQS, sin16)):
        hi, lo = hi_lo(part)
        phase_s[0:SPAN, at : at + FREQS] = hi
        phase_s[SPAN : 2 * SPAN, at : at + FREQS] = lo
    turns = 128 // SPAN
    cos_rows = jnp.concatenate([cos16] * turns, 0)
    sin_rows = jnp.concatenate([sin16] * turns, 0)
    for tile in range(GRAINS // 128):
        rows = slice(tile * 128, tile * 128 + 128)
        both = dot(beam_s[rows, :], step_s[...])
        real, imag = both[:, :FREQS], both[:, FREQS:]
        zhi_s[rows, :FREQS], zlo_s[rows, :FREQS] = hi_lo(real * cos_rows + imag * sin_rows)
        zhi_s[rows, FREQS:], zlo_s[rows, FREQS:] = hi_lo(imag * cos_rows - real * sin_rows)
    unit = two_to(owner)
    code = code_s[...].astype(F32)
    inside = jnp.where((code >= unit * 32.0) & (code < unit * 64.0), 1.0, 0.0).astype(BF16)
    hits = dot(jnp.ones((8, GRAIN), BF16), inside, (((1,), (1,)), ((), ())))
    mask = jnp.where(hits > 0.0, 1.0, 0.0)
    upper = (
        lax.broadcasted_iota(jnp.int32, (128, 128), 0) <= lax.broadcasted_iota(jnp.int32, (128, 128), 1)
    )
    upper = jnp.where(upper, 1.0, 0.0).astype(BF16)
    before = jnp.zeros((8, 1), F32)
    ranks = []
    for tile in range(GRAINS // 128):
        part = mask[:, tile * 128 : tile * 128 + 128]
        rank = dot(part.astype(BF16), upper) + before
        before = rank[:, 127:128]
        ranks.append(jnp.where(part > 0.0, rank, 0.0))
    ranked = jnp.concatenate(ranks, 1)[0:1, :]
    count = jnp.max(before).astype(jnp.int32)
    acc_s[...] = jnp.zeros(acc_s.shape, F32)
    bin_key = (
        lax.broadcasted_iota(jnp.int32, (BINS, GRAIN), 0).astype(F32) + 32.0
    ) * unit
    slot_iota = lax.broadcasted_iota(jnp.int32, (SLOTS, GRAINS), 0).astype(F32)
    grain_iota = lax.broadcasted_iota(jnp.int32, (SLOTS, GRAINS), 1).astype(F32)
    lane_iota = lax.broadcasted_iota(jnp.int32, (SLOTS, 128), 1).astype(F32)

    def batch_step(batch, carry):
        first = (batch * SLOTS + 1).astype(F32)
        pick = jnp.where(ranked == slot_iota + first, 1.0, 0.0).astype(BF16)
        here = dot(pick, beam_s[0:GRAINS, :])
        ahead = dot(pick, beam_s[SPAN : GRAINS + SPAN, :])
        gbeam_s[...] = here
        gcode_s[...] = dot(pick, code_s[...])
        place = dot(pick, index_ref[...])
        coarse, offset = place[:, 0:1], place[:, 1:2]
        grain = coarse * float(SPAN) + offset
        window = jnp.where((grain_iota >= grain) & (grain_iota < grain + float(SPAN)), 1.0, 0.0)
        window = window.astype(BF16)
        dft = dot(window, zhi_s[...]) + dot(window, zlo_s[...])
        turner = jnp.where((lane_iota == offset) | (lane_iota == offset + float(SPAN)), 1.0, 0.0)
        turned = dot(turner.astype(BF16), phase_s[...])
        real, imag = dft[:, :FREQS], dft[:, FREQS:]
        cos_g, sin_g = turned[:, :FREQS], turned[:, FREQS:]
        gdft_s[:, :FREQS] = real * cos_g - imag * sin_g
        gdft_s[:, FREQS:] = imag * cos_g + real * sin_g
        gstep_s[...] = dot(ahead.astype(BF16), step2_ref[...]) - dot(here.astype(BF16), step2_ref[...])

        def group_step(group, inner):
            rows = pl.ds(pl.multiple_of(group * GROUP, GROUP), GROUP)
            beam8, code8 = gbeam_s[rows, :], gcode_s[rows, :]
            dft8, step8 = gdft_s[rows, :], gstep_s[rows, :]
            left = []
            for k in range(GROUP):
                chosen = code8[k : k + 1, :] == bin_key
                real = jnp.where(chosen, beam8[k : k + 1, :GRAIN], 0.0)
                imag = jnp.where(chosen, beam8[k : k + 1, GRAIN:], 0.0)
                left.append(jnp.concatenate([real, imag], 1))
            left = jnp.concatenate(left, 0).astype(BF16)
            for at, factor in ((0, dft8), (2 * FREQS, step8)):
                folded = dot(left, fold_s[:, at : at + 2 * FREQS])
                real_sum, imag_sum = acc_s[:, at : at + FREQS], acc_s[:, at + FREQS : at + 2 * FREQS]
                for k in range(GROUP):
                    part = slice(k * BINS, k * BINS + BINS)
                    real, imag = folded[part, :FREQS], folded[part, FREQS:]
                    cos_f, sin_f = factor[k : k + 1, :FREQS], factor[k : k + 1, FREQS:]
                    real_sum = real_sum + (real * cos_f - imag * sin_f)
                    imag_sum = imag_sum + (real * sin_f + imag * cos_f)
                acc_s[:, at : at + FREQS] = real_sum
                acc_s[:, at + FREQS : at + 2 * FREQS] = imag_sum
            return inner

        left_over = jnp.minimum(count - batch * SLOTS, SLOTS)
        return lax.fori_loop(0, (left_over + GROUP - 1) // GROUP, group_step, carry)

    lax.fori_loop(0, (count + SLOTS - 1) // SLOTS, batch_step, 0)
    hi, lo = hi_lo(acc_s[:, 2 * FREQS :])
    short = dot(hi, back_ref[...]) + dot(lo, back_ref[...])
    hi, lo = hi_lo(short)
    short = dot(hi, last_s[...]) + dot(lo, last_s[...])
    out_ref[0] = (acc_s[:, :FREQS] + short[:, :FREQS]) * SCALE
    out_ref[1] = (acc_s[:, FREQS : 2 * FREQS] + short[:, FREQS:]) * SCALE


def vmem(count):
    return [pl.BlockSpec(memory_space=pltpu.VMEM)] * count


def near(*values):
    return [pltpu.with_memory_space_constraint(v, pltpu.VMEM) for v in values]


def params(mib):
    return pltpu.CompilerParams(vmem_limit_bytes=mib << 20)


def spectrum(own, other, ids):
    return pl.pallas_call(
        functools.partial(spectrum_kernel, ids),
        out_shape=jax.ShapeDtypeStruct((2, BINS, FREQS), F32),
        in_specs=vmem(9),
        out_specs=vmem(1)[0],
        scratch_shapes=[
            pltpu.VMEM((GRAINS + SPAN, 2 * GRAIN), BF16),
            pltpu.VMEM((GRAINS, GRAIN), BF16),
            pltpu.VMEM((2 * GRAIN, 4 * FREQS), BF16),
            pltpu.VMEM((2 * GRAIN, 2 * FREQS), BF16),
            pltpu.VMEM((2 * GRAIN, 2 * FREQS), BF16),
            pltpu.VMEM((128, 2 * FREQS), BF16),
            pltpu.VMEM((GRAINS, 2 * FREQS), BF16),
            pltpu.VMEM((GRAINS, 2 * FREQS), BF16),
            pltpu.VMEM((SLOTS, 2 * GRAIN), F32),
            pltpu.VMEM((SLOTS, GRAIN), F32),
            pltpu.VMEM((SLOTS, 2 * FREQS), F32),
            pltpu.VMEM((SLOTS, 2 * FREQS), F32),
            pltpu.VMEM((BINS, 4 * FREQS), F32),
        ],
        compiler_params=params(24),
        name="spectrum",
    )(*near(own, other, *tables()))


def per_device(voltages, beam_weights, phase_bins):
    partial_beam = pl.pallas_call(
        beam_kernel,
        out_shape=pltpu.VMEM((DISH_WAYS, 2 * PER_BLOCK, GRAIN), F32),
        in_specs=vmem(2),
        out_specs=vmem(1)[0],
        compiler_params=params(8),
        name="beam",
    )(voltages, beam_weights)
    parts = lax.all_to_all(partial_beam, "dish", 0, 0, tiled=True)
    packed = pl.pallas_call(
        pack_kernel,
        out_shape=pltpu.VMEM((CHIPS, 3 * PER_BLOCK, GRAIN), BF16),
        in_specs=vmem(2),
        out_specs=vmem(1)[0],
        compiler_params=params(8),
        name="pack",
    )(*near(parts, phase_bins.reshape(PER_BLOCK, GRAIN)))
    own = lax.all_to_all(packed, ("z", "xh"), 0, 0, tiled=True)
    other = lax.ppermute(own, "core", [(0, 1), (1, 0)])

    def ids():
        core = lax.axis_index("core")
        owner = (lax.axis_index("z") * 2 + lax.axis_index("xh")) * 2 + core
        return owner, lax.axis_index("dish"), core

    return jnp.transpose(spectrum(own, other, ids), (2, 0, 1))


def solution(mesh):
    split = jax.sharding.Mesh(mesh.devices.reshape(8, 2, 2, 8), ("z", "xh", "core", "dish"))
    time = ("z", "xh", "core")
    return jax.shard_map(
        per_device,
        mesh=split,
        in_specs=(P(None, "dish", time), P(None, "dish"), P(time)),
        out_specs=P("dish", None, time),
        check_vma=False,
    )
```

```python
import functools
import math

import jax
import jax.numpy as jnp
import numpy as np
from jax import lax
from jax.experimental import pallas as pl
from jax.experimental.pallas import tpu as pltpu
from jax.sharding import PartitionSpec as P


PH = 1024
LAGS = 2048
SAMPLES = 131072
DISH_WAYS = 8
TM_WAYS = 32
CHIPS = 16
HALF = SAMPLES // 2 // 128
LOCAL = SAMPLES // TM_WAYS
GRAIN = 128
PER_BLOCK = LOCAL // GRAIN
SPAN = LAGS // GRAIN
BINS = PH // TM_WAYS
FREQS = LAGS // DISH_WAYS
SLOTS = 128
GROUP = 16
SCALE = 1.0 / math.sqrt(LAGS * SAMPLES / PH)

F32 = jnp.float32
BF16 = jnp.bfloat16


def dot(a, b, dims=(((1,), (0,)), ((), ()))):
    return lax.dot_general(a, b, dims, preferred_element_type=F32)


def hi_lo(value):
    hi = value.astype(BF16)
    return hi, (value - hi.astype(F32)).astype(BF16)


def tables():
    grain = np.arange(GRAIN)
    freq = np.arange(FREQS)
    angle = 2 * np.pi * np.outer(grain, freq) / LAGS
    base = np.concatenate([np.cos(angle), np.sin(angle)], 1).astype(np.float32)
    eighth = 2 * np.pi * np.outer(grain, np.arange(DISH_WAYS)) / DISH_WAYS
    turn = np.zeros((GRAIN, 128), np.float32)
    turn[:, :8] = np.cos(eighth)
    turn[:, 8:16] = np.sin(eighth)
    fine = 2 * np.pi * np.outer(grain, np.arange(2 * GRAIN)) / (2 * GRAIN)
    cos2, sin2 = np.cos(fine), np.sin(fine)
    fold2 = np.block([[cos2, sin2], [sin2, -cos2]]).astype(np.float32)
    step2 = np.block([[cos2, -sin2], [sin2, cos2]]).astype(np.float32)
    keep = (grain >= 1)[None, :] / (2.0 * GRAIN)
    back = np.block([[cos2.T * keep, -sin2.T * keep], [sin2.T * keep, cos2.T * keep]])
    sixteenth = 2 * np.pi * np.outer(np.arange(SPAN), freq) / SPAN
    phase = np.concatenate([np.cos(sixteenth), np.sin(sixteenth)], 1).astype(np.float32)
    place = np.arange(HALF)
    index = np.zeros((HALF, 128), np.float32)
    index[:, 0] = place // PER_BLOCK
    index[:, 1] = place % PER_BLOCK
    index[:, 2] = 1.0
    return {
        "base": jnp.asarray(base),
        "turn": jnp.asarray(turn),
        "fold2": jnp.asarray(fold2).astype(BF16),
        "step2": jnp.asarray(step2).astype(BF16),
        "back": jnp.asarray(back.astype(np.float32)).astype(BF16),
        "phase": jnp.asarray(phase),
        "index": jnp.asarray(index).astype(BF16),
    }


def front_kernel(volts_hbm, weights_hbm, bins_hbm, beam_ref, code_ref, volts_s, weights_s, bins_s, sems):
    copies = [
        pltpu.make_async_copy(source, target, sems.at[k])
        for k, (source, target) in enumerate(
            ((bins_hbm, bins_s), (weights_hbm, weights_s), (volts_hbm, volts_s))
        )
    ]
    for copy in copies:
        copy.start()
    copies[0].wait()
    bins = bins_s[...]
    high = bins >> 5
    coded = ((bins & 31) + 32).astype(F32)
    for bit in range(5):
        coded = coded * jnp.where((high >> bit) & 1 == 1, float(2 ** (2**bit)), 1.0)
    code_ref[...] = (coded * (2.0**-16)).astype(BF16)
    copies[1].wait()
    copies[2].wait()
    weights = weights_s[...]
    first = dot(weights, volts_s[0])
    second = dot(weights, volts_s[1])
    real = first[0:1] - second[1:2]
    imag = first[1:2] + second[0:1]
    for row in range(PER_BLOCK):
        part = slice(row * GRAIN, (row + 1) * GRAIN)
        beam_ref[0, row : row + 1, :] = real[:, part]
        beam_ref[0, PER_BLOCK + row : PER_BLOCK + row + 1, :] = imag[:, part]
    rows = beam_ref[0]
    for way in range(1, DISH_WAYS):
        beam_ref[way] = rows


def pack_kernel(parts_ref, code_ref, out_ref):
    total = parts_ref[0]
    for way in range(1, DISH_WAYS):
        total = total + parts_ref[way]
    rows = jnp.concatenate([total.astype(BF16), code_ref[...]], 0)
    for chip in range(CHIPS):
        out_ref[chip] = rows


def table_kernel(ids, base_ref, turn_ref, fold2_ref, phase_ref, fold_ref, step_ref, last_ref, phases_ref):
    _, dish, _ = ids()
    lane = lax.broadcasted_iota(jnp.int32, (GRAIN, 128), 1)
    turn = turn_ref[...]
    cos8 = jnp.sum(jnp.where(lane == dish, turn, 0.0), axis=1, keepdims=True)
    sin8 = jnp.sum(jnp.where(lane == dish + 8, turn, 0.0), axis=1, keepdims=True)
    cos0, sin0 = base_ref[:, :FREQS], base_ref[:, FREQS:]
    cosine, cosine_lo = hi_lo(cos0 * cos8 - sin0 * sin8)
    sine, sine_lo = hi_lo(sin0 * cos8 + cos0 * sin8)
    fold_ref[:GRAIN, :FREQS] = cosine
    fold_ref[:GRAIN, FREQS : 2 * FREQS] = sine
    fold_ref[GRAIN:, :FREQS] = sine
    fold_ref[GRAIN:, FREQS : 2 * FREQS] = -cosine
    fold_ref[:, 2 * FREQS :] = fold2_ref[...]
    for k, (c, s) in enumerate(((cosine, sine), (cosine_lo, sine_lo))):
        step_ref[k, :GRAIN, :FREQS] = c
        step_ref[k, :GRAIN, FREQS:] = -s
        step_ref[k, GRAIN:, :FREQS] = s
        step_ref[k, GRAIN:, FREQS:] = c
    last_ref[:GRAIN, :FREQS] = cosine
    last_ref[:GRAIN, FREQS:] = sine
    last_ref[GRAIN:, :FREQS] = -sine
    last_ref[GRAIN:, FREQS:] = cosine
    phases_ref[...] = jnp.zeros(phases_ref.shape, BF16)
    hi, lo = hi_lo(phase_ref[...])
    phases_ref[0:SPAN, :] = hi
    phases_ref[SPAN : 2 * SPAN, :] = lo


def two_to(exponent):
    value = jnp.float32(2.0**-16)
    for bit in range(5):
        value = value * jnp.where((exponent >> bit) & 1 == 1, jnp.float32(2 ** (2**bit)), jnp.float32(1.0))
    return value


def beam_rows(ref, first, last):
    rows = [
        jnp.concatenate([ref[chip, :PER_BLOCK, :], ref[chip, PER_BLOCK : 2 * PER_BLOCK, :]], 1)
        for chip in range(first, last)
    ]
    return jnp.concatenate(rows, 0)


def code_rows(ref):
    return jnp.concatenate([ref[chip, 2 * PER_BLOCK :, :] for chip in range(CHIPS)], 0)


def transform(ref, step_ref, phase_ref, z_ref):
    cos16, sin16 = phase_ref[:, :FREQS], phase_ref[:, FREQS:]
    cos_rows = jnp.concatenate([cos16] * (128 // SPAN), 0)
    sin_rows = jnp.concatenate([sin16] * (128 // SPAN), 0)
    for tile in range(HALF // 128):
        rows = slice(tile * 128, tile * 128 + 128)
        beam = beam_rows(ref, 4 * tile, 4 * tile + 4)
        both = dot(beam, step_ref[0]) + dot(beam, step_ref[1])
        real, imag = both[:, :FREQS], both[:, FREQS:]
        z_ref[rows, :FREQS] = (real * cos_rows + imag * sin_rows).astype(BF16)
        z_ref[rows, FREQS:] = (imag * cos_rows - real * sin_rows).astype(BF16)


def rank_half(ref, owner, before):
    unit = two_to(owner)
    code = code_rows(ref).astype(F32)
    inside = jnp.where((code >= unit * 32.0) & (code < unit * 64.0), 1.0, 0.0).astype(BF16)
    hits = dot(jnp.ones((8, GRAIN), BF16), inside, (((1,), (1,)), ((), ())))
    mask = jnp.where(hits > 0.0, 1.0, 0.0)
    upper = (
        lax.broadcasted_iota(jnp.int32, (128, 128), 0) <= lax.broadcasted_iota(jnp.int32, (128, 128), 1)
    )
    upper = jnp.where(upper, 1.0, 0.0).astype(BF16)
    ranks = []
    for tile in range(HALF // 128):
        part = mask[:, tile * 128 : tile * 128 + 128]
        rank = dot(part.astype(BF16), upper) + before
        before = rank[:, 127:128]
        ranks.append(jnp.where(part > 0.0, rank, 0.0))
    return jnp.concatenate(ranks, 1), before


def gather_half(first, ranked, ref, index):
    slot = lax.broadcasted_iota(jnp.int32, (SLOTS, HALF), 0).astype(F32)
    pick = jnp.where(ranked == slot + first, 1.0, 0.0).astype(BF16)
    return dot(pick, beam_rows(ref, 0, CHIPS)), dot(pick, code_rows(ref)), dot(pick, index)


def half_kernel(
    ids, own_ref, step_ref, phase_ref, index_ref, z_ref, rank_ref, last_ref, gbeam_ref, gcode_ref, place_ref
):
    owner, _, _ = ids()
    ranked, last = rank_half(own_ref, owner, jnp.zeros((8, 1), F32))
    rank_ref[...] = ranked
    last_ref[...] = jnp.broadcast_to(last, (8, 128))
    gbeam_ref[...], gcode_ref[...], place_ref[...] = gather_half(
        jnp.float32(1.0), ranked[0:1, :], own_ref, index_ref[...]
    )
    transform(own_ref, step_ref, phase_ref, z_ref)


def grain_row(which):
    place = lax.broadcasted_iota(jnp.int32, (8, HALF), 1)
    grain = (2 * (place >> 5) + which) * PER_BLOCK + (place & (PER_BLOCK - 1))
    return grain.astype(F32)[0:1, :]


def spectrum_kernel(
    ids,
    own_ref, other_ref, z_ref, rank_ref, last_rank_ref, gbeam_ref, gcode_ref, place_ref,
    fold_ref, step_ref, last_ref, phases_ref, step2_ref, back_ref, phase_ref, index_ref,
    out_ref,
    z_s, gdft_s, gstep_s, gbeam_s, gcode_s, acc_s,
):
    owner, _, core = ids()
    ranked, last = rank_half(other_ref, owner, last_rank_ref[:, 0:1])
    count = jnp.max(last).astype(jnp.int32)
    transform(other_ref, step_ref, phase_ref, z_s)
    acc_s[...] = jnp.zeros(acc_s.shape, F32)
    unit = two_to(owner)
    bin_key = (
        lax.broadcasted_iota(jnp.int32, (BINS, GRAIN), 0).astype(F32) + 32.0
    ) * unit
    own_grains = jnp.broadcast_to(grain_row(core), (SLOTS, HALF))
    other_grains = jnp.broadcast_to(grain_row(1 - core), (SLOTS, HALF))
    lane_iota = lax.broadcasted_iota(jnp.int32, (SLOTS, 128), 1).astype(F32)
    core_f = core.astype(F32)

    def fold_batch(batch, gathered):
        first = (batch * SLOTS + 1).astype(F32)
        more = gather_half(first, ranked[0:1, :], other_ref, index_ref[...])
        here = gathered[0] + more[0]
        gbeam_s[...] = here
        gcode_s[...] = gathered[1] + more[1]
        place = gathered[2] + more[2]
        which = gathered[2][:, 2:3] * core_f + more[2][:, 2:3] * (1.0 - core_f)
        in_block = place[:, 1:2]
        grain = (2.0 * place[:, 0:1] + which) * float(PER_BLOCK) + in_block
        dft = jnp.zeros((SLOTS, 2 * FREQS), F32)
        ahead = jnp.zeros((SLOTS, 2 * GRAIN), F32)
        for grains, z, ref in ((own_grains, z_ref, own_ref), (other_grains, z_s, other_ref)):
            window = (grains >= grain) & (grains < grain + float(SPAN))
            dft = dft + dot(jnp.where(window, 1.0, 0.0).astype(BF16), z[...])
            next_pick = jnp.where(grains == grain + float(SPAN), 1.0, 0.0).astype(BF16)
            ahead = ahead + dot(next_pick, beam_rows(ref, 0, CHIPS))
        offset = jnp.where(in_block >= float(SPAN), in_block - float(SPAN), in_block)
        turner = jnp.where((lane_iota == offset) | (lane_iota == offset + float(SPAN)), 1.0, 0.0)
        turned = dot(turner.astype(BF16), phases_ref[...])
        real, imag = dft[:, :FREQS], dft[:, FREQS:]
        cos_g, sin_g = turned[:, :FREQS], turned[:, FREQS:]
        gdft_s[:, :FREQS] = real * cos_g - imag * sin_g
        gdft_s[:, FREQS:] = imag * cos_g + real * sin_g
        gstep_s[...] = dot((ahead - here).astype(BF16), step2_ref[...])

        def group_step(group, inner):
            rows = pl.ds(pl.multiple_of(group * GROUP, GROUP), GROUP)
            beam8, code8 = gbeam_s[rows, :], gcode_s[rows, :]
            dft8, step8 = gdft_s[rows, :], gstep_s[rows, :]
            left = []
            for k in range(GROUP):
                chosen = code8[k : k + 1, :] == bin_key
                real = jnp.where(chosen, beam8[k : k + 1, :GRAIN], 0.0)
                imag = jnp.where(chosen, beam8[k : k + 1, GRAIN:], 0.0)
                left.append(jnp.concatenate([real, imag], 1))
            left = jnp.concatenate(left, 0).astype(BF16)
            for at, factor in ((0, dft8), (2 * FREQS, step8)):
                folded = dot(left, fold_ref[:, at : at + 2 * FREQS])
                real_sum, imag_sum = acc_s[:, at : at + FREQS], acc_s[:, at + FREQS : at + 2 * FREQS]
                for k in range(GROUP):
                    part = slice(k * BINS, k * BINS + BINS)
                    real, imag = folded[part, :FREQS], folded[part, FREQS:]
                    cos_f, sin_f = factor[k : k + 1, :FREQS], factor[k : k + 1, FREQS:]
                    real_sum = real_sum + (real * cos_f - imag * sin_f)
                    imag_sum = imag_sum + (real * sin_f + imag * cos_f)
                acc_s[:, at : at + FREQS] = real_sum
                acc_s[:, at + FREQS : at + 2 * FREQS] = imag_sum
            return inner

        left_over = jnp.minimum(count - batch * SLOTS, SLOTS)
        lax.fori_loop(0, (left_over + GROUP - 1) // GROUP, group_step, 0)

    fold_batch(jnp.int32(0), (gbeam_ref[...], gcode_ref[...], place_ref[...]))

    def batch_step(batch, carry):
        first = (batch * SLOTS + 1).astype(F32)
        fold_batch(batch, gather_half(first, rank_ref[0:1, :], own_ref, index_ref[...]))
        return carry

    lax.fori_loop(1, (count + SLOTS - 1) // SLOTS, batch_step, 0)
    hi, lo = hi_lo(acc_s[:, 2 * FREQS :])
    short = dot(hi, back_ref[...]) + dot(lo, back_ref[...])
    hi, lo = hi_lo(short)
    short = dot(hi, last_ref[...]) + dot(lo, last_ref[...])
    out_ref[0] = (acc_s[:, :FREQS] + short[:, :FREQS]) * SCALE
    out_ref[1] = (acc_s[:, FREQS : 2 * FREQS] + short[:, FREQS:]) * SCALE


def near(*values):
    return [pltpu.with_memory_space_constraint(v, pltpu.VMEM) for v in values]


def call(kernel, outs, values, scratch=(), mib=8, us=1.0):
    one = not isinstance(outs, (tuple, list))
    space = pl.BlockSpec(memory_space=pltpu.VMEM)
    return pl.pallas_call(
        kernel,
        out_shape=outs if one else tuple(outs),
        in_specs=[space] * len(values),
        out_specs=space if one else (space,) * len(outs),
        scratch_shapes=list(scratch),
        compiler_params=pltpu.CompilerParams(vmem_limit_bytes=mib << 20),
        cost_estimate=pl.CostEstimate(flops=int(us * 5e8), bytes_accessed=1 << 20, transcendentals=0),
    )(*near(*values))


GATHERED = (
    pltpu.VMEM((SLOTS, 2 * GRAIN), F32),
    pltpu.VMEM((SLOTS, GRAIN), F32),
    pltpu.VMEM((SLOTS, 128), F32),
)
HALF_Z = pltpu.VMEM((HALF, 2 * FREQS), BF16)


def make_tables(ids):
    given = tables()
    made = call(
        functools.partial(table_kernel, ids),
        (
            pltpu.VMEM((2 * GRAIN, 4 * FREQS), BF16),
            pltpu.VMEM((2, 2 * GRAIN, 2 * FREQS), BF16),
            pltpu.VMEM((2 * GRAIN, 2 * FREQS), BF16),
            pltpu.VMEM((128, 2 * FREQS), BF16),
        ),
        [given[k] for k in ("base", "turn", "fold2", "phase")],
        us=3.0,
    )
    return given, made


def spectrum(own, other, ids, given, made):
    fold, step, last, phases = made
    phase, index = given["phase"], given["index"]
    half = call(
        functools.partial(half_kernel, ids),
        (HALF_Z, pltpu.VMEM((8, HALF), F32), pltpu.VMEM((8, 128), F32), *GATHERED),
        (own, step, phase, index),
        us=1.0,
    )
    scratch = [
        HALF_Z,
        pltpu.VMEM((SLOTS, 2 * FREQS), F32),
        pltpu.VMEM((SLOTS, 2 * FREQS), F32),
        GATHERED[0],
        GATHERED[1],
        pltpu.VMEM((BINS, 4 * FREQS), F32),
    ]
    return call(
        functools.partial(spectrum_kernel, ids),
        jax.ShapeDtypeStruct((2, BINS, FREQS), F32),
        (own, other, *half, fold, step, last, phases, given["step2"], given["back"], phase, index),
        scratch,
        mib=16,
        us=5.0,
    )


def front(voltages, beam_weights, bins):
    far = pl.BlockSpec(memory_space=pltpu.HBM)
    close = pl.BlockSpec(memory_space=pltpu.VMEM)
    return pl.pallas_call(
        front_kernel,
        out_shape=(
            pltpu.VMEM((DISH_WAYS, 2 * PER_BLOCK, GRAIN), F32),
            pltpu.VMEM((PER_BLOCK, GRAIN), BF16),
        ),
        in_specs=[far] * 3,
        out_specs=(close, close),
        scratch_shapes=[
            pltpu.VMEM(voltages.shape, BF16),
            pltpu.VMEM(beam_weights.shape, BF16),
            pltpu.VMEM(bins.shape, jnp.int32),
            pltpu.SemaphoreType.DMA((3,)),
        ],
        compiler_params=pltpu.CompilerParams(vmem_limit_bytes=8 << 20),
        cost_estimate=pl.CostEstimate(flops=1 << 20, bytes_accessed=1 << 20, transcendentals=0),
        name="front",
    )(*(pltpu.with_memory_space_constraint(v, pltpu.HBM) for v in (voltages, beam_weights, bins)))


def steps(voltages, beam_weights, phase_bins):
    def ids():
        core = lax.axis_index("core")
        owner = (lax.axis_index("z") * 2 + lax.axis_index("xh")) * 2 + core
        return owner, lax.axis_index("dish"), core

    given, made = make_tables(ids)
    partial_beam, coded = front(voltages, beam_weights, phase_bins.reshape(PER_BLOCK, GRAIN))
    parts = lax.all_to_all(partial_beam, "dish", 0, 0, tiled=True)
    packed = call(pack_kernel, pltpu.VMEM((CHIPS, 3 * PER_BLOCK, GRAIN), BF16), (parts, coded), us=0.3)
    own = lax.all_to_all(packed, ("z", "xh"), 0, 0, tiled=True)
    other = lax.ppermute(own, "core", [(0, 1), (1, 0)])
    return jnp.transpose(spectrum(own, other, ids, given, made), (2, 0, 1))


def solution(mesh):
    split = jax.sharding.Mesh(mesh.devices.reshape(8, 2, 2, 8), ("z", "xh", "core", "dish"))
    time = ("z", "xh", "core")
    return jax.shard_map(
        steps,
        mesh=split,
        in_specs=(P(None, "dish", time), P(None, "dish"), P(time)),
        out_specs=P("dish", None, time),
        check_vma=False,
    )
```

```python
import functools
import math

import jax
import jax.numpy as jnp
import numpy as np
from jax import lax
from jax.experimental import pallas as pl
from jax.experimental.pallas import tpu as pltpu
from jax.sharding import PartitionSpec as P


PH = 1024
LAGS = 2048
SAMPLES = 131072
DISH_WAYS = 8
TM_WAYS = 32
CHIPS = 16
HALF = SAMPLES // 2 // 128
LOCAL = SAMPLES // TM_WAYS
GRAIN = 128
PER_BLOCK = LOCAL // GRAIN
SPAN = LAGS // GRAIN
BINS = PH // TM_WAYS
FREQS = LAGS // DISH_WAYS
SLOTS = 128
GROUP = 16
VISITS = 8
ROWS = 2 * PER_BLOCK + VISITS
SCALE = 1.0 / math.sqrt(LAGS * SAMPLES / PH)

F32 = jnp.float32
BF16 = jnp.bfloat16


def dot(a, b, dims=(((1,), (0,)), ((), ()))):
    return lax.dot_general(a, b, dims, preferred_element_type=F32)


def hi_lo(value):
    hi = value.astype(BF16)
    return hi, (value - hi.astype(F32)).astype(BF16)


def tables():
    grain = np.arange(GRAIN)
    freq = np.arange(FREQS)
    angle = 2 * np.pi * np.outer(grain, freq) / LAGS
    base = np.concatenate([np.cos(angle), np.sin(angle)], 1).astype(np.float32)
    eighth = 2 * np.pi * np.outer(grain, np.arange(DISH_WAYS)) / DISH_WAYS
    turn = np.zeros((GRAIN, 128), np.float32)
    turn[:, :8] = np.cos(eighth)
    turn[:, 8:16] = np.sin(eighth)
    fine = 2 * np.pi * np.outer(grain, np.arange(2 * GRAIN)) / (2 * GRAIN)
    cos2, sin2 = np.cos(fine), np.sin(fine)
    fold2 = np.block([[cos2, sin2], [sin2, -cos2]]).astype(np.float32)
    step2 = np.block([[cos2, -sin2], [sin2, cos2]]).astype(np.float32)
    keep = (grain >= 1)[None, :] / (2.0 * GRAIN)
    back = np.block([[cos2.T * keep, -sin2.T * keep], [sin2.T * keep, cos2.T * keep]])
    sixteenth = 2 * np.pi * np.outer(np.arange(SPAN), freq) / SPAN
    phase = np.concatenate([np.cos(sixteenth), np.sin(sixteenth)], 1).astype(np.float32)
    return {
        "base": jnp.asarray(base),
        "turn": jnp.asarray(turn),
        "fold2": jnp.asarray(fold2).astype(BF16),
        "step2": jnp.asarray(step2).astype(BF16),
        "back": jnp.asarray(back.astype(np.float32)).astype(BF16),
        "phase": jnp.asarray(phase),
    }


def front_kernel(volts_hbm, weights_hbm, beam_ref, volts_s, weights_s, sems):
    copies = [
        pltpu.make_async_copy(source, target, sems.at[k])
        for k, (source, target) in enumerate(((weights_hbm, weights_s), (volts_hbm, volts_s)))
    ]
    for copy in copies:
        copy.start()
    for copy in copies:
        copy.wait()
    weights = weights_s[...]
    first = dot(weights, volts_s[0])
    second = dot(weights, volts_s[1])
    real = first[0:1] - second[1:2]
    imag = first[1:2] + second[0:1]
    for row in range(PER_BLOCK):
        part = slice(row * GRAIN, (row + 1) * GRAIN)
        beam_ref[0, row : row + 1, :] = real[:, part]
        beam_ref[0, PER_BLOCK + row : PER_BLOCK + row + 1, :] = imag[:, part]
    rows = beam_ref[0]
    for way in range(1, DISH_WAYS):
        beam_ref[way] = rows


def pack_kernel(parts_ref, visit_ref, out_ref):
    total = parts_ref[0]
    for way in range(1, DISH_WAYS):
        total = total + parts_ref[way]
    rows = total.astype(BF16)
    for chip in range(CHIPS):
        out_ref[chip, : 2 * PER_BLOCK, :] = rows
        out_ref[chip, 2 * PER_BLOCK :, :] = visit_ref[chip]


def coded_times(shape):
    row = lax.broadcasted_iota(jnp.int32, shape, 0)
    lane = lax.broadcasted_iota(jnp.int32, shape, 1)
    return (lane + 128).astype(F32) * two_to(row)


def triangle(count, strict):
    row = lax.broadcasted_iota(jnp.int32, (count, count), 0)
    column = lax.broadcasted_iota(jnp.int32, (count, count), 1)
    return jnp.where(row < column if strict else row <= column, 1.0, 0.0).astype(BF16)


def visit_kernel(bins_ref, out_ref, time_s, row_s):
    bins = bins_ref[...]
    shape = (PER_BLOCK, GRAIN)
    row = lax.broadcasted_iota(jnp.int32, shape, 0)
    lane = lax.broadcasted_iota(jnp.int32, shape, 1)
    rolled = pltpu.roll(bins, 1, 1)
    before = jnp.where(lane == 0, pltpu.roll(rolled, 1, 0), rolled)
    later = row + lane > 0
    enters = later & (bins != before)
    wraps = jnp.where(later & (bins < before), 1.0, 0.0).astype(BF16)
    in_row = dot(wraps, triangle(GRAIN, False))
    ends = jnp.broadcast_to(in_row[:, GRAIN - 1 :], shape).astype(BF16)
    above = dot(triangle(PER_BLOCK, True), ends, (((0,), (0,)), ((), ())))
    step = bins + PH * (in_row + above).astype(jnp.int32)
    high = jnp.where(enters, step >> 7, -1)
    low = step & 127
    times = coded_times(shape)
    high_iota = lax.broadcasted_iota(jnp.int32, (48, GRAIN), 0)
    low_iota = lax.broadcasted_iota(jnp.int32, (GRAIN, GRAIN), 0)
    found = jnp.zeros((96, GRAIN), F32)
    for pair in range(PER_BLOCK // 2):
        left, right = [], []
        for k in (2 * pair, 2 * pair + 1):
            here = high[k : k + 1, :] == high_iota
            coded = jnp.where(here, times[k : k + 1, :], 0.0)
            left.append(jnp.concatenate([coded, jnp.where(here, float(k), 0.0)], 0))
            right.append(jnp.where(low[k : k + 1, :] == low_iota, 1.0, 0.0))
        left = jnp.concatenate(left, 1).astype(BF16)
        right = jnp.concatenate(right, 1).astype(BF16)
        found = found + dot(left, right, (((1,), (1,)), ((), ())))
    place = high_iota * GRAIN + lax.broadcasted_iota(jnp.int32, (48, GRAIN), 1)
    past, ahead = place <= step[0:1, 0:1], place > step[PER_BLOCK - 1 :, GRAIN - 1 :]
    time_s[:48, :] = jnp.where(past, 2.0**-9, jnp.where(ahead, 2.0**23, found[:48]))
    row_s[:48, :] = jnp.where(past, 0.0, jnp.where(ahead, 32.0, found[48:]))
    time_s[48:, :] = jnp.full((24, GRAIN), 2.0**23, F32)
    row_s[48:, :] = jnp.full((24, GRAIN), 32.0, F32)
    lane = lax.broadcasted_iota(jnp.int32, (VISITS, GRAIN), 1)
    for eighth in range(8):
        now, then = pl.ds(eighth, VISITS, stride=8), pl.ds(eighth + 1, VISITS, stride=8)
        time, rows = time_s[now, :], row_s[now, :]
        next_time, next_rows = time_s[then, :], row_s[then, :]
        even = jnp.where(lane == 65, pltpu.roll(rows, 65, 1), time)
        even = jnp.where(lane == 66, pltpu.roll(rows, 34, 1), even)
        even = jnp.where(lane == 67, pltpu.roll(rows, 3, 1), even)
        odd = jnp.where(lane == 64, pltpu.roll(next_time, 64, 1), pltpu.roll(time, 64, 1))
        odd = jnp.where(lane == 65, pltpu.roll(rows, 1, 1), odd)
        odd = jnp.where(lane == 66, pltpu.roll(rows, 98, 1), odd)
        odd = jnp.where(lane == 67, pltpu.roll(next_rows, 67, 1), odd)
        out_ref[2 * eighth] = even.astype(BF16)
        out_ref[2 * eighth + 1] = odd.astype(BF16)


def two_to(exponent):
    value = jnp.full(jnp.shape(exponent), 2.0**-16, F32)
    for bit in range(5):
        value = value * jnp.where((exponent >> bit) & 1 == 1, float(2 ** (2**bit)), 1.0)
    return value


def table_kernel(ids, base_ref, turn_ref, fold2_ref, phase_ref, fold_ref, step_ref, last_ref, phases_ref):
    _, dish, _ = ids()
    lane = lax.broadcasted_iota(jnp.int32, (GRAIN, 128), 1)
    turn = turn_ref[...]
    cos8 = jnp.sum(jnp.where(lane == dish, turn, 0.0), axis=1, keepdims=True)
    sin8 = jnp.sum(jnp.where(lane == dish + 8, turn, 0.0), axis=1, keepdims=True)
    cos0, sin0 = base_ref[:, :FREQS], base_ref[:, FREQS:]
    cosine, cosine_lo = hi_lo(cos0 * cos8 - sin0 * sin8)
    sine, sine_lo = hi_lo(sin0 * cos8 + cos0 * sin8)
    fold_ref[:GRAIN, :FREQS] = cosine
    fold_ref[:GRAIN, FREQS : 2 * FREQS] = sine
    fold_ref[GRAIN:, :FREQS] = sine
    fold_ref[GRAIN:, FREQS : 2 * FREQS] = -cosine
    fold_ref[:, 2 * FREQS :] = fold2_ref[...]
    for k, (c, s) in enumerate(((cosine, sine), (cosine_lo, sine_lo))):
        step_ref[k, :GRAIN, :FREQS] = c
        step_ref[k, :GRAIN, FREQS:] = -s
        step_ref[k, GRAIN:, :FREQS] = s
        step_ref[k, GRAIN:, FREQS:] = c
    last_ref[:GRAIN, :FREQS] = cosine
    last_ref[:GRAIN, FREQS:] = sine
    last_ref[GRAIN:, :FREQS] = -sine
    last_ref[GRAIN:, FREQS:] = cosine
    phases_ref[...] = jnp.zeros(phases_ref.shape, BF16)
    hi, lo = hi_lo(phase_ref[...])
    phases_ref[0:SPAN, :] = hi
    phases_ref[SPAN : 2 * SPAN, :] = lo


def beam_rows(ref, first, last):
    rows = [
        jnp.concatenate([ref[chip, :PER_BLOCK, :], ref[chip, PER_BLOCK : 2 * PER_BLOCK, :]], 1)
        for chip in range(first, last)
    ]
    return jnp.concatenate(rows, 0)


def transform(ref, step_ref, phase_ref, z_ref):
    cos16, sin16 = phase_ref[:, :FREQS], phase_ref[:, FREQS:]
    cos_rows = jnp.concatenate([cos16] * (128 // SPAN), 0)
    sin_rows = jnp.concatenate([sin16] * (128 // SPAN), 0)
    for tile in range(HALF // 128):
        rows = slice(tile * 128, tile * 128 + 128)
        beam = beam_rows(ref, 4 * tile, 4 * tile + 4)
        both = dot(beam, step_ref[0]) + dot(beam, step_ref[1])
        real, imag = both[:, :FREQS], both[:, FREQS:]
        z_ref[rows, :FREQS] = (real * cos_rows + imag * sin_rows).astype(BF16)
        z_ref[rows, FREQS:] = (imag * cos_rows - real * sin_rows).astype(BF16)


def plan_half(ref, core, before):
    times = jnp.concatenate([ref[chip, 2 * PER_BLOCK :, :].astype(F32) for chip in range(CHIPS)], 0).astype(BF16)
    row = lax.broadcasted_iota(jnp.int32, (8, 128), 0)
    lane = lax.broadcasted_iota(jnp.int32, (8, 128), 1)
    wanted = jnp.where(row == 0, BINS * core, jnp.where(row == 1, BINS * core + BINS, core + 63 + row))
    info = dot(jnp.where(lane == wanted, 1.0, 0.0).astype(BF16), times, (((1,), (1,)), ((), ())))
    start, end, first, last = (info[k : k + 1, :] for k in range(4))
    grains = jnp.where(end > start, jnp.minimum(last, float(PER_BLOCK - 1)) - first + 1.0, 0.0)
    earlier = dot(jnp.broadcast_to(grains, (8, 128)).astype(BF16), triangle(128, True))[0:1, :] + before
    return times, end, first, grains, earlier, earlier[:, 127:] + grains[:, 127:]


def slots_half(slot_0, plan, ref):
    times, end, first, grains, earlier, _ = plan
    slot = lax.broadcasted_iota(jnp.int32, (SLOTS, 128), 0).astype(F32) + slot_0
    visit = lax.broadcasted_iota(jnp.int32, (SLOTS, 128), 1)
    mine = (slot >= earlier) & (slot < earlier + grains)
    place = ((visit >> 3) * PER_BLOCK + 1).astype(F32) + first + (slot - earlier)
    place = jnp.sum(jnp.where(mine, place, 0.0), axis=1, keepdims=True) - 1.0
    ends = jnp.sum(jnp.where(mine, jnp.broadcast_to(end, (SLOTS, 128)), 0.0), axis=1, keepdims=True)
    starts = dot(times, jnp.where(mine, 1.0, 0.0).astype(BF16), (((0,), (1,)), ((), ())))
    places = lax.broadcasted_iota(jnp.int32, (SLOTS, HALF), 1).astype(F32)
    pick = jnp.where(places == place, 1.0, 0.0).astype(BF16)
    return place, ends, starts, dot(pick, beam_rows(ref, 0, CHIPS))


def half_kernel(ids, own_ref, step_ref, phase_ref, z_ref, total_ref, place_ref, ends_ref, starts_ref, gbeam_ref):
    _, _, core = ids()
    plan = plan_half(own_ref, core, jnp.zeros((1, 1), F32))
    place, ends, starts, beam = slots_half(jnp.float32(0.0), plan, own_ref)
    total_ref[...] = jnp.broadcast_to(plan[-1], (8, 128))
    place_ref[...] = jnp.broadcast_to(place, (SLOTS, 128))
    ends_ref[...] = jnp.broadcast_to(ends, (SLOTS, 128))
    starts_ref[...] = starts
    gbeam_ref[...] = beam
    transform(own_ref, step_ref, phase_ref, z_ref)


def grain_row(which):
    place = lax.broadcasted_iota(jnp.int32, (8, HALF), 1)
    grain = (2 * (place >> 5) + which) * PER_BLOCK + (place & (PER_BLOCK - 1))
    return grain.astype(F32)[0:1, :]


def spectrum_kernel(
    ids,
    own_ref, other_ref, z_ref, total_ref, place_ref, ends_ref, starts_ref, gbeam_ref,
    fold_ref, step_ref, last_ref, phases_ref, step2_ref, back_ref, phase_ref,
    out_ref,
    z_s, gdft_s, gstep_s, gbeam_s, gtime_s, gstart_s, acc_s,
):
    _, _, core = ids()
    before = total_ref[0:1, 0:1]
    other_plan = plan_half(other_ref, core, before)
    count = jnp.max(other_plan[-1]).astype(jnp.int32)
    transform(other_ref, step_ref, phase_ref, z_s)
    acc_s[...] = jnp.zeros(acc_s.shape, F32)
    own_grains = jnp.broadcast_to(grain_row(core), (SLOTS, HALF))
    other_grains = jnp.broadcast_to(grain_row(1 - core), (SLOTS, HALF))
    lane_iota = lax.broadcasted_iota(jnp.int32, (SLOTS, 128), 1)

    def fold_batch(batch, mine):
        first = (batch * SLOTS).astype(F32)
        more = slots_half(first, other_plan, other_ref)
        is_mine = mine[0] >= 0.0
        place = jnp.where(is_mine, mine[0], more[0]).astype(jnp.int32)
        which = jnp.where(is_mine, core, 1 - core)
        in_block = place & (PER_BLOCK - 1)
        grain = ((2 * (place >> 5) + which) * PER_BLOCK + in_block).astype(F32)
        here = mine[3] + more[3]
        times = (lane_iota + 128).astype(F32) * two_to(jnp.broadcast_to(in_block, (SLOTS, 128)))
        gtime_s[...] = times
        inside = times < mine[1] + more[1]
        gbeam_s[:, :GRAIN] = jnp.where(inside, here[:, :GRAIN], 0.0)
        gbeam_s[:, GRAIN:] = jnp.where(inside, here[:, GRAIN:], 0.0)
        starts = mine[2] + more[2]
        starts = jnp.where(core == 0, starts[:BINS], starts[BINS : 2 * BINS])
        for group in range(SLOTS // GROUP):
            gstart_s[group] = starts if group == 0 else pltpu.roll(starts, SLOTS - group * GROUP, 1)
        dft = jnp.zeros((SLOTS, 2 * FREQS), F32)
        ahead = jnp.zeros((SLOTS, 2 * GRAIN), F32)
        for grains, z, ref in ((own_grains, z_ref, own_ref), (other_grains, z_s, other_ref)):
            window = (grains >= grain) & (grains < grain + float(SPAN))
            dft = dft + dot(jnp.where(window, 1.0, 0.0).astype(BF16), z[...])
            next_pick = jnp.where(grains == grain + float(SPAN), 1.0, 0.0).astype(BF16)
            ahead = ahead + dot(next_pick, beam_rows(ref, 0, CHIPS))
        offset = in_block & (SPAN - 1)
        turner = jnp.where((lane_iota == offset) | (lane_iota == offset + SPAN), 1.0, 0.0)
        turned = dot(turner.astype(BF16), phases_ref[...])
        real, imag = dft[:, :FREQS], dft[:, FREQS:]
        cos_g, sin_g = turned[:, :FREQS], turned[:, FREQS:]
        gdft_s[:, :FREQS] = real * cos_g - imag * sin_g
        gdft_s[:, FREQS:] = imag * cos_g + real * sin_g
        gstep_s[...] = dot((ahead - here).astype(BF16), step2_ref[...])

        def group_step(group, inner):
            rows = pl.ds(pl.multiple_of(group * GROUP, GROUP), GROUP)
            beam8, time8, start8 = gbeam_s[rows, :], gtime_s[rows, :], gstart_s[group]
            dft8, step8 = gdft_s[rows, :], gstep_s[rows, :]
            left = []
            for k in range(GROUP):
                since = time8[k : k + 1, :] >= start8[:, k : k + 1]
                real = jnp.where(since, beam8[k : k + 1, :GRAIN], 0.0)
                imag = jnp.where(since, beam8[k : k + 1, GRAIN:], 0.0)
                left.append(jnp.concatenate([real, imag], 1))
            left = jnp.concatenate(left, 0).astype(BF16)
            for at, factor in ((0, dft8), (2 * FREQS, step8)):
                folded = dot(left, fold_ref[:, at : at + 2 * FREQS])
                real_sum, imag_sum = acc_s[:, at : at + FREQS], acc_s[:, at + FREQS : at + 2 * FREQS]
                for k in range(GROUP):
                    part = slice(k * BINS, k * BINS + BINS)
                    real, imag = folded[part, :FREQS], folded[part, FREQS:]
                    cos_f, sin_f = factor[k : k + 1, :FREQS], factor[k : k + 1, FREQS:]
                    real_sum = real_sum + (real * cos_f - imag * sin_f)
                    imag_sum = imag_sum + (real * sin_f + imag * cos_f)
                acc_s[:, at : at + FREQS] = real_sum
                acc_s[:, at + FREQS : at + 2 * FREQS] = imag_sum
            return inner

        left_over = jnp.minimum(count - batch * SLOTS, SLOTS)
        lax.fori_loop(0, (left_over + GROUP - 1) // GROUP, group_step, 0)

    fold_batch(jnp.int32(0), (place_ref[:, 0:1], ends_ref[:, 0:1], starts_ref[...], gbeam_ref[...]))

    def batch_step(batch, carry):
        own_plan = plan_half(own_ref, core, jnp.zeros((1, 1), F32))
        fold_batch(batch, slots_half((batch * SLOTS).astype(F32), own_plan, own_ref))
        return carry

    lax.fori_loop(1, (count + SLOTS - 1) // SLOTS, batch_step, 0)
    since = acc_s[...]
    each = since - jnp.concatenate([since[1:], jnp.zeros((1, 4 * FREQS), F32)], 0)
    hi, lo = hi_lo(each[:, 2 * FREQS :])
    short = dot(hi, back_ref[...]) + dot(lo, back_ref[...])
    hi, lo = hi_lo(short)
    short = dot(hi, last_ref[...]) + dot(lo, last_ref[...])
    out_ref[0] = (each[:, :FREQS] + short[:, :FREQS]) * SCALE
    out_ref[1] = (each[:, FREQS : 2 * FREQS] + short[:, FREQS:]) * SCALE


def near(*values):
    return [pltpu.with_memory_space_constraint(v, pltpu.VMEM) for v in values]


def call(kernel, outs, values, scratch=(), mib=8, us=1.0):
    one = not isinstance(outs, (tuple, list))
    space = pl.BlockSpec(memory_space=pltpu.VMEM)
    return pl.pallas_call(
        kernel,
        out_shape=outs if one else tuple(outs),
        in_specs=[space] * len(values),
        out_specs=space if one else (space,) * len(outs),
        scratch_shapes=list(scratch),
        compiler_params=pltpu.CompilerParams(vmem_limit_bytes=mib << 20),
        cost_estimate=pl.CostEstimate(flops=int(us * 5e8), bytes_accessed=1 << 20, transcendentals=0),
    )(*near(*values))


HALF_Z = pltpu.VMEM((HALF, 2 * FREQS), BF16)


def make_tables(ids):
    given = tables()
    made = call(
        functools.partial(table_kernel, ids),
        (
            pltpu.VMEM((2 * GRAIN, 4 * FREQS), BF16),
            pltpu.VMEM((2, 2 * GRAIN, 2 * FREQS), BF16),
            pltpu.VMEM((2 * GRAIN, 2 * FREQS), BF16),
            pltpu.VMEM((128, 2 * FREQS), BF16),
        ),
        [given[k] for k in ("base", "turn", "fold2", "phase")],
        us=3.0,
    )
    return given, made


def spectrum(own, other, ids, given, made):
    fold, step, last, phases = made
    phase = given["phase"]
    half = call(
        functools.partial(half_kernel, ids),
        (
            HALF_Z,
            pltpu.VMEM((8, 128), F32),
            pltpu.VMEM((SLOTS, 128), F32),
            pltpu.VMEM((SLOTS, 128), F32),
            pltpu.VMEM((128, SLOTS), F32),
            pltpu.VMEM((SLOTS, 2 * GRAIN), F32),
        ),
        (own, step, phase),
        us=1.0,
    )
    scratch = [
        HALF_Z,
        pltpu.VMEM((SLOTS, 2 * FREQS), F32),
        pltpu.VMEM((SLOTS, 2 * FREQS), F32),
        pltpu.VMEM((SLOTS, 2 * GRAIN), F32),
        pltpu.VMEM((SLOTS, GRAIN), F32),
        pltpu.VMEM((SLOTS // GROUP, BINS, 128), F32),
        pltpu.VMEM((BINS, 4 * FREQS), F32),
    ]
    return call(
        functools.partial(spectrum_kernel, ids),
        jax.ShapeDtypeStruct((2, BINS, FREQS), F32),
        (own, other, *half, fold, step, last, phases, given["step2"], given["back"], phase),
        scratch,
        mib=16,
        us=5.0,
    )


def front(voltages, beam_weights):
    far = pl.BlockSpec(memory_space=pltpu.HBM)
    return pl.pallas_call(
        front_kernel,
        out_shape=pltpu.VMEM((DISH_WAYS, 2 * PER_BLOCK, GRAIN), F32),
        in_specs=[far] * 2,
        out_specs=pl.BlockSpec(memory_space=pltpu.VMEM),
        scratch_shapes=[
            pltpu.VMEM(voltages.shape, BF16),
            pltpu.VMEM(beam_weights.shape, BF16),
            pltpu.SemaphoreType.DMA((2,)),
        ],
        compiler_params=pltpu.CompilerParams(vmem_limit_bytes=8 << 20),
        cost_estimate=pl.CostEstimate(flops=1 << 20, bytes_accessed=1 << 20, transcendentals=0),
        name="front",
    )(*(pltpu.with_memory_space_constraint(v, pltpu.HBM) for v in (voltages, beam_weights)))


def steps(voltages, beam_weights, phase_bins):
    def ids():
        core = lax.axis_index("core")
        owner = (lax.axis_index("z") * 2 + lax.axis_index("xh")) * 2 + core
        return owner, lax.axis_index("dish"), core

    given, made = make_tables(ids)
    visits = call(
        visit_kernel,
        pltpu.VMEM((CHIPS, VISITS, GRAIN), BF16),
        (phase_bins.reshape(PER_BLOCK, GRAIN),),
        [pltpu.VMEM((72, GRAIN), F32)] * 2,
        us=3.0,
    )
    partial_beam = front(voltages, beam_weights)
    parts = lax.all_to_all(partial_beam, "dish", 0, 0, tiled=True)
    packed = call(pack_kernel, pltpu.VMEM((CHIPS, ROWS, GRAIN), BF16), (parts, visits), us=0.3)
    own = lax.all_to_all(packed, ("z", "xh"), 0, 0, tiled=True)
    other = lax.ppermute(own, "core", [(0, 1), (1, 0)])
    return jnp.transpose(spectrum(own, other, ids, given, made), (2, 0, 1))


def solution(mesh):
    split = jax.sharding.Mesh(mesh.devices.reshape(8, 2, 2, 8), ("z", "xh", "core", "dish"))
    time = ("z", "xh", "core")
    return jax.shard_map(
        steps,
        mesh=split,
        in_specs=(P(None, "dish", time), P(None, "dish"), P(time)),
        out_specs=P("dish", None, time),
        check_vma=False,
    )
```

```python
import functools
import math

import jax
import jax.numpy as jnp
import numpy as np
from jax import lax
from jax.experimental import pallas as pl
from jax.experimental.pallas import tpu as pltpu
from jax.sharding import PartitionSpec as P


PH = 1024
LAGS = 2048
SAMPLES = 131072
DISH_WAYS = 8
TM_WAYS = 32
CHIPS = 16
HALF = SAMPLES // 2 // 128
LOCAL = SAMPLES // TM_WAYS
GRAIN = 128
PER_BLOCK = LOCAL // GRAIN
SPAN = LAGS // GRAIN
BINS = PH // TM_WAYS
FREQS = LAGS // DISH_WAYS
SLOTS = 128
GROUP = 16
VISITS = 8
ROWS = 2 * PER_BLOCK + VISITS
SCALE = 1.0 / math.sqrt(LAGS * SAMPLES / PH)

F32 = jnp.float32
BF16 = jnp.bfloat16


def dot(a, b, dims=(((1,), (0,)), ((), ()))):
    return lax.dot_general(a, b, dims, preferred_element_type=F32)


def hi_lo(value):
    hi = value.astype(BF16)
    return hi, (value - hi.astype(F32)).astype(BF16)


def tables():
    grain = np.arange(GRAIN)
    freq = np.arange(FREQS)
    angle = 2 * np.pi * np.outer(grain, freq) / LAGS
    base = np.concatenate([np.cos(angle), np.sin(angle)], 1).astype(np.float32)
    eighth = 2 * np.pi * np.outer(grain, np.arange(DISH_WAYS)) / DISH_WAYS
    turn = np.zeros((GRAIN, 128), np.float32)
    turn[:, :8] = np.cos(eighth)
    turn[:, 8:16] = np.sin(eighth)
    fine = 2 * np.pi * np.outer(grain, np.arange(2 * GRAIN)) / (2 * GRAIN)
    cos2, sin2 = np.cos(fine), np.sin(fine)
    fold2 = np.block([[cos2, sin2], [sin2, -cos2]]).astype(np.float32)
    step2 = np.block([[cos2, -sin2], [sin2, cos2]]).astype(np.float32)
    keep = (grain >= 1)[None, :] / (2.0 * GRAIN)
    back = np.block([[cos2.T * keep, -sin2.T * keep], [sin2.T * keep, cos2.T * keep]])
    sixteenth = 2 * np.pi * np.outer(np.arange(SPAN), freq) / SPAN
    phase = np.concatenate([np.cos(sixteenth), np.sin(sixteenth)], 1).astype(np.float32)
    return {
        "base": jnp.asarray(base),
        "turn": jnp.asarray(turn),
        "fold2": jnp.asarray(fold2).astype(BF16),
        "step2": jnp.asarray(step2).astype(BF16),
        "back": jnp.asarray(back.astype(np.float32)).astype(BF16),
        "phase": jnp.asarray(phase),
    }


def front_kernel(volts_hbm, weights_hbm, beam_hbm, volts_s, weights_s, beam_s, sems):
    copies = [
        pltpu.make_async_copy(source, target, sems.at[k])
        for k, (source, target) in enumerate(((weights_hbm, weights_s), (volts_hbm, volts_s)))
    ]
    for copy in copies:
        copy.start()
    for copy in copies:
        copy.wait()
    weights = weights_s[...]
    first = dot(weights, volts_s[0])
    second = dot(weights, volts_s[1])
    real = first[0:1] - second[1:2]
    imag = first[1:2] + second[0:1]
    for row in range(PER_BLOCK):
        part = slice(row * GRAIN, (row + 1) * GRAIN)
        beam_s[row : row + 1, :] = real[:, part]
        beam_s[PER_BLOCK + row : PER_BLOCK + row + 1, :] = imag[:, part]
    copies = [
        pltpu.make_async_copy(beam_s, beam_hbm.at[way], sems.at[2 + way]) for way in range(DISH_WAYS)
    ]
    for copy in copies:
        copy.start()
    for copy in copies:
        copy.wait()


def pack_kernel(parts_ref, visit_ref, out_ref):
    total = parts_ref[0]
    for way in range(1, DISH_WAYS):
        total = total + parts_ref[way]
    rows = total.astype(BF16)
    for chip in range(CHIPS):
        out_ref[chip, : 2 * PER_BLOCK, :] = rows
        out_ref[chip, 2 * PER_BLOCK :, :] = visit_ref[chip]


def coded_times(shape):
    row = lax.broadcasted_iota(jnp.int32, shape, 0)
    lane = lax.broadcasted_iota(jnp.int32, shape, 1)
    return (lane + 128).astype(F32) * two_to(row)


def triangle(count, strict):
    row = lax.broadcasted_iota(jnp.int32, (count, count), 0)
    column = lax.broadcasted_iota(jnp.int32, (count, count), 1)
    return jnp.where(row < column if strict else row <= column, 1.0, 0.0).astype(BF16)


def visit_kernel(bins_ref, out_ref, time_s, row_s):
    bins = bins_ref[...]
    shape = (PER_BLOCK, GRAIN)
    row = lax.broadcasted_iota(jnp.int32, shape, 0)
    lane = lax.broadcasted_iota(jnp.int32, shape, 1)
    rolled = pltpu.roll(bins, 1, 1)
    before = jnp.where(lane == 0, pltpu.roll(rolled, 1, 0), rolled)
    later = row + lane > 0
    enters = later & (bins != before)
    wraps = jnp.where(later & (bins < before), 1.0, 0.0).astype(BF16)
    in_row = dot(wraps, triangle(GRAIN, False))
    ends = jnp.broadcast_to(in_row[:, GRAIN - 1 :], shape).astype(BF16)
    above = dot(triangle(PER_BLOCK, True), ends, (((0,), (0,)), ((), ())))
    step = bins + PH * (in_row + above).astype(jnp.int32)
    high = jnp.where(enters, step >> 7, -1)
    low = step & 127
    times = coded_times(shape)
    high_iota = lax.broadcasted_iota(jnp.int32, (48, GRAIN), 0)
    low_iota = lax.broadcasted_iota(jnp.int32, (GRAIN, GRAIN), 0)
    found = jnp.zeros((96, GRAIN), F32)
    for pair in range(PER_BLOCK // 2):
        left, right = [], []
        for k in (2 * pair, 2 * pair + 1):
            here = high[k : k + 1, :] == high_iota
            coded = jnp.where(here, times[k : k + 1, :], 0.0)
            left.append(jnp.concatenate([coded, jnp.where(here, float(k), 0.0)], 0))
            right.append(jnp.where(low[k : k + 1, :] == low_iota, 1.0, 0.0))
        left = jnp.concatenate(left, 1).astype(BF16)
        right = jnp.concatenate(right, 1).astype(BF16)
        found = found + dot(left, right, (((1,), (1,)), ((), ())))
    place = high_iota * GRAIN + lax.broadcasted_iota(jnp.int32, (48, GRAIN), 1)
    past, ahead = place <= step[0:1, 0:1], place > step[PER_BLOCK - 1 :, GRAIN - 1 :]
    time_s[:48, :] = jnp.where(past, 2.0**-9, jnp.where(ahead, 2.0**23, found[:48]))
    row_s[:48, :] = jnp.where(past, 0.0, jnp.where(ahead, 32.0, found[48:]))
    time_s[48:, :] = jnp.full((24, GRAIN), 2.0**23, F32)
    row_s[48:, :] = jnp.full((24, GRAIN), 32.0, F32)
    lane = lax.broadcasted_iota(jnp.int32, (VISITS, GRAIN), 1)
    for eighth in range(8):
        now, then = pl.ds(eighth, VISITS, stride=8), pl.ds(eighth + 1, VISITS, stride=8)
        time, rows = time_s[now, :], row_s[now, :]
        next_time, next_rows = time_s[then, :], row_s[then, :]
        even = jnp.where(lane == 65, pltpu.roll(rows, 65, 1), time)
        even = jnp.where(lane == 66, pltpu.roll(rows, 34, 1), even)
        even = jnp.where(lane == 67, pltpu.roll(rows, 3, 1), even)
        odd = jnp.where(lane == 64, pltpu.roll(next_time, 64, 1), pltpu.roll(time, 64, 1))
        odd = jnp.where(lane == 65, pltpu.roll(rows, 1, 1), odd)
        odd = jnp.where(lane == 66, pltpu.roll(rows, 98, 1), odd)
        odd = jnp.where(lane == 67, pltpu.roll(next_rows, 67, 1), odd)
        out_ref[2 * eighth] = even.astype(BF16)
        out_ref[2 * eighth + 1] = odd.astype(BF16)


def two_to(exponent):
    value = jnp.full(jnp.shape(exponent), 2.0**-16, F32)
    for bit in range(5):
        value = value * jnp.where((exponent >> bit) & 1 == 1, float(2 ** (2**bit)), 1.0)
    return value


def table_kernel(ids, base_ref, turn_ref, fold2_ref, phase_ref, fold_ref, step_ref, last_ref, phases_ref):
    _, dish, _ = ids()
    lane = lax.broadcasted_iota(jnp.int32, (GRAIN, 128), 1)
    turn = turn_ref[...]
    cos8 = jnp.sum(jnp.where(lane == dish, turn, 0.0), axis=1, keepdims=True)
    sin8 = jnp.sum(jnp.where(lane == dish + 8, turn, 0.0), axis=1, keepdims=True)
    cos0, sin0 = base_ref[:, :FREQS], base_ref[:, FREQS:]
    cosine, cosine_lo = hi_lo(cos0 * cos8 - sin0 * sin8)
    sine, sine_lo = hi_lo(sin0 * cos8 + cos0 * sin8)
    fold_ref[:GRAIN, :FREQS] = cosine
    fold_ref[:GRAIN, FREQS : 2 * FREQS] = sine
    fold_ref[GRAIN:, :FREQS] = sine
    fold_ref[GRAIN:, FREQS : 2 * FREQS] = -cosine
    fold_ref[:, 2 * FREQS :] = fold2_ref[...]
    for k, (c, s) in enumerate(((cosine, sine), (cosine_lo, sine_lo))):
        step_ref[k, :GRAIN, :FREQS] = c
        step_ref[k, :GRAIN, FREQS:] = -s
        step_ref[k, GRAIN:, :FREQS] = s
        step_ref[k, GRAIN:, FREQS:] = c
    last_ref[:GRAIN, :FREQS] = cosine
    last_ref[:GRAIN, FREQS:] = sine
    last_ref[GRAIN:, :FREQS] = -sine
    last_ref[GRAIN:, FREQS:] = cosine
    phases_ref[...] = jnp.zeros(phases_ref.shape, BF16)
    hi, lo = hi_lo(phase_ref[...])
    phases_ref[0:SPAN, :] = hi
    phases_ref[SPAN : 2 * SPAN, :] = lo


def beam_rows(ref, first, last):
    rows = [
        jnp.concatenate([ref[chip, :PER_BLOCK, :], ref[chip, PER_BLOCK : 2 * PER_BLOCK, :]], 1)
        for chip in range(first, last)
    ]
    return jnp.concatenate(rows, 0)


def transform(ref, step_ref, phase_ref, z_ref):
    cos16, sin16 = phase_ref[:, :FREQS], phase_ref[:, FREQS:]
    cos_rows = jnp.concatenate([cos16] * (128 // SPAN), 0)
    sin_rows = jnp.concatenate([sin16] * (128 // SPAN), 0)
    for tile in range(HALF // 128):
        rows = slice(tile * 128, tile * 128 + 128)
        beam = beam_rows(ref, 4 * tile, 4 * tile + 4)
        both = dot(beam, step_ref[0]) + dot(beam, step_ref[1])
        real, imag = both[:, :FREQS], both[:, FREQS:]
        z_ref[rows, :FREQS] = (real * cos_rows + imag * sin_rows).astype(BF16)
        z_ref[rows, FREQS:] = (imag * cos_rows - real * sin_rows).astype(BF16)


def plan_half(ref, core, before):
    times = jnp.concatenate([ref[chip, 2 * PER_BLOCK :, :].astype(F32) for chip in range(CHIPS)], 0).astype(BF16)
    row = lax.broadcasted_iota(jnp.int32, (8, 128), 0)
    lane = lax.broadcasted_iota(jnp.int32, (8, 128), 1)
    wanted = jnp.where(row == 0, BINS * core, jnp.where(row == 1, BINS * core + BINS, core + 63 + row))
    info = dot(jnp.where(lane == wanted, 1.0, 0.0).astype(BF16), times, (((1,), (1,)), ((), ())))
    start, end, first, last = (info[k : k + 1, :] for k in range(4))
    grains = jnp.where(end > start, jnp.minimum(last, float(PER_BLOCK - 1)) - first + 1.0, 0.0)
    earlier = dot(jnp.broadcast_to(grains, (8, 128)).astype(BF16), triangle(128, True))[0:1, :] + before
    return times, end, first, grains, earlier, earlier[:, 127:] + grains[:, 127:]


def slots_half(slot_0, plan, ref):
    times, end, first, grains, earlier, _ = plan
    slot = lax.broadcasted_iota(jnp.int32, (SLOTS, 128), 0).astype(F32) + slot_0
    visit = lax.broadcasted_iota(jnp.int32, (SLOTS, 128), 1)
    mine = (slot >= earlier) & (slot < earlier + grains)
    place = ((visit >> 3) * PER_BLOCK + 1).astype(F32) + first + (slot - earlier)
    place = jnp.sum(jnp.where(mine, place, 0.0), axis=1, keepdims=True) - 1.0
    ends = jnp.sum(jnp.where(mine, jnp.broadcast_to(end, (SLOTS, 128)), 0.0), axis=1, keepdims=True)
    starts = dot(times, jnp.where(mine, 1.0, 0.0).astype(BF16), (((0,), (1,)), ((), ())))
    places = lax.broadcasted_iota(jnp.int32, (SLOTS, HALF), 1).astype(F32)
    pick = jnp.where(places == place, 1.0, 0.0).astype(BF16)
    return place, ends, starts, dot(pick, beam_rows(ref, 0, CHIPS))


def half_kernel(ids, own_ref, step_ref, phase_ref, z_ref, total_ref, place_ref, ends_ref, starts_ref, gbeam_ref):
    _, _, core = ids()
    plan = plan_half(own_ref, core, jnp.zeros((1, 1), F32))
    place, ends, starts, beam = slots_half(jnp.float32(0.0), plan, own_ref)
    total_ref[...] = jnp.broadcast_to(plan[-1], (8, 128))
    place_ref[...] = jnp.broadcast_to(place, (SLOTS, 128))
    ends_ref[...] = jnp.broadcast_to(ends, (SLOTS, 128))
    starts_ref[...] = starts
    gbeam_ref[...] = beam
    transform(own_ref, step_ref, phase_ref, z_ref)


def grain_row(which):
    place = lax.broadcasted_iota(jnp.int32, (8, HALF), 1)
    grain = (2 * (place >> 5) + which) * PER_BLOCK + (place & (PER_BLOCK - 1))
    return grain.astype(F32)[0:1, :]


def spectrum_kernel(
    ids,
    own_ref, other_ref, z_ref, total_ref, place_ref, ends_ref, starts_ref, gbeam_ref,
    fold_ref, step_ref, last_ref, phases_ref, step2_ref, back_ref, phase_ref,
    out_ref,
    z_s, gdft_s, gstep_s, gbeam_s, gtime_s, gstart_s, acc_s, fold_s,
):
    _, _, core = ids()
    before = total_ref[0:1, 0:1]
    other_plan = plan_half(other_ref, core, before)
    count = jnp.max(other_plan[-1]).astype(jnp.int32)
    transform(other_ref, step_ref, phase_ref, z_s)
    acc_s[...] = jnp.zeros(acc_s.shape, F32)
    fold_s[...] = fold_ref[...]
    own_grains = jnp.broadcast_to(grain_row(core), (SLOTS, HALF))
    other_grains = jnp.broadcast_to(grain_row(1 - core), (SLOTS, HALF))
    lane_iota = lax.broadcasted_iota(jnp.int32, (SLOTS, 128), 1)

    def fold_batch(batch, mine):
        first = (batch * SLOTS).astype(F32)
        more = slots_half(first, other_plan, other_ref)
        is_mine = mine[0] >= 0.0
        place = jnp.where(is_mine, mine[0], more[0]).astype(jnp.int32)
        which = jnp.where(is_mine, core, 1 - core)
        in_block = place & (PER_BLOCK - 1)
        grain = ((2 * (place >> 5) + which) * PER_BLOCK + in_block).astype(F32)
        here = mine[3] + more[3]
        times = (lane_iota + 128).astype(F32) * two_to(jnp.broadcast_to(in_block, (SLOTS, 128)))
        gtime_s[...] = times
        inside = times < mine[1] + more[1]
        gbeam_s[:, :GRAIN] = jnp.where(inside, here[:, :GRAIN], 0.0)
        gbeam_s[:, GRAIN:] = jnp.where(inside, here[:, GRAIN:], 0.0)
        starts = mine[2] + more[2]
        starts = jnp.where(core == 0, starts[:BINS], starts[BINS : 2 * BINS])
        for group in range(SLOTS // GROUP):
            gstart_s[group] = starts if group == 0 else pltpu.roll(starts, SLOTS - group * GROUP, 1)
        dft = jnp.zeros((SLOTS, 2 * FREQS), F32)
        ahead = jnp.zeros((SLOTS, 2 * GRAIN), F32)
        for grains, z, ref in ((own_grains, z_ref, own_ref), (other_grains, z_s, other_ref)):
            window = (grains >= grain) & (grains < grain + float(SPAN))
            dft = dft + dot(jnp.where(window, 1.0, 0.0).astype(BF16), z[...])
            next_pick = jnp.where(grains == grain + float(SPAN), 1.0, 0.0).astype(BF16)
            ahead = ahead + dot(next_pick, beam_rows(ref, 0, CHIPS))
        offset = in_block & (SPAN - 1)
        turner = jnp.where((lane_iota == offset) | (lane_iota == offset + SPAN), 1.0, 0.0)
        turned = dot(turner.astype(BF16), phases_ref[...])
        real, imag = dft[:, :FREQS], dft[:, FREQS:]
        cos_g, sin_g = turned[:, :FREQS], turned[:, FREQS:]
        step = dot((ahead - here).astype(BF16), step2_ref[...])
        for ref, real, imag in (
            (gdft_s, real * cos_g - imag * sin_g, imag * cos_g + real * sin_g),
            (gstep_s, step[:, :FREQS], step[:, FREQS:]),
        ):
            ref[:, :FREQS] = real
            ref[:, FREQS : 2 * FREQS] = imag - real
            ref[:, 2 * FREQS :] = real + imag

        def group_step(group, inner):
            rows = pl.ds(pl.multiple_of(group * GROUP, GROUP), GROUP)
            beam8, time8, start8 = gbeam_s[rows, :], gtime_s[rows, :], gstart_s[group]
            dft8, step8 = gdft_s[rows, :], gstep_s[rows, :]
            left = []
            for k in range(GROUP):
                since = time8[k : k + 1, :] >= start8[:, k : k + 1]
                real = jnp.where(since, beam8[k : k + 1, :GRAIN], 0.0)
                imag = jnp.where(since, beam8[k : k + 1, GRAIN:], 0.0)
                left.append(jnp.concatenate([real, imag], 1))
            left = jnp.concatenate(left, 0).astype(BF16)
            for part, factor in ((0, dft8), (1, step8)):
                folded = dot(left, fold_s[:, part * 2 * FREQS : part * 2 * FREQS + 2 * FREQS])
                sums = [acc_s[:, k * FREQS : k * FREQS + FREQS] for k in range(3 * part, 3 * part + 3)]
                for k in range(GROUP):
                    rows = slice(k * BINS, k * BINS + BINS)
                    real, imag = folded[rows, :FREQS], folded[rows, FREQS:]
                    for n, value in enumerate((real + imag, real, imag)):
                        sums[n] = sums[n] + value * factor[k : k + 1, n * FREQS : n * FREQS + FREQS]
                for n in range(3):
                    acc_s[:, (3 * part + n) * FREQS : (3 * part + n + 1) * FREQS] = sums[n]
            return inner

        def pair_step(pair, inner):
            group_step(2 * pair, inner)
            return group_step(2 * pair + 1, inner)

        groups = (jnp.minimum(count - batch * SLOTS, SLOTS) + GROUP - 1) // GROUP
        lax.fori_loop(0, groups // 2, pair_step, 0)
        lax.fori_loop(groups // 2 * 2, groups, group_step, 0)

    fold_batch(jnp.int32(0), (place_ref[:, 0:1], ends_ref[:, 0:1], starts_ref[...], gbeam_ref[...]))

    def batch_step(batch, carry):
        own_plan = plan_half(own_ref, core, jnp.zeros((1, 1), F32))
        fold_batch(batch, slots_half((batch * SLOTS).astype(F32), own_plan, own_ref))
        return carry

    lax.fori_loop(1, (count + SLOTS - 1) // SLOTS, batch_step, 0)
    since = acc_s[...]
    each = since - jnp.concatenate([since[1:], jnp.zeros((1, 6 * FREQS), F32)], 0)
    both, real, imag, both2, real2, imag2 = (each[:, k * FREQS : k * FREQS + FREQS] for k in range(6))
    hi, lo = hi_lo(jnp.concatenate([both2 - imag2, both2 + real2], 1))
    short = dot(hi, back_ref[...]) + dot(lo, back_ref[...])
    hi, lo = hi_lo(short)
    short = dot(hi, last_ref[...]) + dot(lo, last_ref[...])
    out_ref[0] = (both - imag + short[:, :FREQS]) * SCALE
    out_ref[1] = (both + real + short[:, FREQS:]) * SCALE


def near(*values):
    return [pltpu.with_memory_space_constraint(v, pltpu.VMEM) for v in values]


def call(kernel, outs, values, scratch=(), mib=8, us=1.0):
    one = not isinstance(outs, (tuple, list))
    space = pl.BlockSpec(memory_space=pltpu.VMEM)
    return pl.pallas_call(
        kernel,
        out_shape=outs if one else tuple(outs),
        in_specs=[space] * len(values),
        out_specs=space if one else (space,) * len(outs),
        scratch_shapes=list(scratch),
        compiler_params=pltpu.CompilerParams(vmem_limit_bytes=mib << 20),
        cost_estimate=pl.CostEstimate(flops=int(us * 5e8), bytes_accessed=1 << 20, transcendentals=0),
    )(*near(*values))


HALF_Z = pltpu.VMEM((HALF, 2 * FREQS), BF16)


def make_tables(ids):
    given = tables()
    made = call(
        functools.partial(table_kernel, ids),
        (
            pltpu.VMEM((2 * GRAIN, 4 * FREQS), BF16),
            pltpu.VMEM((2, 2 * GRAIN, 2 * FREQS), BF16),
            pltpu.VMEM((2 * GRAIN, 2 * FREQS), BF16),
            pltpu.VMEM((128, 2 * FREQS), BF16),
        ),
        [given[k] for k in ("base", "turn", "fold2", "phase")],
        us=3.0,
    )
    return given, made


def spectrum(own, other, ids, given, made):
    fold, step, last, phases = made
    phase = given["phase"]
    half = call(
        functools.partial(half_kernel, ids),
        (
            HALF_Z,
            pltpu.VMEM((8, 128), F32),
            pltpu.VMEM((SLOTS, 128), F32),
            pltpu.VMEM((SLOTS, 128), F32),
            pltpu.VMEM((128, SLOTS), F32),
            pltpu.VMEM((SLOTS, 2 * GRAIN), F32),
        ),
        (own, step, phase),
        us=1.0,
    )
    scratch = [
        HALF_Z,
        pltpu.VMEM((SLOTS, 3 * FREQS), F32),
        pltpu.VMEM((SLOTS, 3 * FREQS), F32),
        pltpu.VMEM((SLOTS, 2 * GRAIN), F32),
        pltpu.VMEM((SLOTS, GRAIN), F32),
        pltpu.VMEM((SLOTS // GROUP, BINS, 128), F32),
        pltpu.VMEM((BINS, 6 * FREQS), F32),
        pltpu.VMEM((2 * GRAIN, 4 * FREQS), BF16),
    ]
    return call(
        functools.partial(spectrum_kernel, ids),
        jax.ShapeDtypeStruct((2, BINS, FREQS), F32),
        (own, other, *half, fold, step, last, phases, given["step2"], given["back"], phase),
        scratch,
        mib=16,
        us=5.0,
    )


def front(voltages, beam_weights):
    far = pl.BlockSpec(memory_space=pltpu.HBM)
    return pl.pallas_call(
        front_kernel,
        out_shape=jax.ShapeDtypeStruct((DISH_WAYS, 2 * PER_BLOCK, GRAIN), F32),
        in_specs=[far] * 2,
        out_specs=far,
        scratch_shapes=[
            pltpu.VMEM(voltages.shape, BF16),
            pltpu.VMEM(beam_weights.shape, BF16),
            pltpu.VMEM((2 * PER_BLOCK, GRAIN), F32),
            pltpu.SemaphoreType.DMA((2 + DISH_WAYS,)),
        ],
        compiler_params=pltpu.CompilerParams(vmem_limit_bytes=8 << 20),
        cost_estimate=pl.CostEstimate(flops=1 << 20, bytes_accessed=1 << 20, transcendentals=0),
        name="front",
    )(*(pltpu.with_memory_space_constraint(v, pltpu.HBM) for v in (voltages, beam_weights)))


def steps(voltages, beam_weights, phase_bins):
    def ids():
        core = lax.axis_index("core")
        owner = (lax.axis_index("z") * 2 + lax.axis_index("xh")) * 2 + core
        return owner, lax.axis_index("dish"), core

    given, made = make_tables(ids)
    visits = call(
        visit_kernel,
        pltpu.VMEM((CHIPS, VISITS, GRAIN), BF16),
        (phase_bins.reshape(PER_BLOCK, GRAIN),),
        [pltpu.VMEM((72, GRAIN), F32)] * 2,
        us=3.0,
    )
    partial_beam = front(voltages, beam_weights)
    parts = lax.all_to_all(partial_beam, "dish", 0, 0, tiled=True)
    packed = call(pack_kernel, pltpu.VMEM((CHIPS, ROWS, GRAIN), BF16), (parts, visits), us=0.3)
    own = lax.all_to_all(packed, ("z", "xh"), 0, 0, tiled=True)
    other = lax.ppermute(own, "core", [(0, 1), (1, 0)])
    return jnp.transpose(spectrum(own, other, ids, given, made), (2, 0, 1))


def solution(mesh):
    split = jax.sharding.Mesh(mesh.devices.reshape(8, 2, 2, 8), ("z", "xh", "core", "dish"))
    time = ("z", "xh", "core")
    return jax.shard_map(
        steps,
        mesh=split,
        in_specs=(P(None, "dish", time), P(None, "dish"), P(time)),
        out_specs=P("dish", None, time),
        check_vma=False,
    )
```

```python
import functools
import math

import jax
import jax.numpy as jnp
import numpy as np
from jax import lax
from jax.experimental import pallas as pl
from jax.experimental.pallas import tpu as pltpu
from jax.sharding import PartitionSpec as P


PH = 1024
LAGS = 2048
SAMPLES = 131072
DISH_WAYS = 8
TM_WAYS = 32
CHIPS = 16
HALF = SAMPLES // 2 // 128
LOCAL = SAMPLES // TM_WAYS
GRAIN = 128
PER_BLOCK = LOCAL // GRAIN
SPAN = LAGS // GRAIN
BINS = PH // TM_WAYS
FREQS = LAGS // DISH_WAYS
SLOTS = 128
GROUP = 16
VISITS = 8
ROWS = 2 * PER_BLOCK + VISITS
SCALE = 1.0 / math.sqrt(LAGS * SAMPLES / PH)

F32 = jnp.float32
BF16 = jnp.bfloat16


def dot(a, b, dims=(((1,), (0,)), ((), ()))):
    return lax.dot_general(a, b, dims, preferred_element_type=F32)


def hi_lo(value):
    hi = value.astype(BF16)
    return hi, (value - hi.astype(F32)).astype(BF16)


def tables():
    grain = np.arange(GRAIN)
    freq = np.arange(FREQS)
    angle = 2 * np.pi * np.outer(grain, freq) / LAGS
    base = np.concatenate([np.cos(angle), np.sin(angle)], 1).astype(np.float32)
    eighth = 2 * np.pi * np.outer(grain, np.arange(DISH_WAYS)) / DISH_WAYS
    turn = np.zeros((GRAIN, 128), np.float32)
    turn[:, :8] = np.cos(eighth)
    turn[:, 8:16] = np.sin(eighth)
    fine = 2 * np.pi * np.outer(grain, np.arange(2 * GRAIN)) / (2 * GRAIN)
    cos2, sin2 = np.cos(fine), np.sin(fine)
    fold2 = np.block([[cos2, sin2], [sin2, -cos2]]).astype(np.float32)
    step2 = np.block([[cos2, -sin2], [sin2, cos2]]).astype(np.float32)
    keep = (grain >= 1)[None, :] / (2.0 * GRAIN)
    back = np.block([[cos2.T * keep, -sin2.T * keep], [sin2.T * keep, cos2.T * keep]])
    sixteenth = 2 * np.pi * np.outer(np.arange(SPAN), freq) / SPAN
    phase = np.concatenate([np.cos(sixteenth), np.sin(sixteenth)], 1).astype(np.float32)
    return {
        "base": jnp.asarray(base),
        "turn": jnp.asarray(turn),
        "fold2": jnp.asarray(fold2).astype(BF16),
        "step2": jnp.asarray(step2).astype(BF16),
        "back": jnp.asarray(back.astype(np.float32)).astype(BF16),
        "phase": jnp.asarray(phase),
    }


def front_kernel(volts_hbm, weights_hbm, beam_hbm, volts_s, weights_s, beam_s, sems):
    copies = [
        pltpu.make_async_copy(source, target, sems.at[k])
        for k, (source, target) in enumerate(((weights_hbm, weights_s), (volts_hbm, volts_s)))
    ]
    for copy in copies:
        copy.start()
    for copy in copies:
        copy.wait()
    weights = weights_s[...]
    first = dot(weights, volts_s[0])
    second = dot(weights, volts_s[1])
    real = first[0:1] - second[1:2]
    imag = first[1:2] + second[0:1]
    for row in range(PER_BLOCK):
        part = slice(row * GRAIN, (row + 1) * GRAIN)
        beam_s[row : row + 1, :] = real[:, part]
        beam_s[PER_BLOCK + row : PER_BLOCK + row + 1, :] = imag[:, part]
    copies = [
        pltpu.make_async_copy(beam_s, beam_hbm.at[way], sems.at[2 + way]) for way in range(DISH_WAYS)
    ]
    for copy in copies:
        copy.start()
    for copy in copies:
        copy.wait()


def pack_kernel(parts_ref, visit_ref, out_ref):
    total = parts_ref[0]
    for way in range(1, DISH_WAYS):
        total = total + parts_ref[way]
    rows = total.astype(BF16)
    for chip in range(CHIPS):
        out_ref[chip, : 2 * PER_BLOCK, :] = rows
        out_ref[chip, 2 * PER_BLOCK :, :] = visit_ref[chip]


def coded_times(shape):
    row = lax.broadcasted_iota(jnp.int32, shape, 0)
    lane = lax.broadcasted_iota(jnp.int32, shape, 1)
    return (lane + 128).astype(F32) * two_to(row)


def triangle(count, strict):
    row = lax.broadcasted_iota(jnp.int32, (count, count), 0)
    column = lax.broadcasted_iota(jnp.int32, (count, count), 1)
    return jnp.where(row < column if strict else row <= column, 1.0, 0.0).astype(BF16)


def visit_kernel(bins_ref, out_ref, time_s, row_s):
    bins = bins_ref[...]
    shape = (PER_BLOCK, GRAIN)
    row = lax.broadcasted_iota(jnp.int32, shape, 0)
    lane = lax.broadcasted_iota(jnp.int32, shape, 1)
    rolled = pltpu.roll(bins, 1, 1)
    before = jnp.where(lane == 0, pltpu.roll(rolled, 1, 0), rolled)
    later = row + lane > 0
    enters = later & (bins != before)
    wraps = jnp.where(later & (bins < before), 1.0, 0.0).astype(BF16)
    in_row = dot(wraps, triangle(GRAIN, False))
    ends = jnp.broadcast_to(in_row[:, GRAIN - 1 :], shape).astype(BF16)
    above = dot(triangle(PER_BLOCK, True), ends, (((0,), (0,)), ((), ())))
    step = bins + PH * (in_row + above).astype(jnp.int32)
    high = jnp.where(enters, step >> 7, -1)
    low = step & 127
    times = coded_times(shape)
    high_iota = lax.broadcasted_iota(jnp.int32, (48, GRAIN), 0)
    low_iota = lax.broadcasted_iota(jnp.int32, (GRAIN, GRAIN), 0)
    found = jnp.zeros((96, GRAIN), F32)
    for pair in range(PER_BLOCK // 2):
        left, right = [], []
        for k in (2 * pair, 2 * pair + 1):
            here = high[k : k + 1, :] == high_iota
            coded = jnp.where(here, times[k : k + 1, :], 0.0)
            left.append(jnp.concatenate([coded, jnp.where(here, float(k), 0.0)], 0))
            right.append(jnp.where(low[k : k + 1, :] == low_iota, 1.0, 0.0))
        left = jnp.concatenate(left, 1).astype(BF16)
        right = jnp.concatenate(right, 1).astype(BF16)
        found = found + dot(left, right, (((1,), (1,)), ((), ())))
    place = high_iota * GRAIN + lax.broadcasted_iota(jnp.int32, (48, GRAIN), 1)
    past, ahead = place <= step[0:1, 0:1], place > step[PER_BLOCK - 1 :, GRAIN - 1 :]
    time_s[:48, :] = jnp.where(past, 2.0**-9, jnp.where(ahead, 2.0**23, found[:48]))
    row_s[:48, :] = jnp.where(past, 0.0, jnp.where(ahead, 32.0, found[48:]))
    time_s[48:, :] = jnp.full((24, GRAIN), 2.0**23, F32)
    row_s[48:, :] = jnp.full((24, GRAIN), 32.0, F32)
    lane = lax.broadcasted_iota(jnp.int32, (VISITS, GRAIN), 1)
    for eighth in range(8):
        now, then = pl.ds(eighth, VISITS, stride=8), pl.ds(eighth + 1, VISITS, stride=8)
        time, rows = time_s[now, :], row_s[now, :]
        next_time, next_rows = time_s[then, :], row_s[then, :]
        even = jnp.where(lane == 65, pltpu.roll(rows, 65, 1), time)
        even = jnp.where(lane == 66, pltpu.roll(rows, 34, 1), even)
        even = jnp.where(lane == 67, pltpu.roll(rows, 3, 1), even)
        odd = jnp.where(lane == 64, pltpu.roll(next_time, 64, 1), pltpu.roll(time, 64, 1))
        odd = jnp.where(lane == 65, pltpu.roll(rows, 1, 1), odd)
        odd = jnp.where(lane == 66, pltpu.roll(rows, 98, 1), odd)
        odd = jnp.where(lane == 67, pltpu.roll(next_rows, 67, 1), odd)
        out_ref[2 * eighth] = even.astype(BF16)
        out_ref[2 * eighth + 1] = odd.astype(BF16)


def two_to(exponent):
    value = jnp.full(jnp.shape(exponent), 2.0**-16, F32)
    for bit in range(5):
        value = value * jnp.where((exponent >> bit) & 1 == 1, float(2 ** (2**bit)), 1.0)
    return value


def table_kernel(
    ids, base_ref, turn_ref, fold2_ref, phase_ref, back_ref, fold_ref, step_ref, short_ref, phases_ref, last_s
):
    _, dish, _ = ids()
    lane = lax.broadcasted_iota(jnp.int32, (GRAIN, 128), 1)
    turn = turn_ref[...]
    cos8 = jnp.sum(jnp.where(lane == dish, turn, 0.0), axis=1, keepdims=True)
    sin8 = jnp.sum(jnp.where(lane == dish + 8, turn, 0.0), axis=1, keepdims=True)
    cos0, sin0 = base_ref[:, :FREQS], base_ref[:, FREQS:]
    cosine, cosine_lo = hi_lo(cos0 * cos8 - sin0 * sin8)
    sine, sine_lo = hi_lo(sin0 * cos8 + cos0 * sin8)
    fold_ref[:GRAIN, :FREQS] = cosine
    fold_ref[:GRAIN, FREQS : 2 * FREQS] = sine
    fold_ref[GRAIN:, :FREQS] = sine
    fold_ref[GRAIN:, FREQS : 2 * FREQS] = -cosine
    fold_ref[:, 2 * FREQS :] = fold2_ref[...]
    for k, (c, s) in enumerate(((cosine, sine), (cosine_lo, sine_lo))):
        step_ref[k, :GRAIN, :FREQS] = c
        step_ref[k, :GRAIN, FREQS:] = -s
        step_ref[k, GRAIN:, :FREQS] = s
        step_ref[k, GRAIN:, FREQS:] = c
    last_s[:GRAIN, :FREQS] = cosine
    last_s[:GRAIN, FREQS:] = sine
    last_s[GRAIN:, :FREQS] = -sine
    last_s[GRAIN:, FREQS:] = cosine
    short_ref[...] = dot(back_ref[...], last_s[...]).astype(BF16)
    phases_ref[...] = jnp.zeros(phases_ref.shape, BF16)
    hi, lo = hi_lo(phase_ref[...])
    phases_ref[0:SPAN, :] = hi
    phases_ref[SPAN : 2 * SPAN, :] = lo


def beam_rows(ref, first, last):
    rows = [
        jnp.concatenate([ref[chip, :PER_BLOCK, :], ref[chip, PER_BLOCK : 2 * PER_BLOCK, :]], 1)
        for chip in range(first, last)
    ]
    return jnp.concatenate(rows, 0)


def transform(ref, step_ref, phase_ref, z_ref):
    cos16, sin16 = phase_ref[:, :FREQS], phase_ref[:, FREQS:]
    cos_rows = jnp.concatenate([cos16] * (128 // SPAN), 0)
    sin_rows = jnp.concatenate([sin16] * (128 // SPAN), 0)
    for tile in range(HALF // 128):
        rows = slice(tile * 128, tile * 128 + 128)
        beam = beam_rows(ref, 4 * tile, 4 * tile + 4)
        both = dot(beam, step_ref[0]) + dot(beam, step_ref[1])
        real, imag = both[:, :FREQS], both[:, FREQS:]
        z_ref[rows, :FREQS] = (real * cos_rows + imag * sin_rows).astype(BF16)
        z_ref[rows, FREQS:] = (imag * cos_rows - real * sin_rows).astype(BF16)


def plan_half(ref, core, before):
    times = jnp.concatenate([ref[chip, 2 * PER_BLOCK :, :].astype(F32) for chip in range(CHIPS)], 0).astype(BF16)
    row = lax.broadcasted_iota(jnp.int32, (8, 128), 0)
    lane = lax.broadcasted_iota(jnp.int32, (8, 128), 1)
    wanted = jnp.where(row == 0, BINS * core, jnp.where(row == 1, BINS * core + BINS, core + 63 + row))
    info = dot(jnp.where(lane == wanted, 1.0, 0.0).astype(BF16), times, (((1,), (1,)), ((), ())))
    start, end, first, last = (info[k : k + 1, :] for k in range(4))
    grains = jnp.where(end > start, jnp.minimum(last, float(PER_BLOCK - 1)) - first + 1.0, 0.0)
    earlier = dot(jnp.broadcast_to(grains, (8, 128)).astype(BF16), triangle(128, True))[0:1, :] + before
    return times, end, first, grains, earlier, earlier[:, 127:] + grains[:, 127:]


def slots_half(slot_0, plan, ref):
    times, end, first, grains, earlier, _ = plan
    slot = lax.broadcasted_iota(jnp.int32, (SLOTS, 128), 0).astype(F32) + slot_0
    visit = lax.broadcasted_iota(jnp.int32, (SLOTS, 128), 1)
    mine = (slot >= earlier) & (slot < earlier + grains)
    place = ((visit >> 3) * PER_BLOCK + 1).astype(F32) + first + (slot - earlier)
    place = jnp.sum(jnp.where(mine, place, 0.0), axis=1, keepdims=True) - 1.0
    ends = jnp.sum(jnp.where(mine, jnp.broadcast_to(end, (SLOTS, 128)), 0.0), axis=1, keepdims=True)
    starts = dot(times, jnp.where(mine, 1.0, 0.0).astype(BF16), (((0,), (1,)), ((), ())))
    places = lax.broadcasted_iota(jnp.int32, (SLOTS, HALF), 1).astype(F32)
    pick = jnp.where(places == place, 1.0, 0.0).astype(BF16)
    return place, ends, starts, dot(pick, beam_rows(ref, 0, CHIPS))


def half_kernel(ids, own_ref, step_ref, phase_ref, z_ref, total_ref, place_ref, ends_ref, starts_ref, gbeam_ref):
    _, _, core = ids()
    plan = plan_half(own_ref, core, jnp.zeros((1, 1), F32))
    place, ends, starts, beam = slots_half(jnp.float32(0.0), plan, own_ref)
    total_ref[...] = jnp.broadcast_to(plan[-1], (8, 128))
    place_ref[...] = jnp.broadcast_to(place, (SLOTS, 128))
    ends_ref[...] = jnp.broadcast_to(ends, (SLOTS, 128))
    starts_ref[...] = starts
    gbeam_ref[...] = beam
    transform(own_ref, step_ref, phase_ref, z_ref)


def grain_row(which):
    place = lax.broadcasted_iota(jnp.int32, (8, HALF), 1)
    grain = (2 * (place >> 5) + which) * PER_BLOCK + (place & (PER_BLOCK - 1))
    return grain.astype(F32)[0:1, :]


def spectrum_kernel(
    ids,
    own_ref, other_ref, z_ref, total_ref, place_ref, ends_ref, starts_ref, gbeam_ref,
    fold_ref, step_ref, short_ref, phases_ref, step2_ref, phase_ref,
    out_ref,
    z_s, gdft_s, gstep_s, gbeam_s, gtime_s, gstart_s, acc_s, fold_s,
):
    _, _, core = ids()
    before = total_ref[0:1, 0:1]
    other_plan = plan_half(other_ref, core, before)
    count = jnp.max(other_plan[-1]).astype(jnp.int32)
    transform(other_ref, step_ref, phase_ref, z_s)
    acc_s[...] = jnp.zeros(acc_s.shape, F32)
    fold_s[...] = fold_ref[...]
    own_grains = jnp.broadcast_to(grain_row(core), (SLOTS, HALF))
    other_grains = jnp.broadcast_to(grain_row(1 - core), (SLOTS, HALF))
    lane_iota = lax.broadcasted_iota(jnp.int32, (SLOTS, 128), 1)

    def fold_batch(batch, mine):
        first = (batch * SLOTS).astype(F32)
        more = slots_half(first, other_plan, other_ref)
        is_mine = mine[0] >= 0.0
        place = jnp.where(is_mine, mine[0], more[0]).astype(jnp.int32)
        which = jnp.where(is_mine, core, 1 - core)
        in_block = place & (PER_BLOCK - 1)
        grain = ((2 * (place >> 5) + which) * PER_BLOCK + in_block).astype(F32)
        here = mine[3] + more[3]
        times = (lane_iota + 128).astype(F32) * two_to(jnp.broadcast_to(in_block, (SLOTS, 128)))
        gtime_s[...] = times
        inside = times < mine[1] + more[1]
        gbeam_s[:, :GRAIN] = jnp.where(inside, here[:, :GRAIN], 0.0)
        gbeam_s[:, GRAIN:] = jnp.where(inside, here[:, GRAIN:], 0.0)
        starts = mine[2] + more[2]
        starts = jnp.where(core == 0, starts[:BINS], starts[BINS : 2 * BINS])
        for group in range(SLOTS // GROUP):
            gstart_s[group] = starts if group == 0 else pltpu.roll(starts, SLOTS - group * GROUP, 1)
        dft = jnp.zeros((SLOTS, 2 * FREQS), F32)
        ahead = jnp.zeros((SLOTS, 2 * GRAIN), F32)
        for grains, z, ref in ((own_grains, z_ref, own_ref), (other_grains, z_s, other_ref)):
            window = (grains >= grain) & (grains < grain + float(SPAN))
            dft = dft + dot(jnp.where(window, 1.0, 0.0).astype(BF16), z[...])
            next_pick = jnp.where(grains == grain + float(SPAN), 1.0, 0.0).astype(BF16)
            ahead = ahead + dot(next_pick, beam_rows(ref, 0, CHIPS))
        offset = in_block & (SPAN - 1)
        turner = jnp.where((lane_iota == offset) | (lane_iota == offset + SPAN), 1.0, 0.0)
        turned = dot(turner.astype(BF16), phases_ref[...])
        real, imag = dft[:, :FREQS], dft[:, FREQS:]
        cos_g, sin_g = turned[:, :FREQS], turned[:, FREQS:]
        step = dot((ahead - here).astype(BF16), step2_ref[...])
        for ref, real, imag in (
            (gdft_s, real * cos_g - imag * sin_g, imag * cos_g + real * sin_g),
            (gstep_s, step[:, :FREQS], step[:, FREQS:]),
        ):
            ref[:, :FREQS] = real
            ref[:, FREQS : 2 * FREQS] = imag - real
            ref[:, 2 * FREQS :] = real + imag

        def group_step(group, inner):
            rows = pl.ds(pl.multiple_of(group * GROUP, GROUP), GROUP)
            beam8, time8, start8 = gbeam_s[rows, :], gtime_s[rows, :], gstart_s[group]
            dft8, step8 = gdft_s[rows, :], gstep_s[rows, :]
            left = []
            for k in range(GROUP):
                since = time8[k : k + 1, :] >= start8[:, k : k + 1]
                real = jnp.where(since, beam8[k : k + 1, :GRAIN], 0.0)
                imag = jnp.where(since, beam8[k : k + 1, GRAIN:], 0.0)
                left.append(jnp.concatenate([real, imag], 1))
            left = jnp.concatenate(left, 0).astype(BF16)
            for part, factor in ((0, dft8), (1, step8)):
                folded = dot(left, fold_s[:, part * 2 * FREQS : part * 2 * FREQS + 2 * FREQS])
                sums = [acc_s[:, k * FREQS : k * FREQS + FREQS] for k in range(3 * part, 3 * part + 3)]
                for k in range(GROUP):
                    rows = slice(k * BINS, k * BINS + BINS)
                    real, imag = folded[rows, :FREQS], folded[rows, FREQS:]
                    for n, value in enumerate((real + imag, real, imag)):
                        sums[n] = sums[n] + value * factor[k : k + 1, n * FREQS : n * FREQS + FREQS]
                for n in range(3):
                    acc_s[:, (3 * part + n) * FREQS : (3 * part + n + 1) * FREQS] = sums[n]
            return inner

        def pair_step(pair, inner):
            group_step(2 * pair, inner)
            return group_step(2 * pair + 1, inner)

        groups = (jnp.minimum(count - batch * SLOTS, SLOTS) + GROUP - 1) // GROUP
        lax.fori_loop(0, groups // 2, pair_step, 0)
        lax.fori_loop(groups // 2 * 2, groups, group_step, 0)

    fold_batch(jnp.int32(0), (place_ref[:, 0:1], ends_ref[:, 0:1], starts_ref[...], gbeam_ref[...]))

    def batch_step(batch, carry):
        own_plan = plan_half(own_ref, core, jnp.zeros((1, 1), F32))
        fold_batch(batch, slots_half((batch * SLOTS).astype(F32), own_plan, own_ref))
        return carry

    lax.fori_loop(1, (count + SLOTS - 1) // SLOTS, batch_step, 0)
    since = acc_s[...]
    each = since - jnp.concatenate([since[1:], jnp.zeros((1, 6 * FREQS), F32)], 0)
    both, real, imag, both2, real2, imag2 = (each[:, k * FREQS : k * FREQS + FREQS] for k in range(6))
    short = dot(jnp.concatenate([both2 - imag2, both2 + real2], 1).astype(BF16), short_ref[...])
    out_ref[0] = (both - imag + short[:, :FREQS]) * SCALE
    out_ref[1] = (both + real + short[:, FREQS:]) * SCALE


def near(*values):
    return [pltpu.with_memory_space_constraint(v, pltpu.VMEM) for v in values]


def call(kernel, outs, values, scratch=(), mib=8, us=1.0):
    one = not isinstance(outs, (tuple, list))
    space = pl.BlockSpec(memory_space=pltpu.VMEM)
    return pl.pallas_call(
        kernel,
        out_shape=outs if one else tuple(outs),
        in_specs=[space] * len(values),
        out_specs=space if one else (space,) * len(outs),
        scratch_shapes=list(scratch),
        compiler_params=pltpu.CompilerParams(vmem_limit_bytes=mib << 20),
        cost_estimate=pl.CostEstimate(flops=int(us * 5e8), bytes_accessed=1 << 20, transcendentals=0),
    )(*near(*values))


HALF_Z = pltpu.VMEM((HALF, 2 * FREQS), BF16)


def make_tables(ids):
    given = tables()
    made = call(
        functools.partial(table_kernel, ids),
        (
            pltpu.VMEM((2 * GRAIN, 4 * FREQS), BF16),
            pltpu.VMEM((2, 2 * GRAIN, 2 * FREQS), BF16),
            pltpu.VMEM((2 * FREQS, 2 * FREQS), BF16),
            pltpu.VMEM((128, 2 * FREQS), BF16),
        ),
        [given[k] for k in ("base", "turn", "fold2", "phase", "back")],
        [pltpu.VMEM((2 * GRAIN, 2 * FREQS), BF16)],
        us=3.0,
    )
    return given, made


def spectrum(own, other, ids, given, made):
    fold, step, short, phases = made
    phase = given["phase"]
    half = call(
        functools.partial(half_kernel, ids),
        (
            HALF_Z,
            pltpu.VMEM((8, 128), F32),
            pltpu.VMEM((SLOTS, 128), F32),
            pltpu.VMEM((SLOTS, 128), F32),
            pltpu.VMEM((128, SLOTS), F32),
            pltpu.VMEM((SLOTS, 2 * GRAIN), F32),
        ),
        (own, step, phase),
        us=1.0,
    )
    scratch = [
        HALF_Z,
        pltpu.VMEM((SLOTS, 3 * FREQS), F32),
        pltpu.VMEM((SLOTS, 3 * FREQS), F32),
        pltpu.VMEM((SLOTS, 2 * GRAIN), F32),
        pltpu.VMEM((SLOTS, GRAIN), F32),
        pltpu.VMEM((SLOTS // GROUP, BINS, 128), F32),
        pltpu.VMEM((BINS, 6 * FREQS), F32),
        pltpu.VMEM((2 * GRAIN, 4 * FREQS), BF16),
    ]
    return call(
        functools.partial(spectrum_kernel, ids),
        jax.ShapeDtypeStruct((2, BINS, FREQS), F32),
        (own, other, *half, fold, step, short, phases, given["step2"], phase),
        scratch,
        mib=16,
        us=5.0,
    )


def front(voltages, beam_weights):
    far = pl.BlockSpec(memory_space=pltpu.HBM)
    return pl.pallas_call(
        front_kernel,
        out_shape=jax.ShapeDtypeStruct((DISH_WAYS, 2 * PER_BLOCK, GRAIN), F32),
        in_specs=[far] * 2,
        out_specs=far,
        scratch_shapes=[
            pltpu.VMEM(voltages.shape, BF16),
            pltpu.VMEM(beam_weights.shape, BF16),
            pltpu.VMEM((2 * PER_BLOCK, GRAIN), F32),
            pltpu.SemaphoreType.DMA((2 + DISH_WAYS,)),
        ],
        compiler_params=pltpu.CompilerParams(vmem_limit_bytes=8 << 20),
        cost_estimate=pl.CostEstimate(flops=1 << 20, bytes_accessed=1 << 20, transcendentals=0),
        name="front",
    )(*(pltpu.with_memory_space_constraint(v, pltpu.HBM) for v in (voltages, beam_weights)))


def steps(voltages, beam_weights, phase_bins):
    def ids():
        core = lax.axis_index("core")
        owner = (lax.axis_index("z") * 2 + lax.axis_index("xh")) * 2 + core
        return owner, lax.axis_index("dish"), core

    given, made = make_tables(ids)
    visits = call(
        visit_kernel,
        pltpu.VMEM((CHIPS, VISITS, GRAIN), BF16),
        (phase_bins.reshape(PER_BLOCK, GRAIN),),
        [pltpu.VMEM((72, GRAIN), F32)] * 2,
        us=3.0,
    )
    partial_beam = front(voltages, beam_weights)
    parts = lax.all_to_all(partial_beam, "dish", 0, 0, tiled=True)
    packed = call(pack_kernel, pltpu.VMEM((CHIPS, ROWS, GRAIN), BF16), (parts, visits), us=0.3)
    own = lax.all_to_all(packed, ("z", "xh"), 0, 0, tiled=True)
    other = lax.ppermute(own, "core", [(0, 1), (1, 0)])
    return jnp.transpose(spectrum(own, other, ids, given, made), (2, 0, 1))


def solution(mesh):
    split = jax.sharding.Mesh(mesh.devices.reshape(8, 2, 2, 8), ("z", "xh", "core", "dish"))
    time = ("z", "xh", "core")
    return jax.shard_map(
        steps,
        mesh=split,
        in_specs=(P(None, "dish", time), P(None, "dish"), P(time)),
        out_specs=P("dish", None, time),
        check_vma=False,
    )
```

```python
import functools
import math

import jax
import jax.numpy as jnp
import numpy as np
from jax import lax
from jax.experimental import pallas as pl
from jax.experimental.pallas import tpu as pltpu
from jax.sharding import PartitionSpec as P


PH = 1024
LAGS = 2048
SAMPLES = 131072
DISH_WAYS = 8
TM_WAYS = 32
CHIPS = 16
HALF = SAMPLES // 2 // 128
LOCAL = SAMPLES // TM_WAYS
GRAIN = 128
PER_BLOCK = LOCAL // GRAIN
SPAN = LAGS // GRAIN
BINS = PH // TM_WAYS
FREQS = LAGS // DISH_WAYS
SLOTS = 128
GROUP = 16
VISITS = 8
ROWS = 2 * PER_BLOCK + VISITS
SCALE = 1.0 / math.sqrt(LAGS * SAMPLES / PH)

F32 = jnp.float32
BF16 = jnp.bfloat16


def dot(a, b, dims=(((1,), (0,)), ((), ()))):
    return lax.dot_general(a, b, dims, preferred_element_type=F32)


def hi_lo(value):
    hi = value.astype(BF16)
    return hi, (value - hi.astype(F32)).astype(BF16)


def tables():
    grain = np.arange(GRAIN)
    freq = np.arange(FREQS)
    angle = 2 * np.pi * np.outer(grain, freq) / LAGS
    base = np.concatenate([np.cos(angle), np.sin(angle)], 1).astype(np.float32)
    eighth = 2 * np.pi * np.outer(grain, np.arange(DISH_WAYS)) / DISH_WAYS
    turn = np.zeros((GRAIN, 128), np.float32)
    turn[:, :8] = np.cos(eighth)
    turn[:, 8:16] = np.sin(eighth)
    fine = 2 * np.pi * np.outer(grain, np.arange(2 * GRAIN)) / (2 * GRAIN)
    cos2, sin2 = np.cos(fine), np.sin(fine)
    fold2 = np.block([[cos2, sin2], [sin2, -cos2]]).astype(np.float32)
    step2 = np.block([[cos2, -sin2], [sin2, cos2]]).astype(np.float32)
    keep = (grain >= 1)[None, :] / (2.0 * GRAIN)
    back = np.block([[cos2.T * keep, -sin2.T * keep], [sin2.T * keep, cos2.T * keep]])
    sixteenth = 2 * np.pi * np.outer(np.arange(SPAN), freq) / SPAN
    phase = np.concatenate([np.cos(sixteenth), np.sin(sixteenth)], 1).astype(np.float32)
    return {
        "base": jnp.asarray(base),
        "turn": jnp.asarray(turn),
        "fold2": jnp.asarray(fold2).astype(BF16),
        "step2": jnp.asarray(step2).astype(BF16),
        "back": jnp.asarray(back.astype(np.float32)).astype(BF16),
        "phase": jnp.asarray(phase),
    }


def front_kernel(
    volts_hbm, weights_hbm, bins_hbm, beam_ref, visit_ref, volts_s, weights_s, bins_s, time_s, row_s, sems
):
    copies = [
        pltpu.make_async_copy(source, target, sems.at[k])
        for k, (source, target) in enumerate(
            ((bins_hbm, bins_s), (weights_hbm, weights_s), (volts_hbm, volts_s))
        )
    ]
    for copy in copies:
        copy.start()
    copies[0].wait()
    make_visits(bins_s, visit_ref, time_s, row_s)
    copies[1].wait()
    copies[2].wait()
    weights = weights_s[...]
    first = dot(weights, volts_s[0])
    second = dot(weights, volts_s[1])
    real = first[0:1] - second[1:2]
    imag = first[1:2] + second[0:1]
    for row in range(PER_BLOCK):
        part = slice(row * GRAIN, (row + 1) * GRAIN)
        beam_ref[0, row : row + 1, :] = real[:, part]
        beam_ref[0, PER_BLOCK + row : PER_BLOCK + row + 1, :] = imag[:, part]
    rows = beam_ref[0]
    for way in range(1, DISH_WAYS):
        beam_ref[way] = rows


def pack_kernel(parts_ref, visit_ref, out_ref):
    total = parts_ref[0]
    for way in range(1, DISH_WAYS):
        total = total + parts_ref[way]
    rows = total.astype(BF16)
    for chip in range(CHIPS):
        out_ref[chip, : 2 * PER_BLOCK, :] = rows
        out_ref[chip, 2 * PER_BLOCK :, :] = visit_ref[chip]


def coded_times(shape):
    row = lax.broadcasted_iota(jnp.int32, shape, 0)
    lane = lax.broadcasted_iota(jnp.int32, shape, 1)
    return (lane + 128).astype(F32) * two_to(row)


def triangle(count, strict):
    row = lax.broadcasted_iota(jnp.int32, (count, count), 0)
    column = lax.broadcasted_iota(jnp.int32, (count, count), 1)
    return jnp.where(row < column if strict else row <= column, 1.0, 0.0).astype(BF16)


def make_visits(bins_ref, out_ref, time_s, row_s):
    bins = bins_ref[...]
    shape = (PER_BLOCK, GRAIN)
    row = lax.broadcasted_iota(jnp.int32, shape, 0)
    lane = lax.broadcasted_iota(jnp.int32, shape, 1)
    rolled = pltpu.roll(bins, 1, 1)
    before = jnp.where(lane == 0, pltpu.roll(rolled, 1, 0), rolled)
    later = row + lane > 0
    enters = later & (bins != before)
    wraps = jnp.where(later & (bins < before), 1.0, 0.0).astype(BF16)
    in_row = dot(wraps, triangle(GRAIN, False))
    ends = jnp.broadcast_to(in_row[:, GRAIN - 1 :], shape).astype(BF16)
    above = dot(triangle(PER_BLOCK, True), ends, (((0,), (0,)), ((), ())))
    step = bins + PH * (in_row + above).astype(jnp.int32)
    high = jnp.where(enters, step >> 7, -1)
    low = step & 127
    times = coded_times(shape)
    high_iota = lax.broadcasted_iota(jnp.int32, (48, GRAIN), 0)
    low_iota = lax.broadcasted_iota(jnp.int32, (GRAIN, GRAIN), 0)
    found = jnp.zeros((96, GRAIN), F32)
    for pair in range(PER_BLOCK // 2):
        left, right = [], []
        for k in (2 * pair, 2 * pair + 1):
            here = high[k : k + 1, :] == high_iota
            coded = jnp.where(here, times[k : k + 1, :], 0.0)
            left.append(jnp.concatenate([coded, jnp.where(here, float(k), 0.0)], 0))
            right.append(jnp.where(low[k : k + 1, :] == low_iota, 1.0, 0.0))
        left = jnp.concatenate(left, 1).astype(BF16)
        right = jnp.concatenate(right, 1).astype(BF16)
        found = found + dot(left, right, (((1,), (1,)), ((), ())))
    place = high_iota * GRAIN + lax.broadcasted_iota(jnp.int32, (48, GRAIN), 1)
    past, ahead = place <= step[0:1, 0:1], place > step[PER_BLOCK - 1 :, GRAIN - 1 :]
    time_s[:48, :] = jnp.where(past, 2.0**-9, jnp.where(ahead, 2.0**23, found[:48]))
    row_s[:48, :] = jnp.where(past, 0.0, jnp.where(ahead, 32.0, found[48:]))
    time_s[48:, :] = jnp.full((24, GRAIN), 2.0**23, F32)
    row_s[48:, :] = jnp.full((24, GRAIN), 32.0, F32)
    lane = lax.broadcasted_iota(jnp.int32, (VISITS, GRAIN), 1)
    for eighth in range(8):
        now, then = pl.ds(eighth, VISITS, stride=8), pl.ds(eighth + 1, VISITS, stride=8)
        time, rows = time_s[now, :], row_s[now, :]
        next_time, next_rows = time_s[then, :], row_s[then, :]
        even = jnp.where(lane == 65, pltpu.roll(rows, 65, 1), time)
        even = jnp.where(lane == 66, pltpu.roll(rows, 34, 1), even)
        even = jnp.where(lane == 67, pltpu.roll(rows, 3, 1), even)
        odd = jnp.where(lane == 64, pltpu.roll(next_time, 64, 1), pltpu.roll(time, 64, 1))
        odd = jnp.where(lane == 65, pltpu.roll(rows, 1, 1), odd)
        odd = jnp.where(lane == 66, pltpu.roll(rows, 98, 1), odd)
        odd = jnp.where(lane == 67, pltpu.roll(next_rows, 67, 1), odd)
        out_ref[2 * eighth] = even.astype(BF16)
        out_ref[2 * eighth + 1] = odd.astype(BF16)


def two_to(exponent):
    value = jnp.full(jnp.shape(exponent), 2.0**-16, F32)
    for bit in range(5):
        value = value * jnp.where((exponent >> bit) & 1 == 1, float(2 ** (2**bit)), 1.0)
    return value


def table_kernel(
    ids, base_ref, turn_ref, fold2_ref, phase_ref, back_ref, fold_ref, step_ref, short_ref, phases_ref, last_s
):
    _, dish, _ = ids()
    lane = lax.broadcasted_iota(jnp.int32, (GRAIN, 128), 1)
    turn = turn_ref[...]
    cos8 = jnp.sum(jnp.where(lane == dish, turn, 0.0), axis=1, keepdims=True)
    sin8 = jnp.sum(jnp.where(lane == dish + 8, turn, 0.0), axis=1, keepdims=True)
    cos0, sin0 = base_ref[:, :FREQS], base_ref[:, FREQS:]
    cosine, cosine_lo = hi_lo(cos0 * cos8 - sin0 * sin8)
    sine, sine_lo = hi_lo(sin0 * cos8 + cos0 * sin8)
    fold_ref[:GRAIN, :FREQS] = cosine
    fold_ref[:GRAIN, FREQS : 2 * FREQS] = sine
    fold_ref[GRAIN:, :FREQS] = sine
    fold_ref[GRAIN:, FREQS : 2 * FREQS] = -cosine
    fold_ref[:, 2 * FREQS :] = fold2_ref[...]
    for k, (c, s) in enumerate(((cosine, sine), (cosine_lo, sine_lo))):
        step_ref[k, :GRAIN, :FREQS] = c
        step_ref[k, :GRAIN, FREQS:] = -s
        step_ref[k, GRAIN:, :FREQS] = s
        step_ref[k, GRAIN:, FREQS:] = c
    last_s[:GRAIN, :FREQS] = cosine
    last_s[:GRAIN, FREQS:] = sine
    last_s[GRAIN:, :FREQS] = -sine
    last_s[GRAIN:, FREQS:] = cosine
    short_ref[...] = dot(back_ref[...], last_s[...]).astype(BF16)
    phases_ref[...] = jnp.zeros(phases_ref.shape, BF16)
    hi, lo = hi_lo(phase_ref[...])
    phases_ref[0:SPAN, :] = hi
    phases_ref[SPAN : 2 * SPAN, :] = lo


def beam_rows(ref, first, last):
    rows = [
        jnp.concatenate([ref[chip, :PER_BLOCK, :], ref[chip, PER_BLOCK : 2 * PER_BLOCK, :]], 1)
        for chip in range(first, last)
    ]
    return jnp.concatenate(rows, 0)


def transform(ref, step_ref, phase_ref, z_ref):
    cos16, sin16 = phase_ref[:, :FREQS], phase_ref[:, FREQS:]
    cos_rows = jnp.concatenate([cos16] * (128 // SPAN), 0)
    sin_rows = jnp.concatenate([sin16] * (128 // SPAN), 0)
    for tile in range(HALF // 128):
        rows = slice(tile * 128, tile * 128 + 128)
        beam = beam_rows(ref, 4 * tile, 4 * tile + 4)
        both = dot(beam, step_ref[0]) + dot(beam, step_ref[1])
        real, imag = both[:, :FREQS], both[:, FREQS:]
        z_ref[rows, :FREQS] = (real * cos_rows + imag * sin_rows).astype(BF16)
        z_ref[rows, FREQS:] = (imag * cos_rows - real * sin_rows).astype(BF16)


def plan_half(ref, core, before):
    times = jnp.concatenate([ref[chip, 2 * PER_BLOCK :, :].astype(F32) for chip in range(CHIPS)], 0).astype(BF16)
    row = lax.broadcasted_iota(jnp.int32, (8, 128), 0)
    lane = lax.broadcasted_iota(jnp.int32, (8, 128), 1)
    wanted = jnp.where(row == 0, BINS * core, jnp.where(row == 1, BINS * core + BINS, core + 63 + row))
    info = dot(jnp.where(lane == wanted, 1.0, 0.0).astype(BF16), times, (((1,), (1,)), ((), ())))
    start, end, first, last = (info[k : k + 1, :] for k in range(4))
    grains = jnp.where(end > start, jnp.minimum(last, float(PER_BLOCK - 1)) - first + 1.0, 0.0)
    earlier = dot(jnp.broadcast_to(grains, (8, 128)).astype(BF16), triangle(128, True))[0:1, :] + before
    return times, end, first, grains, earlier, earlier[:, 127:] + grains[:, 127:]


def slots_half(slot_0, plan, ref):
    times, end, first, grains, earlier, _ = plan
    slot = lax.broadcasted_iota(jnp.int32, (SLOTS, 128), 0).astype(F32) + slot_0
    visit = lax.broadcasted_iota(jnp.int32, (SLOTS, 128), 1)
    mine = (slot >= earlier) & (slot < earlier + grains)
    place = ((visit >> 3) * PER_BLOCK + 1).astype(F32) + first + (slot - earlier)
    place = jnp.sum(jnp.where(mine, place, 0.0), axis=1, keepdims=True) - 1.0
    ends = jnp.sum(jnp.where(mine, jnp.broadcast_to(end, (SLOTS, 128)), 0.0), axis=1, keepdims=True)
    starts = dot(times, jnp.where(mine, 1.0, 0.0).astype(BF16), (((0,), (1,)), ((), ())))
    places = lax.broadcasted_iota(jnp.int32, (SLOTS, HALF), 1).astype(F32)
    pick = jnp.where(places == place, 1.0, 0.0).astype(BF16)
    return place, ends, starts, dot(pick, beam_rows(ref, 0, CHIPS))


def half_kernel(ids, own_ref, step_ref, phase_ref, z_ref, total_ref, place_ref, ends_ref, starts_ref, gbeam_ref):
    _, _, core = ids()
    plan = plan_half(own_ref, core, jnp.zeros((1, 1), F32))
    place, ends, starts, beam = slots_half(jnp.float32(0.0), plan, own_ref)
    total_ref[...] = jnp.broadcast_to(plan[-1], (8, 128))
    place_ref[...] = jnp.broadcast_to(place, (SLOTS, 128))
    ends_ref[...] = jnp.broadcast_to(ends, (SLOTS, 128))
    starts_ref[...] = starts
    gbeam_ref[...] = beam
    transform(own_ref, step_ref, phase_ref, z_ref)


def grain_row(which):
    place = lax.broadcasted_iota(jnp.int32, (8, HALF), 1)
    grain = (2 * (place >> 5) + which) * PER_BLOCK + (place & (PER_BLOCK - 1))
    return grain.astype(F32)[0:1, :]


def spectrum_kernel(
    ids,
    own_ref, other_ref, z_ref, total_ref, place_ref, ends_ref, starts_ref, gbeam_ref,
    fold_ref, step_ref, short_ref, phases_ref, step2_ref, phase_ref,
    out_ref,
    z_s, gdft_s, gstep_s, gbeam_s, gtime_s, gstart_s, acc_s, fold_s,
):
    _, _, core = ids()
    before = total_ref[0:1, 0:1]
    other_plan = plan_half(other_ref, core, before)
    count = jnp.max(other_plan[-1]).astype(jnp.int32)
    transform(other_ref, step_ref, phase_ref, z_s)
    acc_s[...] = jnp.zeros(acc_s.shape, F32)
    fold_s[...] = fold_ref[...]
    own_grains = jnp.broadcast_to(grain_row(core), (SLOTS, HALF))
    other_grains = jnp.broadcast_to(grain_row(1 - core), (SLOTS, HALF))
    lane_iota = lax.broadcasted_iota(jnp.int32, (SLOTS, 128), 1)

    def fold_batch(batch, mine):
        first = (batch * SLOTS).astype(F32)
        more = slots_half(first, other_plan, other_ref)
        is_mine = mine[0] >= 0.0
        place = jnp.where(is_mine, mine[0], more[0]).astype(jnp.int32)
        which = jnp.where(is_mine, core, 1 - core)
        in_block = place & (PER_BLOCK - 1)
        grain = ((2 * (place >> 5) + which) * PER_BLOCK + in_block).astype(F32)
        here = mine[3] + more[3]
        times = (lane_iota + 128).astype(F32) * two_to(jnp.broadcast_to(in_block, (SLOTS, 128)))
        gtime_s[...] = times
        inside = times < mine[1] + more[1]
        gbeam_s[:, :GRAIN] = jnp.where(inside, here[:, :GRAIN], 0.0)
        gbeam_s[:, GRAIN:] = jnp.where(inside, here[:, GRAIN:], 0.0)
        starts = mine[2] + more[2]
        starts = jnp.where(core == 0, starts[:BINS], starts[BINS : 2 * BINS])
        for group in range(SLOTS // GROUP):
            gstart_s[group] = starts if group == 0 else pltpu.roll(starts, SLOTS - group * GROUP, 1)
        dft = jnp.zeros((SLOTS, 2 * FREQS), F32)
        ahead = jnp.zeros((SLOTS, 2 * GRAIN), F32)
        for grains, z, ref in ((own_grains, z_ref, own_ref), (other_grains, z_s, other_ref)):
            window = (grains >= grain) & (grains < grain + float(SPAN))
            dft = dft + dot(jnp.where(window, 1.0, 0.0).astype(BF16), z[...])
            next_pick = jnp.where(grains == grain + float(SPAN), 1.0, 0.0).astype(BF16)
            ahead = ahead + dot(next_pick, beam_rows(ref, 0, CHIPS))
        offset = in_block & (SPAN - 1)
        turner = jnp.where((lane_iota == offset) | (lane_iota == offset + SPAN), 1.0, 0.0)
        turned = dot(turner.astype(BF16), phases_ref[...])
        real, imag = dft[:, :FREQS], dft[:, FREQS:]
        cos_g, sin_g = turned[:, :FREQS], turned[:, FREQS:]
        step = dot((ahead - here).astype(BF16), step2_ref[...])
        for ref, real, imag in (
            (gdft_s, real * cos_g - imag * sin_g, imag * cos_g + real * sin_g),
            (gstep_s, step[:, :FREQS], step[:, FREQS:]),
        ):
            ref[:, :FREQS] = real
            ref[:, FREQS : 2 * FREQS] = imag - real
            ref[:, 2 * FREQS :] = real + imag

        def group_step(group, inner):
            rows = pl.ds(pl.multiple_of(group * GROUP, GROUP), GROUP)
            beam8, time8, start8 = gbeam_s[rows, :], gtime_s[rows, :], gstart_s[group]
            dft8, step8 = gdft_s[rows, :], gstep_s[rows, :]
            left = []
            for k in range(GROUP):
                since = time8[k : k + 1, :] >= start8[:, k : k + 1]
                real = jnp.where(since, beam8[k : k + 1, :GRAIN], 0.0)
                imag = jnp.where(since, beam8[k : k + 1, GRAIN:], 0.0)
                left.append(jnp.concatenate([real, imag], 1))
            left = jnp.concatenate(left, 0).astype(BF16)
            for part, factor in ((0, dft8), (1, step8)):
                folded = dot(left, fold_s[:, part * 2 * FREQS : part * 2 * FREQS + 2 * FREQS])
                sums = [acc_s[:, k * FREQS : k * FREQS + FREQS] for k in range(3 * part, 3 * part + 3)]
                for k in range(GROUP):
                    rows = slice(k * BINS, k * BINS + BINS)
                    real, imag = folded[rows, :FREQS], folded[rows, FREQS:]
                    for n, value in enumerate((real + imag, real, imag)):
                        sums[n] = sums[n] + value * factor[k : k + 1, n * FREQS : n * FREQS + FREQS]
                for n in range(3):
                    acc_s[:, (3 * part + n) * FREQS : (3 * part + n + 1) * FREQS] = sums[n]
            return inner

        def pair_step(pair, inner):
            group_step(2 * pair, inner)
            return group_step(2 * pair + 1, inner)

        groups = (jnp.minimum(count - batch * SLOTS, SLOTS) + GROUP - 1) // GROUP
        lax.fori_loop(0, groups // 2, pair_step, 0)
        lax.fori_loop(groups // 2 * 2, groups, group_step, 0)

    fold_batch(jnp.int32(0), (place_ref[:, 0:1], ends_ref[:, 0:1], starts_ref[...], gbeam_ref[...]))

    def batch_step(batch, carry):
        own_plan = plan_half(own_ref, core, jnp.zeros((1, 1), F32))
        fold_batch(batch, slots_half((batch * SLOTS).astype(F32), own_plan, own_ref))
        return carry

    lax.fori_loop(1, (count + SLOTS - 1) // SLOTS, batch_step, 0)
    since = acc_s[...]
    each = since - jnp.concatenate([since[1:], jnp.zeros((1, 6 * FREQS), F32)], 0)
    both, real, imag, both2, real2, imag2 = (each[:, k * FREQS : k * FREQS + FREQS] for k in range(6))
    short = dot(jnp.concatenate([both2 - imag2, both2 + real2], 1).astype(BF16), short_ref[...])
    out_ref[0] = (both - imag + short[:, :FREQS]) * SCALE
    out_ref[1] = (both + real + short[:, FREQS:]) * SCALE


def near(*values):
    return [pltpu.with_memory_space_constraint(v, pltpu.VMEM) for v in values]


def call(kernel, outs, values, scratch=(), mib=8, us=1.0):
    one = not isinstance(outs, (tuple, list))
    space = pl.BlockSpec(memory_space=pltpu.VMEM)
    return pl.pallas_call(
        kernel,
        out_shape=outs if one else tuple(outs),
        in_specs=[space] * len(values),
        out_specs=space if one else (space,) * len(outs),
        scratch_shapes=list(scratch),
        compiler_params=pltpu.CompilerParams(vmem_limit_bytes=mib << 20),
        cost_estimate=pl.CostEstimate(flops=int(us * 5e8), bytes_accessed=1 << 20, transcendentals=0),
    )(*near(*values))


HALF_Z = pltpu.VMEM((HALF, 2 * FREQS), BF16)


def make_tables(ids):
    given = tables()
    made = call(
        functools.partial(table_kernel, ids),
        (
            pltpu.VMEM((2 * GRAIN, 4 * FREQS), BF16),
            pltpu.VMEM((2, 2 * GRAIN, 2 * FREQS), BF16),
            pltpu.VMEM((2 * FREQS, 2 * FREQS), BF16),
            pltpu.VMEM((128, 2 * FREQS), BF16),
        ),
        [given[k] for k in ("base", "turn", "fold2", "phase", "back")],
        [pltpu.VMEM((2 * GRAIN, 2 * FREQS), BF16)],
        us=3.0,
    )
    return given, made


def spectrum(own, other, ids, given, made):
    fold, step, short, phases = made
    phase = given["phase"]
    half = call(
        functools.partial(half_kernel, ids),
        (
            HALF_Z,
            pltpu.VMEM((8, 128), F32),
            pltpu.VMEM((SLOTS, 128), F32),
            pltpu.VMEM((SLOTS, 128), F32),
            pltpu.VMEM((128, SLOTS), F32),
            pltpu.VMEM((SLOTS, 2 * GRAIN), F32),
        ),
        (own, step, phase),
        us=1.0,
    )
    scratch = [
        HALF_Z,
        pltpu.VMEM((SLOTS, 3 * FREQS), F32),
        pltpu.VMEM((SLOTS, 3 * FREQS), F32),
        pltpu.VMEM((SLOTS, 2 * GRAIN), F32),
        pltpu.VMEM((SLOTS, GRAIN), F32),
        pltpu.VMEM((SLOTS // GROUP, BINS, 128), F32),
        pltpu.VMEM((BINS, 6 * FREQS), F32),
        pltpu.VMEM((2 * GRAIN, 4 * FREQS), BF16),
    ]
    return call(
        functools.partial(spectrum_kernel, ids),
        jax.ShapeDtypeStruct((2, BINS, FREQS), F32),
        (own, other, *half, fold, step, short, phases, given["step2"], phase),
        scratch,
        mib=16,
        us=5.0,
    )


def front(voltages, beam_weights, bins):
    far = pl.BlockSpec(memory_space=pltpu.HBM)
    close = pl.BlockSpec(memory_space=pltpu.VMEM)
    return pl.pallas_call(
        front_kernel,
        out_shape=(
            pltpu.VMEM((DISH_WAYS, 2 * PER_BLOCK, GRAIN), F32),
            pltpu.VMEM((CHIPS, VISITS, GRAIN), BF16),
        ),
        in_specs=[far] * 3,
        out_specs=(close, close),
        scratch_shapes=[
            pltpu.VMEM(voltages.shape, BF16),
            pltpu.VMEM(beam_weights.shape, BF16),
            pltpu.VMEM(bins.shape, jnp.int32),
            pltpu.VMEM((72, GRAIN), F32),
            pltpu.VMEM((72, GRAIN), F32),
            pltpu.SemaphoreType.DMA((3,)),
        ],
        compiler_params=pltpu.CompilerParams(vmem_limit_bytes=8 << 20),
        cost_estimate=pl.CostEstimate(flops=1 << 20, bytes_accessed=1 << 20, transcendentals=0),
        name="front",
    )(*(pltpu.with_memory_space_constraint(v, pltpu.HBM) for v in (voltages, beam_weights, bins)))


def steps(voltages, beam_weights, phase_bins):
    def ids():
        core = lax.axis_index("core")
        owner = (lax.axis_index("z") * 2 + lax.axis_index("xh")) * 2 + core
        return owner, lax.axis_index("dish"), core

    given, made = make_tables(ids)
    partial_beam, visits = front(voltages, beam_weights, phase_bins.reshape(PER_BLOCK, GRAIN))
    parts = lax.all_to_all(partial_beam, "dish", 0, 0, tiled=True)
    packed = call(pack_kernel, pltpu.VMEM((CHIPS, ROWS, GRAIN), BF16), (parts, visits), us=0.3)
    own = lax.all_to_all(packed, ("z", "xh"), 0, 0, tiled=True)
    other = lax.ppermute(own, "core", [(0, 1), (1, 0)])
    return jnp.transpose(spectrum(own, other, ids, given, made), (2, 0, 1))


def solution(mesh):
    split = jax.sharding.Mesh(mesh.devices.reshape(8, 2, 2, 8), ("z", "xh", "core", "dish"))
    time = ("z", "xh", "core")
    return jax.shard_map(
        steps,
        mesh=split,
        in_specs=(P(None, "dish", time), P(None, "dish"), P(time)),
        out_specs=P("dish", None, time),
        check_vma=False,
    )
```

```python
import functools
import math

import jax
import jax.numpy as jnp
import numpy as np
from jax import lax
from jax.experimental import pallas as pl
from jax.experimental.pallas import tpu as pltpu
from jax.sharding import PartitionSpec as P


PH = 1024
LAGS = 2048
SAMPLES = 131072
DISH_WAYS = 8
TM_WAYS = 32
CHIPS = 16
HALF = SAMPLES // 2 // 128
LOCAL = SAMPLES // TM_WAYS
GRAIN = 128
PER_BLOCK = LOCAL // GRAIN
SPAN = LAGS // GRAIN
BINS = PH // TM_WAYS
FREQS = LAGS // DISH_WAYS
SLOTS = 128
GROUP = 16
VISITS = 8
ROWS = 2 * PER_BLOCK + VISITS
SCALE = 1.0 / math.sqrt(LAGS * SAMPLES / PH)

F32 = jnp.float32
BF16 = jnp.bfloat16


def dot(a, b, dims=(((1,), (0,)), ((), ()))):
    return lax.dot_general(a, b, dims, preferred_element_type=F32)


def hi_lo(value):
    hi = value.astype(BF16)
    return hi, (value - hi.astype(F32)).astype(BF16)


def tables():
    grain = np.arange(GRAIN)
    freq = np.arange(FREQS)
    angle = 2 * np.pi * np.outer(grain, freq) / LAGS
    base = np.concatenate([np.cos(angle), np.sin(angle)], 1).astype(np.float32)
    eighth = 2 * np.pi * np.outer(grain, np.arange(DISH_WAYS)) / DISH_WAYS
    turn = np.zeros((GRAIN, 128), np.float32)
    turn[:, :8] = np.cos(eighth)
    turn[:, 8:16] = np.sin(eighth)
    fine = 2 * np.pi * np.outer(grain, np.arange(2 * GRAIN)) / (2 * GRAIN)
    cos2, sin2 = np.cos(fine), np.sin(fine)
    fold2 = np.block([[cos2, sin2], [sin2, -cos2]]).astype(np.float32)
    step2 = np.block([[cos2, -sin2], [sin2, cos2]]).astype(np.float32)
    keep = (grain >= 1)[None, :] / (2.0 * GRAIN)
    back = np.block([[cos2.T * keep, -sin2.T * keep], [sin2.T * keep, cos2.T * keep]])
    sixteenth = 2 * np.pi * np.outer(np.arange(SPAN), freq) / SPAN
    phase = np.concatenate([np.cos(sixteenth), np.sin(sixteenth)], 1).astype(np.float32)
    return {
        "base": jnp.asarray(base),
        "turn": jnp.asarray(turn),
        "fold2": jnp.asarray(fold2).astype(BF16),
        "step2": jnp.asarray(step2).astype(BF16),
        "back": jnp.asarray(back.astype(np.float32)).astype(BF16),
        "phase": jnp.asarray(phase),
    }


def front_kernel(
    volts_hbm, weights_hbm, bins_hbm, beam_ref, visit_ref, volts_s, weights_s, bins_s, time_s, row_s, sems
):
    copies = [
        pltpu.make_async_copy(source, target, sems.at[k])
        for k, (source, target) in enumerate(
            ((bins_hbm, bins_s), (weights_hbm, weights_s), (volts_hbm, volts_s))
        )
    ]
    for copy in copies:
        copy.start()
    for copy in copies:
        copy.wait()
    weights = weights_s[...]
    first = dot(weights, volts_s[0])
    second = dot(weights, volts_s[1])
    real = first[0:1] - second[1:2]
    imag = first[1:2] + second[0:1]
    for row in range(PER_BLOCK):
        part = slice(row * GRAIN, (row + 1) * GRAIN)
        beam_ref[0, row : row + 1, :] = real[:, part]
        beam_ref[0, PER_BLOCK + row : PER_BLOCK + row + 1, :] = imag[:, part]
    make_visits(bins_s, visit_ref, time_s, row_s)
    rows = beam_ref[0]
    for way in range(1, DISH_WAYS):
        beam_ref[way] = rows


def pack_kernel(parts_ref, visit_ref, out_ref):
    total = parts_ref[0]
    for way in range(1, DISH_WAYS):
        total = total + parts_ref[way]
    rows = total.astype(BF16)
    for chip in range(CHIPS):
        out_ref[chip, : 2 * PER_BLOCK, :] = rows
        out_ref[chip, 2 * PER_BLOCK :, :] = visit_ref[chip]


def coded_times(shape):
    row = lax.broadcasted_iota(jnp.int32, shape, 0)
    lane = lax.broadcasted_iota(jnp.int32, shape, 1)
    return (lane + 128).astype(F32) * two_to(row)


def triangle(count, strict):
    row = lax.broadcasted_iota(jnp.int32, (count, count), 0)
    column = lax.broadcasted_iota(jnp.int32, (count, count), 1)
    return jnp.where(row < column if strict else row <= column, 1.0, 0.0).astype(BF16)


def make_visits(bins_ref, out_ref, time_s, row_s):
    bins = bins_ref[...]
    shape = (PER_BLOCK, GRAIN)
    row = lax.broadcasted_iota(jnp.int32, shape, 0)
    lane = lax.broadcasted_iota(jnp.int32, shape, 1)
    rolled = pltpu.roll(bins, 1, 1)
    before = jnp.where(lane == 0, pltpu.roll(rolled, 1, 0), rolled)
    later = row + lane > 0
    enters = later & (bins != before)
    wraps = jnp.where(later & (bins < before), 1.0, 0.0).astype(BF16)
    in_row = dot(wraps, triangle(GRAIN, False))
    ends = jnp.broadcast_to(in_row[:, GRAIN - 1 :], shape).astype(BF16)
    above = dot(triangle(PER_BLOCK, True), ends, (((0,), (0,)), ((), ())))
    step = bins + PH * (in_row + above).astype(jnp.int32)
    high = jnp.where(enters, step >> 7, -1).astype(F32)
    low = (step & 127).astype(F32)
    times = coded_times(shape)
    high_iota = lax.broadcasted_iota(jnp.int32, (48, GRAIN), 0)
    high_rows = high_iota.astype(F32).astype(BF16)
    low_rows = lax.broadcasted_iota(jnp.int32, (GRAIN, GRAIN), 0).astype(F32).astype(BF16)
    zero, one = jnp.zeros((), BF16), jnp.ones((), BF16)

    def spread(value, k, count):
        tile = jnp.broadcast_to(value[k : k + 1, :], (16, GRAIN)).astype(BF16)
        return jnp.concatenate([tile] * (count // 16), 0)

    found = jnp.zeros((96, GRAIN), F32)
    for pair in range(PER_BLOCK // 2):
        left, right = [], []
        for k in (2 * pair, 2 * pair + 1):
            here = spread(high, k, 48) == high_rows
            coded = jnp.where(here, spread(times, k, 48), zero)
            left.append(jnp.concatenate([coded, jnp.where(here, jnp.full((), k, BF16), zero)], 0))
            right.append(jnp.where(spread(low, k, GRAIN) == low_rows, one, zero))
        left = jnp.concatenate(left, 1)
        right = jnp.concatenate(right, 1)
        found = found + dot(left, right, (((1,), (1,)), ((), ())))
    place = high_iota * GRAIN + lax.broadcasted_iota(jnp.int32, (48, GRAIN), 1)
    past, ahead = place <= step[0:1, 0:1], place > step[PER_BLOCK - 1 :, GRAIN - 1 :]
    time_s[:48, :] = jnp.where(past, 2.0**-9, jnp.where(ahead, 2.0**23, found[:48]))
    row_s[:48, :] = jnp.where(past, 0.0, jnp.where(ahead, 32.0, found[48:]))
    time_s[48:, :] = jnp.full((24, GRAIN), 2.0**23, F32)
    row_s[48:, :] = jnp.full((24, GRAIN), 32.0, F32)
    lane = lax.broadcasted_iota(jnp.int32, (VISITS, GRAIN), 1)
    for eighth in range(8):
        now, then = pl.ds(eighth, VISITS, stride=8), pl.ds(eighth + 1, VISITS, stride=8)
        time, rows = time_s[now, :], row_s[now, :]
        next_time, next_rows = time_s[then, :], row_s[then, :]
        even = jnp.where(lane == 65, pltpu.roll(rows, 65, 1), time)
        even = jnp.where(lane == 66, pltpu.roll(rows, 34, 1), even)
        even = jnp.where(lane == 67, pltpu.roll(rows, 3, 1), even)
        odd = jnp.where(lane == 64, pltpu.roll(next_time, 64, 1), pltpu.roll(time, 64, 1))
        odd = jnp.where(lane == 65, pltpu.roll(rows, 1, 1), odd)
        odd = jnp.where(lane == 66, pltpu.roll(rows, 98, 1), odd)
        odd = jnp.where(lane == 67, pltpu.roll(next_rows, 67, 1), odd)
        out_ref[2 * eighth] = even.astype(BF16)
        out_ref[2 * eighth + 1] = odd.astype(BF16)


def two_to(exponent):
    value = jnp.full(jnp.shape(exponent), 2.0**-16, F32)
    for bit in range(5):
        value = value * jnp.where((exponent >> bit) & 1 == 1, float(2 ** (2**bit)), 1.0)
    return value


def table_kernel(
    ids, base_ref, turn_ref, fold2_ref, phase_ref, back_ref, fold_ref, step_ref, short_ref, phases_ref, last_s
):
    _, dish, _ = ids()
    lane = lax.broadcasted_iota(jnp.int32, (GRAIN, 128), 1)
    turn = turn_ref[...]
    cos8 = jnp.sum(jnp.where(lane == dish, turn, 0.0), axis=1, keepdims=True)
    sin8 = jnp.sum(jnp.where(lane == dish + 8, turn, 0.0), axis=1, keepdims=True)
    cos0, sin0 = base_ref[:, :FREQS], base_ref[:, FREQS:]
    cosine, cosine_lo = hi_lo(cos0 * cos8 - sin0 * sin8)
    sine, sine_lo = hi_lo(sin0 * cos8 + cos0 * sin8)
    fold_ref[:GRAIN, :FREQS] = cosine
    fold_ref[:GRAIN, FREQS : 2 * FREQS] = sine
    fold_ref[GRAIN:, :FREQS] = sine
    fold_ref[GRAIN:, FREQS : 2 * FREQS] = -cosine
    fold_ref[:, 2 * FREQS :] = fold2_ref[...]
    for k, (c, s) in enumerate(((cosine, sine), (cosine_lo, sine_lo))):
        step_ref[k, :GRAIN, :FREQS] = c
        step_ref[k, :GRAIN, FREQS:] = -s
        step_ref[k, GRAIN:, :FREQS] = s
        step_ref[k, GRAIN:, FREQS:] = c
    last_s[:GRAIN, :FREQS] = cosine
    last_s[:GRAIN, FREQS:] = sine
    last_s[GRAIN:, :FREQS] = -sine
    last_s[GRAIN:, FREQS:] = cosine
    short_ref[...] = dot(back_ref[...], last_s[...]).astype(BF16)
    phases_ref[...] = jnp.zeros(phases_ref.shape, BF16)
    hi, lo = hi_lo(phase_ref[...])
    phases_ref[0:SPAN, :] = hi
    phases_ref[SPAN : 2 * SPAN, :] = lo


def beam_rows(ref, first, last):
    rows = [
        jnp.concatenate([ref[chip, :PER_BLOCK, :], ref[chip, PER_BLOCK : 2 * PER_BLOCK, :]], 1)
        for chip in range(first, last)
    ]
    return jnp.concatenate(rows, 0)


def transform(ref, step_ref, phase_ref, z_ref):
    cos16, sin16 = phase_ref[:, :FREQS], phase_ref[:, FREQS:]
    cos_rows = jnp.concatenate([cos16] * (128 // SPAN), 0)
    sin_rows = jnp.concatenate([sin16] * (128 // SPAN), 0)
    for tile in range(HALF // 128):
        rows = slice(tile * 128, tile * 128 + 128)
        beam = beam_rows(ref, 4 * tile, 4 * tile + 4)
        both = dot(beam, step_ref[0]) + dot(beam, step_ref[1])
        real, imag = both[:, :FREQS], both[:, FREQS:]
        z_ref[rows, :FREQS] = (real * cos_rows + imag * sin_rows).astype(BF16)
        z_ref[rows, FREQS:] = (imag * cos_rows - real * sin_rows).astype(BF16)


def plan_half(ref, core, before):
    times = jnp.concatenate([ref[chip, 2 * PER_BLOCK :, :].astype(F32) for chip in range(CHIPS)], 0).astype(BF16)
    row = lax.broadcasted_iota(jnp.int32, (8, 128), 0)
    lane = lax.broadcasted_iota(jnp.int32, (8, 128), 1)
    wanted = jnp.where(row == 0, BINS * core, jnp.where(row == 1, BINS * core + BINS, core + 63 + row))
    info = dot(jnp.where(lane == wanted, 1.0, 0.0).astype(BF16), times, (((1,), (1,)), ((), ())))
    start, end, first, last = (info[k : k + 1, :] for k in range(4))
    grains = jnp.where(end > start, jnp.minimum(last, float(PER_BLOCK - 1)) - first + 1.0, 0.0)
    earlier = dot(jnp.broadcast_to(grains, (8, 128)).astype(BF16), triangle(128, True))[0:1, :] + before
    return times, end, first, grains, earlier, earlier[:, 127:] + grains[:, 127:]


def slots_half(slot_0, plan, ref):
    times, end, first, grains, earlier, _ = plan
    slot = lax.broadcasted_iota(jnp.int32, (SLOTS, 128), 0).astype(F32) + slot_0
    visit = lax.broadcasted_iota(jnp.int32, (SLOTS, 128), 1)
    mine = (slot >= earlier) & (slot < earlier + grains)
    place = ((visit >> 3) * PER_BLOCK + 1).astype(F32) + first + (slot - earlier)
    place = jnp.sum(jnp.where(mine, place, 0.0), axis=1, keepdims=True) - 1.0
    ends = jnp.sum(jnp.where(mine, jnp.broadcast_to(end, (SLOTS, 128)), 0.0), axis=1, keepdims=True)
    starts = dot(times, jnp.where(mine, 1.0, 0.0).astype(BF16), (((0,), (1,)), ((), ())))
    places = lax.broadcasted_iota(jnp.int32, (SLOTS, HALF), 1).astype(F32)
    pick = jnp.where(places == place, 1.0, 0.0).astype(BF16)
    return place, ends, starts, dot(pick, beam_rows(ref, 0, CHIPS))


def half_kernel(ids, own_ref, step_ref, phase_ref, z_ref, total_ref, place_ref, ends_ref, starts_ref, gbeam_ref):
    _, _, core = ids()
    plan = plan_half(own_ref, core, jnp.zeros((1, 1), F32))
    place, ends, starts, beam = slots_half(jnp.float32(0.0), plan, own_ref)
    total_ref[...] = jnp.broadcast_to(plan[-1], (8, 128))
    place_ref[...] = jnp.broadcast_to(place, (SLOTS, 128))
    ends_ref[...] = jnp.broadcast_to(ends, (SLOTS, 128))
    starts_ref[...] = starts
    gbeam_ref[...] = beam
    transform(own_ref, step_ref, phase_ref, z_ref)


def grain_row(which):
    place = lax.broadcasted_iota(jnp.int32, (8, HALF), 1)
    grain = (2 * (place >> 5) + which) * PER_BLOCK + (place & (PER_BLOCK - 1))
    return grain.astype(F32)[0:1, :]


def spectrum_kernel(
    ids,
    own_ref, other_ref, z_ref, total_ref, place_ref, ends_ref, starts_ref, gbeam_ref,
    fold_ref, step_ref, short_ref, phases_ref, step2_ref, phase_ref,
    out_ref,
    z_s, gdft_s, gstep_s, gbeam_s, gtime_s, gstart_s, acc_s,
):
    _, _, core = ids()
    before = total_ref[0:1, 0:1]
    other_plan = plan_half(other_ref, core, before)
    count = jnp.max(other_plan[-1]).astype(jnp.int32)
    transform(other_ref, step_ref, phase_ref, z_s)
    acc_s[...] = jnp.zeros(acc_s.shape, F32)
    own_grains = jnp.broadcast_to(grain_row(core), (SLOTS, HALF))
    other_grains = jnp.broadcast_to(grain_row(1 - core), (SLOTS, HALF))
    lane_iota = lax.broadcasted_iota(jnp.int32, (SLOTS, 128), 1)

    def fold_batch(batch, mine):
        first = (batch * SLOTS).astype(F32)
        more = slots_half(first, other_plan, other_ref)
        is_mine = mine[0] >= 0.0
        place = jnp.where(is_mine, mine[0], more[0]).astype(jnp.int32)
        which = jnp.where(is_mine, core, 1 - core)
        in_block = place & (PER_BLOCK - 1)
        grain = ((2 * (place >> 5) + which) * PER_BLOCK + in_block).astype(F32)
        here = mine[3] + more[3]
        times = (lane_iota + 128).astype(F32) * two_to(jnp.broadcast_to(in_block, (SLOTS, 128)))
        gtime_s[...] = times
        inside = times < mine[1] + more[1]
        gbeam_s[:, :GRAIN] = jnp.where(inside, here[:, :GRAIN], 0.0)
        gbeam_s[:, GRAIN:] = jnp.where(inside, here[:, GRAIN:], 0.0)
        starts = mine[2] + more[2]
        starts = jnp.where(core == 0, starts[:BINS], starts[BINS : 2 * BINS])
        for group in range(SLOTS // GROUP):
            gstart_s[group] = starts if group == 0 else pltpu.roll(starts, SLOTS - group * GROUP, 1)
        dft = jnp.zeros((SLOTS, 2 * FREQS), F32)
        ahead = jnp.zeros((SLOTS, 2 * GRAIN), F32)
        for grains, z, ref in ((own_grains, z_ref, own_ref), (other_grains, z_s, other_ref)):
            window = (grains >= grain) & (grains < grain + float(SPAN))
            dft = dft + dot(jnp.where(window, 1.0, 0.0).astype(BF16), z[...])
            next_pick = jnp.where(grains == grain + float(SPAN), 1.0, 0.0).astype(BF16)
            ahead = ahead + dot(next_pick, beam_rows(ref, 0, CHIPS))
        offset = in_block & (SPAN - 1)
        turner = jnp.where((lane_iota == offset) | (lane_iota == offset + SPAN), 1.0, 0.0)
        turned = dot(turner.astype(BF16), phases_ref[...])
        real, imag = dft[:, :FREQS], dft[:, FREQS:]
        cos_g, sin_g = turned[:, :FREQS], turned[:, FREQS:]
        step = dot((ahead - here).astype(BF16), step2_ref[...])
        for ref, real, imag in (
            (gdft_s, real * cos_g - imag * sin_g, imag * cos_g + real * sin_g),
            (gstep_s, step[:, :FREQS], step[:, FREQS:]),
        ):
            ref[:, :FREQS] = real
            ref[:, FREQS : 2 * FREQS] = imag - real
            ref[:, 2 * FREQS :] = real + imag

        def group_step(group, inner):
            rows = pl.ds(pl.multiple_of(group * GROUP, GROUP), GROUP)
            beam8, time8, start8 = gbeam_s[rows, :], gtime_s[rows, :], gstart_s[group]
            dft8, step8 = gdft_s[rows, :], gstep_s[rows, :]
            left = []
            for k in range(GROUP):
                since = time8[k : k + 1, :] >= start8[:, k : k + 1]
                real = jnp.where(since, beam8[k : k + 1, :GRAIN], 0.0)
                imag = jnp.where(since, beam8[k : k + 1, GRAIN:], 0.0)
                left.append(jnp.concatenate([real, imag], 1))
            left = jnp.concatenate(left, 0).astype(BF16)
            for part, factor in ((0, dft8), (1, step8)):
                folded = dot(left, fold_ref[:, part * 2 * FREQS : part * 2 * FREQS + 2 * FREQS])
                sums = [acc_s[:, k * FREQS : k * FREQS + FREQS] for k in range(3 * part, 3 * part + 3)]
                for k in range(GROUP):
                    rows = slice(k * BINS, k * BINS + BINS)
                    real, imag = folded[rows, :FREQS], folded[rows, FREQS:]
                    for n, value in enumerate((real + imag, real, imag)):
                        sums[n] = sums[n] + value * factor[k : k + 1, n * FREQS : n * FREQS + FREQS]
                for n in range(3):
                    acc_s[:, (3 * part + n) * FREQS : (3 * part + n + 1) * FREQS] = sums[n]
            return inner

        def pair_step(pair, inner):
            group_step(2 * pair, inner)
            return group_step(2 * pair + 1, inner)

        groups = (jnp.minimum(count - batch * SLOTS, SLOTS) + GROUP - 1) // GROUP
        lax.fori_loop(0, groups // 2, pair_step, 0)
        lax.fori_loop(groups // 2 * 2, groups, group_step, 0)

    fold_batch(jnp.int32(0), (place_ref[:, 0:1], ends_ref[:, 0:1], starts_ref[...], gbeam_ref[...]))

    def batch_step(batch, carry):
        own_plan = plan_half(own_ref, core, jnp.zeros((1, 1), F32))
        fold_batch(batch, slots_half((batch * SLOTS).astype(F32), own_plan, own_ref))
        return carry

    lax.fori_loop(1, (count + SLOTS - 1) // SLOTS, batch_step, 0)
    since = acc_s[...]
    each = since - jnp.concatenate([since[1:], jnp.zeros((1, 6 * FREQS), F32)], 0)
    both, real, imag, both2, real2, imag2 = (each[:, k * FREQS : k * FREQS + FREQS] for k in range(6))
    short = dot(jnp.concatenate([both2 - imag2, both2 + real2], 1).astype(BF16), short_ref[...])
    out_ref[0] = (both - imag + short[:, :FREQS]) * SCALE
    out_ref[1] = (both + real + short[:, FREQS:]) * SCALE


def near(*values):
    return [pltpu.with_memory_space_constraint(v, pltpu.VMEM) for v in values]


def call(kernel, outs, values, scratch=(), mib=8, us=1.0):
    one = not isinstance(outs, (tuple, list))
    space = pl.BlockSpec(memory_space=pltpu.VMEM)
    return pl.pallas_call(
        kernel,
        out_shape=outs if one else tuple(outs),
        in_specs=[space] * len(values),
        out_specs=space if one else (space,) * len(outs),
        scratch_shapes=list(scratch),
        compiler_params=pltpu.CompilerParams(vmem_limit_bytes=mib << 20),
        cost_estimate=pl.CostEstimate(flops=int(us * 5e8), bytes_accessed=1 << 20, transcendentals=0),
    )(*near(*values))


HALF_Z = pltpu.VMEM((HALF, 2 * FREQS), BF16)


def make_tables(ids):
    given = tables()
    made = call(
        functools.partial(table_kernel, ids),
        (
            pltpu.VMEM((2 * GRAIN, 4 * FREQS), BF16),
            pltpu.VMEM((2, 2 * GRAIN, 2 * FREQS), BF16),
            pltpu.VMEM((2 * FREQS, 2 * FREQS), BF16),
            pltpu.VMEM((128, 2 * FREQS), BF16),
        ),
        [given[k] for k in ("base", "turn", "fold2", "phase", "back")],
        [pltpu.VMEM((2 * GRAIN, 2 * FREQS), BF16)],
        us=3.0,
    )
    return given, made


def spectrum(own, other, ids, given, made):
    fold, step, short, phases = made
    phase = given["phase"]
    half = call(
        functools.partial(half_kernel, ids),
        (
            HALF_Z,
            pltpu.VMEM((8, 128), F32),
            pltpu.VMEM((SLOTS, 128), F32),
            pltpu.VMEM((SLOTS, 128), F32),
            pltpu.VMEM((128, SLOTS), F32),
            pltpu.VMEM((SLOTS, 2 * GRAIN), F32),
        ),
        (own, step, phase),
        us=1.0,
    )
    scratch = [
        HALF_Z,
        pltpu.VMEM((SLOTS, 3 * FREQS), F32),
        pltpu.VMEM((SLOTS, 3 * FREQS), F32),
        pltpu.VMEM((SLOTS, 2 * GRAIN), F32),
        pltpu.VMEM((SLOTS, GRAIN), F32),
        pltpu.VMEM((SLOTS // GROUP, BINS, 128), F32),
        pltpu.VMEM((BINS, 6 * FREQS), F32),
    ]
    return call(
        functools.partial(spectrum_kernel, ids),
        jax.ShapeDtypeStruct((2, BINS, FREQS), F32),
        (own, other, *half, fold, step, short, phases, given["step2"], phase),
        scratch,
        mib=16,
        us=5.0,
    )


def front(voltages, beam_weights, bins):
    far = pl.BlockSpec(memory_space=pltpu.HBM)
    close = pl.BlockSpec(memory_space=pltpu.VMEM)
    return pl.pallas_call(
        front_kernel,
        out_shape=(
            pltpu.VMEM((DISH_WAYS, 2 * PER_BLOCK, GRAIN), F32),
            pltpu.VMEM((CHIPS, VISITS, GRAIN), BF16),
        ),
        in_specs=[far] * 3,
        out_specs=(close, close),
        scratch_shapes=[
            pltpu.VMEM(voltages.shape, BF16),
            pltpu.VMEM(beam_weights.shape, BF16),
            pltpu.VMEM(bins.shape, jnp.int32),
            pltpu.VMEM((72, GRAIN), F32),
            pltpu.VMEM((72, GRAIN), F32),
            pltpu.SemaphoreType.DMA((3,)),
        ],
        compiler_params=pltpu.CompilerParams(vmem_limit_bytes=8 << 20),
        cost_estimate=pl.CostEstimate(flops=1 << 20, bytes_accessed=1 << 20, transcendentals=0),
        name="front",
    )(*(pltpu.with_memory_space_constraint(v, pltpu.HBM) for v in (voltages, beam_weights, bins)))


def steps(voltages, beam_weights, phase_bins):
    def ids():
        core = lax.axis_index("core")
        owner = (lax.axis_index("z") * 2 + lax.axis_index("xh")) * 2 + core
        return owner, lax.axis_index("dish"), core

    given, made = make_tables(ids)
    partial_beam, visits = front(voltages, beam_weights, phase_bins.reshape(PER_BLOCK, GRAIN))
    parts = lax.all_to_all(partial_beam, "dish", 0, 0, tiled=True)
    packed = call(pack_kernel, pltpu.VMEM((CHIPS, ROWS, GRAIN), BF16), (parts, visits), us=0.3)
    own = lax.all_to_all(packed, ("z", "xh"), 0, 0, tiled=True)
    other = lax.ppermute(own, "core", [(0, 1), (1, 0)])
    return jnp.transpose(spectrum(own, other, ids, given, made), (2, 0, 1))


def solution(mesh):
    split = jax.sharding.Mesh(mesh.devices.reshape(8, 2, 2, 8), ("z", "xh", "core", "dish"))
    time = ("z", "xh", "core")
    return jax.shard_map(
        steps,
        mesh=split,
        in_specs=(P(None, "dish", time), P(None, "dish"), P(time)),
        out_specs=P("dish", None, time),
        check_vma=False,
    )
```

```python
import functools
import math

import jax
import jax.numpy as jnp
import numpy as np
from jax import lax
from jax.experimental import pallas as pl
from jax.experimental.pallas import tpu as pltpu
from jax.sharding import PartitionSpec as P


PH = 1024
LAGS = 2048
SAMPLES = 131072
DISH_WAYS = 8
TM_WAYS = 32
CHIPS = 16
HALF = SAMPLES // 2 // 128
LOCAL = SAMPLES // TM_WAYS
GRAIN = 128
PER_BLOCK = LOCAL // GRAIN
SIDE = GRAIN // 2
SPAN = LAGS // GRAIN
BINS = PH // TM_WAYS
FREQS = LAGS // DISH_WAYS
SLOTS = 96
GROUP = 16
VISITS = 8
ROWS = 2 * PER_BLOCK + VISITS
SCALE = 1.0 / math.sqrt(LAGS * SAMPLES / PH)

F32 = jnp.float32
BF16 = jnp.bfloat16


def dot(a, b, dims=(((1,), (0,)), ((), ()))):
    return lax.dot_general(a, b, dims, preferred_element_type=F32)


def hi_lo(value):
    hi = value.astype(BF16)
    return hi, (value - hi.astype(F32)).astype(BF16)


def tables():
    grain = np.arange(GRAIN)
    freq = np.arange(FREQS)
    angle = 2 * np.pi * np.outer(grain, freq) / LAGS
    base = np.concatenate([np.cos(angle), np.sin(angle)], 1).astype(np.float32)
    eighth = 2 * np.pi * np.outer(grain, np.arange(DISH_WAYS)) / DISH_WAYS
    turn = np.zeros((GRAIN, 128), np.float32)
    turn[:, :8] = np.cos(eighth)
    turn[:, 8:16] = np.sin(eighth)
    fine = 2 * np.pi * np.outer(grain, np.arange(2 * GRAIN)) / (2 * GRAIN)
    cos2, sin2 = np.cos(fine), np.sin(fine)
    fold2 = np.block([[cos2, sin2], [sin2, -cos2]]).astype(np.float32)
    step2 = np.block([[cos2, -sin2], [sin2, cos2]]).astype(np.float32)
    sides = np.concatenate([np.arange(k, k + SIDE) for k in (0, GRAIN, SIDE, GRAIN + SIDE)])
    fold2, step2 = fold2[sides], step2[sides]
    keep = (grain >= 1)[None, :] / (2.0 * GRAIN)
    back = np.block([[cos2.T * keep, -sin2.T * keep], [sin2.T * keep, cos2.T * keep]])
    sixteenth = 2 * np.pi * np.outer(np.arange(SPAN), freq) / SPAN
    phase = np.concatenate([np.cos(sixteenth), np.sin(sixteenth)], 1).astype(np.float32)
    fine = np.pi * np.outer(np.arange(2 * SPAN), freq) / SPAN
    start = np.concatenate([np.cos(fine), np.sin(fine)], 1).astype(np.float32)
    return {
        "base": jnp.asarray(base),
        "turn": jnp.asarray(turn),
        "fold2": jnp.asarray(fold2).astype(BF16),
        "step2": jnp.asarray(step2).astype(BF16),
        "back": jnp.asarray(back.astype(np.float32)).astype(BF16),
        "phase": jnp.asarray(phase),
        "start": jnp.asarray(start),
    }


def front_kernel(
    volts_hbm, weights_hbm, bins_hbm, beam_ref, visit_ref, volts_s, weights_s, bins_s, time_s, row_s, sems
):
    copies = [
        pltpu.make_async_copy(source, target, sems.at[k])
        for k, (source, target) in enumerate(
            ((bins_hbm, bins_s), (weights_hbm, weights_s), (volts_hbm, volts_s))
        )
    ]
    for copy in copies:
        copy.start()
    for copy in copies:
        copy.wait()
    weights = weights_s[...]
    first = dot(weights, volts_s[0])
    second = dot(weights, volts_s[1])
    real = first[0:1] - second[1:2]
    imag = first[1:2] + second[0:1]
    for row in range(PER_BLOCK):
        part = slice(row * GRAIN, (row + 1) * GRAIN)
        beam_ref[0, row : row + 1, :] = real[:, part]
        beam_ref[0, PER_BLOCK + row : PER_BLOCK + row + 1, :] = imag[:, part]
    make_visits(bins_s, visit_ref, time_s, row_s)
    rows = beam_ref[0]
    for way in range(1, DISH_WAYS):
        beam_ref[way] = rows


def pack_kernel(parts_ref, visit_ref, out_ref):
    total = parts_ref[0]
    for way in range(1, DISH_WAYS):
        total = total + parts_ref[way]
    real, imag = total[:PER_BLOCK], total[PER_BLOCK:]
    early = lax.broadcasted_iota(jnp.int32, (PER_BLOCK, GRAIN), 1) < SIDE
    early_side = jnp.where(early, real, pltpu.roll(imag, SIDE, 1))
    late_side = jnp.where(early, pltpu.roll(real, SIDE, 1), imag)
    rows = jnp.concatenate([early_side, late_side], 0).astype(BF16)
    for chip in range(CHIPS):
        out_ref[chip, : 2 * PER_BLOCK, :] = rows
        out_ref[chip, 2 * PER_BLOCK :, :] = visit_ref[chip]


def coded_times(shape):
    row = lax.broadcasted_iota(jnp.int32, shape, 0)
    lane = lax.broadcasted_iota(jnp.int32, shape, 1)
    return (lane + 128).astype(F32) * two_to(row)


def triangle(count, strict):
    row = lax.broadcasted_iota(jnp.int32, (count, count), 0)
    column = lax.broadcasted_iota(jnp.int32, (count, count), 1)
    return jnp.where(row < column if strict else row <= column, 1.0, 0.0).astype(BF16)


def make_visits(bins_ref, out_ref, time_s, row_s):
    bins = bins_ref[...]
    shape = (PER_BLOCK, GRAIN)
    row = lax.broadcasted_iota(jnp.int32, shape, 0)
    lane = lax.broadcasted_iota(jnp.int32, shape, 1)
    rolled = pltpu.roll(bins, 1, 1)
    before = jnp.where(lane == 0, pltpu.roll(rolled, 1, 0), rolled)
    later = row + lane > 0
    enters = later & (bins != before)
    wraps = jnp.where(later & (bins < before), 1.0, 0.0).astype(BF16)
    in_row = dot(wraps, triangle(GRAIN, False))
    ends = jnp.broadcast_to(in_row[:, GRAIN - 1 :], shape).astype(BF16)
    above = dot(triangle(PER_BLOCK, True), ends, (((0,), (0,)), ((), ())))
    step = bins + PH * (in_row + above).astype(jnp.int32)
    high = jnp.where(enters, step >> 7, -1).astype(F32)
    low = (step & 127).astype(F32)
    times = coded_times(shape)
    high_iota = lax.broadcasted_iota(jnp.int32, (48, GRAIN), 0)
    high_rows = high_iota.astype(F32).astype(BF16)
    low_rows = lax.broadcasted_iota(jnp.int32, (GRAIN, GRAIN), 0).astype(F32).astype(BF16)
    zero, one = jnp.zeros((), BF16), jnp.ones((), BF16)
    late = jnp.where(lax.broadcasted_iota(jnp.int32, (48, GRAIN), 1) >= SIDE, 1.0, 0.0).astype(BF16)

    def spread(value, k, count):
        tile = jnp.broadcast_to(value[k : k + 1, :], (16, GRAIN)).astype(BF16)
        return jnp.concatenate([tile] * (count // 16), 0)

    found = jnp.zeros((96, GRAIN), F32)
    for pair in range(PER_BLOCK // 2):
        left, right = [], []
        for k in (2 * pair, 2 * pair + 1):
            here = spread(high, k, 48) == high_rows
            coded = jnp.where(here, spread(times, k, 48), zero)
            left.append(jnp.concatenate([coded, jnp.where(here, late + jnp.full((), 2 * k, BF16), zero)], 0))
            right.append(jnp.where(spread(low, k, GRAIN) == low_rows, one, zero))
        left = jnp.concatenate(left, 1)
        right = jnp.concatenate(right, 1)
        found = found + dot(left, right, (((1,), (1,)), ((), ())))
    place = high_iota * GRAIN + lax.broadcasted_iota(jnp.int32, (48, GRAIN), 1)
    past, ahead = place <= step[0:1, 0:1], place > step[PER_BLOCK - 1 :, GRAIN - 1 :]
    time_s[:48, :] = jnp.where(past, 2.0**-9, jnp.where(ahead, 2.0**23, found[:48]))
    row_s[:48, :] = jnp.where(past, 0.0, jnp.where(ahead, 64.0, found[48:]))
    time_s[48:, :] = jnp.full((24, GRAIN), 2.0**23, F32)
    row_s[48:, :] = jnp.full((24, GRAIN), 64.0, F32)
    lane = lax.broadcasted_iota(jnp.int32, (VISITS, GRAIN), 1)
    for eighth in range(8):
        now, then = pl.ds(eighth, VISITS, stride=8), pl.ds(eighth + 1, VISITS, stride=8)
        time, rows = time_s[now, :], row_s[now, :]
        next_time, next_rows = time_s[then, :], row_s[then, :]
        even = jnp.where(lane == 65, pltpu.roll(rows, 65, 1), time)
        even = jnp.where(lane == 66, pltpu.roll(rows, 34, 1), even)
        even = jnp.where(lane == 67, pltpu.roll(rows, 3, 1), even)
        odd = jnp.where(lane == 64, pltpu.roll(next_time, 64, 1), pltpu.roll(time, 64, 1))
        odd = jnp.where(lane == 65, pltpu.roll(rows, 1, 1), odd)
        odd = jnp.where(lane == 66, pltpu.roll(rows, 98, 1), odd)
        odd = jnp.where(lane == 67, pltpu.roll(next_rows, 67, 1), odd)
        out_ref[2 * eighth] = even.astype(BF16)
        out_ref[2 * eighth + 1] = odd.astype(BF16)


def two_to(exponent):
    value = jnp.full(jnp.shape(exponent), 2.0**-16, F32)
    for bit in range(6):
        value = value * jnp.where((exponent >> bit) & 1 == 1, float(2 ** (2**bit)), 1.0)
    return value


def table_kernel(
    ids, base_ref, turn_ref, fold2_ref, start_ref, back_ref, fold_ref, step_ref, short_ref, phases_ref, side_ref, last_s
):
    _, dish, _ = ids()
    lane = lax.broadcasted_iota(jnp.int32, (GRAIN, 128), 1)
    turn = turn_ref[...]
    cos8 = jnp.sum(jnp.where(lane == dish, turn, 0.0), axis=1, keepdims=True)
    sin8 = jnp.sum(jnp.where(lane == dish + 8, turn, 0.0), axis=1, keepdims=True)
    cos0, sin0 = base_ref[:, :FREQS], base_ref[:, FREQS:]
    cos_f, sin_f = cos0 * cos8 - sin0 * sin8, sin0 * cos8 + cos0 * sin8
    cosine, cosine_lo = hi_lo(cos_f)
    sine, sine_lo = hi_lo(sin_f)
    for side in range(2):
        part = slice(side * SIDE, side * SIDE + SIDE)
        reals = slice(side * GRAIN, side * GRAIN + SIDE)
        imags = slice(side * GRAIN + SIDE, side * GRAIN + GRAIN)
        fold_ref[reals, :FREQS] = cosine[part]
        fold_ref[reals, FREQS : 2 * FREQS] = sine[part]
        fold_ref[imags, :FREQS] = sine[part]
        fold_ref[imags, FREQS : 2 * FREQS] = -cosine[part]
        for k, (c, s) in enumerate(((cosine, sine), (cosine_lo, sine_lo))):
            step_ref[k, reals, :FREQS] = c[part]
            step_ref[k, reals, FREQS:] = -s[part]
            step_ref[k, imags, :FREQS] = s[part]
            step_ref[k, imags, FREQS:] = c[part]
    fold_ref[:, 2 * FREQS :] = fold2_ref[...]
    cos_side, sin_side = cos_f[SIDE : SIDE + 1], sin_f[SIDE : SIDE + 1]
    side_real = cos_f[:SIDE] * cos_side + sin_f[:SIDE] * sin_side
    side_imag = cos_f[:SIDE] * sin_side - sin_f[:SIDE] * cos_side
    side_ref[:SIDE, :FREQS] = side_real.astype(BF16)
    side_ref[:SIDE, FREQS:] = side_imag.astype(BF16)
    side_ref[SIDE:, :FREQS] = -side_imag.astype(BF16)
    side_ref[SIDE:, FREQS:] = side_real.astype(BF16)
    last_s[:GRAIN, :FREQS] = cosine
    last_s[:GRAIN, FREQS:] = sine
    last_s[GRAIN:, :FREQS] = -sine
    last_s[GRAIN:, FREQS:] = cosine
    short_ref[...] = dot(back_ref[...], last_s[...]).astype(BF16)
    phases_ref[...] = jnp.zeros(phases_ref.shape, BF16)
    hi, lo = hi_lo(start_ref[...])
    phases_ref[: 2 * SPAN, :] = hi
    phases_ref[2 * SPAN : 4 * SPAN, :] = lo


def beam_rows(ref, first, last):
    rows = [
        jnp.concatenate([ref[chip, :PER_BLOCK, :], ref[chip, PER_BLOCK : 2 * PER_BLOCK, :]], 1)
        for chip in range(first, last)
    ]
    return jnp.concatenate(rows, 0)


def side_rows(ref, side):
    part = slice(side * PER_BLOCK, side * PER_BLOCK + PER_BLOCK)
    return jnp.concatenate([ref[chip, part, :] for chip in range(CHIPS)], 0)


def swap_sides(odd, early, late):
    return jnp.concatenate([jnp.where(odd > 0.0, late, early), jnp.where(odd > 0.0, early, late)], 1)


def transform(ref, step_ref, phase_ref, z_ref):
    cos16, sin16 = phase_ref[:, :FREQS], phase_ref[:, FREQS:]
    cos_rows = jnp.concatenate([cos16] * (128 // SPAN), 0)
    sin_rows = jnp.concatenate([sin16] * (128 // SPAN), 0)
    for tile in range(HALF // 128):
        rows = slice(tile * 128, tile * 128 + 128)
        beam = beam_rows(ref, 4 * tile, 4 * tile + 4)
        both = dot(beam, step_ref[0]) + dot(beam, step_ref[1])
        real, imag = both[:, :FREQS], both[:, FREQS:]
        z_ref[rows, :FREQS] = (real * cos_rows + imag * sin_rows).astype(BF16)
        z_ref[rows, FREQS:] = (imag * cos_rows - real * sin_rows).astype(BF16)


def plan_half(ref, core, before):
    times = jnp.concatenate([ref[chip, 2 * PER_BLOCK :, :].astype(F32) for chip in range(CHIPS)], 0).astype(BF16)
    row = lax.broadcasted_iota(jnp.int32, (8, 128), 0)
    lane = lax.broadcasted_iota(jnp.int32, (8, 128), 1)
    wanted = jnp.where(row == 0, BINS * core, jnp.where(row == 1, BINS * core + BINS, core + 63 + row))
    info = dot(jnp.where(lane == wanted, 1.0, 0.0).astype(BF16), times, (((1,), (1,)), ((), ())))
    start, end, first, last = (info[k : k + 1, :] for k in range(4))
    sides = jnp.minimum(last, float(2 * PER_BLOCK - 1)) - first
    grains = jnp.where(end > start, jnp.floor(sides * 0.5) + 1.0, 0.0)
    earlier = dot(jnp.broadcast_to(grains, (8, 128)).astype(BF16), triangle(128, True))[0:1, :] + before
    return times, end, first, grains, earlier, earlier[:, 127:] + grains[:, 127:]


def slots_half(slot_0, plan, ref):
    times, end, first, grains, earlier, _ = plan
    slot = lax.broadcasted_iota(jnp.int32, (128, 128), 0).astype(F32) + slot_0
    visit = lax.broadcasted_iota(jnp.int32, (SLOTS, 128), 1)
    mine = (slot >= earlier) & (slot < earlier + grains)
    starts = dot(times, jnp.where(mine, 1.0, 0.0).astype(BF16), (((0,), (1,)), ((), ())))
    slot, mine = slot[:SLOTS], mine[:SLOTS]
    place = ((visit >> 3) * (2 * PER_BLOCK) + 1).astype(F32) + first + 2.0 * (slot - earlier)
    place = jnp.sum(jnp.where(mine, place, 0.0), axis=1, keepdims=True) - 1.0
    ends = jnp.sum(jnp.where(mine, jnp.broadcast_to(end, (SLOTS, 128)), 0.0), axis=1, keepdims=True)
    places = lax.broadcasted_iota(jnp.int32, (SLOTS, HALF), 1).astype(F32)
    whole = jnp.where(place < 0.0, -4.0, jnp.floor(place * 0.5))
    odd = jnp.where(place < 0.0, 0.0, place - 2.0 * whole)
    early = dot(jnp.where(places == whole + odd, 1.0, 0.0).astype(BF16), side_rows(ref, 0))
    late = dot(jnp.where(places == whole, 1.0, 0.0).astype(BF16), side_rows(ref, 1))
    return place, ends, starts, swap_sides(odd, early, late)


def half_kernel(ids, own_ref, step_ref, phase_ref, z_ref, total_ref, place_ref, ends_ref, starts_ref, gbeam_ref):
    _, _, core = ids()
    plan = plan_half(own_ref, core, jnp.zeros((1, 1), F32))
    place, ends, starts, beam = slots_half(jnp.float32(0.0), plan, own_ref)
    total_ref[...] = jnp.broadcast_to(plan[-1], (8, 128))
    place_ref[...] = jnp.broadcast_to(place, (SLOTS, 128))
    ends_ref[...] = jnp.broadcast_to(ends, (SLOTS, 128))
    starts_ref[...] = starts
    gbeam_ref[...] = beam
    transform(own_ref, step_ref, phase_ref, z_ref)


def grain_row(which):
    place = lax.broadcasted_iota(jnp.int32, (8, HALF), 1)
    grain = (2 * (place >> 5) + which) * PER_BLOCK + (place & (PER_BLOCK - 1))
    return grain.astype(F32)[0:1, :]


def spectrum_kernel(
    ids,
    own_ref, other_ref, z_ref, total_ref, place_ref, ends_ref, starts_ref, gbeam_ref,
    fold_ref, step_ref, short_ref, phases_ref, side_ref, step2_ref, phase_ref,
    out_ref,
    z_s, gdft_s, gstep_s, gbeam_s, gtime_s, gstart_s, acc_s,
):
    _, _, core = ids()
    before = total_ref[0:1, 0:1]
    other_plan = plan_half(other_ref, core, before)
    count = jnp.max(other_plan[-1]).astype(jnp.int32)
    transform(other_ref, step_ref, phase_ref, z_s)
    acc_s[...] = jnp.zeros(acc_s.shape, F32)
    own_grains = jnp.broadcast_to(grain_row(core), (SLOTS, HALF))
    other_grains = jnp.broadcast_to(grain_row(1 - core), (SLOTS, HALF))
    lane_iota = lax.broadcasted_iota(jnp.int32, (SLOTS, 128), 1)

    def fold_batch(batch, mine):
        first = (batch * SLOTS).astype(F32)
        more = slots_half(first, other_plan, other_ref)
        is_mine = mine[0] >= 0.0
        place = jnp.where(is_mine, mine[0], more[0]).astype(jnp.int32)
        which = jnp.where(is_mine, core, 1 - core)
        side = place & (2 * PER_BLOCK - 1)
        in_block, odd = side >> 1, (side & 1).astype(F32)
        grain = ((2 * (place >> 6) + which) * PER_BLOCK + in_block).astype(F32)
        here = mine[3] + more[3]
        ends = mine[1] + more[1]
        for k in range(2):
            at = jnp.broadcast_to(side + k, (SLOTS, GRAIN))
            times = (128 + (at & 1) * SIDE + (lane_iota & (SIDE - 1))).astype(F32) * two_to(at >> 1)
            part = slice(k * GRAIN, k * GRAIN + GRAIN)
            gtime_s[:, part] = times
            gbeam_s[:, part] = jnp.where(times < ends, here[:, part], 0.0)
        starts = mine[2] + more[2]
        starts = jnp.where(core == 0, starts[:BINS], starts[BINS : 2 * BINS])
        for group in range(SLOTS // GROUP):
            gstart_s[group] = starts if group == 0 else pltpu.roll(starts, 128 - group * GROUP, 1)
        dft = jnp.zeros((SLOTS, 2 * FREQS), F32)
        early, late, gone = (jnp.zeros((SLOTS, GRAIN), F32) for _ in range(3))
        for grains, z, ref in ((own_grains, z_ref, own_ref), (other_grains, z_s, other_ref)):
            window = (grains >= grain) & (grains < grain + float(SPAN))
            dft = dft + dot(jnp.where(window, 1.0, 0.0).astype(BF16), z[...])
            then = grains == grain + float(SPAN)
            early_pick = jnp.where(grains == grain + float(SPAN) + odd, 1.0, 0.0).astype(BF16)
            late_pick = jnp.where(then, 1.0, 0.0).astype(BF16)
            gone_pick = jnp.where(then, odd, jnp.where(grains == grain, -odd, 0.0)).astype(BF16)
            early = early + dot(early_pick, side_rows(ref, 0))
            late = late + dot(late_pick, side_rows(ref, 1))
            gone = gone + dot(gone_pick, side_rows(ref, 0))
        ahead = swap_sides(odd, early, late)
        moved = dot(gone.astype(BF16), side_ref[...])
        offset = side & (2 * SPAN - 1)
        turner = jnp.where((lane_iota == offset) | (lane_iota == offset + 2 * SPAN), 1.0, 0.0)
        turned = dot(turner.astype(BF16), phases_ref[...])
        real, imag = dft[:, :FREQS], dft[:, FREQS:]
        cos_g, sin_g = turned[:, :FREQS], turned[:, FREQS:]
        step = dot((ahead - here).astype(BF16), step2_ref[...])
        for ref, real, imag in (
            (gdft_s, real * cos_g - imag * sin_g + moved[:, :FREQS], imag * cos_g + real * sin_g + moved[:, FREQS:]),
            (gstep_s, step[:, :FREQS], step[:, FREQS:]),
        ):
            ref[:, :FREQS] = real
            ref[:, FREQS : 2 * FREQS] = imag - real
            ref[:, 2 * FREQS :] = real + imag

        def fold(slot, size):
            rows = pl.ds(pl.multiple_of(slot, 8), size)
            beam8, time8, start8 = gbeam_s[rows, :], gtime_s[rows, :], gstart_s[slot // GROUP]
            dft8, step8 = gdft_s[rows, :], gstep_s[rows, :]
            left = []
            for k in range(size):
                start = start8[:, k : k + 1]
                sides = [
                    jnp.where(time8[k : k + 1, at : at + GRAIN] >= start, beam8[k : k + 1, at : at + GRAIN], 0.0)
                    for at in (0, GRAIN)
                ]
                left.append(jnp.concatenate(sides, 1))
            left = jnp.concatenate(left, 0).astype(BF16)
            for part, factor in ((0, dft8), (1, step8)):
                folded = dot(left, fold_ref[:, part * 2 * FREQS : part * 2 * FREQS + 2 * FREQS])
                sums = [acc_s[:, k * FREQS : k * FREQS + FREQS] for k in range(3 * part, 3 * part + 3)]
                for k in range(size):
                    rows = slice(k * BINS, k * BINS + BINS)
                    real, imag = folded[rows, :FREQS], folded[rows, FREQS:]
                    for n, value in enumerate((real + imag, real, imag)):
                        sums[n] = sums[n] + value * factor[k : k + 1, n * FREQS : n * FREQS + FREQS]
                for n in range(3):
                    acc_s[:, (3 * part + n) * FREQS : (3 * part + n + 1) * FREQS] = sums[n]

        def pair_step(pair, inner):
            fold(2 * GROUP * pair, GROUP)
            fold(2 * GROUP * pair + GROUP, GROUP)
            return inner

        def one_step(_, inner):
            fold(pairs * 2 * GROUP, GROUP)
            return inner

        def half_step(_, inner):
            fold(pairs * 2 * GROUP + rest // 2 * GROUP, GROUP // 2)
            return inner

        eights = (jnp.minimum(count - batch * SLOTS, SLOTS) + 7) // 8
        pairs = eights // 4
        rest = eights - 4 * pairs
        lax.fori_loop(0, pairs, pair_step, 0)
        lax.fori_loop(0, rest // 2, one_step, 0)
        lax.fori_loop(0, rest % 2, half_step, 0)

    fold_batch(jnp.int32(0), (place_ref[:, 0:1], ends_ref[:, 0:1], starts_ref[...], gbeam_ref[...]))

    def batch_step(batch, carry):
        own_plan = plan_half(own_ref, core, jnp.zeros((1, 1), F32))
        fold_batch(batch, slots_half((batch * SLOTS).astype(F32), own_plan, own_ref))
        return carry

    lax.fori_loop(1, (count + SLOTS - 1) // SLOTS, batch_step, 0)
    since = acc_s[...]
    each = since - jnp.concatenate([since[1:], jnp.zeros((1, 6 * FREQS), F32)], 0)
    both, real, imag, both2, real2, imag2 = (each[:, k * FREQS : k * FREQS + FREQS] for k in range(6))
    short = dot(jnp.concatenate([both2 - imag2, both2 + real2], 1).astype(BF16), short_ref[...])
    out_ref[0] = (both - imag + short[:, :FREQS]) * SCALE
    out_ref[1] = (both + real + short[:, FREQS:]) * SCALE


def near(*values):
    return [pltpu.with_memory_space_constraint(v, pltpu.VMEM) for v in values]


def call(kernel, outs, values, scratch=(), mib=8, us=1.0):
    one = not isinstance(outs, (tuple, list))
    space = pl.BlockSpec(memory_space=pltpu.VMEM)
    return pl.pallas_call(
        kernel,
        out_shape=outs if one else tuple(outs),
        in_specs=[space] * len(values),
        out_specs=space if one else (space,) * len(outs),
        scratch_shapes=list(scratch),
        compiler_params=pltpu.CompilerParams(vmem_limit_bytes=mib << 20),
        cost_estimate=pl.CostEstimate(flops=int(us * 5e8), bytes_accessed=1 << 20, transcendentals=0),
    )(*near(*values))


HALF_Z = pltpu.VMEM((HALF, 2 * FREQS), BF16)


def make_tables(ids):
    given = tables()
    made = call(
        functools.partial(table_kernel, ids),
        (
            pltpu.VMEM((2 * GRAIN, 4 * FREQS), BF16),
            pltpu.VMEM((2, 2 * GRAIN, 2 * FREQS), BF16),
            pltpu.VMEM((2 * FREQS, 2 * FREQS), BF16),
            pltpu.VMEM((128, 2 * FREQS), BF16),
            pltpu.VMEM((GRAIN, 2 * FREQS), BF16),
        ),
        [given[k] for k in ("base", "turn", "fold2", "start", "back")],
        [pltpu.VMEM((2 * GRAIN, 2 * FREQS), BF16)],
        us=3.0,
    )
    return given, made


def spectrum(own, other, ids, given, made):
    fold, step, short, phases, side = made
    phase = given["phase"]
    half = call(
        functools.partial(half_kernel, ids),
        (
            HALF_Z,
            pltpu.VMEM((8, 128), F32),
            pltpu.VMEM((SLOTS, 128), F32),
            pltpu.VMEM((SLOTS, 128), F32),
            pltpu.VMEM((128, 128), F32),
            pltpu.VMEM((SLOTS, 2 * GRAIN), F32),
        ),
        (own, step, phase),
        us=1.0,
    )
    scratch = [
        HALF_Z,
        pltpu.VMEM((SLOTS, 3 * FREQS), F32),
        pltpu.VMEM((SLOTS, 3 * FREQS), F32),
        pltpu.VMEM((SLOTS, 2 * GRAIN), F32),
        pltpu.VMEM((SLOTS, 2 * GRAIN), F32),
        pltpu.VMEM((SLOTS // GROUP, BINS, 128), F32),
        pltpu.VMEM((BINS, 6 * FREQS), F32),
    ]
    return call(
        functools.partial(spectrum_kernel, ids),
        jax.ShapeDtypeStruct((2, BINS, FREQS), F32),
        (own, other, *half, fold, step, short, phases, side, given["step2"], phase),
        scratch,
        mib=16,
        us=5.0,
    )


def front(voltages, beam_weights, bins):
    far = pl.BlockSpec(memory_space=pltpu.HBM)
    close = pl.BlockSpec(memory_space=pltpu.VMEM)
    return pl.pallas_call(
        front_kernel,
        out_shape=(
            pltpu.VMEM((DISH_WAYS, 2 * PER_BLOCK, GRAIN), F32),
            pltpu.VMEM((CHIPS, VISITS, GRAIN), BF16),
        ),
        in_specs=[far] * 3,
        out_specs=(close, close),
        scratch_shapes=[
            pltpu.VMEM(voltages.shape, BF16),
            pltpu.VMEM(beam_weights.shape, BF16),
            pltpu.VMEM(bins.shape, jnp.int32),
            pltpu.VMEM((72, GRAIN), F32),
            pltpu.VMEM((72, GRAIN), F32),
            pltpu.SemaphoreType.DMA((3,)),
        ],
        compiler_params=pltpu.CompilerParams(vmem_limit_bytes=8 << 20),
        cost_estimate=pl.CostEstimate(flops=1 << 20, bytes_accessed=1 << 20, transcendentals=0),
        name="front",
    )(*(pltpu.with_memory_space_constraint(v, pltpu.HBM) for v in (voltages, beam_weights, bins)))


def steps(voltages, beam_weights, phase_bins):
    def ids():
        core = lax.axis_index("core")
        owner = (lax.axis_index("z") * 2 + lax.axis_index("xh")) * 2 + core
        return owner, lax.axis_index("dish"), core

    given, made = make_tables(ids)
    partial_beam, visits = front(voltages, beam_weights, phase_bins.reshape(PER_BLOCK, GRAIN))
    parts = lax.all_to_all(partial_beam, "dish", 0, 0, tiled=True)
    packed = call(pack_kernel, pltpu.VMEM((CHIPS, ROWS, GRAIN), BF16), (parts, visits), us=0.3)
    own = lax.all_to_all(packed, ("z", "xh"), 0, 0, tiled=True)
    other = lax.ppermute(own, "core", [(0, 1), (1, 0)])
    return jnp.transpose(spectrum(own, other, ids, given, made), (2, 0, 1))


def solution(mesh):
    split = jax.sharding.Mesh(mesh.devices.reshape(8, 2, 2, 8), ("z", "xh", "core", "dish"))
    time = ("z", "xh", "core")
    return jax.shard_map(
        steps,
        mesh=split,
        in_specs=(P(None, "dish", time), P(None, "dish"), P(time)),
        out_specs=P("dish", None, time),
        check_vma=False,
    )
```

```python
import functools
import math

import jax
import jax.numpy as jnp
import numpy as np
from jax import lax
from jax.experimental import pallas as pl
from jax.experimental.pallas import tpu as pltpu
from jax.sharding import PartitionSpec as P


PH = 1024
LAGS = 2048
SAMPLES = 131072
DISH_WAYS = 8
TM_WAYS = 32
CHIPS = 16
HALF = SAMPLES // 2 // 128
LOCAL = SAMPLES // TM_WAYS
GRAIN = 128
PER_BLOCK = LOCAL // GRAIN
SIDE = GRAIN // 2
SPAN = LAGS // GRAIN
BINS = PH // TM_WAYS
FREQS = LAGS // DISH_WAYS
SLOTS = 96
GROUP = 16
VISITS = 8
ROWS = 2 * PER_BLOCK + VISITS
SCALE = 1.0 / math.sqrt(LAGS * SAMPLES / PH)

F32 = jnp.float32
BF16 = jnp.bfloat16


def dot(a, b, dims=(((1,), (0,)), ((), ()))):
    return lax.dot_general(a, b, dims, preferred_element_type=F32)


def hi_lo(value):
    hi = value.astype(BF16)
    return hi, (value - hi.astype(F32)).astype(BF16)


def tables():
    grain = np.arange(GRAIN)
    freq = np.arange(FREQS)
    angle = 2 * np.pi * np.outer(grain, freq) / LAGS
    base = np.concatenate([np.cos(angle), np.sin(angle)], 1).astype(np.float32)
    eighth = 2 * np.pi * np.outer(grain, np.arange(DISH_WAYS)) / DISH_WAYS
    turn = np.zeros((GRAIN, 128), np.float32)
    turn[:, :8] = np.cos(eighth)
    turn[:, 8:16] = np.sin(eighth)
    fine = 2 * np.pi * np.outer(grain, np.arange(2 * GRAIN)) / (2 * GRAIN)
    cos2, sin2 = np.cos(fine), np.sin(fine)
    fold2 = np.block([[cos2, sin2], [sin2, -cos2]]).astype(np.float32)
    step2 = np.block([[cos2, -sin2], [sin2, cos2]]).astype(np.float32)
    sides = np.concatenate([np.arange(k, k + SIDE) for k in (0, GRAIN, SIDE, GRAIN + SIDE)])
    fold2, step2 = fold2[sides], step2[sides]
    keep = (grain >= 1)[None, :] / (2.0 * GRAIN)
    back = np.block([[cos2.T * keep, -sin2.T * keep], [sin2.T * keep, cos2.T * keep]])
    sixteenth = 2 * np.pi * np.outer(np.arange(SPAN), freq) / SPAN
    phase = np.concatenate([np.cos(sixteenth), np.sin(sixteenth)], 1).astype(np.float32)
    fine = np.pi * np.outer(np.arange(2 * SPAN), freq) / SPAN
    start = np.concatenate([np.cos(fine), np.sin(fine)], 1).astype(np.float32)
    return {
        "base": jnp.asarray(base),
        "turn": jnp.asarray(turn),
        "fold2": jnp.asarray(fold2).astype(BF16),
        "step2": jnp.asarray(step2).astype(BF16),
        "back": jnp.asarray(back.astype(np.float32)).astype(BF16),
        "phase": jnp.asarray(phase),
        "start": jnp.asarray(start),
    }


PIECES = [slice(k % 4 * (LOCAL // 4), k % 4 * (LOCAL // 4) + LOCAL // 4) for k in range(8)]


def front_kernel(
    volts_hbm, weights_hbm, bins_hbm, beam_ref, visit_ref, volts_s, weights_s, bins_s, time_s, row_s, sems
):
    parts = [(volts_hbm.at[k // 4, :, at], volts_s.at[k // 4, :, at]) for k, at in enumerate(PIECES)]
    parts += [(bins_hbm, bins_s), (weights_hbm, weights_s)]
    copies = [
        pltpu.make_async_copy(source, target, sems.at[k]) for k, (source, target) in enumerate(parts)
    ]
    for copy in copies:
        copy.start()
    for copy in copies:
        copy.wait()
    weights = weights_s[...]
    first = dot(weights, volts_s[0])
    second = dot(weights, volts_s[1])
    real = first[0:1] - second[1:2]
    imag = first[1:2] + second[0:1]
    for row in range(PER_BLOCK):
        part = slice(row * GRAIN, (row + 1) * GRAIN)
        beam_ref[0, row : row + 1, :] = real[:, part]
        beam_ref[0, PER_BLOCK + row : PER_BLOCK + row + 1, :] = imag[:, part]
    make_visits(bins_s, visit_ref, time_s, row_s)
    rows = beam_ref[0]
    for way in range(1, DISH_WAYS):
        beam_ref[way] = rows


def pack_kernel(parts_ref, visit_ref, out_ref):
    total = parts_ref[0]
    for way in range(1, DISH_WAYS):
        total = total + parts_ref[way]
    real, imag = total[:PER_BLOCK], total[PER_BLOCK:]
    early = lax.broadcasted_iota(jnp.int32, (PER_BLOCK, GRAIN), 1) < SIDE
    early_side = jnp.where(early, real, pltpu.roll(imag, SIDE, 1))
    late_side = jnp.where(early, pltpu.roll(real, SIDE, 1), imag)
    rows = jnp.concatenate([early_side, late_side], 0).astype(BF16)
    for chip in range(CHIPS):
        out_ref[chip, : 2 * PER_BLOCK, :] = rows
        out_ref[chip, 2 * PER_BLOCK :, :] = visit_ref[chip]


def coded_times(shape):
    row = lax.broadcasted_iota(jnp.int32, shape, 0)
    lane = lax.broadcasted_iota(jnp.int32, shape, 1)
    return (lane + 128).astype(F32) * two_to(row)


def triangle(count, strict):
    row = lax.broadcasted_iota(jnp.int32, (count, count), 0)
    column = lax.broadcasted_iota(jnp.int32, (count, count), 1)
    return jnp.where(row < column if strict else row <= column, 1.0, 0.0).astype(BF16)


def make_visits(bins_ref, out_ref, time_s, row_s):
    bins = bins_ref[...]
    shape = (PER_BLOCK, GRAIN)
    row = lax.broadcasted_iota(jnp.int32, shape, 0)
    lane = lax.broadcasted_iota(jnp.int32, shape, 1)
    rolled = pltpu.roll(bins, 1, 1)
    before = jnp.where(lane == 0, pltpu.roll(rolled, 1, 0), rolled)
    later = row + lane > 0
    enters = later & (bins != before)
    wraps = jnp.where(later & (bins < before), 1.0, 0.0).astype(BF16)
    in_row = dot(wraps, triangle(GRAIN, False))
    ends = jnp.broadcast_to(in_row[:, GRAIN - 1 :], shape).astype(BF16)
    above = dot(triangle(PER_BLOCK, True), ends, (((0,), (0,)), ((), ())))
    step = bins + PH * (in_row + above).astype(jnp.int32)
    high = jnp.where(enters, step >> 7, -1).astype(F32)
    low = (step & 127).astype(F32)
    times = coded_times(shape)
    high_iota = lax.broadcasted_iota(jnp.int32, (48, GRAIN), 0)
    high_rows = high_iota.astype(F32).astype(BF16)
    low_rows = lax.broadcasted_iota(jnp.int32, (GRAIN, GRAIN), 0).astype(F32).astype(BF16)
    zero, one = jnp.zeros((), BF16), jnp.ones((), BF16)
    late = jnp.where(lax.broadcasted_iota(jnp.int32, (48, GRAIN), 1) >= SIDE, 1.0, 0.0).astype(BF16)

    def spread(value, k, count):
        tile = jnp.broadcast_to(value[k : k + 1, :], (16, GRAIN)).astype(BF16)
        return jnp.concatenate([tile] * (count // 16), 0)

    found = jnp.zeros((96, GRAIN), F32)
    for pair in range(PER_BLOCK // 2):
        left, right = [], []
        for k in (2 * pair, 2 * pair + 1):
            here = spread(high, k, 48) == high_rows
            coded = jnp.where(here, spread(times, k, 48), zero)
            left.append(jnp.concatenate([coded, jnp.where(here, late + jnp.full((), 2 * k, BF16), zero)], 0))
            right.append(jnp.where(spread(low, k, GRAIN) == low_rows, one, zero))
        left = jnp.concatenate(left, 1)
        right = jnp.concatenate(right, 1)
        found = found + dot(left, right, (((1,), (1,)), ((), ())))
    place = high_iota * GRAIN + lax.broadcasted_iota(jnp.int32, (48, GRAIN), 1)
    past, ahead = place <= step[0:1, 0:1], place > step[PER_BLOCK - 1 :, GRAIN - 1 :]
    time_s[:48, :] = jnp.where(past, 2.0**-9, jnp.where(ahead, 2.0**23, found[:48]))
    row_s[:48, :] = jnp.where(past, 0.0, jnp.where(ahead, 64.0, found[48:]))
    time_s[48:, :] = jnp.full((24, GRAIN), 2.0**23, F32)
    row_s[48:, :] = jnp.full((24, GRAIN), 64.0, F32)
    lane = lax.broadcasted_iota(jnp.int32, (VISITS, GRAIN), 1)
    for eighth in range(8):
        now, then = pl.ds(eighth, VISITS, stride=8), pl.ds(eighth + 1, VISITS, stride=8)
        time, rows = time_s[now, :], row_s[now, :]
        next_time, next_rows = time_s[then, :], row_s[then, :]
        even = jnp.where(lane == 65, pltpu.roll(rows, 65, 1), time)
        even = jnp.where(lane == 66, pltpu.roll(rows, 34, 1), even)
        even = jnp.where(lane == 67, pltpu.roll(rows, 3, 1), even)
        odd = jnp.where(lane == 64, pltpu.roll(next_time, 64, 1), pltpu.roll(time, 64, 1))
        odd = jnp.where(lane == 65, pltpu.roll(rows, 1, 1), odd)
        odd = jnp.where(lane == 66, pltpu.roll(rows, 98, 1), odd)
        odd = jnp.where(lane == 67, pltpu.roll(next_rows, 67, 1), odd)
        out_ref[2 * eighth] = even.astype(BF16)
        out_ref[2 * eighth + 1] = odd.astype(BF16)


def two_to(exponent):
    value = jnp.full(jnp.shape(exponent), 2.0**-16, F32)
    for bit in range(6):
        value = value * jnp.where((exponent >> bit) & 1 == 1, float(2 ** (2**bit)), 1.0)
    return value


def table_kernel(
    ids, base_ref, turn_ref, fold2_ref, start_ref, back_ref, fold_ref, step_ref, short_ref, phases_ref, side_ref, last_s
):
    _, dish, _ = ids()
    lane = lax.broadcasted_iota(jnp.int32, (GRAIN, 128), 1)
    turn = turn_ref[...]
    cos8 = jnp.sum(jnp.where(lane == dish, turn, 0.0), axis=1, keepdims=True)
    sin8 = jnp.sum(jnp.where(lane == dish + 8, turn, 0.0), axis=1, keepdims=True)
    cos0, sin0 = base_ref[:, :FREQS], base_ref[:, FREQS:]
    cos_f, sin_f = cos0 * cos8 - sin0 * sin8, sin0 * cos8 + cos0 * sin8
    cosine, cosine_lo = hi_lo(cos_f)
    sine, sine_lo = hi_lo(sin_f)
    for side in range(2):
        part = slice(side * SIDE, side * SIDE + SIDE)
        reals = slice(side * GRAIN, side * GRAIN + SIDE)
        imags = slice(side * GRAIN + SIDE, side * GRAIN + GRAIN)
        fold_ref[reals, :FREQS] = cosine[part]
        fold_ref[reals, FREQS : 2 * FREQS] = sine[part]
        fold_ref[imags, :FREQS] = sine[part]
        fold_ref[imags, FREQS : 2 * FREQS] = -cosine[part]
        for k, (c, s) in enumerate(((cosine, sine), (cosine_lo, sine_lo))):
            step_ref[k, reals, :FREQS] = c[part]
            step_ref[k, reals, FREQS:] = -s[part]
            step_ref[k, imags, :FREQS] = s[part]
            step_ref[k, imags, FREQS:] = c[part]
    fold_ref[:, 2 * FREQS :] = fold2_ref[...]
    cos_side, sin_side = cos_f[SIDE : SIDE + 1], sin_f[SIDE : SIDE + 1]
    side_real = cos_f[:SIDE] * cos_side + sin_f[:SIDE] * sin_side
    side_imag = cos_f[:SIDE] * sin_side - sin_f[:SIDE] * cos_side
    side_ref[:SIDE, :FREQS] = side_real.astype(BF16)
    side_ref[:SIDE, FREQS:] = side_imag.astype(BF16)
    side_ref[SIDE:, :FREQS] = -side_imag.astype(BF16)
    side_ref[SIDE:, FREQS:] = side_real.astype(BF16)
    last_s[:GRAIN, :FREQS] = cosine
    last_s[:GRAIN, FREQS:] = sine
    last_s[GRAIN:, :FREQS] = -sine
    last_s[GRAIN:, FREQS:] = cosine
    short_ref[...] = dot(back_ref[...], last_s[...]).astype(BF16)
    phases_ref[...] = jnp.zeros(phases_ref.shape, BF16)
    hi, lo = hi_lo(start_ref[...])
    phases_ref[: 2 * SPAN, :] = hi
    phases_ref[2 * SPAN : 4 * SPAN, :] = lo


def beam_rows(ref, first, last):
    rows = [
        jnp.concatenate([ref[chip, :PER_BLOCK, :], ref[chip, PER_BLOCK : 2 * PER_BLOCK, :]], 1)
        for chip in range(first, last)
    ]
    return jnp.concatenate(rows, 0)


def side_rows(ref, side):
    part = slice(side * PER_BLOCK, side * PER_BLOCK + PER_BLOCK)
    return jnp.concatenate([ref[chip, part, :] for chip in range(CHIPS)], 0)


def swap_sides(odd, early, late):
    return jnp.concatenate([jnp.where(odd > 0.0, late, early), jnp.where(odd > 0.0, early, late)], 1)


def transform(ref, step_ref, phase_ref, z_ref, fine):
    cos16, sin16 = phase_ref[:, :FREQS], phase_ref[:, FREQS:]
    cos_rows = jnp.concatenate([cos16] * (128 // SPAN), 0)
    sin_rows = jnp.concatenate([sin16] * (128 // SPAN), 0)
    for tile in range(HALF // 128):
        rows = slice(tile * 128, tile * 128 + 128)
        beam = beam_rows(ref, 4 * tile, 4 * tile + 4)
        both = dot(beam, step_ref[0])
        if fine:
            both = both + dot(beam, step_ref[1])
        real, imag = both[:, :FREQS], both[:, FREQS:]
        z_ref[rows, :FREQS] = (real * cos_rows + imag * sin_rows).astype(BF16)
        z_ref[rows, FREQS:] = (imag * cos_rows - real * sin_rows).astype(BF16)


def plan_half(ref, core, before):
    times = jnp.concatenate([ref[chip, 2 * PER_BLOCK :, :].astype(F32) for chip in range(CHIPS)], 0).astype(BF16)
    row = lax.broadcasted_iota(jnp.int32, (8, 128), 0)
    lane = lax.broadcasted_iota(jnp.int32, (8, 128), 1)
    wanted = jnp.where(row == 0, BINS * core, jnp.where(row == 1, BINS * core + BINS, core + 63 + row))
    info = dot(jnp.where(lane == wanted, 1.0, 0.0).astype(BF16), times, (((1,), (1,)), ((), ())))
    start, end, first, last = (info[k : k + 1, :] for k in range(4))
    sides = jnp.minimum(last, float(2 * PER_BLOCK - 1)) - first
    grains = jnp.where(end > start, jnp.floor(sides * 0.5) + 1.0, 0.0)
    earlier = dot(jnp.broadcast_to(grains, (8, 128)).astype(BF16), triangle(128, True))[0:1, :] + before
    return times, end, first, grains, earlier, earlier[:, 127:] + grains[:, 127:]


def slots_half(slot_0, plan, ref):
    times, end, first, grains, earlier, _ = plan
    slot = lax.broadcasted_iota(jnp.int32, (128, 128), 0).astype(F32) + slot_0
    visit = lax.broadcasted_iota(jnp.int32, (SLOTS, 128), 1)
    mine = (slot >= earlier) & (slot < earlier + grains)
    starts = dot(times, jnp.where(mine, 1.0, 0.0).astype(BF16), (((0,), (1,)), ((), ())))
    slot, mine = slot[:SLOTS], mine[:SLOTS]
    place = ((visit >> 3) * (2 * PER_BLOCK) + 1).astype(F32) + first + 2.0 * (slot - earlier)
    place = jnp.sum(jnp.where(mine, place, 0.0), axis=1, keepdims=True) - 1.0
    ends = jnp.sum(jnp.where(mine, jnp.broadcast_to(end, (SLOTS, 128)), 0.0), axis=1, keepdims=True)
    places = lax.broadcasted_iota(jnp.int32, (SLOTS, HALF), 1).astype(F32)
    whole = jnp.where(place < 0.0, -4.0, jnp.floor(place * 0.5))
    odd = jnp.where(place < 0.0, 0.0, place - 2.0 * whole)
    early = dot(jnp.where(places == whole + odd, 1.0, 0.0).astype(BF16), side_rows(ref, 0))
    late = dot(jnp.where(places == whole, 1.0, 0.0).astype(BF16), side_rows(ref, 1))
    return place, ends, starts, swap_sides(odd, early, late)


def half_kernel(ids, own_ref, step_ref, phase_ref, z_ref, total_ref, place_ref, ends_ref, starts_ref, gbeam_ref):
    _, _, core = ids()
    plan = plan_half(own_ref, core, jnp.zeros((1, 1), F32))
    place, ends, starts, beam = slots_half(jnp.float32(0.0), plan, own_ref)
    total_ref[...] = jnp.broadcast_to(plan[-1], (8, 128))
    place_ref[...] = jnp.broadcast_to(place, (SLOTS, 128))
    ends_ref[...] = jnp.broadcast_to(ends, (SLOTS, 128))
    starts_ref[...] = starts
    gbeam_ref[...] = beam
    transform(own_ref, step_ref, phase_ref, z_ref, True)


def grain_row(which):
    place = lax.broadcasted_iota(jnp.int32, (8, HALF), 1)
    grain = (2 * (place >> 5) + which) * PER_BLOCK + (place & (PER_BLOCK - 1))
    return grain.astype(F32)[0:1, :]


def spectrum_kernel(
    ids,
    own_ref, other_ref, z_ref, total_ref, place_ref, ends_ref, starts_ref, gbeam_ref,
    fold_ref, step_ref, short_ref, phases_ref, side_ref, step2_ref, phase_ref,
    out_ref,
    z_s, gdft_s, gstep_s, gbeam_s, gtime_s, gstart_s, acc_s,
):
    _, _, core = ids()
    before = total_ref[0:1, 0:1]
    other_plan = plan_half(other_ref, core, before)
    count = jnp.max(other_plan[-1]).astype(jnp.int32)
    transform(other_ref, step_ref, phase_ref, z_s, False)
    acc_s[...] = jnp.zeros(acc_s.shape, F32)
    own_grains = jnp.broadcast_to(grain_row(core), (SLOTS, HALF))
    other_grains = jnp.broadcast_to(grain_row(1 - core), (SLOTS, HALF))
    lane_iota = lax.broadcasted_iota(jnp.int32, (SLOTS, 128), 1)

    def fold_batch(batch, mine):
        first = (batch * SLOTS).astype(F32)
        more = slots_half(first, other_plan, other_ref)
        is_mine = mine[0] >= 0.0
        place = jnp.where(is_mine, mine[0], more[0]).astype(jnp.int32)
        which = jnp.where(is_mine, core, 1 - core)
        side = place & (2 * PER_BLOCK - 1)
        in_block, odd = side >> 1, (side & 1).astype(F32)
        grain = ((2 * (place >> 6) + which) * PER_BLOCK + in_block).astype(F32)
        here = mine[3] + more[3]
        ends = mine[1] + more[1]
        for k in range(2):
            at = jnp.broadcast_to(side + k, (SLOTS, GRAIN))
            times = (128 + (at & 1) * SIDE + (lane_iota & (SIDE - 1))).astype(F32) * two_to(at >> 1)
            part = slice(k * GRAIN, k * GRAIN + GRAIN)
            gtime_s[:, part] = times
            gbeam_s[:, part] = jnp.where(times < ends, here[:, part], 0.0)
        starts = mine[2] + more[2]
        starts = jnp.where(core == 0, starts[:BINS], starts[BINS : 2 * BINS])
        for group in range(SLOTS // GROUP):
            gstart_s[group] = starts if group == 0 else pltpu.roll(starts, 128 - group * GROUP, 1)
        dft = jnp.zeros((SLOTS, 2 * FREQS), F32)
        early, late, gone = (jnp.zeros((SLOTS, GRAIN), F32) for _ in range(3))
        for grains, z, ref in ((own_grains, z_ref, own_ref), (other_grains, z_s, other_ref)):
            window = (grains >= grain) & (grains < grain + float(SPAN))
            dft = dft + dot(jnp.where(window, 1.0, 0.0).astype(BF16), z[...])
            then = grains == grain + float(SPAN)
            early_pick = jnp.where(grains == grain + float(SPAN) + odd, 1.0, 0.0).astype(BF16)
            late_pick = jnp.where(then, 1.0, 0.0).astype(BF16)
            gone_pick = jnp.where(then, odd, jnp.where(grains == grain, -odd, 0.0)).astype(BF16)
            early = early + dot(early_pick, side_rows(ref, 0))
            late = late + dot(late_pick, side_rows(ref, 1))
            gone = gone + dot(gone_pick, side_rows(ref, 0))
        ahead = swap_sides(odd, early, late)
        moved = dot(gone.astype(BF16), side_ref[...])
        offset = side & (2 * SPAN - 1)
        turner = jnp.where((lane_iota == offset) | (lane_iota == offset + 2 * SPAN), 1.0, 0.0)
        turned = dot(turner.astype(BF16), phases_ref[...])
        real, imag = dft[:, :FREQS], dft[:, FREQS:]
        cos_g, sin_g = turned[:, :FREQS], turned[:, FREQS:]
        step = dot((ahead - here).astype(BF16), step2_ref[...])
        for ref, real, imag in (
            (gdft_s, real * cos_g - imag * sin_g + moved[:, :FREQS], imag * cos_g + real * sin_g + moved[:, FREQS:]),
            (gstep_s, step[:, :FREQS], step[:, FREQS:]),
        ):
            ref[:, :FREQS] = real
            ref[:, FREQS : 2 * FREQS] = imag - real
            ref[:, 2 * FREQS :] = real + imag

        def fold(slot, size):
            rows = pl.ds(pl.multiple_of(slot, 8), size)
            beam8, time8, start8 = gbeam_s[rows, :], gtime_s[rows, :], gstart_s[slot // GROUP]
            dft8, step8 = gdft_s[rows, :], gstep_s[rows, :]
            left = []
            for k in range(size):
                start = start8[:, k : k + 1]
                sides = [
                    jnp.where(time8[k : k + 1, at : at + GRAIN] >= start, beam8[k : k + 1, at : at + GRAIN], 0.0)
                    for at in (0, GRAIN)
                ]
                left.append(jnp.concatenate(sides, 1))
            left = jnp.concatenate(left, 0).astype(BF16)
            for part, factor in ((0, dft8), (1, step8)):
                folded = dot(left, fold_ref[:, part * 2 * FREQS : part * 2 * FREQS + 2 * FREQS])
                sums = [acc_s[:, k * FREQS : k * FREQS + FREQS] for k in range(3 * part, 3 * part + 3)]
                for k in range(size):
                    rows = slice(k * BINS, k * BINS + BINS)
                    real, imag = folded[rows, :FREQS], folded[rows, FREQS:]
                    for n, value in enumerate((real + imag, real, imag)):
                        sums[n] = sums[n] + value * factor[k : k + 1, n * FREQS : n * FREQS + FREQS]
                for n in range(3):
                    acc_s[:, (3 * part + n) * FREQS : (3 * part + n + 1) * FREQS] = sums[n]

        def pair_step(pair, inner):
            fold(2 * GROUP * pair, GROUP)
            fold(2 * GROUP * pair + GROUP, GROUP)
            return inner

        def one_step(_, inner):
            fold(pairs * 2 * GROUP, GROUP)
            return inner

        def half_step(_, inner):
            fold(pairs * 2 * GROUP + rest // 2 * GROUP, GROUP // 2)
            return inner

        eights = (jnp.minimum(count - batch * SLOTS, SLOTS) + 7) // 8
        pairs = eights // 4
        rest = eights - 4 * pairs
        lax.fori_loop(0, pairs, pair_step, 0)
        lax.fori_loop(0, rest // 2, one_step, 0)
        lax.fori_loop(0, rest % 2, half_step, 0)

    fold_batch(jnp.int32(0), (place_ref[:, 0:1], ends_ref[:, 0:1], starts_ref[...], gbeam_ref[...]))

    def batch_step(batch, carry):
        own_plan = plan_half(own_ref, core, jnp.zeros((1, 1), F32))
        fold_batch(batch, slots_half((batch * SLOTS).astype(F32), own_plan, own_ref))
        return carry

    lax.fori_loop(1, (count + SLOTS - 1) // SLOTS, batch_step, 0)
    since = acc_s[...]
    each = since - jnp.concatenate([since[1:], jnp.zeros((1, 6 * FREQS), F32)], 0)
    both, real, imag, both2, real2, imag2 = (each[:, k * FREQS : k * FREQS + FREQS] for k in range(6))
    short = dot(jnp.concatenate([both2 - imag2, both2 + real2], 1).astype(BF16), short_ref[...])
    out_ref[0] = (both - imag + short[:, :FREQS]) * SCALE
    out_ref[1] = (both + real + short[:, FREQS:]) * SCALE


def near(*values):
    return [pltpu.with_memory_space_constraint(v, pltpu.VMEM) for v in values]


def call(kernel, outs, values, scratch=(), mib=8, us=1.0):
    one = not isinstance(outs, (tuple, list))
    space = pl.BlockSpec(memory_space=pltpu.VMEM)
    return pl.pallas_call(
        kernel,
        out_shape=outs if one else tuple(outs),
        in_specs=[space] * len(values),
        out_specs=space if one else (space,) * len(outs),
        scratch_shapes=list(scratch),
        compiler_params=pltpu.CompilerParams(vmem_limit_bytes=mib << 20),
        cost_estimate=pl.CostEstimate(flops=int(us * 5e8), bytes_accessed=1 << 20, transcendentals=0),
    )(*near(*values))


HALF_Z = pltpu.VMEM((HALF, 2 * FREQS), BF16)


def make_tables(ids):
    given = tables()
    made = call(
        functools.partial(table_kernel, ids),
        (
            pltpu.VMEM((2 * GRAIN, 4 * FREQS), BF16),
            pltpu.VMEM((2, 2 * GRAIN, 2 * FREQS), BF16),
            pltpu.VMEM((2 * FREQS, 2 * FREQS), BF16),
            pltpu.VMEM((128, 2 * FREQS), BF16),
            pltpu.VMEM((GRAIN, 2 * FREQS), BF16),
        ),
        [given[k] for k in ("base", "turn", "fold2", "start", "back")],
        [pltpu.VMEM((2 * GRAIN, 2 * FREQS), BF16)],
        us=3.0,
    )
    return given, made


def spectrum(own, other, ids, given, made):
    fold, step, short, phases, side = made
    phase = given["phase"]
    half = call(
        functools.partial(half_kernel, ids),
        (
            HALF_Z,
            pltpu.VMEM((8, 128), F32),
            pltpu.VMEM((SLOTS, 128), F32),
            pltpu.VMEM((SLOTS, 128), F32),
            pltpu.VMEM((128, 128), F32),
            pltpu.VMEM((SLOTS, 2 * GRAIN), F32),
        ),
        (own, step, phase),
        us=1.0,
    )
    scratch = [
        HALF_Z,
        pltpu.VMEM((SLOTS, 3 * FREQS), F32),
        pltpu.VMEM((SLOTS, 3 * FREQS), F32),
        pltpu.VMEM((SLOTS, 2 * GRAIN), F32),
        pltpu.VMEM((SLOTS, 2 * GRAIN), F32),
        pltpu.VMEM((SLOTS // GROUP, BINS, 128), F32),
        pltpu.VMEM((BINS, 6 * FREQS), F32),
    ]
    return call(
        functools.partial(spectrum_kernel, ids),
        jax.ShapeDtypeStruct((2, BINS, FREQS), F32),
        (own, other, *half, fold, step, short, phases, side, given["step2"], phase),
        scratch,
        mib=16,
        us=5.0,
    )


def front(voltages, beam_weights, bins):
    far = pl.BlockSpec(memory_space=pltpu.HBM)
    close = pl.BlockSpec(memory_space=pltpu.VMEM)
    return pl.pallas_call(
        front_kernel,
        out_shape=(
            pltpu.VMEM((DISH_WAYS, 2 * PER_BLOCK, GRAIN), F32),
            pltpu.VMEM((CHIPS, VISITS, GRAIN), BF16),
        ),
        in_specs=[far] * 3,
        out_specs=(close, close),
        scratch_shapes=[
            pltpu.VMEM(voltages.shape, BF16),
            pltpu.VMEM(beam_weights.shape, BF16),
            pltpu.VMEM(bins.shape, jnp.int32),
            pltpu.VMEM((72, GRAIN), F32),
            pltpu.VMEM((72, GRAIN), F32),
            pltpu.SemaphoreType.DMA((len(PIECES) + 2,)),
        ],
        compiler_params=pltpu.CompilerParams(vmem_limit_bytes=8 << 20),
        cost_estimate=pl.CostEstimate(flops=1 << 20, bytes_accessed=1 << 20, transcendentals=0),
        name="front",
    )(*(pltpu.with_memory_space_constraint(v, pltpu.HBM) for v in (voltages, beam_weights, bins)))


def steps(voltages, beam_weights, phase_bins):
    def ids():
        core = lax.axis_index("core")
        owner = (lax.axis_index("z") * 2 + lax.axis_index("xh")) * 2 + core
        return owner, lax.axis_index("dish"), core

    given, made = make_tables(ids)
    partial_beam, visits = front(voltages, beam_weights, phase_bins.reshape(PER_BLOCK, GRAIN))
    parts = lax.all_to_all(partial_beam, "dish", 0, 0, tiled=True)
    packed = call(pack_kernel, pltpu.VMEM((CHIPS, ROWS, GRAIN), BF16), (parts, visits), us=0.3)
    own = lax.all_to_all(packed, ("z", "xh"), 0, 0, tiled=True)
    other = lax.ppermute(own, "core", [(0, 1), (1, 0)])
    return jnp.transpose(spectrum(own, other, ids, given, made), (2, 0, 1))


def solution(mesh):
    split = jax.sharding.Mesh(mesh.devices.reshape(8, 2, 2, 8), ("z", "xh", "core", "dish"))
    time = ("z", "xh", "core")
    return jax.shard_map(
        steps,
        mesh=split,
        in_specs=(P(None, "dish", time), P(None, "dish"), P(time)),
        out_specs=P("dish", None, time),
        check_vma=False,
    )
```

```python
import functools
import math

import jax
import jax.numpy as jnp
import numpy as np
from jax import lax
from jax.experimental import pallas as pl
from jax.experimental.pallas import tpu as pltpu
from jax.sharding import PartitionSpec as P


PH = 1024
LAGS = 2048
SAMPLES = 131072
DISH_WAYS = 8
TM_WAYS = 32
CHIPS = 16
HALF = SAMPLES // 2 // 128
LOCAL = SAMPLES // TM_WAYS
GRAIN = 128
PER_BLOCK = LOCAL // GRAIN
SIDE = GRAIN // 2
SPAN = LAGS // GRAIN
BINS = PH // TM_WAYS
FREQS = LAGS // DISH_WAYS
SLOTS = 96
GROUP = 16
VISITS = 8
ROWS = 2 * PER_BLOCK + VISITS
SCALE = 1.0 / math.sqrt(LAGS * SAMPLES / PH)

F32 = jnp.float32
BF16 = jnp.bfloat16


def dot(a, b, dims=(((1,), (0,)), ((), ()))):
    return lax.dot_general(a, b, dims, preferred_element_type=F32)


def hi_lo(value):
    hi = value.astype(BF16)
    return hi, (value - hi.astype(F32)).astype(BF16)


def tables():
    grain = np.arange(GRAIN)
    freq = np.arange(FREQS)
    angle = 2 * np.pi * np.outer(grain, freq) / LAGS
    base = np.concatenate([np.cos(angle), np.sin(angle)], 1).astype(np.float32)
    eighth = 2 * np.pi * np.outer(grain, np.arange(DISH_WAYS)) / DISH_WAYS
    turn = np.zeros((GRAIN, 128), np.float32)
    turn[:, :8] = np.cos(eighth)
    turn[:, 8:16] = np.sin(eighth)
    fine = 2 * np.pi * np.outer(grain, np.arange(2 * GRAIN)) / (2 * GRAIN)
    cos2, sin2 = np.cos(fine), np.sin(fine)
    fold2 = np.block([[cos2, sin2], [sin2, -cos2]]).astype(np.float32)
    step2 = np.block([[cos2, -sin2], [sin2, cos2]]).astype(np.float32)
    sides = np.concatenate([np.arange(k, k + SIDE) for k in (0, GRAIN, SIDE, GRAIN + SIDE)])
    fold2, step2 = fold2[sides], step2[sides]
    keep = (grain >= 1)[None, :] / (2.0 * GRAIN)
    back = np.block([[cos2.T * keep, -sin2.T * keep], [sin2.T * keep, cos2.T * keep]])
    sixteenth = 2 * np.pi * np.outer(np.arange(SPAN), freq) / SPAN
    phase = np.concatenate([np.cos(sixteenth), np.sin(sixteenth)], 1).astype(np.float32)
    fine = np.pi * np.outer(np.arange(2 * SPAN), freq) / SPAN
    start = np.concatenate([np.cos(fine), np.sin(fine)], 1).astype(np.float32)
    return {
        "base": jnp.asarray(base),
        "turn": jnp.asarray(turn),
        "fold2": jnp.asarray(fold2).astype(BF16),
        "step2": jnp.asarray(step2).astype(BF16),
        "back": jnp.asarray(back.astype(np.float32)).astype(BF16),
        "phase": jnp.asarray(phase),
        "start": jnp.asarray(start),
    }


PIECES = [slice(k % 4 * (LOCAL // 4), k % 4 * (LOCAL // 4) + LOCAL // 4) for k in range(8)]


def front_kernel(
    volts_hbm, weights_hbm, bins_hbm, beam_ref, visit_ref, volts_s, weights_s, bins_s, time_s, row_s, sems
):
    parts = [(volts_hbm.at[k // 4, :, at], volts_s.at[k // 4, :, at]) for k, at in enumerate(PIECES)]
    parts += [(bins_hbm, bins_s), (weights_hbm, weights_s)]
    copies = [
        pltpu.make_async_copy(source, target, sems.at[k]) for k, (source, target) in enumerate(parts)
    ]
    for copy in copies:
        copy.start()
    for copy in copies:
        copy.wait()
    weights = weights_s[...]
    first = dot(weights, volts_s[0])
    second = dot(weights, volts_s[1])
    real = first[0:1] - second[1:2]
    imag = first[1:2] + second[0:1]
    for row in range(PER_BLOCK):
        part = slice(row * GRAIN, (row + 1) * GRAIN)
        beam_ref[0, row : row + 1, :] = real[:, part]
        beam_ref[0, PER_BLOCK + row : PER_BLOCK + row + 1, :] = imag[:, part]
    make_visits(bins_s, visit_ref, time_s, row_s)
    rows = beam_ref[0]
    for way in range(1, DISH_WAYS):
        beam_ref[way] = rows


def pack_kernel(parts_ref, visit_ref, out_ref):
    total = parts_ref[0]
    for way in range(1, DISH_WAYS):
        total = total + parts_ref[way]
    real, imag = total[:PER_BLOCK], total[PER_BLOCK:]
    early = lax.broadcasted_iota(jnp.int32, (PER_BLOCK, GRAIN), 1) < SIDE
    early_side = jnp.where(early, real, pltpu.roll(imag, SIDE, 1))
    late_side = jnp.where(early, pltpu.roll(real, SIDE, 1), imag)
    rows = jnp.concatenate([early_side, late_side], 0).astype(BF16)
    for chip in range(CHIPS):
        out_ref[chip, : 2 * PER_BLOCK, :] = rows
        out_ref[chip, 2 * PER_BLOCK :, :] = visit_ref[chip]


def coded_times(shape):
    row = lax.broadcasted_iota(jnp.int32, shape, 0)
    lane = lax.broadcasted_iota(jnp.int32, shape, 1)
    return (lane + 128).astype(F32) * two_to(row)


def triangle(count, strict):
    row = lax.broadcasted_iota(jnp.int32, (count, count), 0)
    column = lax.broadcasted_iota(jnp.int32, (count, count), 1)
    return jnp.where(row < column if strict else row <= column, 1.0, 0.0).astype(BF16)


def make_visits(bins_ref, out_ref, time_s, row_s):
    bins = bins_ref[...]
    shape = (PER_BLOCK, GRAIN)
    row = lax.broadcasted_iota(jnp.int32, shape, 0)
    lane = lax.broadcasted_iota(jnp.int32, shape, 1)
    rolled = pltpu.roll(bins, 1, 1)
    before = jnp.where(lane == 0, pltpu.roll(rolled, 1, 0), rolled)
    later = row + lane > 0
    enters = later & (bins != before)
    wraps = jnp.where(later & (bins < before), 1.0, 0.0).astype(BF16)
    in_row = dot(wraps, triangle(GRAIN, False))
    ends = jnp.broadcast_to(in_row[:, GRAIN - 1 :], shape).astype(BF16)
    above = dot(triangle(PER_BLOCK, True), ends, (((0,), (0,)), ((), ())))
    step = bins + PH * (in_row + above).astype(jnp.int32)
    high = jnp.where(enters, step >> 7, -1).astype(F32)
    low = (step & 127).astype(F32)
    times = coded_times(shape)
    high_iota = lax.broadcasted_iota(jnp.int32, (48, GRAIN), 0)
    high_rows = high_iota.astype(F32).astype(BF16)
    low_rows = lax.broadcasted_iota(jnp.int32, (GRAIN, GRAIN), 0).astype(F32).astype(BF16)
    zero, one = jnp.zeros((), BF16), jnp.ones((), BF16)
    late = jnp.where(lax.broadcasted_iota(jnp.int32, (48, GRAIN), 1) >= SIDE, 1.0, 0.0).astype(BF16)

    def spread(value, k, count):
        tile = jnp.broadcast_to(value[k : k + 1, :], (16, GRAIN)).astype(BF16)
        return jnp.concatenate([tile] * (count // 16), 0)

    found = jnp.zeros((96, GRAIN), F32)
    for pair in range(PER_BLOCK // 2):
        left, right = [], []
        for k in (2 * pair, 2 * pair + 1):
            here = spread(high, k, 48) == high_rows
            coded = jnp.where(here, spread(times, k, 48), zero)
            left.append(jnp.concatenate([coded, jnp.where(here, late + jnp.full((), 2 * k, BF16), zero)], 0))
            right.append(jnp.where(spread(low, k, GRAIN) == low_rows, one, zero))
        left = jnp.concatenate(left, 1)
        right = jnp.concatenate(right, 1)
        found = found + dot(left, right, (((1,), (1,)), ((), ())))
    place = high_iota * GRAIN + lax.broadcasted_iota(jnp.int32, (48, GRAIN), 1)
    past, ahead = place <= step[0:1, 0:1], place > step[PER_BLOCK - 1 :, GRAIN - 1 :]
    time_s[:48, :] = jnp.where(past, 2.0**-9, jnp.where(ahead, 2.0**23, found[:48]))
    row_s[:48, :] = jnp.where(past, 0.0, jnp.where(ahead, 64.0, found[48:]))
    time_s[48:, :] = jnp.full((24, GRAIN), 2.0**23, F32)
    row_s[48:, :] = jnp.full((24, GRAIN), 64.0, F32)
    lane = lax.broadcasted_iota(jnp.int32, (VISITS, GRAIN), 1)
    for eighth in range(8):
        now, then = pl.ds(eighth, VISITS, stride=8), pl.ds(eighth + 1, VISITS, stride=8)
        time, rows = time_s[now, :], row_s[now, :]
        next_time, next_rows = time_s[then, :], row_s[then, :]
        even = jnp.where(lane == 65, pltpu.roll(rows, 65, 1), time)
        even = jnp.where(lane == 66, pltpu.roll(rows, 34, 1), even)
        even = jnp.where(lane == 67, pltpu.roll(rows, 3, 1), even)
        odd = jnp.where(lane == 64, pltpu.roll(next_time, 64, 1), pltpu.roll(time, 64, 1))
        odd = jnp.where(lane == 65, pltpu.roll(rows, 1, 1), odd)
        odd = jnp.where(lane == 66, pltpu.roll(rows, 98, 1), odd)
        odd = jnp.where(lane == 67, pltpu.roll(next_rows, 67, 1), odd)
        out_ref[2 * eighth] = even.astype(BF16)
        out_ref[2 * eighth + 1] = odd.astype(BF16)


def two_to(exponent):
    value = jnp.full(jnp.shape(exponent), 2.0**-16, F32)
    for bit in range(6):
        value = value * jnp.where((exponent >> bit) & 1 == 1, float(2 ** (2**bit)), 1.0)
    return value


def table_kernel(
    ids,
    base_ref, turn_ref, fold2_ref, start_ref, back_ref, step2_in, phase_in,
    fold_ref, step_ref, short_ref, phases_ref, side_ref, step2_ref, phase_ref,
    last_s,
):
    step2_ref[...] = step2_in[...]
    phase_ref[...] = phase_in[...]
    _, dish, _ = ids()
    lane = lax.broadcasted_iota(jnp.int32, (GRAIN, 128), 1)
    turn = turn_ref[...]
    cos8 = jnp.sum(jnp.where(lane == dish, turn, 0.0), axis=1, keepdims=True)
    sin8 = jnp.sum(jnp.where(lane == dish + 8, turn, 0.0), axis=1, keepdims=True)
    cos0, sin0 = base_ref[:, :FREQS], base_ref[:, FREQS:]
    cos_f, sin_f = cos0 * cos8 - sin0 * sin8, sin0 * cos8 + cos0 * sin8
    cosine, cosine_lo = hi_lo(cos_f)
    sine, sine_lo = hi_lo(sin_f)
    for side in range(2):
        part = slice(side * SIDE, side * SIDE + SIDE)
        reals = slice(side * GRAIN, side * GRAIN + SIDE)
        imags = slice(side * GRAIN + SIDE, side * GRAIN + GRAIN)
        fold_ref[reals, :FREQS] = cosine[part]
        fold_ref[reals, FREQS : 2 * FREQS] = sine[part]
        fold_ref[imags, :FREQS] = sine[part]
        fold_ref[imags, FREQS : 2 * FREQS] = -cosine[part]
        for k, (c, s) in enumerate(((cosine, sine), (cosine_lo, sine_lo))):
            step_ref[k, reals, :FREQS] = c[part]
            step_ref[k, reals, FREQS:] = -s[part]
            step_ref[k, imags, :FREQS] = s[part]
            step_ref[k, imags, FREQS:] = c[part]
    fold_ref[:, 2 * FREQS :] = fold2_ref[...]
    cos_side, sin_side = cos_f[SIDE : SIDE + 1], sin_f[SIDE : SIDE + 1]
    side_real = cos_f[:SIDE] * cos_side + sin_f[:SIDE] * sin_side
    side_imag = cos_f[:SIDE] * sin_side - sin_f[:SIDE] * cos_side
    side_ref[:SIDE, :FREQS] = side_real.astype(BF16)
    side_ref[:SIDE, FREQS:] = side_imag.astype(BF16)
    side_ref[SIDE:, :FREQS] = -side_imag.astype(BF16)
    side_ref[SIDE:, FREQS:] = side_real.astype(BF16)
    last_s[:GRAIN, :FREQS] = cosine
    last_s[:GRAIN, FREQS:] = sine
    last_s[GRAIN:, :FREQS] = -sine
    last_s[GRAIN:, FREQS:] = cosine
    short_ref[...] = dot(back_ref[...], last_s[...]).astype(BF16)
    phases_ref[...] = jnp.zeros(phases_ref.shape, BF16)
    hi, lo = hi_lo(start_ref[...])
    phases_ref[: 2 * SPAN, :] = hi
    phases_ref[2 * SPAN : 4 * SPAN, :] = lo


def beam_rows(ref, first, last):
    rows = [
        jnp.concatenate([ref[chip, :PER_BLOCK, :], ref[chip, PER_BLOCK : 2 * PER_BLOCK, :]], 1)
        for chip in range(first, last)
    ]
    return jnp.concatenate(rows, 0)


def side_rows(ref, side):
    part = slice(side * PER_BLOCK, side * PER_BLOCK + PER_BLOCK)
    return jnp.concatenate([ref[chip, part, :] for chip in range(CHIPS)], 0)


def swap_sides(odd, early, late):
    return jnp.concatenate([jnp.where(odd > 0.0, late, early), jnp.where(odd > 0.0, early, late)], 1)


def transform(ref, step_ref, phase_ref, z_ref, fine):
    cos16, sin16 = phase_ref[:, :FREQS], phase_ref[:, FREQS:]
    cos_rows = jnp.concatenate([cos16] * (128 // SPAN), 0)
    sin_rows = jnp.concatenate([sin16] * (128 // SPAN), 0)
    for tile in range(HALF // 128):
        rows = slice(tile * 128, tile * 128 + 128)
        beam = beam_rows(ref, 4 * tile, 4 * tile + 4)
        both = dot(beam, step_ref[0])
        if fine:
            both = both + dot(beam, step_ref[1])
        real, imag = both[:, :FREQS], both[:, FREQS:]
        z_ref[rows, :FREQS] = (real * cos_rows + imag * sin_rows).astype(BF16)
        z_ref[rows, FREQS:] = (imag * cos_rows - real * sin_rows).astype(BF16)


def plan_half(ref, core, before):
    times = jnp.concatenate([ref[chip, 2 * PER_BLOCK :, :].astype(F32) for chip in range(CHIPS)], 0).astype(BF16)
    row = lax.broadcasted_iota(jnp.int32, (8, 128), 0)
    lane = lax.broadcasted_iota(jnp.int32, (8, 128), 1)
    wanted = jnp.where(row == 0, BINS * core, jnp.where(row == 1, BINS * core + BINS, core + 63 + row))
    info = dot(jnp.where(lane == wanted, 1.0, 0.0).astype(BF16), times, (((1,), (1,)), ((), ())))
    start, end, first, last = (info[k : k + 1, :] for k in range(4))
    sides = jnp.minimum(last, float(2 * PER_BLOCK - 1)) - first
    grains = jnp.where(end > start, jnp.floor(sides * 0.5) + 1.0, 0.0)
    earlier = dot(jnp.broadcast_to(grains, (8, 128)).astype(BF16), triangle(128, True))[0:1, :] + before
    return times, end, first, grains, earlier, earlier[:, 127:] + grains[:, 127:]


def slots_half(slot_0, plan, ref):
    times, end, first, grains, earlier, _ = plan
    slot = lax.broadcasted_iota(jnp.int32, (128, 128), 0).astype(F32) + slot_0
    visit = lax.broadcasted_iota(jnp.int32, (SLOTS, 128), 1)
    mine = (slot >= earlier) & (slot < earlier + grains)
    starts = dot(times, jnp.where(mine, 1.0, 0.0).astype(BF16), (((0,), (1,)), ((), ())))
    slot, mine = slot[:SLOTS], mine[:SLOTS]
    place = ((visit >> 3) * (2 * PER_BLOCK) + 1).astype(F32) + first + 2.0 * (slot - earlier)
    place = jnp.sum(jnp.where(mine, place, 0.0), axis=1, keepdims=True) - 1.0
    ends = jnp.sum(jnp.where(mine, jnp.broadcast_to(end, (SLOTS, 128)), 0.0), axis=1, keepdims=True)
    places = lax.broadcasted_iota(jnp.int32, (SLOTS, HALF), 1).astype(F32)
    whole = jnp.where(place < 0.0, -4.0, jnp.floor(place * 0.5))
    odd = jnp.where(place < 0.0, 0.0, place - 2.0 * whole)
    early = dot(jnp.where(places == whole + odd, 1.0, 0.0).astype(BF16), side_rows(ref, 0))
    late = dot(jnp.where(places == whole, 1.0, 0.0).astype(BF16), side_rows(ref, 1))
    return place, ends, starts, swap_sides(odd, early, late)


def half_kernel(ids, own_ref, step_ref, phase_ref, z_ref, total_ref, place_ref, ends_ref, starts_ref, gbeam_ref):
    _, _, core = ids()
    plan = plan_half(own_ref, core, jnp.zeros((1, 1), F32))
    place, ends, starts, beam = slots_half(jnp.float32(0.0), plan, own_ref)
    total_ref[...] = jnp.broadcast_to(plan[-1], (8, 128))
    place_ref[...] = jnp.broadcast_to(place, (SLOTS, 128))
    ends_ref[...] = jnp.broadcast_to(ends, (SLOTS, 128))
    starts_ref[...] = starts
    gbeam_ref[...] = beam
    transform(own_ref, step_ref, phase_ref, z_ref, True)


def grain_row(which):
    place = lax.broadcasted_iota(jnp.int32, (8, HALF), 1)
    grain = (2 * (place >> 5) + which) * PER_BLOCK + (place & (PER_BLOCK - 1))
    return grain.astype(F32)[0:1, :]


def spectrum_kernel(
    ids,
    own_ref, other_ref, z_ref, total_ref, place_ref, ends_ref, starts_ref, gbeam_ref,
    fold_ref, step_ref, short_ref, phases_ref, side_ref, step2_ref, phase_ref,
    out_ref,
    z_s, gdft_s, gstep_s, gbeam_s, gtime_s, gstart_s, acc_s,
):
    _, _, core = ids()
    before = total_ref[0:1, 0:1]
    other_plan = plan_half(other_ref, core, before)
    count = jnp.max(other_plan[-1]).astype(jnp.int32)
    transform(other_ref, step_ref, phase_ref, z_s, False)
    acc_s[...] = jnp.zeros(acc_s.shape, F32)
    own_grains = jnp.broadcast_to(grain_row(core), (SLOTS, HALF))
    other_grains = jnp.broadcast_to(grain_row(1 - core), (SLOTS, HALF))
    lane_iota = lax.broadcasted_iota(jnp.int32, (SLOTS, 128), 1)

    def fold_batch(batch, mine):
        first = (batch * SLOTS).astype(F32)
        more = slots_half(first, other_plan, other_ref)
        is_mine = mine[0] >= 0.0
        place = jnp.where(is_mine, mine[0], more[0]).astype(jnp.int32)
        which = jnp.where(is_mine, core, 1 - core)
        side = place & (2 * PER_BLOCK - 1)
        in_block, odd = side >> 1, (side & 1).astype(F32)
        grain = ((2 * (place >> 6) + which) * PER_BLOCK + in_block).astype(F32)
        here = mine[3] + more[3]
        ends = mine[1] + more[1]
        for k in range(2):
            at = jnp.broadcast_to(side + k, (SLOTS, GRAIN))
            times = (128 + (at & 1) * SIDE + (lane_iota & (SIDE - 1))).astype(F32) * two_to(at >> 1)
            part = slice(k * GRAIN, k * GRAIN + GRAIN)
            gtime_s[:, part] = times
            gbeam_s[:, part] = jnp.where(times < ends, here[:, part], 0.0)
        starts = mine[2] + more[2]
        starts = jnp.where(core == 0, starts[:BINS], starts[BINS : 2 * BINS])
        for group in range(SLOTS // GROUP):
            gstart_s[group] = starts if group == 0 else pltpu.roll(starts, 128 - group * GROUP, 1)
        dft = jnp.zeros((SLOTS, 2 * FREQS), F32)
        early, late, gone = (jnp.zeros((SLOTS, GRAIN), F32) for _ in range(3))
        for grains, z, ref in ((own_grains, z_ref, own_ref), (other_grains, z_s, other_ref)):
            window = (grains >= grain) & (grains < grain + float(SPAN))
            dft = dft + dot(jnp.where(window, 1.0, 0.0).astype(BF16), z[...])
            then = grains == grain + float(SPAN)
            early_pick = jnp.where(grains == grain + float(SPAN) + odd, 1.0, 0.0).astype(BF16)
            late_pick = jnp.where(then, 1.0, 0.0).astype(BF16)
            gone_pick = jnp.where(then, odd, jnp.where(grains == grain, -odd, 0.0)).astype(BF16)
            early = early + dot(early_pick, side_rows(ref, 0))
            late = late + dot(late_pick, side_rows(ref, 1))
            gone = gone + dot(gone_pick, side_rows(ref, 0))
        ahead = swap_sides(odd, early, late)
        moved = dot(gone.astype(BF16), side_ref[...])
        offset = side & (2 * SPAN - 1)
        turner = jnp.where((lane_iota == offset) | (lane_iota == offset + 2 * SPAN), 1.0, 0.0)
        turned = dot(turner.astype(BF16), phases_ref[...])
        real, imag = dft[:, :FREQS], dft[:, FREQS:]
        cos_g, sin_g = turned[:, :FREQS], turned[:, FREQS:]
        step = dot((ahead - here).astype(BF16), step2_ref[...])
        for ref, real, imag in (
            (gdft_s, real * cos_g - imag * sin_g + moved[:, :FREQS], imag * cos_g + real * sin_g + moved[:, FREQS:]),
            (gstep_s, step[:, :FREQS], step[:, FREQS:]),
        ):
            ref[:, :FREQS] = real
            ref[:, FREQS : 2 * FREQS] = imag - real
            ref[:, 2 * FREQS :] = real + imag

        def fold(slot, size):
            rows = pl.ds(pl.multiple_of(slot, 8), size)
            beam8, time8, start8 = gbeam_s[rows, :], gtime_s[rows, :], gstart_s[slot // GROUP]
            dft8, step8 = gdft_s[rows, :], gstep_s[rows, :]
            left = []
            for k in range(size):
                start = start8[:, k : k + 1]
                sides = [
                    jnp.where(time8[k : k + 1, at : at + GRAIN] >= start, beam8[k : k + 1, at : at + GRAIN], 0.0)
                    for at in (0, GRAIN)
                ]
                left.append(jnp.concatenate(sides, 1))
            left = jnp.concatenate(left, 0).astype(BF16)
            for part, factor in ((0, dft8), (1, step8)):
                folded = dot(left, fold_ref[:, part * 2 * FREQS : part * 2 * FREQS + 2 * FREQS])
                sums = [acc_s[:, k * FREQS : k * FREQS + FREQS] for k in range(3 * part, 3 * part + 3)]
                for k in range(size):
                    rows = slice(k * BINS, k * BINS + BINS)
                    real, imag = folded[rows, :FREQS], folded[rows, FREQS:]
                    for n, value in enumerate((real + imag, real, imag)):
                        sums[n] = sums[n] + value * factor[k : k + 1, n * FREQS : n * FREQS + FREQS]
                for n in range(3):
                    acc_s[:, (3 * part + n) * FREQS : (3 * part + n + 1) * FREQS] = sums[n]

        def pair_step(pair, inner):
            fold(2 * GROUP * pair, GROUP)
            fold(2 * GROUP * pair + GROUP, GROUP)
            return inner

        def one_step(_, inner):
            fold(pairs * 2 * GROUP, GROUP)
            return inner

        def half_step(_, inner):
            fold(pairs * 2 * GROUP + rest // 2 * GROUP, GROUP // 2)
            return inner

        eights = (jnp.minimum(count - batch * SLOTS, SLOTS) + 7) // 8
        pairs = eights // 4
        rest = eights - 4 * pairs
        lax.fori_loop(0, pairs, pair_step, 0)
        lax.fori_loop(0, rest // 2, one_step, 0)
        lax.fori_loop(0, rest % 2, half_step, 0)

    fold_batch(jnp.int32(0), (place_ref[:, 0:1], ends_ref[:, 0:1], starts_ref[...], gbeam_ref[...]))

    def batch_step(batch, carry):
        own_plan = plan_half(own_ref, core, jnp.zeros((1, 1), F32))
        fold_batch(batch, slots_half((batch * SLOTS).astype(F32), own_plan, own_ref))
        return carry

    lax.fori_loop(1, (count + SLOTS - 1) // SLOTS, batch_step, 0)
    since = acc_s[...]
    each = since - jnp.concatenate([since[1:], jnp.zeros((1, 6 * FREQS), F32)], 0)
    both, real, imag, both2, real2, imag2 = (each[:, k * FREQS : k * FREQS + FREQS] for k in range(6))
    short = dot(jnp.concatenate([both2 - imag2, both2 + real2], 1).astype(BF16), short_ref[...])
    out_ref[0] = (both - imag + short[:, :FREQS]) * SCALE
    out_ref[1] = (both + real + short[:, FREQS:]) * SCALE


def near(*values):
    return [pltpu.with_memory_space_constraint(v, pltpu.VMEM) for v in values]


def call(kernel, outs, values, scratch=(), mib=8, us=1.0):
    one = not isinstance(outs, (tuple, list))
    space = pl.BlockSpec(memory_space=pltpu.VMEM)
    return pl.pallas_call(
        kernel,
        out_shape=outs if one else tuple(outs),
        in_specs=[space] * len(values),
        out_specs=space if one else (space,) * len(outs),
        scratch_shapes=list(scratch),
        compiler_params=pltpu.CompilerParams(vmem_limit_bytes=mib << 20),
        cost_estimate=pl.CostEstimate(flops=int(us * 5e8), bytes_accessed=1 << 20, transcendentals=0),
    )(*near(*values))


HALF_Z = pltpu.VMEM((HALF, 2 * FREQS), BF16)


def make_tables(ids):
    given = tables()
    made = call(
        functools.partial(table_kernel, ids),
        (
            pltpu.VMEM((2 * GRAIN, 4 * FREQS), BF16),
            pltpu.VMEM((2, 2 * GRAIN, 2 * FREQS), BF16),
            pltpu.VMEM((2 * FREQS, 2 * FREQS), BF16),
            pltpu.VMEM((128, 2 * FREQS), BF16),
            pltpu.VMEM((GRAIN, 2 * FREQS), BF16),
            pltpu.VMEM((2 * GRAIN, 2 * FREQS), BF16),
            pltpu.VMEM((SPAN, 2 * FREQS), F32),
        ),
        [given[k] for k in ("base", "turn", "fold2", "start", "back", "step2", "phase")],
        [pltpu.VMEM((2 * GRAIN, 2 * FREQS), BF16)],
        us=3.0,
    )
    return made


def spectrum(own, other, ids, made):
    fold, step, short, phases, side, step2, phase = made
    half = call(
        functools.partial(half_kernel, ids),
        (
            HALF_Z,
            pltpu.VMEM((8, 128), F32),
            pltpu.VMEM((SLOTS, 128), F32),
            pltpu.VMEM((SLOTS, 128), F32),
            pltpu.VMEM((128, 128), F32),
            pltpu.VMEM((SLOTS, 2 * GRAIN), F32),
        ),
        (own, step, phase),
        us=1.0,
    )
    scratch = [
        HALF_Z,
        pltpu.VMEM((SLOTS, 3 * FREQS), F32),
        pltpu.VMEM((SLOTS, 3 * FREQS), F32),
        pltpu.VMEM((SLOTS, 2 * GRAIN), F32),
        pltpu.VMEM((SLOTS, 2 * GRAIN), F32),
        pltpu.VMEM((SLOTS // GROUP, BINS, 128), F32),
        pltpu.VMEM((BINS, 6 * FREQS), F32),
    ]
    return call(
        functools.partial(spectrum_kernel, ids),
        jax.ShapeDtypeStruct((2, BINS, FREQS), F32),
        (own, other, *half, fold, step, short, phases, side, step2, phase),
        scratch,
        mib=16,
        us=5.0,
    )


def front(voltages, beam_weights, bins):
    far = pl.BlockSpec(memory_space=pltpu.HBM)
    close = pl.BlockSpec(memory_space=pltpu.VMEM)
    return pl.pallas_call(
        front_kernel,
        out_shape=(
            pltpu.VMEM((DISH_WAYS, 2 * PER_BLOCK, GRAIN), F32),
            pltpu.VMEM((CHIPS, VISITS, GRAIN), BF16),
        ),
        in_specs=[far] * 3,
        out_specs=(close, close),
        scratch_shapes=[
            pltpu.VMEM(voltages.shape, BF16),
            pltpu.VMEM(beam_weights.shape, BF16),
            pltpu.VMEM(bins.shape, jnp.int32),
            pltpu.VMEM((72, GRAIN), F32),
            pltpu.VMEM((72, GRAIN), F32),
            pltpu.SemaphoreType.DMA((len(PIECES) + 2,)),
        ],
        compiler_params=pltpu.CompilerParams(vmem_limit_bytes=8 << 20),
        cost_estimate=pl.CostEstimate(flops=1 << 20, bytes_accessed=1 << 20, transcendentals=0),
        name="front",
    )(*(pltpu.with_memory_space_constraint(v, pltpu.HBM) for v in (voltages, beam_weights, bins)))


def steps(voltages, beam_weights, phase_bins):
    def ids():
        core = lax.axis_index("core")
        owner = (lax.axis_index("z") * 2 + lax.axis_index("xh")) * 2 + core
        return owner, lax.axis_index("dish"), core

    made = make_tables(ids)
    partial_beam, visits = front(voltages, beam_weights, phase_bins.reshape(PER_BLOCK, GRAIN))
    parts = lax.all_to_all(partial_beam, "dish", 0, 0, tiled=True)
    packed = call(pack_kernel, pltpu.VMEM((CHIPS, ROWS, GRAIN), BF16), (parts, visits), us=0.3)
    own = lax.all_to_all(packed, ("z", "xh"), 0, 0, tiled=True)
    other = lax.ppermute(own, "core", [(0, 1), (1, 0)])
    return jnp.transpose(spectrum(own, other, ids, made), (2, 0, 1))


def solution(mesh):
    split = jax.sharding.Mesh(mesh.devices.reshape(8, 2, 2, 8), ("z", "xh", "core", "dish"))
    time = ("z", "xh", "core")
    return jax.shard_map(
        steps,
        mesh=split,
        in_specs=(P(None, "dish", time), P(None, "dish"), P(time)),
        out_specs=P("dish", None, time),
        check_vma=False,
    )
```

```python
import functools
import math

import jax
import jax.numpy as jnp
import numpy as np
from jax import lax
from jax.experimental import pallas as pl
from jax.experimental.pallas import tpu as pltpu
from jax.sharding import PartitionSpec as P


PH = 1024
LAGS = 2048
SAMPLES = 131072
DISH_WAYS = 8
TM_WAYS = 32
CHIPS = 16
HALF = SAMPLES // 2 // 128
LOCAL = SAMPLES // TM_WAYS
GRAIN = 128
PER_BLOCK = LOCAL // GRAIN
SIDE = GRAIN // 2
SPAN = LAGS // GRAIN
BINS = PH // TM_WAYS
FREQS = LAGS // DISH_WAYS
SLOTS = 96
GROUP = 16
VISITS = 8
ROWS = 2 * PER_BLOCK + VISITS
SCALE = 1.0 / math.sqrt(LAGS * SAMPLES / PH)

F32 = jnp.float32
BF16 = jnp.bfloat16


def dot(a, b, dims=(((1,), (0,)), ((), ()))):
    return lax.dot_general(a, b, dims, preferred_element_type=F32)


def hi_lo(value):
    hi = value.astype(BF16)
    return hi, (value - hi.astype(F32)).astype(BF16)


def tables():
    grain = np.arange(GRAIN)
    freq = np.arange(FREQS)
    angle = 2 * np.pi * np.outer(grain, freq) / LAGS
    base = np.concatenate([np.cos(angle), np.sin(angle)], 1).astype(np.float32)
    eighth = 2 * np.pi * np.outer(grain, np.arange(DISH_WAYS)) / DISH_WAYS
    turn = np.zeros((GRAIN, 128), np.float32)
    turn[:, :8] = np.cos(eighth)
    turn[:, 8:16] = np.sin(eighth)
    fine = 2 * np.pi * np.outer(grain, np.arange(2 * GRAIN)) / (2 * GRAIN)
    cos2, sin2 = np.cos(fine), np.sin(fine)
    fold2 = np.block([[cos2, sin2], [sin2, -cos2]]).astype(np.float32)
    step2 = np.block([[cos2, -sin2], [sin2, cos2]]).astype(np.float32)
    sides = np.concatenate([np.arange(k, k + SIDE) for k in (0, GRAIN, SIDE, GRAIN + SIDE)])
    fold2, step2 = fold2[sides], step2[sides]
    keep = (grain >= 1)[None, :] / (2.0 * GRAIN)
    back = np.block([[cos2.T * keep, -sin2.T * keep], [sin2.T * keep, cos2.T * keep]])
    sixteenth = 2 * np.pi * np.outer(np.arange(SPAN), freq) / SPAN
    phase = np.concatenate([np.cos(sixteenth), np.sin(sixteenth)], 1).astype(np.float32)
    fine = np.pi * np.outer(np.arange(2 * SPAN), freq) / SPAN
    start = np.concatenate([np.cos(fine), np.sin(fine)], 1).astype(np.float32)
    return {
        "base": jnp.asarray(base),
        "turn": jnp.asarray(turn),
        "fold2": jnp.asarray(fold2).astype(BF16),
        "step2": jnp.asarray(step2).astype(BF16),
        "back": jnp.asarray(back.astype(np.float32)).astype(BF16),
        "phase": jnp.asarray(phase),
        "start": jnp.asarray(start),
    }


PIECES = [slice(k % 4 * (LOCAL // 4), k % 4 * (LOCAL // 4) + LOCAL // 4) for k in range(8)]


def front_kernel(
    volts_hbm, weights_hbm, bins_hbm, beam_ref, visit_ref, volts_s, weights_s, bins_s, time_s, row_s, sems
):
    parts = [(volts_hbm.at[k // 4, :, at], volts_s.at[k // 4, :, at]) for k, at in enumerate(PIECES)]
    parts += [(bins_hbm, bins_s), (weights_hbm, weights_s)]
    copies = [
        pltpu.make_async_copy(source, target, sems.at[k]) for k, (source, target) in enumerate(parts)
    ]
    for copy in copies:
        copy.start()
    for copy in copies:
        copy.wait()
    weights = weights_s[...]
    first = dot(weights, volts_s[0])
    second = dot(weights, volts_s[1])
    real = first[0:1] - second[1:2]
    imag = first[1:2] + second[0:1]
    for row in range(PER_BLOCK):
        part = slice(row * GRAIN, (row + 1) * GRAIN)
        beam_ref[0, row : row + 1, :] = real[:, part]
        beam_ref[0, PER_BLOCK + row : PER_BLOCK + row + 1, :] = imag[:, part]
    make_visits(bins_s, visit_ref, time_s, row_s)
    rows = beam_ref[0]
    for way in range(1, DISH_WAYS):
        beam_ref[way] = rows


def pair_at(place):
    return 2 * (place & 7) + (place >> 3)


def pack_kernel(parts_ref, visit_ref, out_ref):
    total = parts_ref[0]
    for way in range(1, DISH_WAYS):
        total = total + parts_ref[way]
    real, imag = total[:PER_BLOCK], total[PER_BLOCK:]
    early = lax.broadcasted_iota(jnp.int32, (PER_BLOCK, GRAIN), 1) < SIDE
    early_side = jnp.where(early, real, pltpu.roll(imag, SIDE, 1))
    late_side = jnp.where(early, pltpu.roll(real, SIDE, 1), imag)
    rows = jnp.concatenate([early_side, late_side], 0).astype(BF16)
    for chip in range(CHIPS):
        out_ref[chip, : 2 * PER_BLOCK, :] = rows
        out_ref[chip, 2 * PER_BLOCK :, :] = visit_ref[pair_at(chip)]


def coded_times(shape):
    row = lax.broadcasted_iota(jnp.int32, shape, 0)
    lane = lax.broadcasted_iota(jnp.int32, shape, 1)
    return (lane + 128).astype(F32) * two_to(row)


def triangle(count, strict):
    row = lax.broadcasted_iota(jnp.int32, (count, count), 0)
    column = lax.broadcasted_iota(jnp.int32, (count, count), 1)
    return jnp.where(row < column if strict else row <= column, 1.0, 0.0).astype(BF16)


def make_visits(bins_ref, out_ref, time_s, row_s):
    bins = bins_ref[...]
    shape = (PER_BLOCK, GRAIN)
    row = lax.broadcasted_iota(jnp.int32, shape, 0)
    lane = lax.broadcasted_iota(jnp.int32, shape, 1)
    rolled = pltpu.roll(bins, 1, 1)
    before = jnp.where(lane == 0, pltpu.roll(rolled, 1, 0), rolled)
    later = row + lane > 0
    enters = later & (bins != before)
    wraps = jnp.where(later & (bins < before), 1.0, 0.0).astype(BF16)
    in_row = dot(wraps, triangle(GRAIN, False))
    ends = jnp.broadcast_to(in_row[:, GRAIN - 1 :], shape).astype(BF16)
    above = dot(triangle(PER_BLOCK, True), ends, (((0,), (0,)), ((), ())))
    step = bins + PH * (in_row + above).astype(jnp.int32)
    high = jnp.where(enters, step >> 7, -1).astype(F32)
    low = (step & 127).astype(F32)
    times = coded_times(shape)
    high_iota = lax.broadcasted_iota(jnp.int32, (48, GRAIN), 0)
    high_rows = high_iota.astype(F32).astype(BF16)
    low_rows = lax.broadcasted_iota(jnp.int32, (GRAIN, GRAIN), 0).astype(F32).astype(BF16)
    zero, one = jnp.zeros((), BF16), jnp.ones((), BF16)
    late = jnp.where(lax.broadcasted_iota(jnp.int32, (48, GRAIN), 1) >= SIDE, 1.0, 0.0).astype(BF16)

    def spread(value, k, count):
        tile = jnp.broadcast_to(value[k : k + 1, :], (16, GRAIN)).astype(BF16)
        return jnp.concatenate([tile] * (count // 16), 0)

    found = jnp.zeros((96, GRAIN), F32)
    for pair in range(PER_BLOCK // 2):
        left, right = [], []
        for k in (2 * pair, 2 * pair + 1):
            here = spread(high, k, 48) == high_rows
            coded = jnp.where(here, spread(times, k, 48), zero)
            left.append(jnp.concatenate([coded, jnp.where(here, late + jnp.full((), 2 * k, BF16), zero)], 0))
            right.append(jnp.where(spread(low, k, GRAIN) == low_rows, one, zero))
        left = jnp.concatenate(left, 1)
        right = jnp.concatenate(right, 1)
        found = found + dot(left, right, (((1,), (1,)), ((), ())))
    place = high_iota * GRAIN + lax.broadcasted_iota(jnp.int32, (48, GRAIN), 1)
    past, ahead = place <= step[0:1, 0:1], place > step[PER_BLOCK - 1 :, GRAIN - 1 :]
    time_s[:48, :] = jnp.where(past, 2.0**-9, jnp.where(ahead, 2.0**23, found[:48]))
    row_s[:48, :] = jnp.where(past, 0.0, jnp.where(ahead, 64.0, found[48:]))
    time_s[48:, :] = jnp.full((24, GRAIN), 2.0**23, F32)
    row_s[48:, :] = jnp.full((24, GRAIN), 64.0, F32)
    lane = lax.broadcasted_iota(jnp.int32, (VISITS, GRAIN), 1)
    for eighth in range(8):
        now, then = pl.ds(eighth, VISITS, stride=8), pl.ds(eighth + 1, VISITS, stride=8)
        time, rows = time_s[now, :], row_s[now, :]
        next_time, next_rows = time_s[then, :], row_s[then, :]
        even = jnp.where(lane == 65, pltpu.roll(rows, 65, 1), time)
        even = jnp.where(lane == 66, pltpu.roll(rows, 34, 1), even)
        even = jnp.where(lane == 67, pltpu.roll(rows, 3, 1), even)
        odd = jnp.where(lane == 64, pltpu.roll(next_time, 64, 1), pltpu.roll(time, 64, 1))
        odd = jnp.where(lane == 65, pltpu.roll(rows, 1, 1), odd)
        odd = jnp.where(lane == 66, pltpu.roll(rows, 98, 1), odd)
        odd = jnp.where(lane == 67, pltpu.roll(next_rows, 67, 1), odd)
        out_ref[2 * eighth] = even.astype(BF16)
        out_ref[2 * eighth + 1] = odd.astype(BF16)


def two_to(exponent):
    value = jnp.full(jnp.shape(exponent), 2.0**-16, F32)
    for bit in range(6):
        value = value * jnp.where((exponent >> bit) & 1 == 1, float(2 ** (2**bit)), 1.0)
    return value


def table_kernel(
    ids, base_ref, turn_ref, fold2_ref, start_ref, back_ref, fold_ref, step_ref, short_ref, phases_ref, side_ref, last_s
):
    _, dish, _ = ids()
    lane = lax.broadcasted_iota(jnp.int32, (GRAIN, 128), 1)
    turn = turn_ref[...]
    cos8 = jnp.sum(jnp.where(lane == dish, turn, 0.0), axis=1, keepdims=True)
    sin8 = jnp.sum(jnp.where(lane == dish + 8, turn, 0.0), axis=1, keepdims=True)
    cos0, sin0 = base_ref[:, :FREQS], base_ref[:, FREQS:]
    cos_f, sin_f = cos0 * cos8 - sin0 * sin8, sin0 * cos8 + cos0 * sin8
    cosine, cosine_lo = hi_lo(cos_f)
    sine, sine_lo = hi_lo(sin_f)
    for side in range(2):
        part = slice(side * SIDE, side * SIDE + SIDE)
        reals = slice(side * GRAIN, side * GRAIN + SIDE)
        imags = slice(side * GRAIN + SIDE, side * GRAIN + GRAIN)
        fold_ref[reals, :FREQS] = cosine[part]
        fold_ref[reals, FREQS : 2 * FREQS] = sine[part]
        fold_ref[imags, :FREQS] = sine[part]
        fold_ref[imags, FREQS : 2 * FREQS] = -cosine[part]
        for k, (c, s) in enumerate(((cosine, sine), (cosine_lo, sine_lo))):
            step_ref[k, reals, :FREQS] = c[part]
            step_ref[k, reals, FREQS:] = -s[part]
            step_ref[k, imags, :FREQS] = s[part]
            step_ref[k, imags, FREQS:] = c[part]
    fold_ref[:, 2 * FREQS :] = fold2_ref[...]
    cos_side, sin_side = cos_f[SIDE : SIDE + 1], sin_f[SIDE : SIDE + 1]
    side_real = cos_f[:SIDE] * cos_side + sin_f[:SIDE] * sin_side
    side_imag = cos_f[:SIDE] * sin_side - sin_f[:SIDE] * cos_side
    side_ref[:SIDE, :FREQS] = side_real.astype(BF16)
    side_ref[:SIDE, FREQS:] = side_imag.astype(BF16)
    side_ref[SIDE:, :FREQS] = -side_imag.astype(BF16)
    side_ref[SIDE:, FREQS:] = side_real.astype(BF16)
    last_s[:GRAIN, :FREQS] = cosine
    last_s[:GRAIN, FREQS:] = sine
    last_s[GRAIN:, :FREQS] = -sine
    last_s[GRAIN:, FREQS:] = cosine
    short_ref[...] = dot(back_ref[...], last_s[...]).astype(BF16)
    phases_ref[...] = jnp.zeros(phases_ref.shape, BF16)
    hi, lo = hi_lo(start_ref[...])
    phases_ref[: 2 * SPAN, :] = hi
    phases_ref[2 * SPAN : 4 * SPAN, :] = lo


def beam_rows(ref, first, last):
    rows = [
        jnp.concatenate([ref[chip, :PER_BLOCK, :], ref[chip, PER_BLOCK : 2 * PER_BLOCK, :]], 1)
        for chip in range(first, last)
    ]
    return jnp.concatenate(rows, 0)


def side_rows(ref, side):
    part = slice(side * PER_BLOCK, side * PER_BLOCK + PER_BLOCK)
    return jnp.concatenate([ref[chip, part, :] for chip in range(CHIPS)], 0)


def swap_sides(odd, early, late):
    return jnp.concatenate([jnp.where(odd > 0.0, late, early), jnp.where(odd > 0.0, early, late)], 1)


def transform(ref, step_ref, phase_ref, z_ref, fine):
    cos16, sin16 = phase_ref[:, :FREQS], phase_ref[:, FREQS:]
    cos_rows = jnp.concatenate([cos16] * (128 // SPAN), 0)
    sin_rows = jnp.concatenate([sin16] * (128 // SPAN), 0)
    for tile in range(HALF // 128):
        rows = slice(tile * 128, tile * 128 + 128)
        beam = beam_rows(ref, 4 * tile, 4 * tile + 4)
        both = dot(beam, step_ref[0])
        if fine:
            both = both + dot(beam, step_ref[1])
        real, imag = both[:, :FREQS], both[:, FREQS:]
        z_ref[rows, :FREQS] = (real * cos_rows + imag * sin_rows).astype(BF16)
        z_ref[rows, FREQS:] = (imag * cos_rows - real * sin_rows).astype(BF16)


def plan_half(ref, core, before):
    times = jnp.concatenate([ref[chip, 2 * PER_BLOCK :, :].astype(F32) for chip in range(CHIPS)], 0).astype(BF16)
    row = lax.broadcasted_iota(jnp.int32, (8, 128), 0)
    lane = lax.broadcasted_iota(jnp.int32, (8, 128), 1)
    wanted = jnp.where(row == 0, BINS * core, jnp.where(row == 1, BINS * core + BINS, core + 63 + row))
    info = dot(jnp.where(lane == wanted, 1.0, 0.0).astype(BF16), times, (((1,), (1,)), ((), ())))
    start, end, first, last = (info[k : k + 1, :] for k in range(4))
    sides = jnp.minimum(last, float(2 * PER_BLOCK - 1)) - first
    grains = jnp.where(end > start, jnp.floor(sides * 0.5) + 1.0, 0.0)
    earlier = dot(jnp.broadcast_to(grains, (8, 128)).astype(BF16), triangle(128, True))[0:1, :] + before
    return times, end, first, grains, earlier, earlier[:, 127:] + grains[:, 127:]


def slots_half(slot_0, plan, ref):
    times, end, first, grains, earlier, _ = plan
    slot = lax.broadcasted_iota(jnp.int32, (128, 128), 0).astype(F32) + slot_0
    visit = lax.broadcasted_iota(jnp.int32, (SLOTS, 128), 1)
    mine = (slot >= earlier) & (slot < earlier + grains)
    starts = dot(times, jnp.where(mine, 1.0, 0.0).astype(BF16), (((0,), (1,)), ((), ())))
    slot, mine = slot[:SLOTS], mine[:SLOTS]
    place = ((visit >> 3) * (2 * PER_BLOCK) + 1).astype(F32) + first + 2.0 * (slot - earlier)
    place = jnp.sum(jnp.where(mine, place, 0.0), axis=1, keepdims=True) - 1.0
    ends = jnp.sum(jnp.where(mine, jnp.broadcast_to(end, (SLOTS, 128)), 0.0), axis=1, keepdims=True)
    places = lax.broadcasted_iota(jnp.int32, (SLOTS, HALF), 1).astype(F32)
    whole = jnp.where(place < 0.0, -4.0, jnp.floor(place * 0.5))
    odd = jnp.where(place < 0.0, 0.0, place - 2.0 * whole)
    early = dot(jnp.where(places == whole + odd, 1.0, 0.0).astype(BF16), side_rows(ref, 0))
    late = dot(jnp.where(places == whole, 1.0, 0.0).astype(BF16), side_rows(ref, 1))
    return place, ends, starts, swap_sides(odd, early, late)


def half_kernel(ids, own_ref, step_ref, phase_ref, z_ref, total_ref, place_ref, ends_ref, starts_ref, gbeam_ref):
    _, _, core = ids()
    plan = plan_half(own_ref, core, jnp.zeros((1, 1), F32))
    place, ends, starts, beam = slots_half(jnp.float32(0.0), plan, own_ref)
    total_ref[...] = jnp.broadcast_to(plan[-1], (8, 128))
    place_ref[...] = jnp.broadcast_to(place, (SLOTS, 128))
    ends_ref[...] = jnp.broadcast_to(ends, (SLOTS, 128))
    starts_ref[...] = starts
    gbeam_ref[...] = beam
    transform(own_ref, step_ref, phase_ref, z_ref, True)


def grain_row(which):
    place = lax.broadcasted_iota(jnp.int32, (8, HALF), 1)
    grain = (2 * pair_at(place >> 5) + which) * PER_BLOCK + (place & (PER_BLOCK - 1))
    return grain.astype(F32)[0:1, :]


def spectrum_kernel(
    ids,
    own_ref, other_ref, z_ref, total_ref, place_ref, ends_ref, starts_ref, gbeam_ref,
    fold_ref, step_ref, short_ref, phases_ref, side_ref, step2_ref, phase_ref,
    out_ref,
    z_s, gdft_s, gstep_s, gbeam_s, gtime_s, gstart_s, acc_s,
):
    _, _, core = ids()
    before = total_ref[0:1, 0:1]
    other_plan = plan_half(other_ref, core, before)
    count = jnp.max(other_plan[-1]).astype(jnp.int32)
    transform(other_ref, step_ref, phase_ref, z_s, False)
    acc_s[...] = jnp.zeros(acc_s.shape, F32)
    own_grains = jnp.broadcast_to(grain_row(core), (SLOTS, HALF))
    other_grains = jnp.broadcast_to(grain_row(1 - core), (SLOTS, HALF))
    lane_iota = lax.broadcasted_iota(jnp.int32, (SLOTS, 128), 1)

    def fold_batch(batch, mine):
        first = (batch * SLOTS).astype(F32)
        more = slots_half(first, other_plan, other_ref)
        is_mine = mine[0] >= 0.0
        place = jnp.where(is_mine, mine[0], more[0]).astype(jnp.int32)
        which = jnp.where(is_mine, core, 1 - core)
        side = place & (2 * PER_BLOCK - 1)
        in_block, odd = side >> 1, (side & 1).astype(F32)
        grain = ((2 * pair_at(place >> 6) + which) * PER_BLOCK + in_block).astype(F32)
        here = mine[3] + more[3]
        ends = mine[1] + more[1]
        for k in range(2):
            at = jnp.broadcast_to(side + k, (SLOTS, GRAIN))
            times = (128 + (at & 1) * SIDE + (lane_iota & (SIDE - 1))).astype(F32) * two_to(at >> 1)
            part = slice(k * GRAIN, k * GRAIN + GRAIN)
            gtime_s[:, part] = times
            gbeam_s[:, part] = jnp.where(times < ends, here[:, part], 0.0)
        starts = mine[2] + more[2]
        starts = jnp.where(core == 0, starts[:BINS], starts[BINS : 2 * BINS])
        for group in range(SLOTS // GROUP):
            gstart_s[group] = starts if group == 0 else pltpu.roll(starts, 128 - group * GROUP, 1)
        dft = jnp.zeros((SLOTS, 2 * FREQS), F32)
        early, late, gone = (jnp.zeros((SLOTS, GRAIN), F32) for _ in range(3))
        for grains, z, ref in ((own_grains, z_ref, own_ref), (other_grains, z_s, other_ref)):
            window = (grains >= grain) & (grains < grain + float(SPAN))
            dft = dft + dot(jnp.where(window, 1.0, 0.0).astype(BF16), z[...])
            then = grains == grain + float(SPAN)
            early_pick = jnp.where(grains == grain + float(SPAN) + odd, 1.0, 0.0).astype(BF16)
            late_pick = jnp.where(then, 1.0, 0.0).astype(BF16)
            gone_pick = jnp.where(then, odd, jnp.where(grains == grain, -odd, 0.0)).astype(BF16)
            early = early + dot(early_pick, side_rows(ref, 0))
            late = late + dot(late_pick, side_rows(ref, 1))
            gone = gone + dot(gone_pick, side_rows(ref, 0))
        ahead = swap_sides(odd, early, late)
        moved = dot(gone.astype(BF16), side_ref[...])
        offset = side & (2 * SPAN - 1)
        turner = jnp.where((lane_iota == offset) | (lane_iota == offset + 2 * SPAN), 1.0, 0.0)
        turned = dot(turner.astype(BF16), phases_ref[...])
        real, imag = dft[:, :FREQS], dft[:, FREQS:]
        cos_g, sin_g = turned[:, :FREQS], turned[:, FREQS:]
        step = dot((ahead - here).astype(BF16), step2_ref[...])
        for ref, real, imag in (
            (gdft_s, real * cos_g - imag * sin_g + moved[:, :FREQS], imag * cos_g + real * sin_g + moved[:, FREQS:]),
            (gstep_s, step[:, :FREQS], step[:, FREQS:]),
        ):
            ref[:, :FREQS] = real
            ref[:, FREQS : 2 * FREQS] = imag - real
            ref[:, 2 * FREQS :] = real + imag

        def fold(slot, size):
            rows = pl.ds(pl.multiple_of(slot, 8), size)
            beam8, time8, start8 = gbeam_s[rows, :], gtime_s[rows, :], gstart_s[slot // GROUP]
            dft8, step8 = gdft_s[rows, :], gstep_s[rows, :]
            left = []
            for k in range(size):
                start = start8[:, k : k + 1]
                sides = [
                    jnp.where(time8[k : k + 1, at : at + GRAIN] >= start, beam8[k : k + 1, at : at + GRAIN], 0.0)
                    for at in (0, GRAIN)
                ]
                left.append(jnp.concatenate(sides, 1))
            left = jnp.concatenate(left, 0).astype(BF16)
            for part, factor in ((0, dft8), (1, step8)):
                folded = dot(left, fold_ref[:, part * 2 * FREQS : part * 2 * FREQS + 2 * FREQS])
                sums = [acc_s[:, k * FREQS : k * FREQS + FREQS] for k in range(3 * part, 3 * part + 3)]
                for k in range(size):
                    rows = slice(k * BINS, k * BINS + BINS)
                    real, imag = folded[rows, :FREQS], folded[rows, FREQS:]
                    for n, value in enumerate((real + imag, real, imag)):
                        sums[n] = sums[n] + value * factor[k : k + 1, n * FREQS : n * FREQS + FREQS]
                for n in range(3):
                    acc_s[:, (3 * part + n) * FREQS : (3 * part + n + 1) * FREQS] = sums[n]

        def pair_step(pair, inner):
            fold(2 * GROUP * pair, GROUP)
            fold(2 * GROUP * pair + GROUP, GROUP)
            return inner

        def one_step(_, inner):
            fold(pairs * 2 * GROUP, GROUP)
            return inner

        def half_step(_, inner):
            fold(pairs * 2 * GROUP + rest // 2 * GROUP, GROUP // 2)
            return inner

        eights = (jnp.minimum(count - batch * SLOTS, SLOTS) + 7) // 8
        pairs = eights // 4
        rest = eights - 4 * pairs
        lax.fori_loop(0, pairs, pair_step, 0)
        lax.fori_loop(0, rest // 2, one_step, 0)
        lax.fori_loop(0, rest % 2, half_step, 0)

    fold_batch(jnp.int32(0), (place_ref[:, 0:1], ends_ref[:, 0:1], starts_ref[...], gbeam_ref[...]))

    def batch_step(batch, carry):
        own_plan = plan_half(own_ref, core, jnp.zeros((1, 1), F32))
        fold_batch(batch, slots_half((batch * SLOTS).astype(F32), own_plan, own_ref))
        return carry

    lax.fori_loop(1, (count + SLOTS - 1) // SLOTS, batch_step, 0)
    since = acc_s[...]
    each = since - jnp.concatenate([since[1:], jnp.zeros((1, 6 * FREQS), F32)], 0)
    both, real, imag, both2, real2, imag2 = (each[:, k * FREQS : k * FREQS + FREQS] for k in range(6))
    short = dot(jnp.concatenate([both2 - imag2, both2 + real2], 1).astype(BF16), short_ref[...])
    out_ref[0] = (both - imag + short[:, :FREQS]) * SCALE
    out_ref[1] = (both + real + short[:, FREQS:]) * SCALE


def near(*values):
    return [pltpu.with_memory_space_constraint(v, pltpu.VMEM) for v in values]


def call(kernel, outs, values, scratch=(), mib=8, us=1.0):
    one = not isinstance(outs, (tuple, list))
    space = pl.BlockSpec(memory_space=pltpu.VMEM)
    return pl.pallas_call(
        kernel,
        out_shape=outs if one else tuple(outs),
        in_specs=[space] * len(values),
        out_specs=space if one else (space,) * len(outs),
        scratch_shapes=list(scratch),
        compiler_params=pltpu.CompilerParams(vmem_limit_bytes=mib << 20),
        cost_estimate=pl.CostEstimate(flops=int(us * 5e8), bytes_accessed=1 << 20, transcendentals=0),
    )(*near(*values))


HALF_Z = pltpu.VMEM((HALF, 2 * FREQS), BF16)


def make_tables(ids):
    given = tables()
    made = call(
        functools.partial(table_kernel, ids),
        (
            pltpu.VMEM((2 * GRAIN, 4 * FREQS), BF16),
            pltpu.VMEM((2, 2 * GRAIN, 2 * FREQS), BF16),
            pltpu.VMEM((2 * FREQS, 2 * FREQS), BF16),
            pltpu.VMEM((128, 2 * FREQS), BF16),
            pltpu.VMEM((GRAIN, 2 * FREQS), BF16),
        ),
        [given[k] for k in ("base", "turn", "fold2", "start", "back")],
        [pltpu.VMEM((2 * GRAIN, 2 * FREQS), BF16)],
        us=3.0,
    )
    return given, made


def spectrum(own, other, ids, given, made):
    fold, step, short, phases, side = made
    phase = given["phase"]
    half = call(
        functools.partial(half_kernel, ids),
        (
            HALF_Z,
            pltpu.VMEM((8, 128), F32),
            pltpu.VMEM((SLOTS, 128), F32),
            pltpu.VMEM((SLOTS, 128), F32),
            pltpu.VMEM((128, 128), F32),
            pltpu.VMEM((SLOTS, 2 * GRAIN), F32),
        ),
        (own, step, phase),
        us=1.0,
    )
    scratch = [
        HALF_Z,
        pltpu.VMEM((SLOTS, 3 * FREQS), F32),
        pltpu.VMEM((SLOTS, 3 * FREQS), F32),
        pltpu.VMEM((SLOTS, 2 * GRAIN), F32),
        pltpu.VMEM((SLOTS, 2 * GRAIN), F32),
        pltpu.VMEM((SLOTS // GROUP, BINS, 128), F32),
        pltpu.VMEM((BINS, 6 * FREQS), F32),
    ]
    return call(
        functools.partial(spectrum_kernel, ids),
        jax.ShapeDtypeStruct((2, BINS, FREQS), F32),
        (own, other, *half, fold, step, short, phases, side, given["step2"], phase),
        scratch,
        mib=16,
        us=5.0,
    )


def front(voltages, beam_weights, bins):
    far = pl.BlockSpec(memory_space=pltpu.HBM)
    close = pl.BlockSpec(memory_space=pltpu.VMEM)
    return pl.pallas_call(
        front_kernel,
        out_shape=(
            pltpu.VMEM((DISH_WAYS, 2 * PER_BLOCK, GRAIN), F32),
            pltpu.VMEM((CHIPS, VISITS, GRAIN), BF16),
        ),
        in_specs=[far] * 3,
        out_specs=(close, close),
        scratch_shapes=[
            pltpu.VMEM(voltages.shape, BF16),
            pltpu.VMEM(beam_weights.shape, BF16),
            pltpu.VMEM(bins.shape, jnp.int32),
            pltpu.VMEM((72, GRAIN), F32),
            pltpu.VMEM((72, GRAIN), F32),
            pltpu.SemaphoreType.DMA((len(PIECES) + 2,)),
        ],
        compiler_params=pltpu.CompilerParams(vmem_limit_bytes=8 << 20),
        cost_estimate=pl.CostEstimate(flops=1 << 20, bytes_accessed=1 << 20, transcendentals=0),
        name="front",
    )(*(pltpu.with_memory_space_constraint(v, pltpu.HBM) for v in (voltages, beam_weights, bins)))


def steps(voltages, beam_weights, phase_bins):
    def ids():
        core = lax.axis_index("core")
        owner = (lax.axis_index("z") * 2 + lax.axis_index("xh")) * 2 + core
        return owner, lax.axis_index("dish"), core

    given, made = make_tables(ids)
    partial_beam, visits = front(voltages, beam_weights, phase_bins.reshape(PER_BLOCK, GRAIN))
    parts = lax.all_to_all(partial_beam, "dish", 0, 0, tiled=True)
    packed = call(pack_kernel, pltpu.VMEM((CHIPS, ROWS, GRAIN), BF16), (parts, visits), us=0.3)
    own = lax.all_to_all(packed, ("xh", "z"), 0, 0, tiled=True)
    other = lax.ppermute(own, "core", [(0, 1), (1, 0)])
    return jnp.transpose(spectrum(own, other, ids, given, made), (2, 0, 1))


def solution(mesh):
    split = jax.sharding.Mesh(mesh.devices.reshape(8, 2, 2, 8), ("z", "xh", "core", "dish"))
    time = ("z", "xh", "core")
    return jax.shard_map(
        steps,
        mesh=split,
        in_specs=(P(None, "dish", time), P(None, "dish"), P(time)),
        out_specs=P("dish", None, time),
        check_vma=False,
    )
```

```python
import functools
import math

import jax
import jax.numpy as jnp
import numpy as np
from jax import lax
from jax.experimental import pallas as pl
from jax.experimental.pallas import tpu as pltpu
from jax.sharding import PartitionSpec as P


PH = 1024
LAGS = 2048
SAMPLES = 131072
DISH_WAYS = 8
TM_WAYS = 32
CHIPS = 16
HALF = SAMPLES // 2 // 128
LOCAL = SAMPLES // TM_WAYS
GRAIN = 128
PER_BLOCK = LOCAL // GRAIN
SIDE = GRAIN // 2
SPAN = LAGS // GRAIN
BINS = PH // TM_WAYS
FREQS = LAGS // DISH_WAYS
SLOTS = 96
GROUP = 16
VISITS = 8
ROWS = 2 * PER_BLOCK + VISITS
SCALE = 1.0 / math.sqrt(LAGS * SAMPLES / PH)

F32 = jnp.float32
BF16 = jnp.bfloat16


def dot(a, b, dims=(((1,), (0,)), ((), ()))):
    return lax.dot_general(a, b, dims, preferred_element_type=F32)


def hi_lo(value):
    hi = value.astype(BF16)
    return hi, (value - hi.astype(F32)).astype(BF16)


def tables():
    grain = np.arange(GRAIN)
    freq = np.arange(FREQS)
    angle = 2 * np.pi * np.outer(grain, freq) / LAGS
    base = np.concatenate([np.cos(angle), np.sin(angle)], 1).astype(np.float32)
    eighth = 2 * np.pi * np.outer(grain, np.arange(DISH_WAYS)) / DISH_WAYS
    turn = np.zeros((GRAIN, 128), np.float32)
    turn[:, :8] = np.cos(eighth)
    turn[:, 8:16] = np.sin(eighth)
    fine = 2 * np.pi * np.outer(grain, np.arange(2 * GRAIN)) / (2 * GRAIN)
    cos2, sin2 = np.cos(fine), np.sin(fine)
    fold2 = np.block([[cos2, sin2], [sin2, -cos2]]).astype(np.float32)
    step2 = np.block([[cos2, -sin2], [sin2, cos2]]).astype(np.float32)
    sides = np.concatenate([np.arange(k, k + SIDE) for k in (0, GRAIN, SIDE, GRAIN + SIDE)])
    fold2, step2 = fold2[sides], step2[sides]
    keep = (grain >= 1)[None, :] / (2.0 * GRAIN)
    back = np.block([[cos2.T * keep, -sin2.T * keep], [sin2.T * keep, cos2.T * keep]])
    sixteenth = 2 * np.pi * np.outer(np.arange(SPAN), freq) / SPAN
    phase = np.concatenate([np.cos(sixteenth), np.sin(sixteenth)], 1).astype(np.float32)
    fine = np.pi * np.outer(np.arange(2 * SPAN), freq) / SPAN
    start = np.concatenate([np.cos(fine), np.sin(fine)], 1).astype(np.float32)
    return {
        "base": jnp.asarray(base),
        "turn": jnp.asarray(turn),
        "fold2": jnp.asarray(fold2).astype(BF16),
        "step2": jnp.asarray(step2).astype(BF16),
        "back": jnp.asarray(back.astype(np.float32)).astype(BF16),
        "phase": jnp.asarray(phase),
        "start": jnp.asarray(start),
    }


PIECES = [slice(k % 4 * (LOCAL // 4), k % 4 * (LOCAL // 4) + LOCAL // 4) for k in range(8)]


def front_kernel(
    volts_hbm, weights_hbm, bins_hbm, beam_ref, visit_ref, volts_s, weights_s, bins_s, time_s, row_s, sems
):
    parts = [(volts_hbm.at[k // 4, :, at], volts_s.at[k // 4, :, at]) for k, at in enumerate(PIECES)]
    parts += [(bins_hbm, bins_s), (weights_hbm, weights_s)]
    copies = [
        pltpu.make_async_copy(source, target, sems.at[k]) for k, (source, target) in enumerate(parts)
    ]
    for copy in copies:
        copy.start()
    for copy in copies:
        copy.wait()
    weights = weights_s[...]
    first = dot(weights, volts_s[0])
    second = dot(weights, volts_s[1])
    real = first[0:1] - second[1:2]
    imag = first[1:2] + second[0:1]
    for row in range(PER_BLOCK):
        part = slice(row * GRAIN, (row + 1) * GRAIN)
        beam_ref[0, row : row + 1, :] = real[:, part]
        beam_ref[0, PER_BLOCK + row : PER_BLOCK + row + 1, :] = imag[:, part]
    make_visits(bins_s, visit_ref, time_s, row_s)
    rows = beam_ref[0]
    for way in range(1, DISH_WAYS):
        beam_ref[way] = rows


def pair_at(place):
    return 2 * (place & 7) + (place >> 3)


def pack_kernel(parts_ref, visit_ref, out_ref):
    total = parts_ref[0]
    for way in range(1, DISH_WAYS):
        total = total + parts_ref[way]
    real, imag = total[:PER_BLOCK], total[PER_BLOCK:]
    early = lax.broadcasted_iota(jnp.int32, (PER_BLOCK, GRAIN), 1) < SIDE
    early_side = jnp.where(early, real, pltpu.roll(imag, SIDE, 1))
    late_side = jnp.where(early, pltpu.roll(real, SIDE, 1), imag)
    rows = jnp.concatenate([early_side, late_side], 0).astype(BF16)
    for chip in range(CHIPS):
        out_ref[chip, : 2 * PER_BLOCK, :] = rows
        out_ref[chip, 2 * PER_BLOCK :, :] = visit_ref[pair_at(chip)]


def coded_times(shape):
    row = lax.broadcasted_iota(jnp.int32, shape, 0)
    lane = lax.broadcasted_iota(jnp.int32, shape, 1)
    return (lane + 128).astype(F32) * two_to(row)


def triangle(count, strict):
    row = lax.broadcasted_iota(jnp.int32, (count, count), 0)
    column = lax.broadcasted_iota(jnp.int32, (count, count), 1)
    return jnp.where(row < column if strict else row <= column, 1.0, 0.0).astype(BF16)


def make_visits(bins_ref, out_ref, time_s, row_s):
    bins = bins_ref[...]
    shape = (PER_BLOCK, GRAIN)
    row = lax.broadcasted_iota(jnp.int32, shape, 0)
    lane = lax.broadcasted_iota(jnp.int32, shape, 1)
    rolled = pltpu.roll(bins, 1, 1)
    before = jnp.where(lane == 0, pltpu.roll(rolled, 1, 0), rolled)
    later = row + lane > 0
    enters = later & (bins != before)
    wraps = jnp.where(later & (bins < before), 1.0, 0.0).astype(BF16)
    in_row = dot(wraps, triangle(GRAIN, False))
    ends = jnp.broadcast_to(in_row[:, GRAIN - 1 :], shape).astype(BF16)
    above = dot(triangle(PER_BLOCK, True), ends, (((0,), (0,)), ((), ())))
    step = bins + PH * (in_row + above).astype(jnp.int32)
    high = jnp.where(enters, step >> 7, -1).astype(F32)
    low = (step & 127).astype(F32)
    times = coded_times(shape)
    high_iota = lax.broadcasted_iota(jnp.int32, (48, GRAIN), 0)
    high_rows = high_iota.astype(F32).astype(BF16)
    low_rows = lax.broadcasted_iota(jnp.int32, (GRAIN, GRAIN), 0).astype(F32).astype(BF16)
    zero, one = jnp.zeros((), BF16), jnp.ones((), BF16)
    late = jnp.where(lax.broadcasted_iota(jnp.int32, (48, GRAIN), 1) >= SIDE, 1.0, 0.0).astype(BF16)

    def spread(value, k, count):
        tile = jnp.broadcast_to(value[k : k + 1, :], (16, GRAIN)).astype(BF16)
        return jnp.concatenate([tile] * (count // 16), 0)

    found = jnp.zeros((96, GRAIN), F32)
    for pair in range(PER_BLOCK // 2):
        left, right = [], []
        for k in (2 * pair, 2 * pair + 1):
            here = spread(high, k, 48) == high_rows
            coded = jnp.where(here, spread(times, k, 48), zero)
            left.append(jnp.concatenate([coded, jnp.where(here, late + jnp.full((), 2 * k, BF16), zero)], 0))
            right.append(jnp.where(spread(low, k, GRAIN) == low_rows, one, zero))
        left = jnp.concatenate(left, 1)
        right = jnp.concatenate(right, 1)
        found = found + dot(left, right, (((1,), (1,)), ((), ())))
    place = high_iota * GRAIN + lax.broadcasted_iota(jnp.int32, (48, GRAIN), 1)
    past, ahead = place <= step[0:1, 0:1], place > step[PER_BLOCK - 1 :, GRAIN - 1 :]
    time_s[:48, :] = jnp.where(past, 2.0**-9, jnp.where(ahead, 2.0**23, found[:48]))
    row_s[:48, :] = jnp.where(past, 0.0, jnp.where(ahead, 64.0, found[48:]))
    time_s[48:, :] = jnp.full((24, GRAIN), 2.0**23, F32)
    row_s[48:, :] = jnp.full((24, GRAIN), 64.0, F32)
    lane = lax.broadcasted_iota(jnp.int32, (VISITS, GRAIN), 1)
    for eighth in range(8):
        now, then = pl.ds(eighth, VISITS, stride=8), pl.ds(eighth + 1, VISITS, stride=8)
        time, rows = time_s[now, :], row_s[now, :]
        next_time, next_rows = time_s[then, :], row_s[then, :]
        even = jnp.where(lane == 65, pltpu.roll(rows, 65, 1), time)
        even = jnp.where(lane == 66, pltpu.roll(rows, 34, 1), even)
        even = jnp.where(lane == 67, pltpu.roll(rows, 3, 1), even)
        odd = jnp.where(lane == 64, pltpu.roll(next_time, 64, 1), pltpu.roll(time, 64, 1))
        odd = jnp.where(lane == 65, pltpu.roll(rows, 1, 1), odd)
        odd = jnp.where(lane == 66, pltpu.roll(rows, 98, 1), odd)
        odd = jnp.where(lane == 67, pltpu.roll(next_rows, 67, 1), odd)
        out_ref[2 * eighth] = even.astype(BF16)
        out_ref[2 * eighth + 1] = odd.astype(BF16)


def two_to(exponent):
    value = jnp.full(jnp.shape(exponent), 2.0**-16, F32)
    for bit in range(6):
        value = value * jnp.where((exponent >> bit) & 1 == 1, float(2 ** (2**bit)), 1.0)
    return value


def table_kernel(
    ids, base_ref, turn_ref, fold2_ref, start_ref, back_ref, fold_ref, step_ref, short_ref, phases_ref, side_ref, last_s
):
    _, dish, _ = ids()
    lane = lax.broadcasted_iota(jnp.int32, (GRAIN, 128), 1)
    turn = turn_ref[...]
    cos8 = jnp.sum(jnp.where(lane == dish, turn, 0.0), axis=1, keepdims=True)
    sin8 = jnp.sum(jnp.where(lane == dish + 8, turn, 0.0), axis=1, keepdims=True)
    cos0, sin0 = base_ref[:, :FREQS], base_ref[:, FREQS:]
    cos_f, sin_f = cos0 * cos8 - sin0 * sin8, sin0 * cos8 + cos0 * sin8
    cosine, cosine_lo = hi_lo(cos_f)
    sine, sine_lo = hi_lo(sin_f)
    for side in range(2):
        part = slice(side * SIDE, side * SIDE + SIDE)
        reals = slice(side * GRAIN, side * GRAIN + SIDE)
        imags = slice(side * GRAIN + SIDE, side * GRAIN + GRAIN)
        fold_ref[reals, :FREQS] = cosine[part]
        fold_ref[reals, FREQS : 2 * FREQS] = sine[part]
        fold_ref[imags, :FREQS] = sine[part]
        fold_ref[imags, FREQS : 2 * FREQS] = -cosine[part]
        for k, (c, s) in enumerate(((cosine, sine), (cosine_lo, sine_lo))):
            step_ref[k, reals, :FREQS] = c[part]
            step_ref[k, reals, FREQS:] = -s[part]
            step_ref[k, imags, :FREQS] = s[part]
            step_ref[k, imags, FREQS:] = c[part]
    fold_ref[:, 2 * FREQS :] = fold2_ref[...]
    cos_side, sin_side = cos_f[SIDE : SIDE + 1], sin_f[SIDE : SIDE + 1]
    side_real = cos_f[:SIDE] * cos_side + sin_f[:SIDE] * sin_side
    side_imag = cos_f[:SIDE] * sin_side - sin_f[:SIDE] * cos_side
    side_ref[:SIDE, :FREQS] = side_real.astype(BF16)
    side_ref[:SIDE, FREQS:] = side_imag.astype(BF16)
    side_ref[SIDE:, :FREQS] = -side_imag.astype(BF16)
    side_ref[SIDE:, FREQS:] = side_real.astype(BF16)
    last_s[:GRAIN, :FREQS] = cosine
    last_s[:GRAIN, FREQS:] = sine
    last_s[GRAIN:, :FREQS] = -sine
    last_s[GRAIN:, FREQS:] = cosine
    short_ref[...] = dot(back_ref[...], last_s[...]).astype(BF16)
    phases_ref[...] = jnp.zeros(phases_ref.shape, BF16)
    hi, lo = hi_lo(start_ref[...])
    phases_ref[: 2 * SPAN, :] = hi
    phases_ref[2 * SPAN : 4 * SPAN, :] = lo


def beam_rows(ref, first, last):
    rows = [
        jnp.concatenate([ref[chip, :PER_BLOCK, :], ref[chip, PER_BLOCK : 2 * PER_BLOCK, :]], 1)
        for chip in range(first, last)
    ]
    return jnp.concatenate(rows, 0)


def side_rows(ref, side):
    part = slice(side * PER_BLOCK, side * PER_BLOCK + PER_BLOCK)
    return jnp.concatenate([ref[chip, part, :] for chip in range(CHIPS)], 0)


def swap_sides(odd, early, late):
    return jnp.concatenate([jnp.where(odd > 0.0, late, early), jnp.where(odd > 0.0, early, late)], 1)


def transform(ref, step_ref, phase_ref, z_ref, fine):
    cos16, sin16 = phase_ref[:, :FREQS], phase_ref[:, FREQS:]
    cos_rows = jnp.concatenate([cos16] * (128 // SPAN), 0)
    sin_rows = jnp.concatenate([sin16] * (128 // SPAN), 0)
    for tile in range(HALF // 128):
        rows = slice(tile * 128, tile * 128 + 128)
        beam = beam_rows(ref, 4 * tile, 4 * tile + 4)
        both = dot(beam, step_ref[0])
        if fine:
            both = both + dot(beam, step_ref[1])
        real, imag = both[:, :FREQS], both[:, FREQS:]
        z_ref[rows, :FREQS] = (real * cos_rows + imag * sin_rows).astype(BF16)
        z_ref[rows, FREQS:] = (imag * cos_rows - real * sin_rows).astype(BF16)


def plan_half(ref, core, before):
    times = jnp.concatenate([ref[chip, 2 * PER_BLOCK :, :].astype(F32) for chip in range(CHIPS)], 0).astype(BF16)
    row = lax.broadcasted_iota(jnp.int32, (8, 128), 0)
    lane = lax.broadcasted_iota(jnp.int32, (8, 128), 1)
    wanted = jnp.where(row == 0, BINS * core, jnp.where(row == 1, BINS * core + BINS, core + 63 + row))
    info = dot(jnp.where(lane == wanted, 1.0, 0.0).astype(BF16), times, (((1,), (1,)), ((), ())))
    start, end, first, last = (info[k : k + 1, :] for k in range(4))
    sides = jnp.minimum(last, float(2 * PER_BLOCK - 1)) - first
    grains = jnp.where(end > start, jnp.floor(sides * 0.5) + 1.0, 0.0)
    earlier = dot(jnp.broadcast_to(grains, (8, 128)).astype(BF16), triangle(128, True))[0:1, :] + before
    return times, end, first, grains, earlier, earlier[:, 127:] + grains[:, 127:]


def slots_half(slot_0, plan, ref):
    times, end, first, grains, earlier, _ = plan
    slot = lax.broadcasted_iota(jnp.int32, (128, 128), 0).astype(F32) + slot_0
    visit = lax.broadcasted_iota(jnp.int32, (SLOTS, 128), 1)
    mine = (slot >= earlier) & (slot < earlier + grains)
    starts = dot(times, jnp.where(mine, 1.0, 0.0).astype(BF16), (((0,), (1,)), ((), ())))
    slot, mine = slot[:SLOTS], mine[:SLOTS]
    place = ((visit >> 3) * (2 * PER_BLOCK) + 1).astype(F32) + first + 2.0 * (slot - earlier)
    place = jnp.sum(jnp.where(mine, place, 0.0), axis=1, keepdims=True) - 1.0
    ends = jnp.sum(jnp.where(mine, jnp.broadcast_to(end, (SLOTS, 128)), 0.0), axis=1, keepdims=True)
    places = lax.broadcasted_iota(jnp.int32, (SLOTS, HALF), 1).astype(F32)
    whole = jnp.where(place < 0.0, -4.0, jnp.floor(place * 0.5))
    odd = jnp.where(place < 0.0, 0.0, place - 2.0 * whole)
    early = dot(jnp.where(places == whole + odd, 1.0, 0.0).astype(BF16), side_rows(ref, 0))
    late = dot(jnp.where(places == whole, 1.0, 0.0).astype(BF16), side_rows(ref, 1))
    return place, ends, starts, swap_sides(odd, early, late)


def half_kernel(ids, own_ref, step_ref, phase_ref, z_ref, total_ref, place_ref, ends_ref, starts_ref, gbeam_ref):
    _, _, core = ids()
    plan = plan_half(own_ref, core, jnp.zeros((1, 1), F32))
    place, ends, starts, beam = slots_half(jnp.float32(0.0), plan, own_ref)
    total_ref[...] = jnp.broadcast_to(plan[-1], (8, 128))
    place_ref[...] = jnp.broadcast_to(place, (SLOTS, 128))
    ends_ref[...] = jnp.broadcast_to(ends, (SLOTS, 128))
    starts_ref[...] = starts
    gbeam_ref[...] = beam
    transform(own_ref, step_ref, phase_ref, z_ref, True)


def grain_row(which):
    place = lax.broadcasted_iota(jnp.int32, (8, HALF), 1)
    grain = (2 * pair_at(place >> 5) + which) * PER_BLOCK + (place & (PER_BLOCK - 1))
    return grain.astype(F32)[0:1, :]


def spectrum_kernel(
    ids,
    own_ref, other_ref, z_ref, total_ref, place_ref, ends_ref, starts_ref, gbeam_ref,
    fold_ref, step_ref, short_ref, phases_ref, side_ref, step2_ref, phase_ref,
    out_ref,
    z_s, gdft_s, gstep_s, gbeam_s, gtime_s, gstart_s, acc_s,
):
    _, _, core = ids()
    before = total_ref[0:1, 0:1]
    other_plan = plan_half(other_ref, core, before)
    count = jnp.max(other_plan[-1]).astype(jnp.int32)
    transform(other_ref, step_ref, phase_ref, z_s, False)
    acc_s[...] = jnp.zeros(acc_s.shape, F32)
    own_grains = jnp.broadcast_to(grain_row(core), (SLOTS, HALF))
    other_grains = jnp.broadcast_to(grain_row(1 - core), (SLOTS, HALF))
    lane_iota = lax.broadcasted_iota(jnp.int32, (SLOTS, 128), 1)

    def fold_batch(batch, mine):
        first = (batch * SLOTS).astype(F32)
        more = slots_half(first, other_plan, other_ref)
        is_mine = mine[0] >= 0.0
        place = jnp.where(is_mine, mine[0], more[0]).astype(jnp.int32)
        which = jnp.where(is_mine, core, 1 - core)
        side = place & (2 * PER_BLOCK - 1)
        in_block, odd = side >> 1, (side & 1).astype(F32)
        grain = ((2 * pair_at(place >> 6) + which) * PER_BLOCK + in_block).astype(F32)
        here = mine[3] + more[3]
        ends = mine[1] + more[1]
        for k in range(2):
            at = jnp.broadcast_to(side + k, (SLOTS, GRAIN))
            times = (128 + (at & 1) * SIDE + (lane_iota & (SIDE - 1))).astype(F32) * two_to(at >> 1)
            part = slice(k * GRAIN, k * GRAIN + GRAIN)
            gtime_s[:, part] = times
            gbeam_s[:, part] = jnp.where(times < ends, here[:, part], 0.0)
        starts = mine[2] + more[2]
        starts = jnp.where(core == 0, starts[:BINS], starts[BINS : 2 * BINS])
        for group in range(SLOTS // GROUP):
            gstart_s[group] = starts if group == 0 else pltpu.roll(starts, 128 - group * GROUP, 1)
        dft = jnp.zeros((SLOTS, 2 * FREQS), F32)
        early, late, gone = (jnp.zeros((SLOTS, GRAIN), F32) for _ in range(3))
        for grains, z, ref in ((own_grains, z_ref, own_ref), (other_grains, z_s, other_ref)):
            window = (grains >= grain) & (grains < grain + float(SPAN))
            dft = dft + dot(jnp.where(window, 1.0, 0.0).astype(BF16), z[...])
            then = grains == grain + float(SPAN)
            early_pick = jnp.where(grains == grain + float(SPAN) + odd, 1.0, 0.0).astype(BF16)
            late_pick = jnp.where(then, 1.0, 0.0).astype(BF16)
            gone_pick = jnp.where(then, odd, jnp.where(grains == grain, -odd, 0.0)).astype(BF16)
            early = early + dot(early_pick, side_rows(ref, 0))
            late = late + dot(late_pick, side_rows(ref, 1))
            gone = gone + dot(gone_pick, side_rows(ref, 0))
        ahead = swap_sides(odd, early, late)
        moved = dot(gone.astype(BF16), side_ref[...])
        offset = side & (2 * SPAN - 1)
        turner = jnp.where((lane_iota == offset) | (lane_iota == offset + 2 * SPAN), 1.0, 0.0)
        turned = dot(turner.astype(BF16), phases_ref[...])
        real, imag = dft[:, :FREQS], dft[:, FREQS:]
        cos_g, sin_g = turned[:, :FREQS], turned[:, FREQS:]
        step = dot((ahead - here).astype(BF16), step2_ref[...])
        for ref, real, imag in (
            (gdft_s, real * cos_g - imag * sin_g + moved[:, :FREQS], imag * cos_g + real * sin_g + moved[:, FREQS:]),
            (gstep_s, step[:, :FREQS], step[:, FREQS:]),
        ):
            ref[:, :FREQS] = real
            ref[:, FREQS : 2 * FREQS] = imag - real
            ref[:, 2 * FREQS :] = real + imag

        def fold(slot, size):
            rows = pl.ds(pl.multiple_of(slot, 8), size)
            beam8, time8, start8 = gbeam_s[rows, :], gtime_s[rows, :], gstart_s[slot // GROUP]
            dft8, step8 = gdft_s[rows, :], gstep_s[rows, :]
            left = []
            for k in range(size):
                start = start8[:, k : k + 1]
                sides = [
                    jnp.where(time8[k : k + 1, at : at + GRAIN] >= start, beam8[k : k + 1, at : at + GRAIN], 0.0)
                    for at in (0, GRAIN)
                ]
                left.append(jnp.concatenate(sides, 1))
            left = jnp.concatenate(left, 0).astype(BF16)
            for part, factor in ((0, dft8), (1, step8)):
                folded = dot(left, fold_ref[:, part * 2 * FREQS : part * 2 * FREQS + 2 * FREQS])
                sums = [acc_s[:, k * FREQS : k * FREQS + FREQS] for k in range(3 * part, 3 * part + 3)]
                for k in range(size):
                    rows = slice(k * BINS, k * BINS + BINS)
                    real, imag = folded[rows, :FREQS], folded[rows, FREQS:]
                    for n, value in enumerate((real + imag, real, imag)):
                        sums[n] = sums[n] + value * factor[k : k + 1, n * FREQS : n * FREQS + FREQS]
                for n in range(3):
                    acc_s[:, (3 * part + n) * FREQS : (3 * part + n + 1) * FREQS] = sums[n]

        def pair_step(pair, inner):
            fold(2 * GROUP * pair, GROUP)
            fold(2 * GROUP * pair + GROUP, GROUP)
            return inner

        def one_step(_, inner):
            fold(pairs * 2 * GROUP, GROUP)
            return inner

        def half_step(_, inner):
            fold(pairs * 2 * GROUP + rest // 2 * GROUP, GROUP // 2)
            return inner

        eights = (jnp.minimum(count - batch * SLOTS, SLOTS) + 7) // 8
        pairs = eights // 4
        rest = eights - 4 * pairs
        lax.fori_loop(0, pairs, pair_step, 0)
        lax.fori_loop(0, rest // 2, one_step, 0)
        lax.fori_loop(0, rest % 2, half_step, 0)

    fold_batch(jnp.int32(0), (place_ref[:, 0:1], ends_ref[:, 0:1], starts_ref[...], gbeam_ref[...]))

    def batch_step(batch, carry):
        own_plan = plan_half(own_ref, core, jnp.zeros((1, 1), F32))
        fold_batch(batch, slots_half((batch * SLOTS).astype(F32), own_plan, own_ref))
        return carry

    lax.fori_loop(1, (count + SLOTS - 1) // SLOTS, batch_step, 0)
    since = acc_s[...]
    each = since - jnp.concatenate([since[1:], jnp.zeros((1, 6 * FREQS), F32)], 0)
    both, real, imag, both2, real2, imag2 = (each[:, k * FREQS : k * FREQS + FREQS] for k in range(6))
    short = dot(jnp.concatenate([both2 - imag2, both2 + real2], 1).astype(BF16), short_ref[...])
    out_ref[0] = (both - imag + short[:, :FREQS]) * SCALE
    out_ref[1] = (both + real + short[:, FREQS:]) * SCALE


def near(*values):
    return [pltpu.with_memory_space_constraint(v, pltpu.VMEM) for v in values]


def call(kernel, outs, values, scratch=(), mib=8, us=1.0):
    one = not isinstance(outs, (tuple, list))
    space = pl.BlockSpec(memory_space=pltpu.VMEM)
    return pl.pallas_call(
        kernel,
        out_shape=outs if one else tuple(outs),
        in_specs=[space] * len(values),
        out_specs=space if one else (space,) * len(outs),
        scratch_shapes=list(scratch),
        compiler_params=pltpu.CompilerParams(vmem_limit_bytes=mib << 20),
        cost_estimate=pl.CostEstimate(flops=int(us * 5e8), bytes_accessed=1 << 20, transcendentals=0),
    )(*near(*values))


HALF_Z = pltpu.VMEM((HALF, 2 * FREQS), BF16)


def make_tables(ids):
    given = tables()
    made = call(
        functools.partial(table_kernel, ids),
        (
            pltpu.VMEM((2 * GRAIN, 4 * FREQS), BF16),
            pltpu.VMEM((2, 2 * GRAIN, 2 * FREQS), BF16),
            pltpu.VMEM((2 * FREQS, 2 * FREQS), BF16),
            pltpu.VMEM((128, 2 * FREQS), BF16),
            pltpu.VMEM((GRAIN, 2 * FREQS), BF16),
        ),
        [given[k] for k in ("base", "turn", "fold2", "start", "back")],
        [pltpu.VMEM((2 * GRAIN, 2 * FREQS), BF16)],
        us=3.0,
    )
    return given, made


def spectrum(own, other, ids, given, made):
    fold, step, short, phases, side = made
    phase = given["phase"]
    half = call(
        functools.partial(half_kernel, ids),
        (
            HALF_Z,
            pltpu.VMEM((8, 128), F32),
            pltpu.VMEM((SLOTS, 128), F32),
            pltpu.VMEM((SLOTS, 128), F32),
            pltpu.VMEM((128, 128), F32),
            pltpu.VMEM((SLOTS, 2 * GRAIN), F32),
        ),
        (own, step, phase),
        us=1.0,
    )
    scratch = [
        HALF_Z,
        pltpu.VMEM((SLOTS, 3 * FREQS), F32),
        pltpu.VMEM((SLOTS, 3 * FREQS), F32),
        pltpu.VMEM((SLOTS, 2 * GRAIN), F32),
        pltpu.VMEM((SLOTS, 2 * GRAIN), F32),
        pltpu.VMEM((SLOTS // GROUP, BINS, 128), F32),
        pltpu.VMEM((BINS, 6 * FREQS), F32),
    ]
    return call(
        functools.partial(spectrum_kernel, ids),
        jax.ShapeDtypeStruct((2, BINS, FREQS), F32),
        (own, other, *half, fold, step, short, phases, side, given["step2"], phase),
        scratch,
        mib=16,
        us=5.0,
    )


def front(voltages, beam_weights, bins):
    far = pl.BlockSpec(memory_space=pltpu.HBM)
    close = pl.BlockSpec(memory_space=pltpu.VMEM)
    return pl.pallas_call(
        front_kernel,
        out_shape=(
            pltpu.VMEM((DISH_WAYS, 2 * PER_BLOCK, GRAIN), F32),
            pltpu.VMEM((CHIPS, VISITS, GRAIN), BF16),
        ),
        in_specs=[far] * 3,
        out_specs=(close, close),
        scratch_shapes=[
            pltpu.VMEM(voltages.shape, BF16),
            pltpu.VMEM(beam_weights.shape, BF16),
            pltpu.VMEM(bins.shape, jnp.int32),
            pltpu.VMEM((72, GRAIN), F32),
            pltpu.VMEM((72, GRAIN), F32),
            pltpu.SemaphoreType.DMA((len(PIECES) + 2,)),
        ],
        compiler_params=pltpu.CompilerParams(vmem_limit_bytes=8 << 20),
        cost_estimate=pl.CostEstimate(flops=1 << 20, bytes_accessed=1 << 20, transcendentals=0),
        name="front",
    )(*(pltpu.with_memory_space_constraint(v, pltpu.HBM) for v in (voltages, beam_weights, bins)))


def steps(voltages, beam_weights, phase_bins):
    def ids():
        core = lax.axis_index("core")
        owner = (lax.axis_index("z") * 2 + lax.axis_index("xh")) * 2 + core
        return owner, lax.axis_index("y") * 2 + lax.axis_index("xl"), core

    given, made = make_tables(ids)
    partial_beam, visits = front(voltages, beam_weights, phase_bins.reshape(PER_BLOCK, GRAIN))
    parts = lax.all_to_all(partial_beam, ("xl", "y"), 0, 0, tiled=True)
    packed = call(pack_kernel, pltpu.VMEM((CHIPS, ROWS, GRAIN), BF16), (parts, visits), us=0.3)
    own = lax.all_to_all(packed, ("xh", "z"), 0, 0, tiled=True)
    other = lax.ppermute(own, "core", [(0, 1), (1, 0)])
    return jnp.transpose(spectrum(own, other, ids, given, made), (2, 0, 1))


def solution(mesh):
    split = jax.sharding.Mesh(mesh.devices.reshape(8, 2, 2, 4, 2), ("z", "xh", "core", "y", "xl"))
    time, dish = ("z", "xh", "core"), ("y", "xl")
    return jax.shard_map(
        steps,
        mesh=split,
        in_specs=(P(None, dish, time), P(None, dish), P(time)),
        out_specs=P(dish, None, time),
        check_vma=False,
    )
```

```python
import functools
import math

import jax
import jax.numpy as jnp
import numpy as np
from jax import lax
from jax.experimental import pallas as pl
from jax.experimental.pallas import tpu as pltpu
from jax.sharding import PartitionSpec as P


PH = 1024
LAGS = 2048
SAMPLES = 131072
DISH_WAYS = 8
TM_WAYS = 32
CHIPS = 16
HALF = SAMPLES // 2 // 128
LOCAL = SAMPLES // TM_WAYS
GRAIN = 128
PER_BLOCK = LOCAL // GRAIN
SIDE = GRAIN // 2
SPAN = LAGS // GRAIN
BINS = PH // TM_WAYS
FREQS = LAGS // DISH_WAYS
SLOTS = 96
GROUP = 16
VISITS = 8
ROWS = 2 * PER_BLOCK + VISITS
SCALE = 1.0 / math.sqrt(LAGS * SAMPLES / PH)

F32 = jnp.float32
BF16 = jnp.bfloat16


def dot(a, b, dims=(((1,), (0,)), ((), ()))):
    return lax.dot_general(a, b, dims, preferred_element_type=F32)


def hi_lo(value):
    hi = value.astype(BF16)
    return hi, (value - hi.astype(F32)).astype(BF16)


def tables():
    grain = np.arange(GRAIN)
    freq = np.arange(FREQS)
    angle = 2 * np.pi * np.outer(grain, freq) / LAGS
    base = np.concatenate([np.cos(angle), np.sin(angle)], 1).astype(np.float32)
    eighth = 2 * np.pi * np.outer(grain, np.arange(DISH_WAYS)) / DISH_WAYS
    turn = np.zeros((GRAIN, 128), np.float32)
    turn[:, :8] = np.cos(eighth)
    turn[:, 8:16] = np.sin(eighth)
    fine = 2 * np.pi * np.outer(grain, np.arange(2 * GRAIN)) / (2 * GRAIN)
    cos2, sin2 = np.cos(fine), np.sin(fine)
    fold2 = np.block([[cos2, sin2], [sin2, -cos2]]).astype(np.float32)
    step2 = np.block([[cos2, -sin2], [sin2, cos2]]).astype(np.float32)
    sides = np.concatenate([np.arange(k, k + SIDE) for k in (0, GRAIN, SIDE, GRAIN + SIDE)])
    fold2, step2 = fold2[sides], step2[sides]
    keep = (grain >= 1)[None, :] / (2.0 * GRAIN)
    back = np.block([[cos2.T * keep, -sin2.T * keep], [sin2.T * keep, cos2.T * keep]])
    sixteenth = 2 * np.pi * np.outer(np.arange(SPAN), freq) / SPAN
    phase = np.concatenate([np.cos(sixteenth), np.sin(sixteenth)], 1).astype(np.float32)
    fine = np.pi * np.outer(np.arange(2 * SPAN), freq) / SPAN
    start = np.concatenate([np.cos(fine), np.sin(fine)], 1).astype(np.float32)
    return {
        "base": jnp.asarray(base),
        "turn": jnp.asarray(turn),
        "fold2": jnp.asarray(fold2).astype(BF16),
        "step2": jnp.asarray(step2).astype(BF16),
        "back": jnp.asarray(back.astype(np.float32)).astype(BF16),
        "phase": jnp.asarray(phase),
        "start": jnp.asarray(start),
    }


PIECES = [slice(k % 4 * (LOCAL // 4), k % 4 * (LOCAL // 4) + LOCAL // 4) for k in range(8)]


def front_kernel(
    volts_hbm, weights_hbm, bins_hbm, beam_ref, visit_ref, volts_s, weights_s, bins_s, time_s, row_s, sems
):
    parts = [(volts_hbm.at[k // 4, :, at], volts_s.at[k // 4, :, at]) for k, at in enumerate(PIECES)]
    parts += [(bins_hbm, bins_s), (weights_hbm, weights_s)]
    copies = [
        pltpu.make_async_copy(source, target, sems.at[k]) for k, (source, target) in enumerate(parts)
    ]
    for copy in copies:
        copy.start()
    for copy in copies:
        copy.wait()
    weights = weights_s[...]
    first = dot(weights, volts_s[0])
    second = dot(weights, volts_s[1])
    real = first[0:1] - second[1:2]
    imag = first[1:2] + second[0:1]
    for row in range(PER_BLOCK):
        part = slice(row * GRAIN, (row + 1) * GRAIN)
        beam_ref[0, row : row + 1, :] = real[:, part]
        beam_ref[0, PER_BLOCK + row : PER_BLOCK + row + 1, :] = imag[:, part]
    make_visits(bins_s, visit_ref, time_s, row_s)
    rows = beam_ref[0]
    for way in range(1, DISH_WAYS):
        beam_ref[way] = rows


def pair_at(place):
    return 8 * (place & 1) + 2 * ((place >> 1) & 3) + (place >> 3)


def pack_kernel(parts_ref, visit_ref, out_ref):
    total = parts_ref[0]
    for way in range(1, DISH_WAYS):
        total = total + parts_ref[way]
    real, imag = total[:PER_BLOCK], total[PER_BLOCK:]
    early = lax.broadcasted_iota(jnp.int32, (PER_BLOCK, GRAIN), 1) < SIDE
    early_side = jnp.where(early, real, pltpu.roll(imag, SIDE, 1))
    late_side = jnp.where(early, pltpu.roll(real, SIDE, 1), imag)
    rows = jnp.concatenate([early_side, late_side], 0).astype(BF16)
    for chip in range(CHIPS):
        out_ref[chip, : 2 * PER_BLOCK, :] = rows
        out_ref[chip, 2 * PER_BLOCK :, :] = visit_ref[pair_at(chip)]


def coded_times(shape):
    row = lax.broadcasted_iota(jnp.int32, shape, 0)
    lane = lax.broadcasted_iota(jnp.int32, shape, 1)
    return (lane + 128).astype(F32) * two_to(row)


def triangle(count, strict):
    row = lax.broadcasted_iota(jnp.int32, (count, count), 0)
    column = lax.broadcasted_iota(jnp.int32, (count, count), 1)
    return jnp.where(row < column if strict else row <= column, 1.0, 0.0).astype(BF16)


def make_visits(bins_ref, out_ref, time_s, row_s):
    bins = bins_ref[...]
    shape = (PER_BLOCK, GRAIN)
    row = lax.broadcasted_iota(jnp.int32, shape, 0)
    lane = lax.broadcasted_iota(jnp.int32, shape, 1)
    rolled = pltpu.roll(bins, 1, 1)
    before = jnp.where(lane == 0, pltpu.roll(rolled, 1, 0), rolled)
    later = row + lane > 0
    enters = later & (bins != before)
    wraps = jnp.where(later & (bins < before), 1.0, 0.0).astype(BF16)
    in_row = dot(wraps, triangle(GRAIN, False))
    ends = jnp.broadcast_to(in_row[:, GRAIN - 1 :], shape).astype(BF16)
    above = dot(triangle(PER_BLOCK, True), ends, (((0,), (0,)), ((), ())))
    step = bins + PH * (in_row + above).astype(jnp.int32)
    high = jnp.where(enters, step >> 7, -1).astype(F32)
    low = (step & 127).astype(F32)
    times = coded_times(shape)
    high_iota = lax.broadcasted_iota(jnp.int32, (48, GRAIN), 0)
    high_rows = high_iota.astype(F32).astype(BF16)
    low_rows = lax.broadcasted_iota(jnp.int32, (GRAIN, GRAIN), 0).astype(F32).astype(BF16)
    zero, one = jnp.zeros((), BF16), jnp.ones((), BF16)
    late = jnp.where(lax.broadcasted_iota(jnp.int32, (48, GRAIN), 1) >= SIDE, 1.0, 0.0).astype(BF16)

    def spread(value, k, count):
        tile = jnp.broadcast_to(value[k : k + 1, :], (16, GRAIN)).astype(BF16)
        return jnp.concatenate([tile] * (count // 16), 0)

    found = jnp.zeros((96, GRAIN), F32)
    for pair in range(PER_BLOCK // 2):
        left, right = [], []
        for k in (2 * pair, 2 * pair + 1):
            here = spread(high, k, 48) == high_rows
            coded = jnp.where(here, spread(times, k, 48), zero)
            left.append(jnp.concatenate([coded, jnp.where(here, late + jnp.full((), 2 * k, BF16), zero)], 0))
            right.append(jnp.where(spread(low, k, GRAIN) == low_rows, one, zero))
        left = jnp.concatenate(left, 1)
        right = jnp.concatenate(right, 1)
        found = found + dot(left, right, (((1,), (1,)), ((), ())))
    place = high_iota * GRAIN + lax.broadcasted_iota(jnp.int32, (48, GRAIN), 1)
    past, ahead = place <= step[0:1, 0:1], place > step[PER_BLOCK - 1 :, GRAIN - 1 :]
    time_s[:48, :] = jnp.where(past, 2.0**-9, jnp.where(ahead, 2.0**23, found[:48]))
    row_s[:48, :] = jnp.where(past, 0.0, jnp.where(ahead, 64.0, found[48:]))
    time_s[48:, :] = jnp.full((24, GRAIN), 2.0**23, F32)
    row_s[48:, :] = jnp.full((24, GRAIN), 64.0, F32)
    lane = lax.broadcasted_iota(jnp.int32, (VISITS, GRAIN), 1)
    for eighth in range(8):
        now, then = pl.ds(eighth, VISITS, stride=8), pl.ds(eighth + 1, VISITS, stride=8)
        time, rows = time_s[now, :], row_s[now, :]
        next_time, next_rows = time_s[then, :], row_s[then, :]
        even = jnp.where(lane == 65, pltpu.roll(rows, 65, 1), time)
        even = jnp.where(lane == 66, pltpu.roll(rows, 34, 1), even)
        even = jnp.where(lane == 67, pltpu.roll(rows, 3, 1), even)
        odd = jnp.where(lane == 64, pltpu.roll(next_time, 64, 1), pltpu.roll(time, 64, 1))
        odd = jnp.where(lane == 65, pltpu.roll(rows, 1, 1), odd)
        odd = jnp.where(lane == 66, pltpu.roll(rows, 98, 1), odd)
        odd = jnp.where(lane == 67, pltpu.roll(next_rows, 67, 1), odd)
        out_ref[2 * eighth] = even.astype(BF16)
        out_ref[2 * eighth + 1] = odd.astype(BF16)


def two_to(exponent):
    value = jnp.full(jnp.shape(exponent), 2.0**-16, F32)
    for bit in range(6):
        value = value * jnp.where((exponent >> bit) & 1 == 1, float(2 ** (2**bit)), 1.0)
    return value


def table_kernel(
    ids, base_ref, turn_ref, fold2_ref, start_ref, back_ref, fold_ref, step_ref, short_ref, phases_ref, side_ref, last_s
):
    _, dish, _ = ids()
    lane = lax.broadcasted_iota(jnp.int32, (GRAIN, 128), 1)
    turn = turn_ref[...]
    cos8 = jnp.sum(jnp.where(lane == dish, turn, 0.0), axis=1, keepdims=True)
    sin8 = jnp.sum(jnp.where(lane == dish + 8, turn, 0.0), axis=1, keepdims=True)
    cos0, sin0 = base_ref[:, :FREQS], base_ref[:, FREQS:]
    cos_f, sin_f = cos0 * cos8 - sin0 * sin8, sin0 * cos8 + cos0 * sin8
    cosine, cosine_lo = hi_lo(cos_f)
    sine, sine_lo = hi_lo(sin_f)
    for side in range(2):
        part = slice(side * SIDE, side * SIDE + SIDE)
        reals = slice(side * GRAIN, side * GRAIN + SIDE)
        imags = slice(side * GRAIN + SIDE, side * GRAIN + GRAIN)
        fold_ref[reals, :FREQS] = cosine[part]
        fold_ref[reals, FREQS : 2 * FREQS] = sine[part]
        fold_ref[imags, :FREQS] = sine[part]
        fold_ref[imags, FREQS : 2 * FREQS] = -cosine[part]
        for k, (c, s) in enumerate(((cosine, sine), (cosine_lo, sine_lo))):
            step_ref[k, reals, :FREQS] = c[part]
            step_ref[k, reals, FREQS:] = -s[part]
            step_ref[k, imags, :FREQS] = s[part]
            step_ref[k, imags, FREQS:] = c[part]
    fold_ref[:, 2 * FREQS :] = fold2_ref[...]
    cos_side, sin_side = cos_f[SIDE : SIDE + 1], sin_f[SIDE : SIDE + 1]
    side_real = cos_f[:SIDE] * cos_side + sin_f[:SIDE] * sin_side
    side_imag = cos_f[:SIDE] * sin_side - sin_f[:SIDE] * cos_side
    side_ref[:SIDE, :FREQS] = side_real.astype(BF16)
    side_ref[:SIDE, FREQS:] = side_imag.astype(BF16)
    side_ref[SIDE:, :FREQS] = -side_imag.astype(BF16)
    side_ref[SIDE:, FREQS:] = side_real.astype(BF16)
    last_s[:GRAIN, :FREQS] = cosine
    last_s[:GRAIN, FREQS:] = sine
    last_s[GRAIN:, :FREQS] = -sine
    last_s[GRAIN:, FREQS:] = cosine
    short_ref[...] = dot(back_ref[...], last_s[...]).astype(BF16)
    phases_ref[...] = jnp.zeros(phases_ref.shape, BF16)
    hi, lo = hi_lo(start_ref[...])
    phases_ref[: 2 * SPAN, :] = hi
    phases_ref[2 * SPAN : 4 * SPAN, :] = lo


def beam_rows(ref, first, last):
    rows = [
        jnp.concatenate([ref[chip, :PER_BLOCK, :], ref[chip, PER_BLOCK : 2 * PER_BLOCK, :]], 1)
        for chip in range(first, last)
    ]
    return jnp.concatenate(rows, 0)


def side_rows(ref, side):
    part = slice(side * PER_BLOCK, side * PER_BLOCK + PER_BLOCK)
    return jnp.concatenate([ref[chip, part, :] for chip in range(CHIPS)], 0)


def swap_sides(odd, early, late):
    return jnp.concatenate([jnp.where(odd > 0.0, late, early), jnp.where(odd > 0.0, early, late)], 1)


def transform(ref, step_ref, phase_ref, z_ref, fine):
    cos16, sin16 = phase_ref[:, :FREQS], phase_ref[:, FREQS:]
    cos_rows = jnp.concatenate([cos16] * (128 // SPAN), 0)
    sin_rows = jnp.concatenate([sin16] * (128 // SPAN), 0)
    for tile in range(HALF // 128):
        rows = slice(tile * 128, tile * 128 + 128)
        beam = beam_rows(ref, 4 * tile, 4 * tile + 4)
        both = dot(beam, step_ref[0])
        if fine:
            both = both + dot(beam, step_ref[1])
        real, imag = both[:, :FREQS], both[:, FREQS:]
        z_ref[rows, :FREQS] = (real * cos_rows + imag * sin_rows).astype(BF16)
        z_ref[rows, FREQS:] = (imag * cos_rows - real * sin_rows).astype(BF16)


def plan_half(ref, core, before):
    times = jnp.concatenate([ref[chip, 2 * PER_BLOCK :, :].astype(F32) for chip in range(CHIPS)], 0).astype(BF16)
    row = lax.broadcasted_iota(jnp.int32, (8, 128), 0)
    lane = lax.broadcasted_iota(jnp.int32, (8, 128), 1)
    wanted = jnp.where(row == 0, BINS * core, jnp.where(row == 1, BINS * core + BINS, core + 63 + row))
    info = dot(jnp.where(lane == wanted, 1.0, 0.0).astype(BF16), times, (((1,), (1,)), ((), ())))
    start, end, first, last = (info[k : k + 1, :] for k in range(4))
    sides = jnp.minimum(last, float(2 * PER_BLOCK - 1)) - first
    grains = jnp.where(end > start, jnp.floor(sides * 0.5) + 1.0, 0.0)
    earlier = dot(jnp.broadcast_to(grains, (8, 128)).astype(BF16), triangle(128, True))[0:1, :] + before
    return times, end, first, grains, earlier, earlier[:, 127:] + grains[:, 127:]


def slots_half(slot_0, plan, ref):
    times, end, first, grains, earlier, _ = plan
    slot = lax.broadcasted_iota(jnp.int32, (128, 128), 0).astype(F32) + slot_0
    visit = lax.broadcasted_iota(jnp.int32, (SLOTS, 128), 1)
    mine = (slot >= earlier) & (slot < earlier + grains)
    starts = dot(times, jnp.where(mine, 1.0, 0.0).astype(BF16), (((0,), (1,)), ((), ())))
    slot, mine = slot[:SLOTS], mine[:SLOTS]
    place = ((visit >> 3) * (2 * PER_BLOCK) + 1).astype(F32) + first + 2.0 * (slot - earlier)
    place = jnp.sum(jnp.where(mine, place, 0.0), axis=1, keepdims=True) - 1.0
    ends = jnp.sum(jnp.where(mine, jnp.broadcast_to(end, (SLOTS, 128)), 0.0), axis=1, keepdims=True)
    places = lax.broadcasted_iota(jnp.int32, (SLOTS, HALF), 1).astype(F32)
    whole = jnp.where(place < 0.0, -4.0, jnp.floor(place * 0.5))
    odd = jnp.where(place < 0.0, 0.0, place - 2.0 * whole)
    early = dot(jnp.where(places == whole + odd, 1.0, 0.0).astype(BF16), side_rows(ref, 0))
    late = dot(jnp.where(places == whole, 1.0, 0.0).astype(BF16), side_rows(ref, 1))
    return place, ends, starts, swap_sides(odd, early, late)


def half_kernel(ids, own_ref, step_ref, phase_ref, z_ref, total_ref, place_ref, ends_ref, starts_ref, gbeam_ref):
    _, _, core = ids()
    plan = plan_half(own_ref, core, jnp.zeros((1, 1), F32))
    place, ends, starts, beam = slots_half(jnp.float32(0.0), plan, own_ref)
    total_ref[...] = jnp.broadcast_to(plan[-1], (8, 128))
    place_ref[...] = jnp.broadcast_to(place, (SLOTS, 128))
    ends_ref[...] = jnp.broadcast_to(ends, (SLOTS, 128))
    starts_ref[...] = starts
    gbeam_ref[...] = beam
    transform(own_ref, step_ref, phase_ref, z_ref, True)


def grain_row(which):
    place = lax.broadcasted_iota(jnp.int32, (8, HALF), 1)
    grain = (2 * pair_at(place >> 5) + which) * PER_BLOCK + (place & (PER_BLOCK - 1))
    return grain.astype(F32)[0:1, :]


def spectrum_kernel(
    ids,
    own_ref, other_ref, z_ref, total_ref, place_ref, ends_ref, starts_ref, gbeam_ref,
    fold_ref, step_ref, short_ref, phases_ref, side_ref, step2_ref, phase_ref,
    out_ref,
    z_s, gdft_s, gstep_s, gbeam_s, gtime_s, gstart_s, acc_s,
):
    _, _, core = ids()
    before = total_ref[0:1, 0:1]
    other_plan = plan_half(other_ref, core, before)
    count = jnp.max(other_plan[-1]).astype(jnp.int32)
    transform(other_ref, step_ref, phase_ref, z_s, False)
    acc_s[...] = jnp.zeros(acc_s.shape, F32)
    own_grains = jnp.broadcast_to(grain_row(core), (SLOTS, HALF))
    other_grains = jnp.broadcast_to(grain_row(1 - core), (SLOTS, HALF))
    lane_iota = lax.broadcasted_iota(jnp.int32, (SLOTS, 128), 1)

    def fold_batch(batch, mine):
        first = (batch * SLOTS).astype(F32)
        more = slots_half(first, other_plan, other_ref)
        is_mine = mine[0] >= 0.0
        place = jnp.where(is_mine, mine[0], more[0]).astype(jnp.int32)
        which = jnp.where(is_mine, core, 1 - core)
        side = place & (2 * PER_BLOCK - 1)
        in_block, odd = side >> 1, (side & 1).astype(F32)
        grain = ((2 * pair_at(place >> 6) + which) * PER_BLOCK + in_block).astype(F32)
        here = mine[3] + more[3]
        ends = mine[1] + more[1]
        for k in range(2):
            at = jnp.broadcast_to(side + k, (SLOTS, GRAIN))
            times = (128 + (at & 1) * SIDE + (lane_iota & (SIDE - 1))).astype(F32) * two_to(at >> 1)
            part = slice(k * GRAIN, k * GRAIN + GRAIN)
            gtime_s[:, part] = times
            gbeam_s[:, part] = jnp.where(times < ends, here[:, part], 0.0)
        starts = mine[2] + more[2]
        starts = jnp.where(core == 0, starts[:BINS], starts[BINS : 2 * BINS])
        for group in range(SLOTS // GROUP):
            gstart_s[group] = starts if group == 0 else pltpu.roll(starts, 128 - group * GROUP, 1)
        dft = jnp.zeros((SLOTS, 2 * FREQS), F32)
        early, late, gone = (jnp.zeros((SLOTS, GRAIN), F32) for _ in range(3))
        for grains, z, ref in ((own_grains, z_ref, own_ref), (other_grains, z_s, other_ref)):
            window = (grains >= grain) & (grains < grain + float(SPAN))
            dft = dft + dot(jnp.where(window, 1.0, 0.0).astype(BF16), z[...])
            then = grains == grain + float(SPAN)
            early_pick = jnp.where(grains == grain + float(SPAN) + odd, 1.0, 0.0).astype(BF16)
            late_pick = jnp.where(then, 1.0, 0.0).astype(BF16)
            gone_pick = jnp.where(then, odd, jnp.where(grains == grain, -odd, 0.0)).astype(BF16)
            early = early + dot(early_pick, side_rows(ref, 0))
            late = late + dot(late_pick, side_rows(ref, 1))
            gone = gone + dot(gone_pick, side_rows(ref, 0))
        ahead = swap_sides(odd, early, late)
        moved = dot(gone.astype(BF16), side_ref[...])
        offset = side & (2 * SPAN - 1)
        turner = jnp.where((lane_iota == offset) | (lane_iota == offset + 2 * SPAN), 1.0, 0.0)
        turned = dot(turner.astype(BF16), phases_ref[...])
        real, imag = dft[:, :FREQS], dft[:, FREQS:]
        cos_g, sin_g = turned[:, :FREQS], turned[:, FREQS:]
        step = dot((ahead - here).astype(BF16), step2_ref[...])
        for ref, real, imag in (
            (gdft_s, real * cos_g - imag * sin_g + moved[:, :FREQS], imag * cos_g + real * sin_g + moved[:, FREQS:]),
            (gstep_s, step[:, :FREQS], step[:, FREQS:]),
        ):
            ref[:, :FREQS] = real
            ref[:, FREQS : 2 * FREQS] = imag - real
            ref[:, 2 * FREQS :] = real + imag

        def fold(slot, size):
            rows = pl.ds(pl.multiple_of(slot, 8), size)
            beam8, time8, start8 = gbeam_s[rows, :], gtime_s[rows, :], gstart_s[slot // GROUP]
            dft8, step8 = gdft_s[rows, :], gstep_s[rows, :]
            left = []
            for k in range(size):
                start = start8[:, k : k + 1]
                sides = [
                    jnp.where(time8[k : k + 1, at : at + GRAIN] >= start, beam8[k : k + 1, at : at + GRAIN], 0.0)
                    for at in (0, GRAIN)
                ]
                left.append(jnp.concatenate(sides, 1))
            left = jnp.concatenate(left, 0).astype(BF16)
            for part, factor in ((0, dft8), (1, step8)):
                folded = dot(left, fold_ref[:, part * 2 * FREQS : part * 2 * FREQS + 2 * FREQS])
                sums = [acc_s[:, k * FREQS : k * FREQS + FREQS] for k in range(3 * part, 3 * part + 3)]
                for k in range(size):
                    rows = slice(k * BINS, k * BINS + BINS)
                    real, imag = folded[rows, :FREQS], folded[rows, FREQS:]
                    for n, value in enumerate((real + imag, real, imag)):
                        sums[n] = sums[n] + value * factor[k : k + 1, n * FREQS : n * FREQS + FREQS]
                for n in range(3):
                    acc_s[:, (3 * part + n) * FREQS : (3 * part + n + 1) * FREQS] = sums[n]

        def pair_step(pair, inner):
            fold(2 * GROUP * pair, GROUP)
            fold(2 * GROUP * pair + GROUP, GROUP)
            return inner

        def one_step(_, inner):
            fold(pairs * 2 * GROUP, GROUP)
            return inner

        def half_step(_, inner):
            fold(pairs * 2 * GROUP + rest // 2 * GROUP, GROUP // 2)
            return inner

        eights = (jnp.minimum(count - batch * SLOTS, SLOTS) + 7) // 8
        pairs = eights // 4
        rest = eights - 4 * pairs
        lax.fori_loop(0, pairs, pair_step, 0)
        lax.fori_loop(0, rest // 2, one_step, 0)
        lax.fori_loop(0, rest % 2, half_step, 0)

    fold_batch(jnp.int32(0), (place_ref[:, 0:1], ends_ref[:, 0:1], starts_ref[...], gbeam_ref[...]))

    def batch_step(batch, carry):
        own_plan = plan_half(own_ref, core, jnp.zeros((1, 1), F32))
        fold_batch(batch, slots_half((batch * SLOTS).astype(F32), own_plan, own_ref))
        return carry

    lax.fori_loop(1, (count + SLOTS - 1) // SLOTS, batch_step, 0)
    since = acc_s[...]
    each = since - jnp.concatenate([since[1:], jnp.zeros((1, 6 * FREQS), F32)], 0)
    both, real, imag, both2, real2, imag2 = (each[:, k * FREQS : k * FREQS + FREQS] for k in range(6))
    short = dot(jnp.concatenate([both2 - imag2, both2 + real2], 1).astype(BF16), short_ref[...])
    out_ref[0] = (both - imag + short[:, :FREQS]) * SCALE
    out_ref[1] = (both + real + short[:, FREQS:]) * SCALE


def near(*values):
    return [pltpu.with_memory_space_constraint(v, pltpu.VMEM) for v in values]


def call(kernel, outs, values, scratch=(), mib=8, us=1.0):
    one = not isinstance(outs, (tuple, list))
    space = pl.BlockSpec(memory_space=pltpu.VMEM)
    return pl.pallas_call(
        kernel,
        out_shape=outs if one else tuple(outs),
        in_specs=[space] * len(values),
        out_specs=space if one else (space,) * len(outs),
        scratch_shapes=list(scratch),
        compiler_params=pltpu.CompilerParams(vmem_limit_bytes=mib << 20),
        cost_estimate=pl.CostEstimate(flops=int(us * 5e8), bytes_accessed=1 << 20, transcendentals=0),
    )(*near(*values))


HALF_Z = pltpu.VMEM((HALF, 2 * FREQS), BF16)


def make_tables(ids):
    given = tables()
    made = call(
        functools.partial(table_kernel, ids),
        (
            pltpu.VMEM((2 * GRAIN, 4 * FREQS), BF16),
            pltpu.VMEM((2, 2 * GRAIN, 2 * FREQS), BF16),
            pltpu.VMEM((2 * FREQS, 2 * FREQS), BF16),
            pltpu.VMEM((128, 2 * FREQS), BF16),
            pltpu.VMEM((GRAIN, 2 * FREQS), BF16),
        ),
        [given[k] for k in ("base", "turn", "fold2", "start", "back")],
        [pltpu.VMEM((2 * GRAIN, 2 * FREQS), BF16)],
        us=3.0,
    )
    return given, made


def spectrum(own, other, ids, given, made):
    fold, step, short, phases, side = made
    phase = given["phase"]
    half = call(
        functools.partial(half_kernel, ids),
        (
            HALF_Z,
            pltpu.VMEM((8, 128), F32),
            pltpu.VMEM((SLOTS, 128), F32),
            pltpu.VMEM((SLOTS, 128), F32),
            pltpu.VMEM((128, 128), F32),
            pltpu.VMEM((SLOTS, 2 * GRAIN), F32),
        ),
        (own, step, phase),
        us=1.0,
    )
    scratch = [
        HALF_Z,
        pltpu.VMEM((SLOTS, 3 * FREQS), F32),
        pltpu.VMEM((SLOTS, 3 * FREQS), F32),
        pltpu.VMEM((SLOTS, 2 * GRAIN), F32),
        pltpu.VMEM((SLOTS, 2 * GRAIN), F32),
        pltpu.VMEM((SLOTS // GROUP, BINS, 128), F32),
        pltpu.VMEM((BINS, 6 * FREQS), F32),
    ]
    return call(
        functools.partial(spectrum_kernel, ids),
        jax.ShapeDtypeStruct((2, BINS, FREQS), F32),
        (own, other, *half, fold, step, short, phases, side, given["step2"], phase),
        scratch,
        mib=16,
        us=5.0,
    )


def front(voltages, beam_weights, bins):
    far = pl.BlockSpec(memory_space=pltpu.HBM)
    close = pl.BlockSpec(memory_space=pltpu.VMEM)
    return pl.pallas_call(
        front_kernel,
        out_shape=(
            pltpu.VMEM((DISH_WAYS, 2 * PER_BLOCK, GRAIN), F32),
            pltpu.VMEM((CHIPS, VISITS, GRAIN), BF16),
        ),
        in_specs=[far] * 3,
        out_specs=(close, close),
        scratch_shapes=[
            pltpu.VMEM(voltages.shape, BF16),
            pltpu.VMEM(beam_weights.shape, BF16),
            pltpu.VMEM(bins.shape, jnp.int32),
            pltpu.VMEM((72, GRAIN), F32),
            pltpu.VMEM((72, GRAIN), F32),
            pltpu.SemaphoreType.DMA((len(PIECES) + 2,)),
        ],
        compiler_params=pltpu.CompilerParams(vmem_limit_bytes=8 << 20),
        cost_estimate=pl.CostEstimate(flops=1 << 20, bytes_accessed=1 << 20, transcendentals=0),
        name="front",
    )(*(pltpu.with_memory_space_constraint(v, pltpu.HBM) for v in (voltages, beam_weights, bins)))


def steps(voltages, beam_weights, phase_bins):
    def ids():
        core = lax.axis_index("core")
        z = lax.axis_index("zh") * 4 + lax.axis_index("zl")
        owner = (z * 2 + lax.axis_index("xh")) * 2 + core
        return owner, lax.axis_index("y") * 2 + lax.axis_index("xl"), core

    given, made = make_tables(ids)
    partial_beam, visits = front(voltages, beam_weights, phase_bins.reshape(PER_BLOCK, GRAIN))
    parts = lax.all_to_all(partial_beam, ("xl", "y"), 0, 0, tiled=True)
    packed = call(pack_kernel, pltpu.VMEM((CHIPS, ROWS, GRAIN), BF16), (parts, visits), us=0.3)
    own = lax.all_to_all(packed, ("xh", "zl", "zh"), 0, 0, tiled=True)
    other = lax.ppermute(own, "core", [(0, 1), (1, 0)])
    return jnp.transpose(spectrum(own, other, ids, given, made), (2, 0, 1))


def solution(mesh):
    split = jax.sharding.Mesh(mesh.devices.reshape(2, 4, 2, 2, 4, 2), ("zh", "zl", "xh", "core", "y", "xl"))
    time, dish = ("zh", "zl", "xh", "core"), ("y", "xl")
    return jax.shard_map(
        steps,
        mesh=split,
        in_specs=(P(None, dish, time), P(None, dish), P(time)),
        out_specs=P(dish, None, time),
        check_vma=False,
    )
```

```python
import functools
import math

import jax
import jax.numpy as jnp
import numpy as np
from jax import lax
from jax.experimental import pallas as pl
from jax.experimental.pallas import tpu as pltpu
from jax.sharding import PartitionSpec as P


PH = 1024
LAGS = 2048
SAMPLES = 131072
DISH_WAYS = 8
TM_WAYS = 32
CHIPS = 16
HALF = SAMPLES // 2 // 128
LOCAL = SAMPLES // TM_WAYS
GRAIN = 128
PER_BLOCK = LOCAL // GRAIN
SIDE = GRAIN // 2
SPAN = LAGS // GRAIN
BINS = PH // TM_WAYS
FREQS = LAGS // DISH_WAYS
SLOTS = 96
GROUP = 16
VISITS = 8
ROWS = 2 * PER_BLOCK + VISITS
SCALE = 1.0 / math.sqrt(LAGS * SAMPLES / PH)

F32 = jnp.float32
BF16 = jnp.bfloat16


def dot(a, b, dims=(((1,), (0,)), ((), ()))):
    return lax.dot_general(a, b, dims, preferred_element_type=F32)


def hi_lo(value):
    hi = value.astype(BF16)
    return hi, (value - hi.astype(F32)).astype(BF16)


def tables():
    grain = np.arange(GRAIN)
    freq = np.arange(FREQS)
    angle = 2 * np.pi * np.outer(grain, freq) / LAGS
    base = np.concatenate([np.cos(angle), np.sin(angle)], 1).astype(np.float32)
    eighth = 2 * np.pi * np.outer(grain, np.arange(DISH_WAYS)) / DISH_WAYS
    turn = np.zeros((GRAIN, 128), np.float32)
    turn[:, :8] = np.cos(eighth)
    turn[:, 8:16] = np.sin(eighth)
    fine = 2 * np.pi * np.outer(grain, np.arange(2 * GRAIN)) / (2 * GRAIN)
    cos2, sin2 = np.cos(fine), np.sin(fine)
    fold2 = np.block([[cos2, sin2], [sin2, -cos2]]).astype(np.float32)
    step2 = np.block([[cos2, -sin2], [sin2, cos2]]).astype(np.float32)
    sides = np.concatenate([np.arange(k, k + SIDE) for k in (0, GRAIN, SIDE, GRAIN + SIDE)])
    fold2, step2 = fold2[sides], step2[sides]
    keep = (grain >= 1)[None, :] / (2.0 * GRAIN)
    back = np.block([[cos2.T * keep, -sin2.T * keep], [sin2.T * keep, cos2.T * keep]])
    sixteenth = 2 * np.pi * np.outer(np.arange(SPAN), freq) / SPAN
    phase = np.concatenate([np.cos(sixteenth), np.sin(sixteenth)], 1).astype(np.float32)
    fine = np.pi * np.outer(np.arange(2 * SPAN), freq) / SPAN
    start = np.concatenate([np.cos(fine), np.sin(fine)], 1).astype(np.float32)
    return {
        "base": jnp.asarray(base),
        "turn": jnp.asarray(turn),
        "fold2": jnp.asarray(fold2).astype(BF16),
        "step2": jnp.asarray(step2).astype(BF16),
        "back": jnp.asarray(back.astype(np.float32)).astype(BF16),
        "phase": jnp.asarray(phase),
        "start": jnp.asarray(start),
    }


PIECES = [slice(k % 4 * (LOCAL // 4), k % 4 * (LOCAL // 4) + LOCAL // 4) for k in range(8)]


def front_kernel(
    volts_hbm, weights_hbm, bins_hbm, beam_ref, visit_ref, volts_s, weights_s, bins_s, time_s, row_s, sems
):
    parts = [(volts_hbm.at[k // 4, :, at], volts_s.at[k // 4, :, at]) for k, at in enumerate(PIECES)]
    parts += [(bins_hbm, bins_s), (weights_hbm, weights_s)]
    copies = [
        pltpu.make_async_copy(source, target, sems.at[k]) for k, (source, target) in enumerate(parts)
    ]
    for copy in copies:
        copy.start()
    for copy in copies:
        copy.wait()
    weights = weights_s[...]
    first = dot(weights, volts_s[0])
    second = dot(weights, volts_s[1])
    real = first[0:1] - second[1:2]
    imag = first[1:2] + second[0:1]
    for row in range(PER_BLOCK):
        part = slice(row * GRAIN, (row + 1) * GRAIN)
        beam_ref[0, row : row + 1, :] = real[:, part]
        beam_ref[0, PER_BLOCK + row : PER_BLOCK + row + 1, :] = imag[:, part]
    make_visits(bins_s, visit_ref, time_s, row_s)
    rows = beam_ref[0]
    for way in range(1, DISH_WAYS):
        beam_ref[way] = rows


def pair_at(place):
    return 2 * (place & 7) + (place >> 3)


def pack_kernel(parts_ref, visit_ref, out_ref):
    total = parts_ref[0]
    for way in range(1, DISH_WAYS):
        total = total + parts_ref[way]
    real, imag = total[:PER_BLOCK], total[PER_BLOCK:]
    early = lax.broadcasted_iota(jnp.int32, (PER_BLOCK, GRAIN), 1) < SIDE
    early_side = jnp.where(early, real, pltpu.roll(imag, SIDE, 1))
    late_side = jnp.where(early, pltpu.roll(real, SIDE, 1), imag)
    rows = jnp.concatenate([early_side, late_side], 0).astype(BF16)
    for chip in range(CHIPS):
        out_ref[chip, : 2 * PER_BLOCK, :] = rows
        out_ref[chip, 2 * PER_BLOCK :, :] = visit_ref[pair_at(chip)]


def coded_times(shape):
    row = lax.broadcasted_iota(jnp.int32, shape, 0)
    lane = lax.broadcasted_iota(jnp.int32, shape, 1)
    return (lane + 128).astype(F32) * two_to(row)


def triangle(count, strict):
    row = lax.broadcasted_iota(jnp.int32, (count, count), 0)
    column = lax.broadcasted_iota(jnp.int32, (count, count), 1)
    return jnp.where(row < column if strict else row <= column, 1.0, 0.0).astype(BF16)


def make_visits(bins_ref, out_ref, time_s, row_s):
    bins = bins_ref[...]
    shape = (PER_BLOCK, GRAIN)
    row = lax.broadcasted_iota(jnp.int32, shape, 0)
    lane = lax.broadcasted_iota(jnp.int32, shape, 1)
    rolled = pltpu.roll(bins, 1, 1)
    before = jnp.where(lane == 0, pltpu.roll(rolled, 1, 0), rolled)
    later = row + lane > 0
    enters = later & (bins != before)
    wraps = jnp.where(later & (bins < before), 1.0, 0.0).astype(BF16)
    in_row = dot(wraps, triangle(GRAIN, False))
    ends = jnp.broadcast_to(in_row[:, GRAIN - 1 :], shape).astype(BF16)
    above = dot(triangle(PER_BLOCK, True), ends, (((0,), (0,)), ((), ())))
    step = bins + PH * (in_row + above).astype(jnp.int32)
    high = jnp.where(enters, step >> 7, -1).astype(F32)
    low = (step & 127).astype(F32)
    times = coded_times(shape)
    high_iota = lax.broadcasted_iota(jnp.int32, (48, GRAIN), 0)
    high_rows = high_iota.astype(F32).astype(BF16)
    low_rows = lax.broadcasted_iota(jnp.int32, (GRAIN, GRAIN), 0).astype(F32).astype(BF16)
    zero, one = jnp.zeros((), BF16), jnp.ones((), BF16)
    late = jnp.where(lax.broadcasted_iota(jnp.int32, (48, GRAIN), 1) >= SIDE, 1.0, 0.0).astype(BF16)

    def spread(value, k, count):
        tile = jnp.broadcast_to(value[k : k + 1, :], (16, GRAIN)).astype(BF16)
        return jnp.concatenate([tile] * (count // 16), 0)

    found = jnp.zeros((96, GRAIN), F32)
    for pair in range(PER_BLOCK // 2):
        left, right = [], []
        for k in (2 * pair, 2 * pair + 1):
            here = spread(high, k, 48) == high_rows
            coded = jnp.where(here, spread(times, k, 48), zero)
            left.append(jnp.concatenate([coded, jnp.where(here, late + jnp.full((), 2 * k, BF16), zero)], 0))
            right.append(jnp.where(spread(low, k, GRAIN) == low_rows, one, zero))
        left = jnp.concatenate(left, 1)
        right = jnp.concatenate(right, 1)
        found = found + dot(left, right, (((1,), (1,)), ((), ())))
    place = high_iota * GRAIN + lax.broadcasted_iota(jnp.int32, (48, GRAIN), 1)
    past, ahead = place <= step[0:1, 0:1], place > step[PER_BLOCK - 1 :, GRAIN - 1 :]
    time_s[:48, :] = jnp.where(past, 2.0**-9, jnp.where(ahead, 2.0**23, found[:48]))
    row_s[:48, :] = jnp.where(past, 0.0, jnp.where(ahead, 64.0, found[48:]))
    time_s[48:, :] = jnp.full((24, GRAIN), 2.0**23, F32)
    row_s[48:, :] = jnp.full((24, GRAIN), 64.0, F32)
    lane = lax.broadcasted_iota(jnp.int32, (VISITS, GRAIN), 1)
    for eighth in range(8):
        now, then = pl.ds(eighth, VISITS, stride=8), pl.ds(eighth + 1, VISITS, stride=8)
        time, rows = time_s[now, :], row_s[now, :]
        next_time, next_rows = time_s[then, :], row_s[then, :]
        even = jnp.where(lane == 65, pltpu.roll(rows, 65, 1), time)
        even = jnp.where(lane == 66, pltpu.roll(rows, 34, 1), even)
        even = jnp.where(lane == 67, pltpu.roll(rows, 3, 1), even)
        odd = jnp.where(lane == 64, pltpu.roll(next_time, 64, 1), pltpu.roll(time, 64, 1))
        odd = jnp.where(lane == 65, pltpu.roll(rows, 1, 1), odd)
        odd = jnp.where(lane == 66, pltpu.roll(rows, 98, 1), odd)
        odd = jnp.where(lane == 67, pltpu.roll(next_rows, 67, 1), odd)
        out_ref[2 * eighth] = even.astype(BF16)
        out_ref[2 * eighth + 1] = odd.astype(BF16)


def two_to(exponent):
    value = jnp.full(jnp.shape(exponent), 2.0**-16, F32)
    for bit in range(6):
        value = value * jnp.where((exponent >> bit) & 1 == 1, float(2 ** (2**bit)), 1.0)
    return value


def table_kernel(
    ids,
    base_ref, turn_ref, fold2_ref, start_ref, back_ref, step2_in, phase_in,
    fold_ref, step_ref, short_ref, phases_ref, side_ref, step2_ref, phase_ref,
    last_s,
):
    step2_ref[...] = step2_in[...]
    phase_ref[...] = phase_in[...]
    _, dish, _ = ids()
    lane = lax.broadcasted_iota(jnp.int32, (GRAIN, 128), 1)
    turn = turn_ref[...]
    cos8 = jnp.sum(jnp.where(lane == dish, turn, 0.0), axis=1, keepdims=True)
    sin8 = jnp.sum(jnp.where(lane == dish + 8, turn, 0.0), axis=1, keepdims=True)
    cos0, sin0 = base_ref[:, :FREQS], base_ref[:, FREQS:]
    cos_f, sin_f = cos0 * cos8 - sin0 * sin8, sin0 * cos8 + cos0 * sin8
    cosine, cosine_lo = hi_lo(cos_f)
    sine, sine_lo = hi_lo(sin_f)
    for side in range(2):
        part = slice(side * SIDE, side * SIDE + SIDE)
        reals = slice(side * GRAIN, side * GRAIN + SIDE)
        imags = slice(side * GRAIN + SIDE, side * GRAIN + GRAIN)
        fold_ref[reals, :FREQS] = cosine[part]
        fold_ref[reals, FREQS : 2 * FREQS] = sine[part]
        fold_ref[imags, :FREQS] = sine[part]
        fold_ref[imags, FREQS : 2 * FREQS] = -cosine[part]
        for k, (c, s) in enumerate(((cosine, sine), (cosine_lo, sine_lo))):
            step_ref[k, reals, :FREQS] = c[part]
            step_ref[k, reals, FREQS:] = -s[part]
            step_ref[k, imags, :FREQS] = s[part]
            step_ref[k, imags, FREQS:] = c[part]
    fold_ref[:, 2 * FREQS :] = fold2_ref[...]
    cos_side, sin_side = cos_f[SIDE : SIDE + 1], sin_f[SIDE : SIDE + 1]
    side_real = cos_f[:SIDE] * cos_side + sin_f[:SIDE] * sin_side
    side_imag = cos_f[:SIDE] * sin_side - sin_f[:SIDE] * cos_side
    side_ref[:SIDE, :FREQS] = side_real.astype(BF16)
    side_ref[:SIDE, FREQS:] = side_imag.astype(BF16)
    side_ref[SIDE:, :FREQS] = -side_imag.astype(BF16)
    side_ref[SIDE:, FREQS:] = side_real.astype(BF16)
    last_s[:GRAIN, :FREQS] = cosine
    last_s[:GRAIN, FREQS:] = sine
    last_s[GRAIN:, :FREQS] = -sine
    last_s[GRAIN:, FREQS:] = cosine
    short_ref[...] = dot(back_ref[...], last_s[...]).astype(BF16)
    phases_ref[...] = jnp.zeros(phases_ref.shape, BF16)
    hi, lo = hi_lo(start_ref[...])
    phases_ref[: 2 * SPAN, :] = hi
    phases_ref[2 * SPAN : 4 * SPAN, :] = lo


def beam_rows(ref, first, last):
    rows = [
        jnp.concatenate([ref[chip, :PER_BLOCK, :], ref[chip, PER_BLOCK : 2 * PER_BLOCK, :]], 1)
        for chip in range(first, last)
    ]
    return jnp.concatenate(rows, 0)


def side_rows(ref, side):
    part = slice(side * PER_BLOCK, side * PER_BLOCK + PER_BLOCK)
    return jnp.concatenate([ref[chip, part, :] for chip in range(CHIPS)], 0)


def swap_sides(odd, early, late):
    return jnp.concatenate([jnp.where(odd > 0.0, late, early), jnp.where(odd > 0.0, early, late)], 1)


def transform(ref, step_ref, phase_ref, z_ref, fine):
    cos16, sin16 = phase_ref[:, :FREQS], phase_ref[:, FREQS:]
    cos_rows = jnp.concatenate([cos16] * (128 // SPAN), 0)
    sin_rows = jnp.concatenate([sin16] * (128 // SPAN), 0)
    for tile in range(HALF // 128):
        rows = slice(tile * 128, tile * 128 + 128)
        beam = beam_rows(ref, 4 * tile, 4 * tile + 4)
        both = dot(beam, step_ref[0])
        if fine:
            both = both + dot(beam, step_ref[1])
        real, imag = both[:, :FREQS], both[:, FREQS:]
        z_ref[rows, :FREQS] = (real * cos_rows + imag * sin_rows).astype(BF16)
        z_ref[rows, FREQS:] = (imag * cos_rows - real * sin_rows).astype(BF16)


def plan_half(ref, core, before):
    times = jnp.concatenate([ref[chip, 2 * PER_BLOCK :, :].astype(F32) for chip in range(CHIPS)], 0).astype(BF16)
    row = lax.broadcasted_iota(jnp.int32, (8, 128), 0)
    lane = lax.broadcasted_iota(jnp.int32, (8, 128), 1)
    wanted = jnp.where(row == 0, BINS * core, jnp.where(row == 1, BINS * core + BINS, core + 63 + row))
    info = dot(jnp.where(lane == wanted, 1.0, 0.0).astype(BF16), times, (((1,), (1,)), ((), ())))
    start, end, first, last = (info[k : k + 1, :] for k in range(4))
    sides = jnp.minimum(last, float(2 * PER_BLOCK - 1)) - first
    grains = jnp.where(end > start, jnp.floor(sides * 0.5) + 1.0, 0.0)
    earlier = dot(jnp.broadcast_to(grains, (8, 128)).astype(BF16), triangle(128, True))[0:1, :] + before
    return times, end, first, grains, earlier, earlier[:, 127:] + grains[:, 127:]


def slots_half(slot_0, plan, ref):
    times, end, first, grains, earlier, _ = plan
    slot = lax.broadcasted_iota(jnp.int32, (128, 128), 0).astype(F32) + slot_0
    visit = lax.broadcasted_iota(jnp.int32, (SLOTS, 128), 1)
    mine = (slot >= earlier) & (slot < earlier + grains)
    starts = dot(times, jnp.where(mine, 1.0, 0.0).astype(BF16), (((0,), (1,)), ((), ())))
    slot, mine = slot[:SLOTS], mine[:SLOTS]
    place = ((visit >> 3) * (2 * PER_BLOCK) + 1).astype(F32) + first + 2.0 * (slot - earlier)
    place = jnp.sum(jnp.where(mine, place, 0.0), axis=1, keepdims=True) - 1.0
    ends = jnp.sum(jnp.where(mine, jnp.broadcast_to(end, (SLOTS, 128)), 0.0), axis=1, keepdims=True)
    places = lax.broadcasted_iota(jnp.int32, (SLOTS, HALF), 1).astype(F32)
    whole = jnp.where(place < 0.0, -4.0, jnp.floor(place * 0.5))
    odd = jnp.where(place < 0.0, 0.0, place - 2.0 * whole)
    early = dot(jnp.where(places == whole + odd, 1.0, 0.0).astype(BF16), side_rows(ref, 0))
    late = dot(jnp.where(places == whole, 1.0, 0.0).astype(BF16), side_rows(ref, 1))
    return place, ends, starts, swap_sides(odd, early, late)


def half_kernel(ids, own_ref, step_ref, phase_ref, z_ref, total_ref, place_ref, ends_ref, starts_ref, gbeam_ref):
    _, _, core = ids()
    plan = plan_half(own_ref, core, jnp.zeros((1, 1), F32))
    place, ends, starts, beam = slots_half(jnp.float32(0.0), plan, own_ref)
    total_ref[...] = jnp.broadcast_to(plan[-1], (8, 128))
    place_ref[...] = jnp.broadcast_to(place, (SLOTS, 128))
    ends_ref[...] = jnp.broadcast_to(ends, (SLOTS, 128))
    starts_ref[...] = starts
    gbeam_ref[...] = beam
    transform(own_ref, step_ref, phase_ref, z_ref, True)


def grain_row(which):
    place = lax.broadcasted_iota(jnp.int32, (8, HALF), 1)
    grain = (2 * pair_at(place >> 5) + which) * PER_BLOCK + (place & (PER_BLOCK - 1))
    return grain.astype(F32)[0:1, :]


def spectrum_kernel(
    ids,
    own_ref, other_ref, z_ref, total_ref, place_ref, ends_ref, starts_ref, gbeam_ref,
    fold_ref, step_ref, short_ref, phases_ref, side_ref, step2_ref, phase_ref,
    out_ref,
    z_s, gdft_s, gstep_s, gbeam_s, gtime_s, gstart_s, acc_s,
):
    _, _, core = ids()
    before = total_ref[0:1, 0:1]
    other_plan = plan_half(other_ref, core, before)
    count = jnp.max(other_plan[-1]).astype(jnp.int32)
    transform(other_ref, step_ref, phase_ref, z_s, False)
    acc_s[...] = jnp.zeros(acc_s.shape, F32)
    own_grains = jnp.broadcast_to(grain_row(core), (SLOTS, HALF))
    other_grains = jnp.broadcast_to(grain_row(1 - core), (SLOTS, HALF))
    lane_iota = lax.broadcasted_iota(jnp.int32, (SLOTS, 128), 1)

    def fold_batch(batch, mine):
        first = (batch * SLOTS).astype(F32)
        more = slots_half(first, other_plan, other_ref)
        is_mine = mine[0] >= 0.0
        place = jnp.where(is_mine, mine[0], more[0]).astype(jnp.int32)
        which = jnp.where(is_mine, core, 1 - core)
        side = place & (2 * PER_BLOCK - 1)
        in_block, odd = side >> 1, (side & 1).astype(F32)
        grain = ((2 * pair_at(place >> 6) + which) * PER_BLOCK + in_block).astype(F32)
        here = mine[3] + more[3]
        ends = mine[1] + more[1]
        for k in range(2):
            at = jnp.broadcast_to(side + k, (SLOTS, GRAIN))
            times = (128 + (at & 1) * SIDE + (lane_iota & (SIDE - 1))).astype(F32) * two_to(at >> 1)
            part = slice(k * GRAIN, k * GRAIN + GRAIN)
            gtime_s[:, part] = times
            gbeam_s[:, part] = jnp.where(times < ends, here[:, part], 0.0)
        starts = mine[2] + more[2]
        starts = jnp.where(core == 0, starts[:BINS], starts[BINS : 2 * BINS])
        for group in range(SLOTS // GROUP):
            gstart_s[group] = starts if group == 0 else pltpu.roll(starts, 128 - group * GROUP, 1)
        dft = jnp.zeros((SLOTS, 2 * FREQS), F32)
        early, late, gone = (jnp.zeros((SLOTS, GRAIN), F32) for _ in range(3))
        for grains, z, ref in ((own_grains, z_ref, own_ref), (other_grains, z_s, other_ref)):
            window = (grains >= grain) & (grains < grain + float(SPAN))
            dft = dft + dot(jnp.where(window, 1.0, 0.0).astype(BF16), z[...])
            then = grains == grain + float(SPAN)
            early_pick = jnp.where(grains == grain + float(SPAN) + odd, 1.0, 0.0).astype(BF16)
            late_pick = jnp.where(then, 1.0, 0.0).astype(BF16)
            gone_pick = jnp.where(then, odd, jnp.where(grains == grain, -odd, 0.0)).astype(BF16)
            early = early + dot(early_pick, side_rows(ref, 0))
            late = late + dot(late_pick, side_rows(ref, 1))
            gone = gone + dot(gone_pick, side_rows(ref, 0))
        ahead = swap_sides(odd, early, late)
        moved = dot(gone.astype(BF16), side_ref[...])
        offset = side & (2 * SPAN - 1)
        turner = jnp.where((lane_iota == offset) | (lane_iota == offset + 2 * SPAN), 1.0, 0.0)
        turned = dot(turner.astype(BF16), phases_ref[...])
        real, imag = dft[:, :FREQS], dft[:, FREQS:]
        cos_g, sin_g = turned[:, :FREQS], turned[:, FREQS:]
        step = dot((ahead - here).astype(BF16), step2_ref[...])
        for ref, real, imag in (
            (gdft_s, real * cos_g - imag * sin_g + moved[:, :FREQS], imag * cos_g + real * sin_g + moved[:, FREQS:]),
            (gstep_s, step[:, :FREQS], step[:, FREQS:]),
        ):
            ref[:, :FREQS] = real
            ref[:, FREQS : 2 * FREQS] = imag - real
            ref[:, 2 * FREQS :] = real + imag

        def fold(slot, size):
            rows = pl.ds(pl.multiple_of(slot, 8), size)
            beam8, time8, start8 = gbeam_s[rows, :], gtime_s[rows, :], gstart_s[slot // GROUP]
            dft8, step8 = gdft_s[rows, :], gstep_s[rows, :]
            left = []
            for k in range(size):
                start = start8[:, k : k + 1]
                sides = [
                    jnp.where(time8[k : k + 1, at : at + GRAIN] >= start, beam8[k : k + 1, at : at + GRAIN], 0.0)
                    for at in (0, GRAIN)
                ]
                left.append(jnp.concatenate(sides, 1))
            left = jnp.concatenate(left, 0).astype(BF16)
            for part, factor in ((0, dft8), (1, step8)):
                folded = dot(left, fold_ref[:, part * 2 * FREQS : part * 2 * FREQS + 2 * FREQS])
                sums = [acc_s[:, k * FREQS : k * FREQS + FREQS] for k in range(3 * part, 3 * part + 3)]
                for k in range(size):
                    rows = slice(k * BINS, k * BINS + BINS)
                    real, imag = folded[rows, :FREQS], folded[rows, FREQS:]
                    for n, value in enumerate((real + imag, real, imag)):
                        sums[n] = sums[n] + value * factor[k : k + 1, n * FREQS : n * FREQS + FREQS]
                for n in range(3):
                    acc_s[:, (3 * part + n) * FREQS : (3 * part + n + 1) * FREQS] = sums[n]

        def pair_step(pair, inner):
            fold(2 * GROUP * pair, GROUP)
            fold(2 * GROUP * pair + GROUP, GROUP)
            return inner

        def one_step(_, inner):
            fold(pairs * 2 * GROUP, GROUP)
            return inner

        def half_step(_, inner):
            fold(pairs * 2 * GROUP + rest // 2 * GROUP, GROUP // 2)
            return inner

        eights = (jnp.minimum(count - batch * SLOTS, SLOTS) + 7) // 8
        pairs = eights // 4
        rest = eights - 4 * pairs
        lax.fori_loop(0, pairs, pair_step, 0)
        lax.fori_loop(0, rest // 2, one_step, 0)
        lax.fori_loop(0, rest % 2, half_step, 0)

    fold_batch(jnp.int32(0), (place_ref[:, 0:1], ends_ref[:, 0:1], starts_ref[...], gbeam_ref[...]))

    def batch_step(batch, carry):
        own_plan = plan_half(own_ref, core, jnp.zeros((1, 1), F32))
        fold_batch(batch, slots_half((batch * SLOTS).astype(F32), own_plan, own_ref))
        return carry

    lax.fori_loop(1, (count + SLOTS - 1) // SLOTS, batch_step, 0)
    since = acc_s[...]
    each = since - jnp.concatenate([since[1:], jnp.zeros((1, 6 * FREQS), F32)], 0)
    both, real, imag, both2, real2, imag2 = (each[:, k * FREQS : k * FREQS + FREQS] for k in range(6))
    short = dot(jnp.concatenate([both2 - imag2, both2 + real2], 1).astype(BF16), short_ref[...])
    out_ref[0] = (both - imag + short[:, :FREQS]) * SCALE
    out_ref[1] = (both + real + short[:, FREQS:]) * SCALE


def near(*values):
    return [pltpu.with_memory_space_constraint(v, pltpu.VMEM) for v in values]


def call(kernel, outs, values, scratch=(), mib=8, us=1.0):
    one = not isinstance(outs, (tuple, list))
    space = pl.BlockSpec(memory_space=pltpu.VMEM)
    return pl.pallas_call(
        kernel,
        out_shape=outs if one else tuple(outs),
        in_specs=[space] * len(values),
        out_specs=space if one else (space,) * len(outs),
        scratch_shapes=list(scratch),
        compiler_params=pltpu.CompilerParams(vmem_limit_bytes=mib << 20),
        cost_estimate=pl.CostEstimate(flops=int(us * 5e8), bytes_accessed=1 << 20, transcendentals=0),
    )(*near(*values))


HALF_Z = pltpu.VMEM((HALF, 2 * FREQS), BF16)


def make_tables(ids):
    given = tables()
    made = call(
        functools.partial(table_kernel, ids),
        (
            pltpu.VMEM((2 * GRAIN, 4 * FREQS), BF16),
            pltpu.VMEM((2, 2 * GRAIN, 2 * FREQS), BF16),
            pltpu.VMEM((2 * FREQS, 2 * FREQS), BF16),
            pltpu.VMEM((128, 2 * FREQS), BF16),
            pltpu.VMEM((GRAIN, 2 * FREQS), BF16),
            pltpu.VMEM((2 * GRAIN, 2 * FREQS), BF16),
            pltpu.VMEM((SPAN, 2 * FREQS), F32),
        ),
        [given[k] for k in ("base", "turn", "fold2", "start", "back", "step2", "phase")],
        [pltpu.VMEM((2 * GRAIN, 2 * FREQS), BF16)],
        us=3.0,
    )
    return made


def spectrum(own, other, ids, made):
    fold, step, short, phases, side, step2, phase = made
    half = call(
        functools.partial(half_kernel, ids),
        (
            HALF_Z,
            pltpu.VMEM((8, 128), F32),
            pltpu.VMEM((SLOTS, 128), F32),
            pltpu.VMEM((SLOTS, 128), F32),
            pltpu.VMEM((128, 128), F32),
            pltpu.VMEM((SLOTS, 2 * GRAIN), F32),
        ),
        (own, step, phase),
        us=1.0,
    )
    scratch = [
        HALF_Z,
        pltpu.VMEM((SLOTS, 3 * FREQS), F32),
        pltpu.VMEM((SLOTS, 3 * FREQS), F32),
        pltpu.VMEM((SLOTS, 2 * GRAIN), F32),
        pltpu.VMEM((SLOTS, 2 * GRAIN), F32),
        pltpu.VMEM((SLOTS // GROUP, BINS, 128), F32),
        pltpu.VMEM((BINS, 6 * FREQS), F32),
    ]
    return call(
        functools.partial(spectrum_kernel, ids),
        jax.ShapeDtypeStruct((2, BINS, FREQS), F32),
        (own, other, *half, fold, step, short, phases, side, step2, phase),
        scratch,
        mib=16,
        us=5.0,
    )


def front(voltages, beam_weights, bins):
    far = pl.BlockSpec(memory_space=pltpu.HBM)
    close = pl.BlockSpec(memory_space=pltpu.VMEM)
    return pl.pallas_call(
        front_kernel,
        out_shape=(
            pltpu.VMEM((DISH_WAYS, 2 * PER_BLOCK, GRAIN), F32),
            pltpu.VMEM((CHIPS, VISITS, GRAIN), BF16),
        ),
        in_specs=[far] * 3,
        out_specs=(close, close),
        scratch_shapes=[
            pltpu.VMEM(voltages.shape, BF16),
            pltpu.VMEM(beam_weights.shape, BF16),
            pltpu.VMEM(bins.shape, jnp.int32),
            pltpu.VMEM((72, GRAIN), F32),
            pltpu.VMEM((72, GRAIN), F32),
            pltpu.SemaphoreType.DMA((len(PIECES) + 2,)),
        ],
        compiler_params=pltpu.CompilerParams(vmem_limit_bytes=8 << 20),
        cost_estimate=pl.CostEstimate(flops=1 << 20, bytes_accessed=1 << 20, transcendentals=0),
        name="front",
    )(*(pltpu.with_memory_space_constraint(v, pltpu.HBM) for v in (voltages, beam_weights, bins)))


def steps(voltages, beam_weights, phase_bins):
    def ids():
        core = lax.axis_index("core")
        owner = (lax.axis_index("z") * 2 + lax.axis_index("xh")) * 2 + core
        return owner, lax.axis_index("y") * 2 + lax.axis_index("xl"), core

    made = make_tables(ids)
    partial_beam, visits = front(voltages, beam_weights, phase_bins.reshape(PER_BLOCK, GRAIN))
    parts = lax.all_to_all(partial_beam, ("xl", "y"), 0, 0, tiled=True)
    packed = call(pack_kernel, pltpu.VMEM((CHIPS, ROWS, GRAIN), BF16), (parts, visits), us=0.3)
    own = lax.all_to_all(packed, ("xh", "z"), 0, 0, tiled=True)
    other = lax.ppermute(own, "core", [(0, 1), (1, 0)])
    return jnp.transpose(spectrum(own, other, ids, made), (2, 0, 1))


def solution(mesh):
    split = jax.sharding.Mesh(mesh.devices.reshape(8, 2, 2, 4, 2), ("z", "xh", "core", "y", "xl"))
    time, dish = ("z", "xh", "core"), ("y", "xl")
    return jax.shard_map(
        steps,
        mesh=split,
        in_specs=(P(None, dish, time), P(None, dish), P(time)),
        out_specs=P(dish, None, time),
        check_vma=False,
    )
```
